32 devices in a mesh: dp: 4 (over x, core), ctx: 4 (over z), tensor: 2 (over y).
Axes of the slice: x: 2, y: 2, z: 4, core: 2. Of those that a mesh axis runs over, the one named last changes fastest.
Arguments:
- inputs: bfloat16 [8192, 768], P(('dp', 'ctx')), may hold values from -6 to 6
- segments: int32 [4, 2048], P('dp', 'ctx'), may hold values from 0 to 7, never falling along the last dimension, each value on 1 to 1536 neighbouring positions
- query_proj: bfloat16 [768, 768], P(None, 'tensor'), may hold values from -0.4375 to 0.4375
- key_proj: bfloat16 [768, 768], P(None, 'tensor'), may hold values from -0.21875 to 0.21875
- value_proj: bfloat16 [768, 768], P(None, 'tensor'), may hold values from -0.21875 to 0.21875
- query_bias: bfloat16 [768], P('tensor'), may hold values from -3 to 3
- value_bias: bfloat16 [768], P('tensor'), may hold values from -0.59765625 to 0.59765625
- output_proj: bfloat16 [768, 768], P('tensor'), may hold values from -0.875 to 0.875
- output_bias: bfloat16 [768], replicated, may hold values from -1.1953125 to 1.1953125
- attn_gain: bfloat16 [768], replicated, may hold values from 0.5 to 1.5
- attn_shift: bfloat16 [768], replicated, may hold values from -1.1953125 to 1.1953125
- expand_proj: bfloat16 [768, 3072], P(None, 'tensor'), may hold values from -0.21875 to 0.21875
- expand_bias: bfloat16 [3072], P('tensor'), may hold values from -3 to 3
- shrink_proj: bfloat16 [3072, 768], P('tensor'), may hold values from -0.109375 to 0.109375
- shrink_bias: bfloat16 [768], replicated, may hold values from -1.1953125 to 1.1953125
- final_gain: bfloat16 [768], replicated, may hold values from 0.5 to 1.5
- final_shift: bfloat16 [768], replicated, may hold values from -1.1953125 to 1.1953125
- cotangent: bfloat16 [8192, 768], P(('dp', 'ctx')), may hold values from -6 to 6
Outputs:
- output: bfloat16 [8192, 768], P(('dp', 'ctx'))
- input_grad: float32 [8192, 768], P(('dp', 'ctx'))
- query_grad: float32 [768, 768], P(None, 'tensor')
- key_grad: float32 [768, 768], P(None, 'tensor')
- value_grad: float32 [768, 768], P(None, 'tensor')
- qbias_grad: float32 [768], P('tensor')
- vbias_grad: float32 [768], P('tensor')
- oproj_grad: float32 [768, 768], P('tensor')
- obias_grad: float32 [768], replicated
- again_grad: float32 [768], replicated
- ashift_grad: float32 [768], replicated
- expand_grad: float32 [768, 3072], P(None, 'tensor')
- ebias_grad: float32 [3072], P('tensor')
- shrink_grad: float32 [3072, 768], P('tensor')
- sbias_grad: float32 [768], replicated
- fgain_grad: float32 [768], replicated
- fshift_grad: float32 [768], replicated
The draws below stay inside these ranges and needn't reach their ends.
Inputs may be any that keep to these rules, and one draw needn't show every extreme that they name: `segments`: along each sequence the ids never fall; every id from 0 to 7 names one document of the sequence, and one document has 1536 tokens.
All inputs are finite; a program needn't handle non-finite values.
Results may differ from the reference program's by a relative error of at most 0.019.
Values may be sent and summed in bfloat16 or wider, within the bound.
A program may use at most 256 MiB of HBM per device.

```python
import math
import jax
import jax.numpy as jnp
import numpy as np
from jax import lax

D = 768
HEADS = 12
HEAD_DIM = 64
FF = 3072
SEQS = 4
LENGTH = 2048
TOKENS = 8192
N_CTX = 4


def levels(own_key, shape, shards, low, top_value):
    loudness, own = 1.0, jax.random.fold_in(own_key, 6)
    for axis_at, parts in shards:
        heights = jnp.exp(jax.random.uniform(jax.random.fold_in(own, axis_at), (parts,), jnp.float32, low / len(shards), top_value / len(shards)))
        loudness = loudness * jnp.repeat(heights, shape[axis_at] // parts).reshape([-1 if axis == axis_at else 1 for axis in range(len(shape))])
    return loudness


def profile(number_of, total, most, lean):
    portions = [(1 << 20) // math.isqrt(grade ** lean) + 1 for grade in range(2, number_of + 1)]
    surplus, given = total - most - (number_of - 1), [1] * (number_of - 1)
    while surplus > 0:
        free = [i for i in range(number_of - 1) if given[i] < most]
        mass, left = sum([portions[i] for i in free]), surplus
        for i in free:
            more = min(most - given[i], max(1, left * portions[i] // mass), surplus)
            given[i] = given[i] + more
            surplus = surplus - more
    return np.array([most] + given)


def ragged_sizes(key, amount, total, bound, skew):
    if amount == 2:
        one = jax.random.randint(key, (), max(1, total - bound), min(bound, total - 1) + 1)
        return jnp.stack([one, total - one])
    sizes = jnp.asarray(profile(amount, total, bound, skew), jnp.int32)
    couples = (amount - 1) // 2
    donor, receiver = sizes[1:1 + 2 * couples:2], sizes[2:2 + 2 * couples:2]
    slack = jnp.minimum(donor - 1, bound - receiver)
    shifted = jax.random.randint(jax.random.fold_in(key, 1), (couples,), 0, 1 << 20) % (slack + 1)
    sizes = sizes.at[1:1 + 2 * couples:2].set(donor - shifted).at[2:2 + 2 * couples:2].set(receiver + shifted)
    return sizes[jax.random.permutation(jax.random.fold_in(key, 2), amount)]


def gaussian(own_key, dims, scale, limit, split=(), held_as=jnp.bfloat16):
    loudness = levels(own_key, dims, split, -0.22, 0.18) if split else 1.0
    entries = jax.random.normal(own_key, dims, jnp.float32) * scale * loudness
    return jnp.minimum(jnp.maximum(entries, -limit), limit).astype(held_as)


def setup_inputs(seed: int = 0) -> dict:
    streams_of = jax.random.split(jax.random.key(seed), 19)
    inputs = gaussian(streams_of[0], (TOKENS, D), 1.0, 6.0, ((0, 16),))
    segments = jax.vmap(lambda own: jnp.searchsorted(jnp.cumsum(ragged_sizes(own, 2 * N_CTX, LENGTH, 3 * LENGTH // 4, 2)), jnp.arange(LENGTH), side="right"))(jax.random.split(streams_of[1], SEQS)).reshape((SEQS, LENGTH)).astype(jnp.int32)
    query_proj = gaussian(streams_of[2], (D, D), (D // 4) ** -0.5, 0.4375, ((1, 2),))
    key_proj = gaussian(streams_of[3], (D, D), D ** -0.5, 0.21875, ((1, 2),))
    value_proj = gaussian(streams_of[4], (D, D), D ** -0.5, 0.21875, ((1, 2),))
    query_bias = gaussian(streams_of[5], (D,), 0.5, 3.0, ((0, 2),))
    value_bias = gaussian(streams_of[6], (D,), 0.1, 0.59765625, ((0, 2),))
    output_proj = gaussian(streams_of[7], (D, D), (D // 16) ** -0.5, 0.875, ((0, 2),))
    output_bias = gaussian(streams_of[8], (D,), 0.2, 1.1953125)
    attn_gain = jnp.clip(1.0 + 0.1 * jax.random.normal(streams_of[9], (D,), jnp.float32), 0.5, 1.5).astype(jnp.bfloat16)
    attn_shift = gaussian(streams_of[10], (D,), 0.2, 1.1953125)
    expand_proj = gaussian(streams_of[11], (D, FF), D ** -0.5, 0.21875, ((1, 2),))
    expand_bias = gaussian(streams_of[12], (FF,), 0.5, 3.0, ((0, 2),))
    shrink_proj = gaussian(streams_of[13], (FF, D), FF ** -0.5, 0.109375, ((0, 2),))
    shrink_bias = gaussian(streams_of[14], (D,), 0.2, 1.1953125)
    final_gain = jnp.clip(1.0 + 0.1 * jax.random.normal(streams_of[15], (D,), jnp.float32), 0.5, 1.5).astype(jnp.bfloat16)
    final_shift = gaussian(streams_of[16], (D,), 0.2, 1.1953125)
    cotangent = gaussian(streams_of[17], (TOKENS, D), 1.0, 6.0, ((0, 16),))
    return {"inputs": inputs, "segments": segments, "query_proj": query_proj, "key_proj": key_proj, "value_proj": value_proj, "query_bias": query_bias, "value_bias": value_bias, "output_proj": output_proj, "output_bias": output_bias, "attn_gain": attn_gain, "attn_shift": attn_shift, "expand_proj": expand_proj, "expand_bias": expand_bias, "shrink_proj": shrink_proj, "shrink_bias": shrink_bias, "final_gain": final_gain, "final_shift": final_shift, "cotangent": cotangent}


@jax.custom_vjp
def low(v):
    return lax.optimization_barrier(v.astype(jnp.bfloat16)).astype(jnp.float32)

@jax.custom_vjp
def low_back(v):
    return v

def low_keep(v):
    return (low(v), None)

def low_pass(kept, grad):
    return (grad,)

def back_keep(v):
    return (v, None)

def back_low(kept, grad):
    return (low(grad),)
low.defvjp(low_keep, low_pass)
low_back.defvjp(back_keep, back_low)
norm_eps = 1e-12
masked = -1e+30

def product(left, right):
    return jnp.dot(left, right, precision=lax.Precision.HIGHEST, preferred_element_type=jnp.float32)

def layer_norm(values, gain, shift):
    centred = values - lax.optimization_barrier(jnp.mean(values, axis=-1, keepdims=True))
    spread = lax.optimization_barrier(jnp.mean(centred * centred, axis=-1, keepdims=True))
    return centred * lax.rsqrt(spread + norm_eps) * gain + shift

def attend(queries, keys, values, seg_ids):
    length = queries.shape[0]
    block_rows = math.gcd(length, 512)
    scale = HEAD_DIM ** (-0.5)
    key_heads = keys.reshape(length, HEADS, HEAD_DIM)
    value_heads = values.reshape(length, HEADS, HEAD_DIM)
    query_blocks = queries.reshape(length // block_rows, block_rows, HEADS, HEAD_DIM)
    seg_blocks = seg_ids.reshape(length // block_rows, block_rows)

    def one_block(pair):
        query_blk, seg_blk = pair
        scores = jnp.einsum('qhd,khd->hqk', query_blk, key_heads, precision=lax.Precision.HIGHEST) * scale
        scores = low_back(scores)
        same_seg = (seg_blk[:, None] == seg_ids[None, :])[None]
        scores = jnp.where(same_seg, scores, masked)
        row_max = lax.optimization_barrier(jnp.max(scores, axis=-1, keepdims=True))
        exp_scores = jnp.where(same_seg, jnp.exp(scores - row_max), 0.0)
        attn_probs = low(exp_scores / lax.optimization_barrier(jnp.sum(exp_scores, axis=-1, keepdims=True)))
        mixed = jnp.einsum('hqk,khd->qhd', attn_probs, value_heads, precision=lax.Precision.HIGHEST)
        return mixed.reshape(block_rows, HEADS * HEAD_DIM)
    blocks_out = lax.map(jax.checkpoint(one_block), (query_blocks, seg_blocks))
    return blocks_out.reshape(length, HEADS * HEAD_DIM)

def layer(seq_x, seq_ids, query_proj, key_proj, value_proj, query_bias, value_bias, output_proj, output_bias, attn_gain, attn_shift, expand_proj, expand_bias, shrink_proj, shrink_bias, final_gain, final_shift):
    queries = low_back(low(product(seq_x, query_proj) + query_bias))
    keys = low_back(low(product(seq_x, key_proj)))
    values = low_back(low(product(seq_x, value_proj) + value_bias))
    attended = low_back(low(attend(queries, keys, values, seq_ids)))
    first = layer_norm(seq_x + low_back(product(attended, output_proj)) + output_bias, attn_gain, attn_shift)
    pre_act = low_back(product(low(first), expand_proj) + expand_bias)
    hidden = low(jax.nn.gelu(pre_act, approximate=False))
    second = first + low_back(product(hidden, shrink_proj)) + shrink_bias
    return layer_norm(second, final_gain, final_shift)

def reference(inputs, segments, query_proj, key_proj, value_proj, query_bias, value_bias, output_proj, output_bias, attn_gain, attn_shift, expand_proj, expand_bias, shrink_proj, shrink_bias, final_gain, final_shift, cotangent):
    params = tuple((weight.astype(jnp.float32) for weight in (query_proj, key_proj, value_proj, query_bias, value_bias, output_proj, output_bias, attn_gain, attn_shift, expand_proj, expand_bias, shrink_proj, shrink_bias, final_gain, final_shift)))
    seq_inputs = inputs.astype(jnp.float32).reshape(SEQS, LENGTH, D)
    seq_cotangent = cotangent.astype(jnp.float32).reshape(SEQS, LENGTH, D)

    def one_sequence(totals, scan_item):
        seq_x, seq_ids, seq_grad = scan_item

        def apply_layer(seq_in, *weights):
            return layer(seq_in, seq_ids, *weights)
        result, pullback = jax.vjp(apply_layer, seq_x, *params)
        gradients = pullback(seq_grad)
        totals = tuple((running + fresh for running, fresh in zip(totals, gradients[1:])))
        return (totals, (result.astype(jnp.bfloat16), gradients[0]))
    zero_init = tuple((jnp.zeros_like(weight) for weight in params))
    totals, stacked = lax.scan(one_sequence, zero_init, (seq_inputs, segments, seq_cotangent))
    seq_out, seq_back = stacked
    return (seq_out.reshape(TOKENS, D), seq_back.reshape(TOKENS, D), totals[0], totals[1], totals[2], totals[3], totals[4], totals[5], totals[6], totals[7], totals[8], totals[9], totals[10], totals[11], totals[12], totals[13], totals[14])
```

```python
import functools

import jax
import jax.numpy as jnp
from jax import lax
from jax.sharding import PartitionSpec as P

HEAD_DIM = 64


norm_eps = 1e-12
masked = -1e30
contract_rows = (((0,), (0,)), ((), ()))
contract_cols = (((1,), (1,)), ((), ()))


def matmul(left, right):
    return jnp.dot(left, right, preferred_element_type=jnp.float32)


def inner_rows(left, right):
    return lax.dot_general(left, right, contract_rows, preferred_element_type=jnp.float32)


def inner_cols(left, right):
    return lax.dot_general(left, right, contract_cols, preferred_element_type=jnp.float32)


def norm_forward(values, gain, shift):
    centred = values - jnp.mean(values, axis=-1, keepdims=True)
    spread = jnp.mean(centred * centred, axis=-1, keepdims=True)
    recip = lax.rsqrt(spread + norm_eps)
    normed = centred * recip
    return (normed * gain + shift, normed, recip)


def norm_backward(upstream, normed, recip, gain):
    scaled = upstream * gain
    centred = (
        scaled
        - jnp.mean(scaled, axis=-1, keepdims=True)
        - normed * jnp.mean(scaled * normed, axis=-1, keepdims=True)
    )
    return (centred * recip, jnp.sum(upstream * normed, axis=0), jnp.sum(upstream, axis=0))


def cross_scores(left, right):
    return inner_cols(left, right)


def spread_apply(weights_in, right):
    return matmul(weights_in, right)


def spread_transpose(weights_in, left):
    return inner_rows(weights_in, left)


def swap_tensor(part):
    return lax.ppermute(part, "tensor", [(0, 1), (1, 0)])


def pair_sum(part):
    low = part.astype(jnp.bfloat16)
    return low.astype(jnp.float32) + swap_tensor(low).astype(jnp.float32)


def partners(size, bit):
    return [(i, i ^ bit) for i in range(size)]


def stages(sizes):
    for name in ("dp", "ctx"):
        bit = 1
        while bit < sizes[name]:
            yield name, bit
            bit *= 2


def reduce_rows(sizes, total):
    steps = list(stages(sizes))
    for name, bit in steps:
        half = total.shape[0] // 2
        upper = (lax.axis_index(name) // bit) % 2 == 1
        first, last = total[:half], total[half:]
        kept = jnp.where(upper, last, first)
        sent = jnp.where(upper, first, last).astype(jnp.bfloat16)
        total = kept + lax.ppermute(sent, name, partners(sizes[name], bit)).astype(jnp.float32)
    low = total.astype(jnp.bfloat16)
    for name, bit in reversed(steps):
        upper = (lax.axis_index(name) // bit) % 2 == 1
        other = lax.ppermute(low, name, partners(sizes[name], bit))
        low = jnp.concatenate([jnp.where(upper, other, low), jnp.where(upper, low, other)], axis=0)
    return low.astype(jnp.float32)


def gather_ctx(count, block):
    pieces = [block]
    for shift in range(1, count):
        pieces.append(lax.ppermute(block, "ctx", [(i, (i + shift) % count) for i in range(count)]))
    here = lax.axis_index("ctx")
    rows = block.shape[0]
    whole = jnp.zeros((count * rows,) + block.shape[1:], block.dtype)
    for shift, piece in enumerate(pieces):
        whole = lax.dynamic_update_slice_in_dim(whole, piece, ((here - shift) % count) * rows, 0)
    return whole


def scatter_ctx(count, whole):
    here = lax.axis_index("ctx")
    rows = whole.shape[0] // count
    total = lax.dynamic_slice_in_dim(whole, here * rows, rows, 0).astype(jnp.float32)
    for shift in range(1, count):
        piece = lax.dynamic_slice_in_dim(whole, ((here + shift) % count) * rows, rows, 0)
        total = total + lax.ppermute(
            piece.astype(jnp.bfloat16), "ctx", [(i, (i + shift) % count) for i in range(count)]
        ).astype(jnp.float32)
    return total


def body(
    sizes,
    inputs,
    segments,
    query_proj,
    key_proj,
    value_proj,
    query_bias,
    value_bias,
    output_proj,
    output_bias,
    attn_gain,
    attn_shift,
    expand_proj,
    expand_bias,
    shrink_proj,
    shrink_bias,
    final_gain,
    final_shift,
    cotangent,
):
    head_count = query_proj.shape[1] // HEAD_DIM
    scale = HEAD_DIM ** (-0.5)
    seg_local = segments[0]
    queries = (matmul(inputs, query_proj) + query_bias.astype(jnp.float32)).astype(jnp.bfloat16)
    keys = matmul(inputs, key_proj).astype(jnp.bfloat16)
    values = (matmul(inputs, value_proj) + value_bias.astype(jnp.float32)).astype(jnp.bfloat16)
    count = sizes["ctx"]
    both = gather_ctx(count, jnp.concatenate([keys, values], axis=1))
    all_keys, all_values = both[:, : keys.shape[1]], both[:, keys.shape[1] :]
    key_ids = gather_ctx(count, seg_local.astype(jnp.bfloat16)[:, None])[:, 0]
    query_segs = seg_local.astype(jnp.float32)
    key_segs = key_ids.astype(jnp.float32)
    same_seg = query_segs[:, None] == key_segs[None, :]

    def split_heads(matrix):
        return jnp.swapaxes(matrix.reshape(matrix.shape[0], head_count, HEAD_DIM), 0, 1)

    def join_heads(stack):
        return jnp.swapaxes(stack, 0, 1).reshape(stack.shape[1], head_count * HEAD_DIM)

    query_heads = split_heads(queries)
    key_heads = split_heads(all_keys)
    value_heads = split_heads(all_values)

    def head_forward(state, triple):
        query_head, key_head, value_head = triple
        scores = cross_scores(query_head, key_head) * scale
        scores = jnp.where(same_seg, scores, masked)
        row_max = jnp.max(scores, axis=1, keepdims=True)
        exp_scores = jnp.where(same_seg, jnp.exp(scores - row_max), 0.0)
        row_sum = jnp.sum(exp_scores, axis=1, keepdims=True)
        attn_probs = (exp_scores / row_sum).astype(jnp.bfloat16)
        mixed = spread_apply(attn_probs, value_head)
        return (state, (mixed, row_max + jnp.log(row_sum)))

    mixed_heads, log_sums = lax.scan(head_forward, None, (query_heads, key_heads, value_heads))[1]
    attended = join_heads(mixed_heads).astype(jnp.bfloat16)
    attn_total = pair_sum(matmul(attended, output_proj))
    attn_gain_f = attn_gain.astype(jnp.float32)
    first, first_normed, first_recip = norm_forward(
        inputs.astype(jnp.float32) + attn_total + output_bias.astype(jnp.float32),
        attn_gain_f,
        attn_shift.astype(jnp.float32),
    )
    first_low = first.astype(jnp.bfloat16)
    pre_act = matmul(first_low, expand_proj) + expand_bias.astype(jnp.float32)
    activated, gelu_back = jax.vjp(lambda pre_in: jax.nn.gelu(pre_in, approximate=False), pre_act)
    hidden = activated.astype(jnp.bfloat16)
    feed_total = pair_sum(matmul(hidden, shrink_proj))
    second = first + feed_total + shrink_bias.astype(jnp.float32)
    final_gain_f = final_gain.astype(jnp.float32)
    output, second_normed, second_recip = norm_forward(
        second, final_gain_f, final_shift.astype(jnp.float32)
    )
    upstream = cotangent.astype(jnp.float32)
    grad_second, fgain_grad, fshift_grad = norm_backward(
        upstream, second_normed, second_recip, final_gain_f
    )
    sbias_grad = jnp.sum(grad_second, axis=0)
    grad_second_low = grad_second.astype(jnp.bfloat16)
    shrink_grad = inner_rows(hidden, grad_second_low)
    grad_act = inner_cols(grad_second_low, shrink_proj)
    grad_pre = gelu_back(grad_act)[0].astype(jnp.bfloat16)
    ebias_grad = jnp.sum(grad_pre.astype(jnp.float32), axis=0)
    expand_grad = inner_rows(first_low, grad_pre)
    grad_first = grad_second + pair_sum(inner_cols(grad_pre, expand_proj))
    grad_mix, again_grad, ashift_grad = norm_backward(
        grad_first, first_normed, first_recip, attn_gain_f
    )
    obias_grad = jnp.sum(grad_mix, axis=0)
    grad_mix_low = grad_mix.astype(jnp.bfloat16)
    oproj_grad = inner_rows(attended, grad_mix_low)
    grad_attended = inner_cols(grad_mix_low, output_proj).astype(jnp.bfloat16)
    grad_heads = split_heads(grad_attended)

    def head_backward(state, group):
        query_head, key_head, value_head, grad_head, log_sum = group
        scores = cross_scores(query_head, key_head) * scale
        attn_probs = jnp.where(same_seg, jnp.exp(scores - log_sum), 0.0)
        grad_probs = cross_scores(grad_head, value_head)
        row_dot = jnp.sum(attn_probs * grad_probs, axis=1, keepdims=True)
        grad_scores = (attn_probs * (grad_probs - row_dot)).astype(jnp.bfloat16)
        grad_query = spread_apply(grad_scores, key_head) * scale
        grad_key = spread_transpose(grad_scores, query_head) * scale
        grad_value = spread_transpose(attn_probs.astype(jnp.bfloat16), grad_head)
        return (state, (grad_query, grad_key, grad_value))

    query_back, key_back, value_back = lax.scan(
        head_backward, None, (query_heads, key_heads, value_heads, grad_heads, log_sums)
    )[1]
    grad_queries = join_heads(query_back).astype(jnp.bfloat16)
    both_sum = scatter_ctx(
        count, jnp.concatenate([join_heads(key_back), join_heads(value_back)], axis=1)
    )
    key_sum, value_sum = both_sum[:, : keys.shape[1]], both_sum[:, keys.shape[1] :]
    grad_keys = key_sum.astype(jnp.bfloat16)
    grad_values = value_sum.astype(jnp.bfloat16)
    qbias_grad = jnp.sum(grad_queries.astype(jnp.float32), axis=0)
    vbias_grad = jnp.sum(grad_values.astype(jnp.float32), axis=0)
    query_grad = inner_rows(inputs, grad_queries)
    key_grad = inner_rows(inputs, grad_keys)
    value_grad = inner_rows(inputs, grad_values)
    back_terms = (
        inner_cols(grad_queries, query_proj)
        + inner_cols(grad_keys, key_proj)
        + inner_cols(grad_values, value_proj)
    )
    input_grad = grad_mix + pair_sum(back_terms)
    expand_grad = reduce_rows(sizes, expand_grad)
    shrink_grad = reduce_rows(sizes, shrink_grad)
    oproj_grad = reduce_rows(sizes, oproj_grad)
    joined = reduce_rows(sizes, jnp.concatenate([query_grad, key_grad, value_grad], axis=1))
    query_grad, key_grad, value_grad = jnp.split(joined, 3, axis=1)
    small = [qbias_grad, vbias_grad, obias_grad, again_grad, ashift_grad, ebias_grad, sbias_grad, fgain_grad, fshift_grad]
    widths = [v.shape[0] for v in small]
    packed = jnp.concatenate(small).reshape(-1, 128)
    fold = packed.shape[0]
    packed = jnp.pad(packed, ((0, -fold % 128), (0, 0)))
    flat = reduce_rows(sizes, packed)[:fold].reshape(-1)
    cuts = []
    at = 0
    for width in widths:
        cuts.append(flat[at : at + width])
        at += width
    qbias_grad, vbias_grad, obias_grad, again_grad, ashift_grad, ebias_grad, sbias_grad, fgain_grad, fshift_grad = cuts
    return (
        output.astype(jnp.bfloat16),
        input_grad,
        query_grad,
        key_grad,
        value_grad,
        qbias_grad,
        vbias_grad,
        oproj_grad,
        obias_grad,
        again_grad,
        ashift_grad,
        expand_grad,
        ebias_grad,
        shrink_grad,
        sbias_grad,
        fgain_grad,
        fshift_grad,
    )


def solution(mesh):
    in_specs = (
        P(("dp", "ctx"), None),
        P("dp", "ctx"),
        P(None, "tensor"),
        P(None, "tensor"),
        P(None, "tensor"),
        P("tensor"),
        P("tensor"),
        P("tensor", None),
        P(),
        P(),
        P(),
        P(None, "tensor"),
        P("tensor"),
        P("tensor", None),
        P(),
        P(),
        P(),
        P(("dp", "ctx"), None),
    )
    out_specs = (
        P(("dp", "ctx"), None),
        P(("dp", "ctx"), None),
        P(None, "tensor"),
        P(None, "tensor"),
        P(None, "tensor"),
        P("tensor"),
        P("tensor"),
        P("tensor", None),
        P(),
        P(),
        P(),
        P(None, "tensor"),
        P("tensor"),
        P("tensor", None),
        P(),
        P(),
        P(),
    )
    return jax.shard_map(functools.partial(body, dict(mesh.shape)), mesh=mesh, in_specs=in_specs, out_specs=out_specs, check_vma=False)
```

```python
import functools
import types

import jax
import jax.numpy as jnp
from jax import lax
from jax.experimental import pallas as pl
from jax.experimental.pallas import tpu as pltpu
from jax.sharding import PartitionSpec as P

HEAD_DIM = 64
norm_eps = 1e-12
masked = -1e30
MESH = pl.DeviceIdType.MESH
CORE, XS, YS, Z1, Z2 = range(5)
BF16, F32 = jnp.bfloat16, jnp.float32
INV_SQRT2 = 0.7071067811865476
INV_SQRT_2PI = 0.3989422804014327


def nn(left, right):
    return jnp.dot(left, right, preferred_element_type=F32)


def nt(left, right):
    return lax.dot_general(left, right, (((1,), (1,)), ((), ())), preferred_element_type=F32)


def tn(left, right):
    return lax.dot_general(left, right, (((0,), (0,)), ((), ())), preferred_element_type=F32)


def normalise(values):
    centred = values - jnp.mean(values, axis=-1, keepdims=True)
    spread = jnp.mean(centred * centred, axis=-1, keepdims=True)
    recip = lax.rsqrt(spread + norm_eps)
    return centred * recip, recip


def denormalise(scaled, normed, recip):
    return recip * (
        scaled
        - jnp.mean(scaled, axis=-1, keepdims=True)
        - normed * jnp.mean(scaled * normed, axis=-1, keepdims=True)
    )


def gelu_parts(pre):
    phi_sum = 0.5 + 0.5 * lax.erf(pre * INV_SQRT2)
    slope = phi_sum + pre * (INV_SQRT_2PI * jnp.exp(-0.5 * pre * pre))
    return pre * phi_sum, slope


def column_sum(values):
    return jnp.sum(values, axis=0, keepdims=True)


class Shapes:
    def __init__(self, mesh, tokens, width, heads_width, units):
        self.nd, self.nc = mesh["dp"], mesh["ctx"]
        self.nx = self.nd // 2
        self.tokens, self.mine = tokens, tokens // 2
        self.width, self.hw, self.units = width, heads_width, units
        self.pairs = heads_width // 128


def make_kernel(sh, names, orders):
    T, TM, D, W, F = sh.tokens, sh.mine, sh.width, sh.hw, sh.units
    HP = sh.pairs
    TILE = 512
    NTILE = F // TILE
    SLOTS = 4
    PARTS = 2
    PR = TM // PARTS

    def kernel(*refs):
        r = types.SimpleNamespace(**dict(zip(names, refs)))
        send_ref, recv_ref, local_ref = r.send, r.recv, r.local
        d, c, t = lax.axis_index("dp"), lax.axis_index("ctx"), lax.axis_index("tensor")
        core, xpos = lax.rem(d, 2), d // 2
        low_bit, high_bit = lax.rem(c, 2), c // 2
        next_c = c + 1 - 2 * low_bit
        z1_peer, z2_peer = (d, next_c, t), (d, c + 2 - 4 * high_bit, t)
        z3_peer = (d, next_c + 2 - 4 * high_bit, t)
        y_peer = (d, c, 1 - t)
        core_peer = (d + 1 - 2 * core, c, t)
        x_peer = (d + 2 - 4 * xpos, c, t)
        peer_of = {CORE: core_peer, XS: x_peer, YS: y_peer, Z1: z1_peer, Z2: z2_peer}
        bit_of = {CORE: core, XS: xpos, YS: t, Z1: low_bit, Z2: high_bit}
        my_rows = pl.ds(pl.multiple_of(t * TM, TM), TM)
        peer_rows = pl.ds(pl.multiple_of((1 - t) * TM, TM), TM)
        counts = [0, 0]

        def take(kind, k=1):
            at = counts[kind]
            counts[kind] += k
            assert counts[kind] <= (send_ref, local_ref)[kind].shape[0], counts
            return at

        def remote(src, dst, device, at=None):
            at = take(0) if at is None else at
            return pltpu.make_async_remote_copy(
                src_ref=src, dst_ref=dst, send_sem=send_ref.at[at], recv_sem=recv_ref.at[at],
                device_id=device, device_id_type=MESH,
            )

        def local(src, dst):
            return pltpu.make_async_copy(src, dst, local_ref.at[take(1)])

        unsent = []

        def go(copy):
            copy.start()
            unsent.append(copy)

        def wait_sends(*but):
            for copy in unsent:
                if not any(copy is other for other in but):
                    copy.wait_send()
            unsent[:] = but

        loads = types.SimpleNamespace(
            x=local(r.x_in, r.xall.at[0]),
            wk=local(r.wk_in, r.wqkv.at[:, pl.ds(W, W)]),
            wv=local(r.wv_in, r.wqkv.at[:, pl.ds(2 * W, W)]),
            wq=local(r.wq_in, r.wqkv.at[:, pl.ds(0, W)]),
            wo=local(r.wo_in, r.wo.at[pl.ds(0, W)]),
            we=local(r.we_in, r.we.at[0]),
            ws=local(r.ws_in, r.ws.at[0]),
            cot=local(r.cot_in.at[my_rows], r.cot),
        )
        for copy in vars(loads).values():
            copy.start()

        def row(ref):
            return ref[...].astype(F32).reshape(1, ref.shape[0])

        vec = [row(ref) for ref in (r.ob_in, r.ag_in, r.as_in, r.sb_in, r.fg_in, r.fs_in)]
        r.eb[0] = row(r.eb_in)
        r.segs[0] = r.seg_in[...].astype(F32)
        barrier = pltpu.get_barrier_semaphore()
        greeted = [y_peer, core_peer, x_peer, z1_peer, z2_peer, z3_peer]
        for device in greeted:
            pl.semaphore_signal(barrier, inc=1, device_id=device, device_id_type=MESH)
        pl.semaphore_wait(barrier, len(greeted))

        seg_copies = [None] + [
            remote(r.segs.at[0], r.segs.at[k], peer) for k, peer in ((1, z1_peer), (2, z2_peer), (3, z3_peer))
        ]
        eb_copy = remote(r.eb.at[0], r.eb.at[1], y_peer)
        x_rows = [pl.ds(pl.multiple_of(t * TM + k * PR, PR), PR) for k in range(PARTS)]
        x_z, x_y = {}, {}
        for k in range(PARTS):
            mine = x_rows[k]
            x_z[1, k] = remote(r.x_in.at[mine], r.xall.at[1, mine], z1_peer)
            x_z[2, k] = remote(r.x_in.at[mine], r.xall.at[2, mine], z2_peer)
            x_z[3, k] = remote(r.xall.at[2, mine], r.xall.at[3, mine], z1_peer)
            for slot in (1, 2, 3):
                x_y[slot, k] = remote(r.xall.at[slot, mine], r.xall.at[slot, mine], y_peer)
        for slot in (1, 2):
            for k in range(PARTS):
                go(x_z[slot, k])
        for copy in seg_copies[1:]:
            go(copy)
        go(eb_copy)

        def pass_on(slot, k):
            x_z[slot, k].wait_recv()
            go(x_y[slot, k])
            if slot == 2:
                go(x_z[3, k])

        def block_here(slot):
            seg_copies[slot].wait_recv()
            for k in range(PARTS):
                x_y[slot, k].wait_recv()

        chunks = [
            (r.wo_in, r.wo.at[pl.ds(W, W)], W, 0, 1),
            (r.we_in, r.we.at[1], D, 0, 2),
            (r.we_in, r.we.at[1], D, 1, 2),
            (r.ws_in, r.ws.at[1], F, 0, 2),
            (r.ws_in, r.ws.at[1], F, 1, 2),
        ]
        pieces = sh.nd * 2

        def window(chunk, owner):
            rows, part, parts = chunk[2:]
            size = rows // pieces // parts
            return pl.ds(pl.multiple_of(owner * (rows // pieces) + part * size, size), size)

        own_piece, pair_piece = d * 2 + low_bit, d * 2 + 1 - low_bit
        x_d = d + 2 - 4 * xpos
        x_pieces = (x_d * 2 + low_bit, x_d * 2 + 1 - low_bit)
        w_y, w_z, w_x, w_core = [], [], [], []
        for chunk in chunks:
            source, held = chunk[0], chunk[1]

            def move(owner, peer):
                where = window(chunk, owner)
                return remote(held.at[where], held.at[where], peer)

            own = window(chunk, own_piece)
            w_y.append(remote(source.at[own], held.at[own], y_peer))
            w_z.append(move(own_piece, z1_peer))
            w_x.append([move(piece, x_peer) for piece in (own_piece, pair_piece)])
            w_core.append([move(piece, core_peer) for piece in (own_piece, pair_piece) + x_pieces])

        def hop1(i):
            w_y[i].wait_recv()
            go(w_z[i])
            go(w_x[i][0])
            go(w_core[i][0])

        def hop2(i):
            w_z[i].wait_recv()
            go(w_x[i][1])
            go(w_core[i][1])

        def hop3(i):
            for k in range(2):
                w_x[i][k].wait_recv()
                go(w_core[i][2 + k])

        def weights_done(i):
            for copy in w_core[i]:
                copy.wait_recv()

        for i in range(2):
            go(w_y[i])

        kv = r.kv
        value_bias = row(r.vb_in)
        scale = HEAD_DIM ** (-0.5)
        lane = lax.broadcasted_iota(jnp.int32, (T, 128), 1)

        def split_pair(target, p, pair):
            target[2 * p] = jnp.where(lane < 64, pair, 0.0).astype(BF16)
            target[2 * p + 1] = jnp.where(lane < 64, 0.0, pair).astype(BF16)

        def set_keys_values(slot):
            both = nn(r.xall[slot], r.wqkv[:, W:])
            for p in range(HP):
                kv[slot, p, 0] = both[:, p * 128 : (p + 1) * 128].astype(BF16)
                cols = slice(W + p * 128, W + (p + 1) * 128)
                kv[slot, p, 1] = (both[:, cols] + value_bias[:, p * 128 : (p + 1) * 128]).astype(BF16)

        def set_bias(slot):
            seg_keys = jnp.broadcast_to(r.segs[slot], (128, T)).T
            for j in range(T // 128):
                cols = slice(j * 128, (j + 1) * 128)
                r.bias[:, cols] = jnp.where(seg_keys == r.segs[0, :, cols], 0.0, masked)

        loads.x.wait()
        loads.wk.wait()
        loads.wv.wait()
        set_keys_values(0)
        loads.wq.wait()
        queries = (nn(r.xall[0], r.wqkv[:, :W]) + row(r.qb_in)).astype(BF16).astype(F32) * scale
        for p in range(HP):
            split_pair(r.qm, p, queries[:, p * 128 : (p + 1) * 128])

        m_s, l_s, acc = r.m_s, r.l_s, r.acc
        m_s[...] = jnp.full_like(m_s, masked)
        l_s[...] = jnp.zeros_like(l_s)
        acc[...] = jnp.zeros_like(acc)

        def attend(slot, p):
            pair_keys = kv[slot, p, 0]
            pair_values = kv[slot, p, 1].T
            for hh in range(2):
                h = 2 * p + hh
                s = nt(pair_keys, r.qm[h]) + r.bias[...]
                old = m_s[h]
                new = jnp.maximum(old, jnp.max(s, axis=0, keepdims=True))
                e = jnp.exp(s - new)
                alpha = jnp.exp(old - new)
                l_s[h] = l_s[h] * alpha + jnp.sum(e, axis=0, keepdims=True)
                m_s[h] = new
                acc[h] = acc[h] * alpha + nn(pair_values[hh * 64 : hh * 64 + 64], e.astype(BF16))

        def run(body, services=None):
            def step(p, carry):
                body(p)
                for at, fn in (services or {}).items():
                    pl.when(p == at)(fn)
                return carry

            lax.fori_loop(0, HP, step, 0)

        def together(*fns):
            def all_of():
                for fn, arg in fns:
                    fn(*arg)

            return all_of

        set_bias(0)
        run(lambda p: attend(0, p), {0: together((pass_on, (1, 0))), 2: together((pass_on, (1, 1)))})
        hop1(0)
        go(w_y[2])
        for slot in (1, 2, 3):
            if slot == 1:
                r.xt[:, 0:T] = r.xall[0].T
                block_here(1)
                set_keys_values(1)
                set_bias(1)
                run(lambda p: attend(1, p), {0: together((pass_on, (2, 0))), 2: together((hop2, (0,)), (hop1, (1,)))})
                pass_on(2, 1)
                go(w_y[3])
                r.xt[:, T : 2 * T] = r.xall[1].T
            elif slot == 2:
                block_here(2)
                set_keys_values(2)
                set_bias(2)
                run(lambda p: attend(2, p), {0: together((hop2, (1,)), (hop3, (0,))), 2: together((pass_on, (3, 0)))})
                hop1(2)
                go(w_y[4])
                r.xt[:, 2 * T : 3 * T] = r.xall[2].T
                pass_on(3, 1)
                hop3(1)
                hop2(2)
            else:
                block_here(3)
                set_keys_values(3)
                set_bias(3)
        att_at = take(0, HP)

        def att_copy(p):
            cols = pl.ds(p * 128, 128)
            return remote(r.att.at[peer_rows, cols], r.att_o.at[:, cols], y_peer, att_at + p)

        for p in range(HP):
            attend(3, p)
            for h in (2 * p, 2 * p + 1):
                acc[h] = acc[h] / l_s[h]
                m_s[h] = m_s[h] + jnp.log(l_s[h])
            pair = acc[2 * p : 2 * p + 2].reshape(128, T).T
            r.att[:, p * 128 : (p + 1) * 128] = pair.astype(BF16)
            att_copy(p).start()
            if p == 0:
                hop1(3)
            if p == 1:
                hop3(2)
        hop2(3)
        loads.wo.wait()
        weights_done(0)
        loads.cot.wait()

        mix = nn(r.att[my_rows, :], r.wo[0:W, :])
        r.xt[:, 3 * T :] = r.xall[3].T
        for p in range(HP):
            att_copy(p).wait_recv()
        mix = mix + nn(r.att_o[...], r.wo[W : 2 * W, :])
        normed, recip = normalise(r.xall[0, my_rows, :].astype(F32) + mix + vec[0])
        r.n1[...] = normed
        r.r1[...] = jnp.broadcast_to(recip, (TM, 128))
        first = normed * vec[1] + vec[2]
        r.sec[...] = first + vec[3]
        r.fl[my_rows, :] = first.astype(BF16)
        fl_copy = remote(r.fl.at[my_rows], r.fl.at[my_rows], y_peer)
        loads.we.wait()
        loads.ws.wait()
        hop1(4)
        go(fl_copy)


        def tile_cols(j):
            return pl.ds(pl.multiple_of(j * TILE, TILE), TILE)

        def forward_tile(side, j):
            cols = tile_cols(j)
            pre = nn(r.fl[my_rows, :], r.we[side, :, cols]) + r.eb[side, :, cols]
            hidden, slope = gelu_parts(pre)
            hidden = hidden.astype(BF16)
            r.gp[side, :, cols] = slope
            if side == 0:
                r.hid[my_rows, cols] = hidden
            r.sec[...] += nn(hidden, r.ws[side, cols, :])

        def tiles(fn):
            def step(j, carry):
                fn(j)
                return carry

            lax.fori_loop(0, NTILE, step, 0)

        tiles(lambda j: forward_tile(0, j))
        hop3(3)
        hop2(4)
        eb_copy.wait_recv()
        weights_done(1)
        weights_done(2)
        hop3(4)
        weights_done(3)
        weights_done(4)
        tiles(lambda j: forward_tile(1, j))
        normed2, recip2 = normalise(r.sec[...])
        upstream = r.cot[...].astype(F32)
        grad_second = denormalise(upstream * vec[4], normed2, recip2)
        r.gf[...] = grad_second
        r.gs[my_rows, :] = grad_second.astype(BF16)
        gs_copy = remote(r.gs.at[my_rows], r.gs.at[my_rows], y_peer)
        go(gs_copy)
        small = r.small
        small[0:1, :] = column_sum(upstream * normed2)
        small[1:2, :] = column_sum(upstream)
        small[2:3, :] = column_sum(grad_second)
        r.oy[...] = (normed2 * vec[4] + vec[5]).astype(BF16)
        oy_local = local(r.oy, r.out.at[my_rows])
        oy_local.start()


        def backward_tile(side, j):
            cols = tile_cols(j)
            low = (nt(r.gs[my_rows, :], r.ws[side, cols, :]) * r.gp[side, :, cols]).astype(BF16)
            if side == 0:
                r.gpre[my_rows, cols] = low
            r.gf[...] += nt(low, r.we[side, :, cols])

        tiles(lambda j: backward_tile(0, j))
        tiles(lambda j: backward_tile(1, j))
        grad_first = r.gf[...]
        normed = r.n1[...]
        grad_mix = denormalise(grad_first * vec[1], normed, r.r1[:, 0:1])
        r.gmix[...] = grad_mix
        r.gm[my_rows, :] = grad_mix.astype(BF16)
        gm_copy = remote(r.gm.at[my_rows], r.gm.at[my_rows], y_peer)
        go(gm_copy)
        small[3:4, :] = column_sum(grad_first * normed)
        small[4:5, :] = column_sum(grad_first)
        small[5:6, :] = column_sum(grad_mix)

        def rows_at(ref, first_row, rows):
            return ref.at[pl.ds(pl.multiple_of(first_row, rows), rows)]

        class Unit:
            def __init__(self, grad, whole, out, order, bufs):
                self.grad, self.whole, self.out, self.order, self.bufs = grad, whole, out, order, bufs
                self.first, self.rows = [0], [grad.shape[0]]
                for stage in order:
                    self.rows.append(self.rows[-1] // 2)
                    self.first.append(self.first[-1] + bit_of[stage] * self.rows[-1])
                self.down, self.up = {}, {}

            def send(self, k):
                stage, rows = self.order[k], self.rows[k + 1]
                theirs = self.first[k] + (1 - bit_of[stage]) * rows
                self.down[k] = remote(rows_at(self.grad, theirs, rows), self.bufs[k], peer_of[stage])
                go(self.down[k])

            def add(self, k):
                self.down[k].wait_recv()
                rows, first_row = self.rows[k + 1], self.first[k + 1]
                step = next(v for v in (96, 48) if rows % v == 0)

                def tile(i, carry):
                    window = self.grad.at[pl.ds(pl.multiple_of(first_row + i * step, step), step)]
                    there = pl.ds(pl.multiple_of(i * step, step), step)
                    window[...] = (window[...].astype(F32) + self.bufs[k][there, :].astype(F32)).astype(BF16)
                    return carry

                lax.fori_loop(0, rows // step, tile, 0)

            def forward(self, k):
                self.add(k)
                self.send(k + 1)

            def spread(self, k):
                rows, first_row = self.rows[k + 1], self.first[k + 1]
                target = rows_at(self.whole, first_row, rows)
                last = k == len(self.order) - 1
                source = rows_at(self.grad, first_row, rows) if last else target
                self.up[k] = remote(source, target, peer_of[self.order[k]])
                go(self.up[k])
                if last:
                    self.kept = local(source, target)
                    self.kept.start()

            def turn(self):
                k = len(self.order) - 1
                self.add(k)
                self.spread(k)

            def back(self, k):
                if k == len(self.order) - 1:
                    self.kept.wait()
                self.up[k].wait_recv()
                self.spread(k - 1)

            def store(self):
                self.up[0].wait_recv()
                self.kept = local(self.whole, self.out)
                self.kept.start()

        def all_sum(buf, slots, stages):
            copies = [remote(buf.at[k % 2], slots.at[k], peer_of[stage]) for k, stage in enumerate(stages)]

            def start(k):
                copies[k].start()

            def finish(k):
                copies[k].wait()
                total = buf[k % 2] + slots[k]
                if stages[k] == YS:
                    which = lax.broadcasted_iota(jnp.int32, total.shape, 0)
                    total = jnp.where(which < 6, total, buf[k % 2])
                buf[(k + 1) % 2] = total
                if k + 1 < len(stages):
                    start(k + 1)

            return start, finish

        fl_copy.wait_recv()
        gs_copy.wait_recv()

        def other_tile(j):
            cols = tile_cols(j)
            pre = nn(r.fl[peer_rows, :], r.we[0, :, cols]) + r.eb[0, :, cols]
            hidden, slope = gelu_parts(pre)
            r.hid[peer_rows, cols] = hidden.astype(BF16)
            r.gpre[peer_rows, cols] = (nt(r.gs[peer_rows, :], r.ws[0, cols, :]) * slope).astype(BF16)

        tiles(other_tile)
        wait_sends(gm_copy)
        unit_s = Unit(r.ws.at[1], r.ws.at[0], r.us_out, orders[0], (r.us_r0, r.us_r1, r.us_r2, r.us_r3))
        unit_e = Unit(r.we.at[1], r.we.at[0], r.ue_out, orders[1], (r.ue_r0, r.ue_r1, r.ue_r2, r.ue_r3))

        def half_of(which):
            return which * core + (1 - which) * (1 - core)

        def shrink_tiles(which):
            base = half_of(which) * (F // 2)

            def tile(i, carry):
                at = pl.multiple_of(base + i * 384, 128)
                r.ws[1, pl.ds(at, 384), :] = tn(r.hid[:, pl.ds(at, 384)], r.gs[...]).astype(BF16)
                return carry

            lax.fori_loop(0, F // 2 // 384, tile, 0)

        def half_rows(which):
            return pl.ds(pl.multiple_of(half_of(which) * (D // 2), D // 2), D // 2)

        def expand_tiles(which):
            rows = half_rows(which)

            def tile(j):
                cols = tile_cols(j)
                r.we[1, rows, cols] = nn(r.flt[rows, :], r.gpre[:, cols]).astype(BF16)

            tiles(tile)

        shrink_tiles(0)
        unit_s.send(0)
        r.flt[...] = r.fl[...].T
        shrink_tiles(1)
        expand_tiles(0)
        unit_e.send(0)
        unit_s.forward(0)
        expand_tiles(1)
        unit_e.forward(0)
        totals = column_sum(r.gpre[...].astype(F32))
        small[6:7, :] = totals[:, :D]
        small[7:8, :] = totals[:, D:]
        r.es[0] = small[...]
        early_start, early_finish = all_sum(r.es, r.es_r, (YS, CORE, XS, Z1, Z2))
        early_start(0)

        gm_copy.wait_recv()
        grad_att = nt(r.gm[...], r.wo[0:W, :]).astype(BF16).astype(F32)
        flipped = grad_att.T.reshape(2 * HP, 64, T)
        r.delta[...] = jnp.sum(acc[...] * flipped, axis=1, keepdims=True)
        for p in range(HP):
            split_pair(r.dm, p, grad_att[:, p * 128 : (p + 1) * 128])
        acc[...] = jnp.zeros_like(acc)
        oy_send = remote(r.oy, r.out.at[my_rows], y_peer)
        dkv = r.dkv

        def pull(slot, p):
            pair_keys, pair_values = kv[slot, p, 0], kv[slot, p, 1]
            flipped_keys = pair_keys.T
            grad_k = jnp.zeros((T, 128), F32)
            grad_v = jnp.zeros((T, 128), F32)
            for hh in range(2):
                h = 2 * p + hh
                q, g = r.qm[h], r.dm[h]
                probs = jnp.exp(nt(pair_keys, q) + (r.bias[...] - m_s[h]))
                grad_p = nt(pair_values, g)
                grad_v = grad_v + nn(probs.astype(BF16), g)
                ds = (probs * (grad_p - r.delta[h])).astype(BF16)
                grad_k = grad_k + nn(ds, q)
                acc[h] += nn(flipped_keys[hh * 64 : hh * 64 + 64], ds)
            rows = slice(slot * T, (slot + 1) * T)
            dkv[rows, pl.ds(pl.multiple_of(p * 128, 128), 128)] = grad_k.astype(BF16)
            dkv[rows, pl.ds(pl.multiple_of(W + p * 128, 128), 128)] = grad_v.astype(BF16)

        dx_y = [remote(r.xall.at[k, pl.ds(0, TM)], r.dxy.at[k], y_peer) for k in range(SLOTS)]
        dx_z = {
            3: remote(r.xall.at[3, pl.ds(TM, TM)], r.dxz.at[0], z1_peer),
            1: remote(r.xall.at[1, pl.ds(TM, TM)], r.dxz.at[1], z1_peer),
            2: remote(r.xall.at[2, pl.ds(TM, TM)], r.dxz.at[2], z2_peer),
        }

        def dx_rows(slot, rows):
            here = pl.ds(pl.multiple_of(slot * T + rows.start, TM), TM)
            return nt(dkv[here, :], r.wqkv[:, W:])

        def dx_part(slot):
            r.xall[slot, 0:TM] = dx_rows(slot, peer_rows).astype(BF16)
            go(dx_y[slot])
            r.xall[slot, TM:] = dx_rows(slot, my_rows).astype(BF16)

        def dx_sum(slot):
            dx_y[slot].wait_recv()
            total = r.xall[slot, TM:].astype(F32) + r.dxy[slot].astype(F32)
            if slot == 2:
                dx_z[3].wait_recv()
                total = total + r.dxz[0].astype(F32)
            r.xall[slot, TM:] = total.astype(BF16)
            go(dx_z[slot])

        set_bias(3)
        run(lambda p: pull(3, p))
        dx_part(3)
        early_finish(0)
        set_bias(1)
        run(lambda p: pull(1, p), {1: together((early_finish, (1,)))})
        dx_part(1)
        unit_s.forward(1)
        set_bias(2)
        run(lambda p: pull(2, p), {0: together((dx_sum, (3,))), 1: together((early_finish, (2,)))})
        dx_part(2)
        unit_s.forward(2)
        set_bias(0)
        run(lambda p: pull(0, p), {0: together((early_finish, (3,))), 1: together((dx_sum, (1,)))})
        r.dq[...] = (acc[...].reshape(W, T).T * scale).astype(BF16)

        unit_a = Unit(r.ua, r.us_r0, r.ua_out, orders[2], (r.ua_r0, r.ua_r1, r.ua_r2, r.ua_r3))
        unit_b = Unit(r.ub, r.wo, r.ub_out, orders[3], (r.ub_r0, r.ub_r1, r.ub_r2, r.ub_r3))

        def key_value_tiles(which):
            rows = half_rows(which)
            r.ub[rows, :] = nn(r.xt[rows, :], dkv[...]).astype(BF16)

        def query_output_tiles(which):
            rows = half_rows(which)
            r.ua[rows, 0:W] = nn(r.xt[rows, 0:T], r.dq[...]).astype(BF16)
            cols = pl.ds(pl.multiple_of(half_of(which) * W, 128), W)
            r.ua[rows, W:] = tn(r.att[...], r.gm[:, cols]).astype(BF16)

        key_value_tiles(0)
        unit_b.send(0)
        query_output_tiles(0)
        unit_a.send(0)
        unit_e.forward(1)
        key_value_tiles(1)
        unit_b.forward(0)
        query_output_tiles(1)
        unit_a.forward(0)
        r.xall[0, 0:TM] = (dx_rows(0, peer_rows) + nt(r.dq[peer_rows, :], r.wqkv[:, :W])).astype(BF16)
        go(dx_y[0])
        r.gmix[...] += dx_rows(0, my_rows) + nt(r.dq[my_rows, :], r.wqkv[:, :W])
        late = r.ls
        late[0, 0:1, :] = column_sum(r.dq[...].astype(F32))
        late[0, 1:2, :] = column_sum(dkv[:, W:].astype(F32))
        late[0, 2:8, :] = jnp.zeros((6, W), F32)
        late_start, late_finish = all_sum(late, r.ls_r, (CORE, XS, Z1, Z2))
        late_start(0)
        early_finish(4)
        unit_s.turn()
        late_finish(0)
        dx_sum(2)
        unit_s.back(3)
        unit_e.forward(2)
        late_finish(1)
        unit_b.forward(1)
        unit_s.back(2)
        unit_a.forward(1)
        late_finish(2)
        unit_e.turn()
        unit_s.back(1)
        dx_y[0].wait_recv()
        dx_z[1].wait_recv()
        dx_z[2].wait_recv()
        total = r.gmix[...] + r.dxy[0].astype(F32)
        r.igm[...] = (total + (r.dxz[1].astype(F32) + r.dxz[2].astype(F32))).astype(BF16)
        ig_local = local(r.igm, r.ig_out.at[my_rows])
        ig_local.start()
        ig_send = remote(r.igm, r.ig_out.at[my_rows], y_peer)
        go(ig_send)
        go(oy_send)
        unit_b.forward(2)
        unit_a.forward(2)
        late_finish(3)
        unit_e.back(3)
        unit_b.turn()
        unit_a.turn()
        unit_e.back(2)
        unit_b.back(3)
        unit_a.back(3)
        unit_e.back(1)
        unit_b.back(2)
        unit_a.back(2)
        unit_b.back(1)
        unit_a.back(1)
        for unit in (unit_s, unit_e, unit_b, unit_a):
            unit.store()
        r.small_out[...] = r.es[1]
        r.late_out[...] = late[0]
        oy_local.wait()
        oy_send.wait_recv()
        ig_local.wait()
        ig_send.wait_recv()
        for unit in (unit_s, unit_e, unit_b, unit_a):
            unit.kept.wait()
        for p in range(HP):
            att_copy(p).wait_send()
        wait_sends()

    return kernel


def layer_call(sh, args):
    T, TM, D, W, F = sh.tokens, sh.mine, sh.width, sh.hw, sh.units
    HP = sh.pairs
    any_spec = pl.BlockSpec(memory_space=pl.ANY)
    vmem_spec = pl.BlockSpec(memory_space=pltpu.VMEM)
    orders = ((CORE, XS, Z1, Z2),) * 4
    ins = dict(
        seg_in=vmem_spec, qb_in=vmem_spec, vb_in=vmem_spec, ob_in=vmem_spec, ag_in=vmem_spec,
        as_in=vmem_spec, eb_in=vmem_spec, sb_in=vmem_spec, fg_in=vmem_spec, fs_in=vmem_spec,
        x_in=any_spec, wq_in=any_spec, wk_in=any_spec, wv_in=any_spec,
        wo_in=any_spec, we_in=any_spec, ws_in=any_spec, cot_in=any_spec,
    )
    outs = dict(
        out=((T, D), BF16, any_spec),
        ig_out=((T, D), BF16, any_spec),
        ue_out=((D, F), BF16, any_spec),
        us_out=((F, D), BF16, any_spec),
        ua_out=((D, 2 * W), BF16, any_spec),
        ub_out=((D, 2 * W), BF16, any_spec),
        small_out=((8, D), F32, vmem_spec),
        late_out=((8, W), F32, vmem_spec),
    )
    vm = lambda shape, kind: pltpu.VMEM(shape, kind)
    scratch = dict(
        send=pltpu.SemaphoreType.DMA((128,)),
        recv=pltpu.SemaphoreType.DMA((128,)),
        local=pltpu.SemaphoreType.DMA((24,)),
        xall=vm((4, T, D), BF16),
        xt=vm((D, 4 * T), BF16),
        wqkv=vm((D, 3 * W), BF16),
        wo=vm((2 * W, D), BF16),
        we=vm((2, D, F), BF16),
        ws=vm((2, F, D), BF16),
        eb=vm((2, 1, F), F32),
        cot=vm((TM, D), BF16),
        segs=vm((4, 1, T), F32),
        bias=vm((T, T), F32),
        kv=vm((4, HP, 2, T, 128), BF16),
        qm=vm((2 * HP, T, 128), BF16),
        dm=vm((2 * HP, T, 128), BF16),
        m_s=vm((2 * HP, 1, T), F32),
        l_s=vm((2 * HP, 1, T), F32),
        delta=vm((2 * HP, 1, T), F32),
        acc=vm((2 * HP, 64, T), F32),
        att=vm((T, W), BF16),
        att_o=vm((TM, W), BF16),
        n1=vm((TM, D), F32),
        r1=vm((TM, 128), F32),
        sec=vm((TM, D), F32),
        gf=vm((TM, D), F32),
        gmix=vm((TM, D), F32),
        fl=vm((T, D), BF16),
        flt=vm((D, T), BF16),
        gs=vm((T, D), BF16),
        gm=vm((T, D), BF16),
        gp=vm((2, TM, F), F32),
        hid=vm((T, F), BF16),
        gpre=vm((T, F), BF16),
        oy=vm((TM, D), BF16),
        small=vm((8, D), F32),
        es=vm((2, 8, D), F32),
        es_r=vm((5, 8, D), F32),
        ls=vm((2, 8, W), F32),
        ls_r=vm((4, 8, W), F32),
        dkv=vm((4 * T, 2 * W), BF16),
        dq=vm((T, W), BF16),
        dxy=vm((4, TM, D), BF16),
        dxz=vm((3, TM, D), BF16),
        igm=vm((TM, D), BF16),
        ua=vm((D, 2 * W), BF16),
        ub=vm((D, 2 * W), BF16),
    )
    for name, rows, cols in (("us", F, D), ("ue", D, F), ("ua", D, 2 * W), ("ub", D, 2 * W)):
        for k in range(4):
            rows = rows // 2
            scratch[f"{name}_r{k}"] = vm((rows, cols), BF16)
    names = list(ins) + list(outs) + list(scratch)
    return pl.pallas_call(
        make_kernel(sh, names, orders),
        out_shape=[jax.ShapeDtypeStruct(o[0], o[1]) for o in outs.values()],
        in_specs=list(ins.values()),
        out_specs=[o[2] for o in outs.values()],
        scratch_shapes=list(scratch.values()),
        compiler_params=pltpu.CompilerParams(
            collective_id=0, has_side_effects=True, vmem_limit_bytes=63 * 1024 * 1024
        ),
        name="layer",
    )(*args)


def fused_body(
    mesh_sizes, inputs, segments, query_proj, key_proj, value_proj, query_bias, value_bias, output_proj,
    output_bias, attn_gain, attn_shift, expand_proj, expand_bias, shrink_proj, shrink_bias,
    final_gain, final_shift, cotangent,
):
    sh = Shapes(mesh_sizes, inputs.shape[0], inputs.shape[1], query_proj.shape[1], expand_proj.shape[1])
    W = sh.hw
    out, ig, ue, us, ua, ub, small, late = layer_call(
        sh,
        (
            segments, query_bias, value_bias, output_bias, attn_gain, attn_shift, expand_bias, shrink_bias,
            final_gain, final_shift, inputs, query_proj, key_proj, value_proj, output_proj, expand_proj,
            shrink_proj, cotangent,
        ),
    )
    ua, ub = ua.astype(F32), ub.astype(F32)
    oproj_grad = jnp.concatenate([ua[:W, W:], ua[W:, W:]], axis=1)
    return (
        out, ig.astype(F32), ua[:, :W], ub[:, :W], ub[:, W:], late[0], late[1], oproj_grad,
        small[5], small[3], small[4], ue.astype(F32), small[6:8].reshape(-1), us.astype(F32),
        small[2], small[0], small[1],
    )


contract_rows = (((0,), (0,)), ((), ()))
contract_cols = (((1,), (1,)), ((), ()))


def matmul(left, right):
    return jnp.dot(left, right, preferred_element_type=jnp.float32)


def inner_rows(left, right):
    return lax.dot_general(left, right, contract_rows, preferred_element_type=jnp.float32)


def inner_cols(left, right):
    return lax.dot_general(left, right, contract_cols, preferred_element_type=jnp.float32)


def norm_forward(values, gain, shift):
    centred = values - jnp.mean(values, axis=-1, keepdims=True)
    spread = jnp.mean(centred * centred, axis=-1, keepdims=True)
    recip = lax.rsqrt(spread + norm_eps)
    normed = centred * recip
    return (normed * gain + shift, normed, recip)


def norm_backward(upstream, normed, recip, gain):
    scaled = upstream * gain
    centred = (
        scaled
        - jnp.mean(scaled, axis=-1, keepdims=True)
        - normed * jnp.mean(scaled * normed, axis=-1, keepdims=True)
    )
    return (centred * recip, jnp.sum(upstream * normed, axis=0), jnp.sum(upstream, axis=0))


def cross_scores(left, right):
    return inner_cols(left, right)


def spread_apply(weights_in, right):
    return matmul(weights_in, right)


def spread_transpose(weights_in, left):
    return inner_rows(weights_in, left)


def body(
    inputs,
    segments,
    query_proj,
    key_proj,
    value_proj,
    query_bias,
    value_bias,
    output_proj,
    output_bias,
    attn_gain,
    attn_shift,
    expand_proj,
    expand_bias,
    shrink_proj,
    shrink_bias,
    final_gain,
    final_shift,
    cotangent,
):
    head_count = query_proj.shape[1] // HEAD_DIM
    scale = HEAD_DIM ** (-0.5)
    seg_local = segments[0]
    queries = (matmul(inputs, query_proj) + query_bias.astype(jnp.float32)).astype(jnp.bfloat16)
    keys = matmul(inputs, key_proj).astype(jnp.bfloat16)
    values = (matmul(inputs, value_proj) + value_bias.astype(jnp.float32)).astype(jnp.bfloat16)
    all_keys, all_values, key_ids = (
        lax.all_gather(keys, "ctx", axis=0, tiled=True),
        lax.all_gather(values, "ctx", axis=0, tiled=True),
        lax.all_gather(seg_local.astype(jnp.bfloat16), "ctx", axis=0, tiled=True),
    )
    query_segs = seg_local.astype(jnp.float32)
    key_segs = key_ids.astype(jnp.float32)
    same_seg = query_segs[:, None] == key_segs[None, :]

    def split_heads(matrix):
        return jnp.swapaxes(matrix.reshape(matrix.shape[0], head_count, HEAD_DIM), 0, 1)

    def join_heads(stack):
        return jnp.swapaxes(stack, 0, 1).reshape(stack.shape[1], head_count * HEAD_DIM)

    query_heads = split_heads(queries)
    key_heads = split_heads(all_keys)
    value_heads = split_heads(all_values)

    def head_forward(state, triple):
        query_head, key_head, value_head = triple
        scores = cross_scores(query_head, key_head) * scale
        scores = jnp.where(same_seg, scores, masked)
        row_max = jnp.max(scores, axis=1, keepdims=True)
        exp_scores = jnp.where(same_seg, jnp.exp(scores - row_max), 0.0)
        row_sum = jnp.sum(exp_scores, axis=1, keepdims=True)
        attn_probs = (exp_scores / row_sum).astype(jnp.bfloat16)
        mixed = spread_apply(attn_probs, value_head)
        return (state, (mixed, row_max + jnp.log(row_sum)))

    mixed_heads, log_sums = lax.scan(head_forward, None, (query_heads, key_heads, value_heads))[1]
    attended = join_heads(mixed_heads).astype(jnp.bfloat16)
    attn_total = lax.psum(matmul(attended, output_proj).astype(jnp.bfloat16), "tensor").astype(
        jnp.float32
    )
    attn_gain_f = attn_gain.astype(jnp.float32)
    first, first_normed, first_recip = norm_forward(
        inputs.astype(jnp.float32) + attn_total + output_bias.astype(jnp.float32),
        attn_gain_f,
        attn_shift.astype(jnp.float32),
    )
    first_low = first.astype(jnp.bfloat16)
    pre_act = matmul(first_low, expand_proj) + expand_bias.astype(jnp.float32)
    activated, gelu_back = jax.vjp(lambda pre_in: jax.nn.gelu(pre_in, approximate=False), pre_act)
    hidden = activated.astype(jnp.bfloat16)
    feed_total = lax.psum(matmul(hidden, shrink_proj).astype(jnp.bfloat16), "tensor").astype(
        jnp.float32
    )
    second = first + feed_total + shrink_bias.astype(jnp.float32)
    final_gain_f = final_gain.astype(jnp.float32)
    output, second_normed, second_recip = norm_forward(
        second, final_gain_f, final_shift.astype(jnp.float32)
    )
    upstream = cotangent.astype(jnp.float32)
    grad_second, fgain_grad, fshift_grad = norm_backward(
        upstream, second_normed, second_recip, final_gain_f
    )
    sbias_grad = jnp.sum(grad_second, axis=0)
    grad_second_low = grad_second.astype(jnp.bfloat16)
    shrink_grad = inner_rows(hidden, grad_second_low)
    grad_act = inner_cols(grad_second_low, shrink_proj)
    grad_pre = gelu_back(grad_act)[0].astype(jnp.bfloat16)
    ebias_grad = jnp.sum(grad_pre.astype(jnp.float32), axis=0)
    expand_grad = inner_rows(first_low, grad_pre)
    grad_first = grad_second + lax.psum(
        inner_cols(grad_pre, expand_proj).astype(jnp.bfloat16), "tensor"
    ).astype(jnp.float32)
    grad_mix, again_grad, ashift_grad = norm_backward(
        grad_first, first_normed, first_recip, attn_gain_f
    )
    obias_grad = jnp.sum(grad_mix, axis=0)
    grad_mix_low = grad_mix.astype(jnp.bfloat16)
    oproj_grad = inner_rows(attended, grad_mix_low)
    grad_attended = inner_cols(grad_mix_low, output_proj).astype(jnp.bfloat16)
    grad_heads = split_heads(grad_attended)

    def head_backward(state, group):
        query_head, key_head, value_head, grad_head, log_sum = group
        scores = cross_scores(query_head, key_head) * scale
        attn_probs = jnp.where(same_seg, jnp.exp(scores - log_sum), 0.0)
        grad_probs = cross_scores(grad_head, value_head)
        row_dot = jnp.sum(attn_probs * grad_probs, axis=1, keepdims=True)
        grad_scores = (attn_probs * (grad_probs - row_dot)).astype(jnp.bfloat16)
        grad_query = spread_apply(grad_scores, key_head) * scale
        grad_key = spread_transpose(grad_scores, query_head) * scale
        grad_value = spread_transpose(attn_probs.astype(jnp.bfloat16), grad_head)
        return (state, (grad_query, grad_key, grad_value))

    query_back, key_back, value_back = lax.scan(
        head_backward, None, (query_heads, key_heads, value_heads, grad_heads, log_sums)
    )[1]
    grad_queries = join_heads(query_back).astype(jnp.bfloat16)
    key_sum, value_sum = (
        lax.psum_scatter(
            join_heads(key_back).astype(jnp.bfloat16), "ctx", scatter_dimension=0, tiled=True
        ).astype(jnp.float32),
        lax.psum_scatter(
            join_heads(value_back).astype(jnp.bfloat16), "ctx", scatter_dimension=0, tiled=True
        ).astype(jnp.float32),
    )
    grad_keys = key_sum.astype(jnp.bfloat16)
    grad_values = value_sum.astype(jnp.bfloat16)
    qbias_grad = jnp.sum(grad_queries.astype(jnp.float32), axis=0)
    vbias_grad = jnp.sum(grad_values.astype(jnp.float32), axis=0)
    query_grad = inner_rows(inputs, grad_queries)
    key_grad = inner_rows(inputs, grad_keys)
    value_grad = inner_rows(inputs, grad_values)
    back_terms = (
        inner_cols(grad_queries, query_proj)
        + inner_cols(grad_keys, key_proj)
        + inner_cols(grad_values, value_proj)
    )
    input_grad = grad_mix + lax.psum(back_terms.astype(jnp.bfloat16), "tensor").astype(jnp.float32)
    (
        query_grad,
        key_grad,
        value_grad,
        qbias_grad,
        vbias_grad,
        oproj_grad,
        obias_grad,
        again_grad,
        ashift_grad,
        expand_grad,
        ebias_grad,
        shrink_grad,
        sbias_grad,
        fgain_grad,
        fshift_grad,
    ) = lax.psum(
        (
            query_grad,
            key_grad,
            value_grad,
            qbias_grad,
            vbias_grad,
            oproj_grad,
            obias_grad,
            again_grad,
            ashift_grad,
            expand_grad,
            ebias_grad,
            shrink_grad,
            sbias_grad,
            fgain_grad,
            fshift_grad,
        ),
        ("dp", "ctx"),
    )
    return (
        output.astype(jnp.bfloat16),
        input_grad,
        query_grad,
        key_grad,
        value_grad,
        qbias_grad,
        vbias_grad,
        oproj_grad,
        obias_grad,
        again_grad,
        ashift_grad,
        expand_grad,
        ebias_grad,
        shrink_grad,
        sbias_grad,
        fgain_grad,
        fshift_grad,
    )


def solution(mesh):
    in_specs = (
        P(("dp", "ctx"), None),
        P("dp", "ctx"),
        P(None, "tensor"),
        P(None, "tensor"),
        P(None, "tensor"),
        P("tensor"),
        P("tensor"),
        P("tensor", None),
        P(),
        P(),
        P(),
        P(None, "tensor"),
        P("tensor"),
        P("tensor", None),
        P(),
        P(),
        P(),
        P(("dp", "ctx"), None),
    )
    out_specs = (
        P(("dp", "ctx"), None),
        P(("dp", "ctx"), None),
        P(None, "tensor"),
        P(None, "tensor"),
        P(None, "tensor"),
        P("tensor"),
        P("tensor"),
        P("tensor", None),
        P(),
        P(),
        P(),
        P(None, "tensor"),
        P("tensor"),
        P("tensor", None),
        P(),
        P(),
        P(),
    )
    sizes = dict(mesh.shape)
    fits = sizes == {"dp": 4, "ctx": 4, "tensor": 2}
    chosen = functools.partial(fused_body, sizes) if fits else body
    return jax.shard_map(chosen, mesh=mesh, in_specs=in_specs, out_specs=out_specs, check_vma=False)
```

```python
import functools
import types

import jax
import jax.numpy as jnp
from jax import lax
from jax.experimental import pallas as pl
from jax.experimental.pallas import tpu as pltpu
from jax.sharding import PartitionSpec as P

HEAD_DIM = 64
norm_eps = 1e-12
masked = -1e30
MESH = pl.DeviceIdType.MESH
CORE, XS, YS, Z1, Z2 = range(5)
BF16, F32 = jnp.bfloat16, jnp.float32
INV_SQRT2 = 0.7071067811865476
INV_SQRT_2PI = 0.3989422804014327


def nn(left, right):
    return jnp.dot(left, right, preferred_element_type=F32)


def nt(left, right):
    return lax.dot_general(left, right, (((1,), (1,)), ((), ())), preferred_element_type=F32)


def tn(left, right):
    return lax.dot_general(left, right, (((0,), (0,)), ((), ())), preferred_element_type=F32)


def normalise(values):
    centred = values - jnp.mean(values, axis=-1, keepdims=True)
    spread = jnp.mean(centred * centred, axis=-1, keepdims=True)
    recip = lax.rsqrt(spread + norm_eps)
    return centred * recip, recip


def denormalise(scaled, normed, recip):
    return recip * (
        scaled
        - jnp.mean(scaled, axis=-1, keepdims=True)
        - normed * jnp.mean(scaled * normed, axis=-1, keepdims=True)
    )


def gelu_parts(pre):
    phi_sum = 0.5 + 0.5 * lax.erf(pre * INV_SQRT2)
    slope = phi_sum + pre * (INV_SQRT_2PI * jnp.exp(-0.5 * pre * pre))
    return pre * phi_sum, slope


def column_sum(values):
    return jnp.sum(values, axis=0, keepdims=True)


class Shapes:
    def __init__(self, mesh, tokens, width, heads_width, units):
        self.nd, self.nc = mesh["dp"], mesh["ctx"]
        self.nx = self.nd // 2
        self.tokens, self.mine = tokens, tokens // 2
        self.width, self.hw, self.units = width, heads_width, units
        self.pairs = heads_width // 128


def make_kernel(sh, names, orders):
    T, TM, D, W, F = sh.tokens, sh.mine, sh.width, sh.hw, sh.units
    HP = sh.pairs
    TILE = 512
    NTILE = F // TILE
    SLOTS = 4
    PARTS = 2
    PR = TM // PARTS

    def kernel(*refs):
        r = types.SimpleNamespace(**dict(zip(names, refs)))
        send_ref, recv_ref, local_ref = r.send, r.recv, r.local
        d, c, t = lax.axis_index("dp"), lax.axis_index("ctx"), lax.axis_index("tensor")
        core, xpos = lax.rem(d, 2), d // 2
        low_bit, high_bit = lax.rem(c, 2), c // 2
        next_c = c + 1 - 2 * low_bit
        z1_peer, z2_peer = (d, next_c, t), (d, c + 2 - 4 * high_bit, t)
        z3_peer = (d, next_c + 2 - 4 * high_bit, t)
        y_peer = (d, c, 1 - t)
        core_peer = (d + 1 - 2 * core, c, t)
        x_peer = (d + 2 - 4 * xpos, c, t)
        peer_of = {CORE: core_peer, XS: x_peer, YS: y_peer, Z1: z1_peer, Z2: z2_peer}
        bit_of = {CORE: core, XS: xpos, YS: t, Z1: low_bit, Z2: high_bit}
        my_rows = pl.ds(pl.multiple_of(t * TM, TM), TM)
        peer_rows = pl.ds(pl.multiple_of((1 - t) * TM, TM), TM)
        counts = [0, 0]

        def take(kind, k=1):
            at = counts[kind]
            counts[kind] += k
            assert counts[kind] <= (send_ref, local_ref)[kind].shape[0], counts
            return at

        def remote(src, dst, device, at=None, recv_at=None):
            at = take(0) if at is None else at
            recv_at = at if recv_at is None else recv_at
            return pltpu.make_async_remote_copy(
                src_ref=src, dst_ref=dst, send_sem=send_ref.at[at], recv_sem=recv_ref.at[recv_at],
                device_id=device, device_id_type=MESH,
            )

        def local(src, dst):
            return pltpu.make_async_copy(src, dst, local_ref.at[take(1)])

        unsent = []

        def go(copy, where=None):
            if where is None:
                copy.start()
            else:
                pl.when(where)(lambda: copy.start())
            unsent.append((copy, where))

        def wait_sends(*but):
            kept = [entry for entry in unsent if any(entry[0] is other for other in but)]
            for copy, where in unsent:
                if any(copy is other for other in but):
                    continue
                if where is None:
                    copy.wait_send()
                else:
                    pl.when(where)(lambda copy=copy: copy.wait_send())
            unsent[:] = kept

        loads = types.SimpleNamespace(
            x=local(r.x_in, r.xall.at[0]),
            wk=local(r.wk_in, r.wqkv.at[:, pl.ds(W, W)]),
            wv=local(r.wv_in, r.wqkv.at[:, pl.ds(2 * W, W)]),
            wq=local(r.wq_in, r.wqkv.at[:, pl.ds(0, W)]),
            wo=local(r.wo_in, r.wo.at[pl.ds(0, W)]),
            we=local(r.we_in, r.we.at[0]),
            ws=local(r.ws_in, r.ws.at[0]),
            cot=local(r.cot_in.at[my_rows], r.cot),
        )
        for copy in vars(loads).values():
            copy.start()

        def row(ref):
            return ref[...].astype(F32).reshape(1, ref.shape[0])

        vec = [row(ref) for ref in (r.ob_in, r.ag_in, r.as_in, r.sb_in, r.fg_in, r.fs_in)]
        r.eb[0] = row(r.eb_in)
        r.segs[0] = r.seg_in[...].astype(F32)
        barrier = pltpu.get_barrier_semaphore()
        greeted = [y_peer, core_peer, x_peer, z1_peer, z2_peer, z3_peer]
        for device in greeted:
            pl.semaphore_signal(barrier, inc=1, device_id=device, device_id_type=MESH)
        pl.semaphore_wait(barrier, len(greeted))

        seg_copies = [None] + [
            remote(r.segs.at[0], r.segs.at[k], peer) for k, peer in ((1, z1_peer), (2, z2_peer), (3, z3_peer))
        ]
        eb_copy = remote(r.eb.at[0], r.eb.at[1], y_peer)
        x_rows = [pl.ds(pl.multiple_of(t * TM + k * PR, PR), PR) for k in range(PARTS)]
        mid = lax.rem(low_bit + high_bit, 2)
        is_mid = mid == 1
        slots = (0, 1, 2 + mid, 3 - mid)
        x_at = take(0, 3 * PARTS)

        def x_recv(slot, k):
            return x_at + (slot - 1) * PARTS + k

        def x_move(src_slot, dst_slot, peer, k):
            src = r.x_in.at[x_rows[k]] if src_slot == 0 else r.xall.at[src_slot, x_rows[k]]
            return remote(src, r.xall.at[dst_slot, x_rows[k]], peer, None, x_recv(dst_slot, k))

        x_near = [x_move(0, 1, z1_peer, k) for k in range(PARTS)]
        x_far = [x_move(0, 3, z3_peer, k) for k in range(PARTS)]
        x_next = (
            None,
            [x_move(1, 2, z3_peer, k) for k in range(PARTS)],
            [x_move(3, 2, z1_peer, k) for k in range(PARTS)],
            [x_move(2, 3, z1_peer, k) for k in range(PARTS)],
        )
        x_y = [None] + [
            [remote(r.xall.at[slots[o], x_rows[k]], r.xall.at[slots[o], x_rows[k]], y_peer) for k in range(PARTS)]
            for o in (1, 2, 3)
        ]
        for k in range(PARTS):
            go(x_near[k])
            go(x_far[k], is_mid)
        for copy in seg_copies[1:]:
            go(copy)
        go(eb_copy)

        def arrive(o, k):
            here = r.xall.at[slots[o], x_rows[k]]
            remote(here, here, z1_peer, x_at, x_recv(slots[o], k)).wait_recv()
            go(x_next[o][k], is_mid)
            go(x_y[o][k])

        def block_here(o):
            if o == 1:
                for copy in seg_copies[1:]:
                    copy.wait_recv()
            for k in range(PARTS):
                x_y[o][k].wait_recv()

        chunks = [
            (r.wo_in, r.wo.at[pl.ds(W, W)], W, 0, 1),
            (r.we_in, r.we.at[1], D, 0, 2),
            (r.we_in, r.we.at[1], D, 1, 2),
            (r.ws_in, r.ws.at[1], F, 0, 2),
            (r.ws_in, r.ws.at[1], F, 1, 2),
        ]
        pieces = sh.nd * 2

        def window(chunk, owner):
            rows, part, parts = chunk[2:]
            size = rows // pieces // parts
            return pl.ds(pl.multiple_of(owner * (rows // pieces) + part * size, size), size)

        own_piece, pair_piece = d * 2 + low_bit, d * 2 + 1 - low_bit
        x_d = d + 2 - 4 * xpos
        x_pieces = (x_d * 2 + low_bit, x_d * 2 + 1 - low_bit)
        w_y, w_z, w_x, w_core = [], [], [], []
        for chunk in chunks:
            source, held = chunk[0], chunk[1]

            def move(owner, peer):
                where = window(chunk, owner)
                return remote(held.at[where], held.at[where], peer)

            own = window(chunk, own_piece)
            w_y.append(remote(source.at[own], held.at[own], y_peer))
            w_z.append(move(own_piece, z1_peer))
            w_x.append([move(piece, x_peer) for piece in (own_piece, pair_piece)])
            w_core.append([move(piece, core_peer) for piece in (own_piece, pair_piece) + x_pieces])

        def hop1(i):
            w_y[i].wait_recv()
            go(w_z[i])
            go(w_x[i][0])
            go(w_core[i][0])

        def hop2(i):
            w_z[i].wait_recv()
            go(w_x[i][1])
            go(w_core[i][1])

        def hop3(i):
            for k in range(2):
                w_x[i][k].wait_recv()
                go(w_core[i][2 + k])

        def weights_done(i):
            for copy in w_core[i]:
                copy.wait_recv()

        for i in range(3):
            go(w_y[i])

        kv = r.kv
        value_bias = row(r.vb_in)
        scale = HEAD_DIM ** (-0.5)
        lane = lax.broadcasted_iota(jnp.int32, (T, 128), 1)

        def split_pair(target, p, pair):
            target[2 * p] = jnp.where(lane < 64, pair, 0.0).astype(BF16)
            target[2 * p + 1] = jnp.where(lane < 64, 0.0, pair).astype(BF16)

        def set_keys_values(slot):
            both = nn(r.xall[slot], r.wqkv[:, W:])
            for p in range(HP):
                kv[slot, p, 0] = both[:, p * 128 : (p + 1) * 128].astype(BF16)
                cols = slice(W + p * 128, W + (p + 1) * 128)
                kv[slot, p, 1] = (both[:, cols] + value_bias[:, p * 128 : (p + 1) * 128]).astype(BF16)

        def set_bias(slot):
            seg_keys = jnp.broadcast_to(r.segs[slot], (128, T)).T
            for j in range(T // 128):
                cols = slice(j * 128, (j + 1) * 128)
                r.bias[:, cols] = jnp.where(seg_keys == r.segs[0, :, cols], 0.0, masked)

        loads.x.wait()
        loads.wk.wait()
        loads.wv.wait()
        set_keys_values(0)
        loads.wq.wait()
        queries = (nn(r.xall[0], r.wqkv[:, :W]) + row(r.qb_in)).astype(BF16).astype(F32) * scale
        for p in range(HP):
            split_pair(r.qm, p, queries[:, p * 128 : (p + 1) * 128])

        m_s, l_s, acc = r.m_s, r.l_s, r.acc
        m_s[...] = jnp.full_like(m_s, masked)
        l_s[...] = jnp.zeros_like(l_s)
        acc[...] = jnp.zeros_like(acc)

        def attend(slot, p):
            pair_keys = kv[slot, p, 0]
            pair_values = kv[slot, p, 1].T
            for hh in range(2):
                h = 2 * p + hh
                s = nt(pair_keys, r.qm[h]) + r.bias[...]
                old = m_s[h]
                new = jnp.maximum(old, jnp.max(s, axis=0, keepdims=True))
                e = jnp.exp(s - new)
                alpha = jnp.exp(old - new)
                l_s[h] = l_s[h] * alpha + jnp.sum(e, axis=0, keepdims=True)
                m_s[h] = new
                acc[h] = acc[h] * alpha + nn(pair_values[hh * 64 : hh * 64 + 64], e.astype(BF16))

        def run(body, services=None):
            def step(p, carry):
                body(p)
                for at, fn in (services or {}).items():
                    pl.when(p == at)(fn)
                return carry

            lax.fori_loop(0, HP, step, 0)

        def together(*fns):
            def all_of():
                for fn, arg in fns:
                    fn(*arg)

            return all_of

        set_bias(0)

        def flip_inputs(slot):
            at = slot * T if isinstance(slot, int) else pl.multiple_of(slot * T, T)
            r.xt[:, pl.ds(at, T)] = r.xall[slot].T

        def next_block(o):
            block_here(o)
            set_keys_values(slots[o])
            set_bias(slots[o])

        hop1(0)
        run(lambda p: attend(0, p), {1: together((arrive, (1, 0))), 2: together((hop1, (1,)))})
        arrive(1, 1)
        go(w_y[3])
        hop1(2)
        flip_inputs(0)
        hop2(0)
        arrive(2, 0)
        hop2(1)
        hop3(0)
        arrive(2, 1)
        go(w_y[4])
        next_block(1)
        run(lambda p: attend(1, p), {0: together((hop3, (1,))), 2: together((hop2, (2,)), (hop1, (3,)))})
        arrive(3, 0)
        hop3(2)
        flip_inputs(1)
        arrive(3, 1)
        next_block(2)
        run(lambda p: attend(slots[2], p), {0: together((hop2, (3,))), 2: together((hop1, (4,)))})
        hop3(3)
        flip_inputs(slots[2])
        hop2(4)
        next_block(3)
        att_at = take(0, HP)

        def att_copy(p):
            cols = pl.ds(p * 128, 128)
            return remote(r.att.at[peer_rows, cols], r.att_o.at[:, cols], y_peer, att_at + p)

        for p in range(HP):
            attend(slots[3], p)
            for h in (2 * p, 2 * p + 1):
                acc[h] = acc[h] / l_s[h]
                m_s[h] = m_s[h] + jnp.log(l_s[h])
            pair = acc[2 * p : 2 * p + 2].reshape(128, T).T
            r.att[:, p * 128 : (p + 1) * 128] = pair.astype(BF16)
            att_copy(p).start()
        loads.wo.wait()
        weights_done(0)
        loads.cot.wait()

        mix = nn(r.att[my_rows, :], r.wo[0:W, :])
        flip_inputs(slots[3])
        for p in range(HP):
            att_copy(p).wait_recv()
        mix = mix + nn(r.att_o[...], r.wo[W : 2 * W, :])
        normed, recip = normalise(r.xall[0, my_rows, :].astype(F32) + mix + vec[0])
        r.n1[...] = normed
        r.r1[...] = jnp.broadcast_to(recip, (TM, 128))
        first = normed * vec[1] + vec[2]
        r.sec[...] = first + vec[3]
        r.fl[my_rows, :] = first.astype(BF16)
        fl_copy = remote(r.fl.at[my_rows], r.fl.at[my_rows], y_peer)
        loads.we.wait()
        loads.ws.wait()
        hop3(4)
        go(fl_copy)


        def tile_cols(j):
            return pl.ds(pl.multiple_of(j * TILE, TILE), TILE)

        def forward_tile(side, j):
            cols = tile_cols(j)
            pre = nn(r.fl[my_rows, :], r.we[side, :, cols]) + r.eb[side, :, cols]
            hidden, slope = gelu_parts(pre)
            hidden = hidden.astype(BF16)
            r.gp[side, :, cols] = slope
            if side == 0:
                r.hid[my_rows, cols] = hidden
            r.sec[...] += nn(hidden, r.ws[side, cols, :])

        def tiles(fn):
            def step(j, carry):
                fn(j)
                return carry

            lax.fori_loop(0, NTILE, step, 0)

        tiles(lambda j: forward_tile(0, j))
        eb_copy.wait_recv()
        for i in range(1, len(chunks)):
            weights_done(i)
        tiles(lambda j: forward_tile(1, j))
        normed2, recip2 = normalise(r.sec[...])
        upstream = r.cot[...].astype(F32)
        grad_second = denormalise(upstream * vec[4], normed2, recip2)
        r.gf[...] = grad_second
        r.gs[my_rows, :] = grad_second.astype(BF16)
        gs_copy = remote(r.gs.at[my_rows], r.gs.at[my_rows], y_peer)
        go(gs_copy)
        small = r.small
        small[0:1, :] = column_sum(upstream * normed2)
        small[1:2, :] = column_sum(upstream)
        small[2:3, :] = column_sum(grad_second)
        r.oy[...] = (normed2 * vec[4] + vec[5]).astype(BF16)
        oy_local = local(r.oy, r.out.at[my_rows])
        oy_local.start()


        def backward_tile(side, j):
            cols = tile_cols(j)
            low = (nt(r.gs[my_rows, :], r.ws[side, cols, :]) * r.gp[side, :, cols]).astype(BF16)
            if side == 0:
                r.gpre[my_rows, cols] = low
            r.gf[...] += nt(low, r.we[side, :, cols])

        tiles(lambda j: backward_tile(0, j))
        tiles(lambda j: backward_tile(1, j))
        grad_first = r.gf[...]
        normed = r.n1[...]
        grad_mix = denormalise(grad_first * vec[1], normed, r.r1[:, 0:1])
        r.gmix[...] = grad_mix
        r.gm[my_rows, :] = grad_mix.astype(BF16)
        gm_copy = remote(r.gm.at[my_rows], r.gm.at[my_rows], y_peer)
        go(gm_copy)
        small[3:4, :] = column_sum(grad_first * normed)
        small[4:5, :] = column_sum(grad_first)
        small[5:6, :] = column_sum(grad_mix)

        def rows_at(ref, first_row, rows):
            return ref.at[pl.ds(pl.multiple_of(first_row, rows), rows)]

        class Unit:
            def __init__(self, grad, whole, out, order, bufs):
                self.grad, self.order, self.bufs = grad, order, bufs
                self.first, self.rows = [0], [grad.shape[0]]
                for stage in order:
                    self.rows.append(self.rows[-1] // 2)
                    self.first.append(self.first[-1] + bit_of[stage] * self.rows[-1])
                self.down, self.up = [], []
                for k, stage in enumerate(order):
                    rows = self.rows[k + 1]
                    theirs = rows_at(grad, self.first[k] + (1 - bit_of[stage]) * rows, rows)
                    self.down.append(remote(theirs, bufs[k], peer_of[stage]))
                    target = rows_at(whole, self.first[k + 1], rows)
                    source = target
                    if k == len(order) - 1:
                        source = rows_at(grad, self.first[k + 1], rows)
                        self.kept = local(source, target)
                    self.up.append(remote(source, target, peer_of[stage]))
                self.stored = local(whole, out)

            def send(self, k):
                go(self.down[k])

            def add(self, k):
                self.down[k].wait_recv()
                rows, first_row = self.rows[k + 1], self.first[k + 1]
                step = next(v for v in (96, 48) if rows % v == 0)

                def tile(i, carry):
                    window = self.grad.at[pl.ds(pl.multiple_of(first_row + i * step, step), step)]
                    there = pl.ds(pl.multiple_of(i * step, step), step)
                    window[...] = (window[...].astype(F32) + self.bufs[k][there, :].astype(F32)).astype(BF16)
                    return carry

                lax.fori_loop(0, rows // step, tile, 0)

            def forward(self, k):
                self.add(k)
                self.send(k + 1)

            def spread(self, k):
                go(self.up[k])
                if k == len(self.order) - 1:
                    self.kept.start()

            def turn(self):
                k = len(self.order) - 1
                self.add(k)
                self.spread(k)

            def back(self, k):
                if k == len(self.order) - 1:
                    self.kept.wait()
                self.up[k].wait_recv()
                self.spread(k - 1)

            def store(self):
                self.up[0].wait_recv()
                self.stored.start()

        def all_sum(buf, slots, stages):
            copies = [remote(buf.at[k % 2], slots.at[k], peer_of[stage]) for k, stage in enumerate(stages)]

            def start(k):
                copies[k].start()

            def finish(k):
                copies[k].wait()
                total = buf[k % 2] + slots[k]
                if stages[k] == YS:
                    which = lax.broadcasted_iota(jnp.int32, total.shape, 0)
                    total = jnp.where(which < 6, total, buf[k % 2])
                buf[(k + 1) % 2] = total
                if k + 1 < len(stages):
                    start(k + 1)

            return start, finish

        fl_copy.wait_recv()
        gs_copy.wait_recv()

        def other_tile(j):
            cols = tile_cols(j)
            pre = nn(r.fl[peer_rows, :], r.we[0, :, cols]) + r.eb[0, :, cols]
            hidden, slope = gelu_parts(pre)
            r.hid[peer_rows, cols] = hidden.astype(BF16)
            r.gpre[peer_rows, cols] = (nt(r.gs[peer_rows, :], r.ws[0, cols, :]) * slope).astype(BF16)

        tiles(other_tile)
        wait_sends(gm_copy)
        unit_s = Unit(r.ws.at[1], r.ws.at[0], r.us_out, orders[0], (r.us_r0, r.us_r1, r.us_r2, r.us_r3))
        unit_e = Unit(r.we.at[1], r.we.at[0], r.ue_out, orders[1], (r.ue_r0, r.ue_r1, r.ue_r2, r.ue_r3))

        unit_a = Unit(r.ua, r.us_r0, r.ua_out, orders[2], (r.ua_r0, r.ua_r1, r.ua_r2, r.ua_r3))
        unit_b = Unit(r.ub, r.wo, r.ub_out, orders[3], (r.ub_r0, r.ub_r1, r.ub_r2, r.ub_r3))

        def half_of(which):
            return which * core + (1 - which) * (1 - core)

        def shrink_tiles(which):
            base = half_of(which) * (F // 2)

            def tile(i, carry):
                at = pl.multiple_of(base + i * 384, 128)
                r.ws[1, pl.ds(at, 384), :] = tn(r.hid[:, pl.ds(at, 384)], r.gs[...]).astype(BF16)
                return carry

            lax.fori_loop(0, F // 2 // 384, tile, 0)

        def half_rows(which):
            return pl.ds(pl.multiple_of(half_of(which) * (D // 2), D // 2), D // 2)

        def expand_tiles(which):
            rows = half_rows(which)

            def tile(j):
                cols = tile_cols(j)
                r.we[1, rows, cols] = nn(r.flt[rows, :], r.gpre[:, cols]).astype(BF16)

            tiles(tile)

        shrink_tiles(0)
        unit_s.send(0)
        r.flt[...] = r.fl[...].T
        shrink_tiles(1)
        expand_tiles(0)
        unit_e.send(0)
        unit_s.forward(0)
        expand_tiles(1)
        unit_e.forward(0)
        totals = column_sum(r.gpre[...].astype(F32))
        small[6:7, :] = totals[:, :D]
        small[7:8, :] = totals[:, D:]
        r.es[0] = small[...]
        early_start, early_finish = all_sum(r.es, r.es_r, (YS, CORE, XS, Z1, Z2))
        early_start(0)

        gm_copy.wait_recv()
        grad_att = nt(r.gm[...], r.wo[0:W, :]).astype(BF16).astype(F32)
        flipped = grad_att.T.reshape(2 * HP, 64, T)
        r.delta[...] = jnp.sum(acc[...] * flipped, axis=1, keepdims=True)
        for p in range(HP):
            split_pair(r.dm, p, grad_att[:, p * 128 : (p + 1) * 128])
        acc[...] = jnp.zeros_like(acc)
        oy_send = remote(r.oy, r.out.at[my_rows], y_peer)
        dkv = r.dkv

        def pull(slot, p):
            pair_keys, pair_values = kv[slot, p, 0], kv[slot, p, 1]
            flipped_keys = pair_keys.T
            grad_k = jnp.zeros((T, 128), F32)
            grad_v = jnp.zeros((T, 128), F32)
            for hh in range(2):
                h = 2 * p + hh
                q, g = r.qm[h], r.dm[h]
                probs = jnp.exp(nt(pair_keys, q) + (r.bias[...] - m_s[h]))
                grad_p = nt(pair_values, g)
                grad_v = grad_v + nn(probs.astype(BF16), g)
                ds = (probs * (grad_p - r.delta[h])).astype(BF16)
                grad_k = grad_k + nn(ds, q)
                acc[h] += nn(flipped_keys[hh * 64 : hh * 64 + 64], ds)
            rows = slice(slot * T, (slot + 1) * T)
            dkv[rows, pl.ds(pl.multiple_of(p * 128, 128), 128)] = grad_k.astype(BF16)
            dkv[rows, pl.ds(pl.multiple_of(W + p * 128, 128), 128)] = grad_v.astype(BF16)

        dx_y = [remote(r.xall.at[k, pl.ds(0, TM)], r.dxy.at[k], y_peer) for k in range(SLOTS)]
        dx_z = {
            3: remote(r.xall.at[3, pl.ds(TM, TM)], r.dxz.at[0], z1_peer),
            1: remote(r.xall.at[1, pl.ds(TM, TM)], r.dxz.at[1], z1_peer),
            2: remote(r.xall.at[2, pl.ds(TM, TM)], r.dxz.at[2], z2_peer),
        }

        def dx_rows(slot, rows):
            here = pl.ds(pl.multiple_of(slot * T + rows.start, TM), TM)
            return nt(dkv[here, :], r.wqkv[:, W:])

        def dx_part(slot):
            r.xall[slot, 0:TM] = dx_rows(slot, peer_rows).astype(BF16)
            go(dx_y[slot])
            r.xall[slot, TM:] = dx_rows(slot, my_rows).astype(BF16)

        def dx_sum(slot):
            dx_y[slot].wait_recv()
            total = r.xall[slot, TM:].astype(F32) + r.dxy[slot].astype(F32)
            if slot == 2:
                dx_z[3].wait_recv()
                total = total + r.dxz[0].astype(F32)
            r.xall[slot, TM:] = total.astype(BF16)
            go(dx_z[slot])

        set_bias(3)
        run(lambda p: pull(3, p))
        dx_part(3)
        early_finish(0)
        set_bias(1)
        run(lambda p: pull(1, p), {1: together((unit_s.forward, (1,)))})
        early_finish(1)
        dx_part(1)
        set_bias(2)
        run(lambda p: pull(2, p), {2: together((unit_s.forward, (2,)), (dx_sum, (3,)))})
        dx_part(2)
        set_bias(0)
        run(lambda p: pull(0, p), {1: together((unit_s.turn, ()), (unit_e.forward, (1,)))})
        r.dq[...] = (acc[...].reshape(W, T).T * scale).astype(BF16)
        unit_s.back(3)
        early_finish(2)


        def key_value_tiles(which):
            rows = half_rows(which)
            r.ub[rows, :] = nn(r.xt[rows, :], dkv[...]).astype(BF16)

        def query_output_tiles(which):
            rows = half_rows(which)
            r.ua[rows, 0:W] = nn(r.xt[rows, 0:T], r.dq[...]).astype(BF16)
            cols = pl.ds(pl.multiple_of(half_of(which) * W, 128), W)
            r.ua[rows, W:] = tn(r.att[...], r.gm[:, cols]).astype(BF16)

        key_value_tiles(0)
        unit_b.send(0)
        query_output_tiles(0)
        unit_a.send(0)
        key_value_tiles(1)
        unit_b.forward(0)
        unit_e.forward(2)
        query_output_tiles(1)
        unit_a.forward(0)
        r.xall[0, 0:TM] = (dx_rows(0, peer_rows) + nt(r.dq[peer_rows, :], r.wqkv[:, :W])).astype(BF16)
        go(dx_y[0])
        r.gmix[...] += dx_rows(0, my_rows) + nt(r.dq[my_rows, :], r.wqkv[:, :W])
        late = r.ls
        late[0, 0:1, :] = column_sum(r.dq[...].astype(F32))
        late[0, 1:2, :] = column_sum(dkv[:, W:].astype(F32))
        late[0, 2:8, :] = jnp.zeros((6, W), F32)
        late_start, late_finish = all_sum(late, r.ls_r, (CORE, XS, Z1, Z2))
        late_start(0)
        unit_s.back(2)
        early_finish(3)
        late_finish(0)
        unit_e.turn()
        dx_sum(1)
        dx_sum(2)
        unit_b.forward(1)
        unit_e.back(3)
        unit_a.forward(1)
        early_finish(4)
        unit_b.forward(2)
        unit_e.back(2)
        unit_b.turn()
        unit_a.forward(2)
        unit_b.back(3)
        unit_a.turn()
        unit_b.back(2)
        unit_a.back(3)
        unit_a.back(2)
        late_finish(1)
        dx_y[0].wait_recv()
        dx_z[1].wait_recv()
        dx_z[2].wait_recv()
        total = r.gmix[...] + r.dxy[0].astype(F32)
        r.igm[...] = (total + (r.dxz[1].astype(F32) + r.dxz[2].astype(F32))).astype(BF16)
        ig_local = local(r.igm, r.ig_out.at[my_rows])
        ig_local.start()
        ig_send = remote(r.igm, r.ig_out.at[my_rows], y_peer)
        go(ig_send)
        go(oy_send)
        late_finish(2)
        unit_s.back(1)
        late_finish(3)
        unit_e.back(1)
        unit_s.store()
        unit_b.back(1)
        unit_e.store()
        unit_a.back(1)
        unit_b.store()
        unit_a.store()
        r.small_out[...] = r.es[1]
        r.late_out[...] = late[0]
        oy_local.wait()
        oy_send.wait_recv()
        ig_local.wait()
        ig_send.wait_recv()
        for unit in (unit_s, unit_e, unit_b, unit_a):
            unit.stored.wait()
        for p in range(HP):
            att_copy(p).wait_send()
        wait_sends()

    return kernel


def layer_call(sh, args):
    T, TM, D, W, F = sh.tokens, sh.mine, sh.width, sh.hw, sh.units
    HP = sh.pairs
    any_spec = pl.BlockSpec(memory_space=pl.ANY)
    vmem_spec = pl.BlockSpec(memory_space=pltpu.VMEM)
    orders = ((CORE, XS, Z1, Z2),) * 4
    ins = dict(
        seg_in=vmem_spec, qb_in=vmem_spec, vb_in=vmem_spec, ob_in=vmem_spec, ag_in=vmem_spec,
        as_in=vmem_spec, eb_in=vmem_spec, sb_in=vmem_spec, fg_in=vmem_spec, fs_in=vmem_spec,
        x_in=any_spec, wq_in=any_spec, wk_in=any_spec, wv_in=any_spec,
        wo_in=any_spec, we_in=any_spec, ws_in=any_spec, cot_in=any_spec,
    )
    outs = dict(
        out=((T, D), BF16, any_spec),
        ig_out=((T, D), BF16, any_spec),
        ue_out=((D, F), BF16, any_spec),
        us_out=((F, D), BF16, any_spec),
        ua_out=((D, 2 * W), BF16, any_spec),
        ub_out=((D, 2 * W), BF16, any_spec),
        small_out=((8, D), F32, vmem_spec),
        late_out=((8, W), F32, vmem_spec),
    )
    vm = lambda shape, kind: pltpu.VMEM(shape, kind)
    scratch = dict(
        send=pltpu.SemaphoreType.DMA((128,)),
        recv=pltpu.SemaphoreType.DMA((128,)),
        local=pltpu.SemaphoreType.DMA((24,)),
        xall=vm((4, T, D), BF16),
        xt=vm((D, 4 * T), BF16),
        wqkv=vm((D, 3 * W), BF16),
        wo=vm((2 * W, D), BF16),
        we=vm((2, D, F), BF16),
        ws=vm((2, F, D), BF16),
        eb=vm((2, 1, F), F32),
        cot=vm((TM, D), BF16),
        segs=vm((4, 1, T), F32),
        bias=vm((T, T), F32),
        kv=vm((4, HP, 2, T, 128), BF16),
        qm=vm((2 * HP, T, 128), BF16),
        dm=vm((2 * HP, T, 128), BF16),
        m_s=vm((2 * HP, 1, T), F32),
        l_s=vm((2 * HP, 1, T), F32),
        delta=vm((2 * HP, 1, T), F32),
        acc=vm((2 * HP, 64, T), F32),
        att=vm((T, W), BF16),
        att_o=vm((TM, W), BF16),
        n1=vm((TM, D), F32),
        r1=vm((TM, 128), F32),
        sec=vm((TM, D), F32),
        gf=vm((TM, D), F32),
        gmix=vm((TM, D), F32),
        fl=vm((T, D), BF16),
        flt=vm((D, T), BF16),
        gs=vm((T, D), BF16),
        gm=vm((T, D), BF16),
        gp=vm((2, TM, F), F32),
        hid=vm((T, F), BF16),
        gpre=vm((T, F), BF16),
        oy=vm((TM, D), BF16),
        small=vm((8, D), F32),
        es=vm((2, 8, D), F32),
        es_r=vm((5, 8, D), F32),
        ls=vm((2, 8, W), F32),
        ls_r=vm((4, 8, W), F32),
        dkv=vm((4 * T, 2 * W), BF16),
        dq=vm((T, W), BF16),
        dxy=vm((4, TM, D), BF16),
        dxz=vm((3, TM, D), BF16),
        igm=vm((TM, D), BF16),
        ua=vm((D, 2 * W), BF16),
        ub=vm((D, 2 * W), BF16),
    )
    for name, rows, cols in (("us", F, D), ("ue", D, F), ("ua", D, 2 * W), ("ub", D, 2 * W)):
        for k in range(4):
            rows = rows // 2
            scratch[f"{name}_r{k}"] = vm((rows, cols), BF16)
    names = list(ins) + list(outs) + list(scratch)
    return pl.pallas_call(
        make_kernel(sh, names, orders),
        out_shape=[jax.ShapeDtypeStruct(o[0], o[1]) for o in outs.values()],
        in_specs=list(ins.values()),
        out_specs=[o[2] for o in outs.values()],
        scratch_shapes=list(scratch.values()),
        compiler_params=pltpu.CompilerParams(
            collective_id=0, has_side_effects=True, vmem_limit_bytes=63 * 1024 * 1024
        ),
        name="layer",
    )(*args)


def finish_kernel(sh, names, *refs):
    r = types.SimpleNamespace(**dict(zip(names, refs)))
    W = sh.hw
    half = sh.units // 2
    pieces = []
    for at in range(2):
        pieces.append((r.us.at[pl.ds(at * half, half)], r.us_v.at[at], r.usf.at[at], r.us_out.at[pl.ds(at * half, half)]))
    for at in range(2):
        rows = pl.ds(at * W, W)
        pieces.append((r.ue.at[rows], r.ue_v.at[at], r.uef.at[at], r.ue_out.at[rows]))
    cols = [pl.ds(0, W), pl.ds(W, W)]
    pieces.append((r.ub.at[:, cols[0]], r.ab_v.at[0], r.abf.at[0], r.wk_out))
    pieces.append((r.ub.at[:, cols[1]], r.ab_v.at[1], r.abf.at[1], r.wv_out))
    pieces.append((r.ua.at[:, cols[0]], r.ab_v.at[2], r.abf.at[2], r.wq_out))
    for at in range(2):
        rows = pl.ds(at * W, W)
        pieces.append((r.ua.at[rows, cols[1]], r.o_v.at[at], r.of.at[at], r.wo_out.at[:, cols[at]]))
    pieces.append((r.ig, r.ig_v, r.igf, r.ig_out))
    passed = pltpu.make_async_copy(r.out, r.out_out, r.sems.at[0])
    passed.start()
    reads = [pltpu.make_async_copy(p[0], p[1], r.sems.at[1 + k]) for k, p in enumerate(pieces)]
    for copy in reads:
        copy.start()
    small = r.small[...]
    for name, at in (("fg", 0), ("fs", 1), ("sb", 2), ("ag", 3), ("as_", 4), ("ob", 5)):
        getattr(r, name)[...] = small[at]
    r.eb[0 : sh.width] = small[6]
    r.eb[sh.width :] = small[7]
    r.qb[...] = r.late[0]
    r.vb[...] = r.late[1]
    writes = []
    for k, (_, low, wide, target) in enumerate(pieces):
        reads[k].wait()
        rows = low.shape[0]
        step = 96 if rows % 96 == 0 else 64

        def tile(i, carry):
            at = pl.ds(pl.multiple_of(i * step, step), step)
            wide[at, :] = low[at, :].astype(F32)
            return carry

        lax.fori_loop(0, rows // step, tile, 0)
        copy = pltpu.make_async_copy(wide, target, r.sems.at[1 + len(pieces) + k])
        copy.start()
        writes.append(copy)
    passed.wait()
    for copy in writes:
        copy.wait()


def finish_call(sh, parts):
    T, D, W, F = sh.tokens, sh.width, sh.hw, sh.units
    any_spec = pl.BlockSpec(memory_space=pl.ANY)
    hbm_spec = pl.BlockSpec(memory_space=pltpu.HBM)
    vmem_spec = pl.BlockSpec(memory_space=pltpu.VMEM)
    ins = dict(
        out=hbm_spec, ig=hbm_spec, ue=hbm_spec, us=hbm_spec, ua=hbm_spec, ub=hbm_spec,
        small=vmem_spec, late=vmem_spec,
    )
    outs = dict(
        out_out=((T, D), BF16, any_spec),
        ig_out=((T, D), F32, any_spec),
        wq_out=((D, W), F32, any_spec),
        wk_out=((D, W), F32, any_spec),
        wv_out=((D, W), F32, any_spec),
        qb=((W,), F32, vmem_spec),
        vb=((W,), F32, vmem_spec),
        wo_out=((W, D), F32, any_spec),
        ob=((D,), F32, vmem_spec),
        ag=((D,), F32, vmem_spec),
        as_=((D,), F32, vmem_spec),
        ue_out=((D, F), F32, any_spec),
        eb=((F,), F32, vmem_spec),
        us_out=((F, D), F32, any_spec),
        sb=((D,), F32, vmem_spec),
        fg=((D,), F32, vmem_spec),
        fs=((D,), F32, vmem_spec),
    )
    scratch = dict(sems=pltpu.SemaphoreType.DMA((24,)))
    for low, wide, shape in (
        ("us_v", "usf", (2, F // 2, D)),
        ("ue_v", "uef", (2, W, F)),
        ("ab_v", "abf", (3, D, W)),
        ("o_v", "of", (2, W, W)),
        ("ig_v", "igf", (T, D)),
    ):
        scratch[low], scratch[wide] = pltpu.VMEM(shape, BF16), pltpu.VMEM(shape, F32)
    names = list(ins) + list(outs) + list(scratch)
    return pl.pallas_call(
        functools.partial(finish_kernel, sh, names),
        out_shape=[jax.ShapeDtypeStruct(o[0], o[1]) for o in outs.values()],
        in_specs=list(ins.values()),
        out_specs=[o[2] for o in outs.values()],
        scratch_shapes=list(scratch.values()),
        compiler_params=pltpu.CompilerParams(vmem_limit_bytes=63 * 1024 * 1024),
        name="finish",
    )(*parts)


def fused_body(
    mesh_sizes, inputs, segments, query_proj, key_proj, value_proj, query_bias, value_bias, output_proj,
    output_bias, attn_gain, attn_shift, expand_proj, expand_bias, shrink_proj, shrink_bias,
    final_gain, final_shift, cotangent,
):
    sh = Shapes(mesh_sizes, inputs.shape[0], inputs.shape[1], query_proj.shape[1], expand_proj.shape[1])
    parts = layer_call(
        sh,
        (
            segments, query_bias, value_bias, output_bias, attn_gain, attn_shift, expand_bias, shrink_bias,
            final_gain, final_shift, inputs, query_proj, key_proj, value_proj, output_proj, expand_proj,
            shrink_proj, cotangent,
        ),
    )
    return finish_call(sh, parts)


contract_rows = (((0,), (0,)), ((), ()))
contract_cols = (((1,), (1,)), ((), ()))


def matmul(left, right):
    return jnp.dot(left, right, preferred_element_type=jnp.float32)


def inner_rows(left, right):
    return lax.dot_general(left, right, contract_rows, preferred_element_type=jnp.float32)


def inner_cols(left, right):
    return lax.dot_general(left, right, contract_cols, preferred_element_type=jnp.float32)


def norm_forward(values, gain, shift):
    centred = values - jnp.mean(values, axis=-1, keepdims=True)
    spread = jnp.mean(centred * centred, axis=-1, keepdims=True)
    recip = lax.rsqrt(spread + norm_eps)
    normed = centred * recip
    return (normed * gain + shift, normed, recip)


def norm_backward(upstream, normed, recip, gain):
    scaled = upstream * gain
    centred = (
        scaled
        - jnp.mean(scaled, axis=-1, keepdims=True)
        - normed * jnp.mean(scaled * normed, axis=-1, keepdims=True)
    )
    return (centred * recip, jnp.sum(upstream * normed, axis=0), jnp.sum(upstream, axis=0))


def cross_scores(left, right):
    return inner_cols(left, right)


def spread_apply(weights_in, right):
    return matmul(weights_in, right)


def spread_transpose(weights_in, left):
    return inner_rows(weights_in, left)


def body(
    inputs,
    segments,
    query_proj,
    key_proj,
    value_proj,
    query_bias,
    value_bias,
    output_proj,
    output_bias,
    attn_gain,
    attn_shift,
    expand_proj,
    expand_bias,
    shrink_proj,
    shrink_bias,
    final_gain,
    final_shift,
    cotangent,
):
    head_count = query_proj.shape[1] // HEAD_DIM
    scale = HEAD_DIM ** (-0.5)
    seg_local = segments[0]
    queries = (matmul(inputs, query_proj) + query_bias.astype(jnp.float32)).astype(jnp.bfloat16)
    keys = matmul(inputs, key_proj).astype(jnp.bfloat16)
    values = (matmul(inputs, value_proj) + value_bias.astype(jnp.float32)).astype(jnp.bfloat16)
    all_keys, all_values, key_ids = (
        lax.all_gather(keys, "ctx", axis=0, tiled=True),
        lax.all_gather(values, "ctx", axis=0, tiled=True),
        lax.all_gather(seg_local.astype(jnp.bfloat16), "ctx", axis=0, tiled=True),
    )
    query_segs = seg_local.astype(jnp.float32)
    key_segs = key_ids.astype(jnp.float32)
    same_seg = query_segs[:, None] == key_segs[None, :]

    def split_heads(matrix):
        return jnp.swapaxes(matrix.reshape(matrix.shape[0], head_count, HEAD_DIM), 0, 1)

    def join_heads(stack):
        return jnp.swapaxes(stack, 0, 1).reshape(stack.shape[1], head_count * HEAD_DIM)

    query_heads = split_heads(queries)
    key_heads = split_heads(all_keys)
    value_heads = split_heads(all_values)

    def head_forward(state, triple):
        query_head, key_head, value_head = triple
        scores = cross_scores(query_head, key_head) * scale
        scores = jnp.where(same_seg, scores, masked)
        row_max = jnp.max(scores, axis=1, keepdims=True)
        exp_scores = jnp.where(same_seg, jnp.exp(scores - row_max), 0.0)
        row_sum = jnp.sum(exp_scores, axis=1, keepdims=True)
        attn_probs = (exp_scores / row_sum).astype(jnp.bfloat16)
        mixed = spread_apply(attn_probs, value_head)
        return (state, (mixed, row_max + jnp.log(row_sum)))

    mixed_heads, log_sums = lax.scan(head_forward, None, (query_heads, key_heads, value_heads))[1]
    attended = join_heads(mixed_heads).astype(jnp.bfloat16)
    attn_total = lax.psum(matmul(attended, output_proj).astype(jnp.bfloat16), "tensor").astype(
        jnp.float32
    )
    attn_gain_f = attn_gain.astype(jnp.float32)
    first, first_normed, first_recip = norm_forward(
        inputs.astype(jnp.float32) + attn_total + output_bias.astype(jnp.float32),
        attn_gain_f,
        attn_shift.astype(jnp.float32),
    )
    first_low = first.astype(jnp.bfloat16)
    pre_act = matmul(first_low, expand_proj) + expand_bias.astype(jnp.float32)
    activated, gelu_back = jax.vjp(lambda pre_in: jax.nn.gelu(pre_in, approximate=False), pre_act)
    hidden = activated.astype(jnp.bfloat16)
    feed_total = lax.psum(matmul(hidden, shrink_proj).astype(jnp.bfloat16), "tensor").astype(
        jnp.float32
    )
    second = first + feed_total + shrink_bias.astype(jnp.float32)
    final_gain_f = final_gain.astype(jnp.float32)
    output, second_normed, second_recip = norm_forward(
        second, final_gain_f, final_shift.astype(jnp.float32)
    )
    upstream = cotangent.astype(jnp.float32)
    grad_second, fgain_grad, fshift_grad = norm_backward(
        upstream, second_normed, second_recip, final_gain_f
    )
    sbias_grad = jnp.sum(grad_second, axis=0)
    grad_second_low = grad_second.astype(jnp.bfloat16)
    shrink_grad = inner_rows(hidden, grad_second_low)
    grad_act = inner_cols(grad_second_low, shrink_proj)
    grad_pre = gelu_back(grad_act)[0].astype(jnp.bfloat16)
    ebias_grad = jnp.sum(grad_pre.astype(jnp.float32), axis=0)
    expand_grad = inner_rows(first_low, grad_pre)
    grad_first = grad_second + lax.psum(
        inner_cols(grad_pre, expand_proj).astype(jnp.bfloat16), "tensor"
    ).astype(jnp.float32)
    grad_mix, again_grad, ashift_grad = norm_backward(
        grad_first, first_normed, first_recip, attn_gain_f
    )
    obias_grad = jnp.sum(grad_mix, axis=0)
    grad_mix_low = grad_mix.astype(jnp.bfloat16)
    oproj_grad = inner_rows(attended, grad_mix_low)
    grad_attended = inner_cols(grad_mix_low, output_proj).astype(jnp.bfloat16)
    grad_heads = split_heads(grad_attended)

    def head_backward(state, group):
        query_head, key_head, value_head, grad_head, log_sum = group
        scores = cross_scores(query_head, key_head) * scale
        attn_probs = jnp.where(same_seg, jnp.exp(scores - log_sum), 0.0)
        grad_probs = cross_scores(grad_head, value_head)
        row_dot = jnp.sum(attn_probs * grad_probs, axis=1, keepdims=True)
        grad_scores = (attn_probs * (grad_probs - row_dot)).astype(jnp.bfloat16)
        grad_query = spread_apply(grad_scores, key_head) * scale
        grad_key = spread_transpose(grad_scores, query_head) * scale
        grad_value = spread_transpose(attn_probs.astype(jnp.bfloat16), grad_head)
        return (state, (grad_query, grad_key, grad_value))

    query_back, key_back, value_back = lax.scan(
        head_backward, None, (query_heads, key_heads, value_heads, grad_heads, log_sums)
    )[1]
    grad_queries = join_heads(query_back).astype(jnp.bfloat16)
    key_sum, value_sum = (
        lax.psum_scatter(
            join_heads(key_back).astype(jnp.bfloat16), "ctx", scatter_dimension=0, tiled=True
        ).astype(jnp.float32),
        lax.psum_scatter(
            join_heads(value_back).astype(jnp.bfloat16), "ctx", scatter_dimension=0, tiled=True
        ).astype(jnp.float32),
    )
    grad_keys = key_sum.astype(jnp.bfloat16)
    grad_values = value_sum.astype(jnp.bfloat16)
    qbias_grad = jnp.sum(grad_queries.astype(jnp.float32), axis=0)
    vbias_grad = jnp.sum(grad_values.astype(jnp.float32), axis=0)
    query_grad = inner_rows(inputs, grad_queries)
    key_grad = inner_rows(inputs, grad_keys)
    value_grad = inner_rows(inputs, grad_values)
    back_terms = (
        inner_cols(grad_queries, query_proj)
        + inner_cols(grad_keys, key_proj)
        + inner_cols(grad_values, value_proj)
    )
    input_grad = grad_mix + lax.psum(back_terms.astype(jnp.bfloat16), "tensor").astype(jnp.float32)
    (
        query_grad,
        key_grad,
        value_grad,
        qbias_grad,
        vbias_grad,
        oproj_grad,
        obias_grad,
        again_grad,
        ashift_grad,
        expand_grad,
        ebias_grad,
        shrink_grad,
        sbias_grad,
        fgain_grad,
        fshift_grad,
    ) = lax.psum(
        (
            query_grad,
            key_grad,
            value_grad,
            qbias_grad,
            vbias_grad,
            oproj_grad,
            obias_grad,
            again_grad,
            ashift_grad,
            expand_grad,
            ebias_grad,
            shrink_grad,
            sbias_grad,
            fgain_grad,
            fshift_grad,
        ),
        ("dp", "ctx"),
    )
    return (
        output.astype(jnp.bfloat16),
        input_grad,
        query_grad,
        key_grad,
        value_grad,
        qbias_grad,
        vbias_grad,
        oproj_grad,
        obias_grad,
        again_grad,
        ashift_grad,
        expand_grad,
        ebias_grad,
        shrink_grad,
        sbias_grad,
        fgain_grad,
        fshift_grad,
    )


def solution(mesh):
    in_specs = (
        P(("dp", "ctx"), None),
        P("dp", "ctx"),
        P(None, "tensor"),
        P(None, "tensor"),
        P(None, "tensor"),
        P("tensor"),
        P("tensor"),
        P("tensor", None),
        P(),
        P(),
        P(),
        P(None, "tensor"),
        P("tensor"),
        P("tensor", None),
        P(),
        P(),
        P(),
        P(("dp", "ctx"), None),
    )
    out_specs = (
        P(("dp", "ctx"), None),
        P(("dp", "ctx"), None),
        P(None, "tensor"),
        P(None, "tensor"),
        P(None, "tensor"),
        P("tensor"),
        P("tensor"),
        P("tensor", None),
        P(),
        P(),
        P(),
        P(None, "tensor"),
        P("tensor"),
        P("tensor", None),
        P(),
        P(),
        P(),
    )
    sizes = dict(mesh.shape)
    fits = sizes == {"dp": 4, "ctx": 4, "tensor": 2}
    chosen = functools.partial(fused_body, sizes) if fits else body
    return jax.shard_map(chosen, mesh=mesh, in_specs=in_specs, out_specs=out_specs, check_vma=False)
```

```python
import functools
import types

import jax
import jax.numpy as jnp
from jax import lax
from jax.experimental import pallas as pl
from jax.experimental.pallas import tpu as pltpu
from jax.sharding import PartitionSpec as P

HEAD_DIM = 64
norm_eps = 1e-12
masked = -1e30
MESH = pl.DeviceIdType.MESH
CORE, XS, YS, Z1, Z2, LINE = range(6)
BF16, F32 = jnp.bfloat16, jnp.float32
INV_SQRT2 = 0.7071067811865476
INV_SQRT_2PI = 0.3989422804014327


def nn(left, right):
    return jnp.dot(left, right, preferred_element_type=F32)


def nt(left, right):
    return lax.dot_general(left, right, (((1,), (1,)), ((), ())), preferred_element_type=F32)


def tn(left, right):
    return lax.dot_general(left, right, (((0,), (0,)), ((), ())), preferred_element_type=F32)


def normalise(values):
    centred = values - jnp.mean(values, axis=-1, keepdims=True)
    spread = jnp.mean(centred * centred, axis=-1, keepdims=True)
    recip = lax.rsqrt(spread + norm_eps)
    return centred * recip, recip


def denormalise(scaled, normed, recip):
    return recip * (
        scaled
        - jnp.mean(scaled, axis=-1, keepdims=True)
        - normed * jnp.mean(scaled * normed, axis=-1, keepdims=True)
    )


def gelu_parts(pre):
    phi_sum = 0.5 + 0.5 * lax.erf(pre * INV_SQRT2)
    slope = phi_sum + pre * (INV_SQRT_2PI * jnp.exp(-0.5 * pre * pre))
    return pre * phi_sum, slope


def column_sum(values):
    return jnp.sum(values, axis=0, keepdims=True)


class Shapes:
    def __init__(self, mesh, tokens, width, heads_width, units):
        self.nd, self.nc = mesh["dp"], mesh["ctx"]
        self.nx = self.nd // 2
        self.tokens, self.mine = tokens, tokens // 2
        self.width, self.hw, self.units = width, heads_width, units
        self.pairs = heads_width // 128


def make_kernel(sh, names):
    T, TM, D, W, F = sh.tokens, sh.mine, sh.width, sh.hw, sh.units
    HP = sh.pairs
    TILE = 512
    NTILE = F // TILE
    SLOTS = 4
    PARTS = 2
    PR = TM // PARTS

    def kernel(*refs):
        r = types.SimpleNamespace(**dict(zip(names, refs)))
        send_ref, recv_ref, local_ref = r.send, r.recv, r.local
        d, c, t = lax.axis_index("dp"), lax.axis_index("ctx"), lax.axis_index("tensor")
        core, xpos = lax.rem(d, 2), d // 2
        low_bit, high_bit = lax.rem(c, 2), c // 2
        next_c = c + 1 - 2 * low_bit
        z1_peer, z2_peer = (d, next_c, t), (d, c + 2 - 4 * high_bit, t)
        z3_peer = (d, next_c + 2 - 4 * high_bit, t)
        y_peer = (d, c, 1 - t)
        core_peer = (d + 1 - 2 * core, c, t)
        x_peer = (d + 2 - 4 * xpos, c, t)
        peer_of = {CORE: core_peer, XS: x_peer, YS: y_peer, Z1: z1_peer, Z2: z2_peer}
        bit_of = {CORE: core, XS: xpos, YS: t, Z1: low_bit, Z2: high_bit}
        my_rows = pl.ds(pl.multiple_of(t * TM, TM), TM)
        peer_rows = pl.ds(pl.multiple_of((1 - t) * TM, TM), TM)
        counts = [0, 0]

        def take(kind, k=1):
            at = counts[kind]
            counts[kind] += k
            assert counts[kind] <= (send_ref, local_ref)[kind].shape[0], counts
            return at

        def remote(src, dst, device, at=None, recv_at=None):
            at = take(0) if at is None else at
            recv_at = at if recv_at is None else recv_at
            return pltpu.make_async_remote_copy(
                src_ref=src, dst_ref=dst, send_sem=send_ref.at[at], recv_sem=recv_ref.at[recv_at],
                device_id=device, device_id_type=MESH,
            )

        def local(src, dst):
            return pltpu.make_async_copy(src, dst, local_ref.at[take(1)])

        unsent = []

        def go(copy, where=None):
            if where is None:
                copy.start()
            else:
                pl.when(where)(lambda: copy.start())
            unsent.append((copy, where))

        def wait_sends(*but):
            kept = [entry for entry in unsent if any(entry[0] is other for other in but)]
            for copy, where in unsent:
                if any(copy is other for other in but):
                    continue
                if where is None:
                    copy.wait_send()
                else:
                    pl.when(where)(lambda copy=copy: copy.wait_send())
            unsent[:] = kept

        loads = types.SimpleNamespace(
            x=local(r.x_in, r.xall.at[0]),
            wk=local(r.wk_in, r.wqkv.at[:, pl.ds(W, W)]),
            wv=local(r.wv_in, r.wqkv.at[:, pl.ds(2 * W, W)]),
            wq=local(r.wq_in, r.wqkv.at[:, pl.ds(0, W)]),
            wo=local(r.wo_in, r.wo.at[pl.ds(0, W)]),
            we=local(r.we_in, r.we.at[0]),
            ws=local(r.ws_in, r.ws.at[0]),
            cot=local(r.cot_in.at[my_rows], r.cot),
        )
        for copy in vars(loads).values():
            copy.start()

        def row(ref):
            return ref[...].astype(F32).reshape(1, ref.shape[0])

        vec = [row(ref) for ref in (r.ob_in, r.ag_in, r.as_in, r.sb_in, r.fg_in, r.fs_in)]
        r.eb[0] = row(r.eb_in)
        r.segs[0] = r.seg_in[...].astype(F32)
        barrier = pltpu.get_barrier_semaphore()
        greeted = [y_peer, core_peer, x_peer, z1_peer, z2_peer, z3_peer]
        for device in greeted:
            pl.semaphore_signal(barrier, inc=1, device_id=device, device_id_type=MESH)
        pl.semaphore_wait(barrier, len(greeted))

        seg_copies = [None] + [
            remote(r.segs.at[0], r.segs.at[k], peer) for k, peer in ((1, z1_peer), (2, z2_peer), (3, z3_peer))
        ]
        eb_copy = remote(r.eb.at[0], r.eb.at[1], y_peer)
        x_rows = [pl.ds(pl.multiple_of(t * TM + k * PR, PR), PR) for k in range(PARTS)]
        mid = lax.rem(low_bit + high_bit, 2)
        is_mid, is_end = mid == 1, mid == 0
        slots = (0, 1, 2 + mid, 3 - mid)
        x_at = take(0, 3 * PARTS)

        def x_recv(slot, k):
            return x_at + (slot - 1) * PARTS + k

        def x_move(src_slot, dst_slot, peer, k):
            src = r.x_in.at[x_rows[k]] if src_slot == 0 else r.xall.at[src_slot, x_rows[k]]
            return remote(src, r.xall.at[dst_slot, x_rows[k]], peer, None, x_recv(dst_slot, k))

        x_near = [x_move(0, 1, z1_peer, k) for k in range(PARTS)]
        x_far = [x_move(0, 3, z3_peer, k) for k in range(PARTS)]
        x_next = (
            None,
            [x_move(1, 2, z3_peer, k) for k in range(PARTS)],
            [x_move(3, 2, z1_peer, k) for k in range(PARTS)],
            [x_move(2, 3, z1_peer, k) for k in range(PARTS)],
        )
        x_y = [None] + [
            [remote(r.xall.at[slots[o], x_rows[k]], r.xall.at[slots[o], x_rows[k]], y_peer) for k in range(PARTS)]
            for o in (1, 2, 3)
        ]
        for k in range(PARTS):
            go(x_near[k])
            go(x_far[k], is_mid)
        for copy in seg_copies[1:]:
            go(copy)
        go(eb_copy)

        def arrive(o, k):
            here = r.xall.at[slots[o], x_rows[k]]
            remote(here, here, z1_peer, x_at, x_recv(slots[o], k)).wait_recv()
            go(x_next[o][k], is_mid)
            go(x_y[o][k])

        def block_here(o):
            if o == 1:
                for copy in seg_copies[1:]:
                    copy.wait_recv()
            for k in range(PARTS):
                x_y[o][k].wait_recv()

        chunks = [
            (r.wo_in, r.wo.at[pl.ds(W, W)], W, 0, 1),
            (r.we_in, r.we.at[1], D, 0, 2),
            (r.we_in, r.we.at[1], D, 1, 2),
            (r.ws_in, r.ws.at[1], F, 0, 2),
            (r.ws_in, r.ws.at[1], F, 1, 2),
        ]
        pieces = sh.nd * 2

        def window(chunk, owner):
            rows, part, parts = chunk[2:]
            size = rows // pieces // parts
            return pl.ds(pl.multiple_of(owner * (rows // pieces) + part * size, size), size)

        own_piece, pair_piece = d * 2 + low_bit, d * 2 + 1 - low_bit
        x_d = d + 2 - 4 * xpos
        x_pieces = (x_d * 2 + low_bit, x_d * 2 + 1 - low_bit)
        w_y, w_z, w_x, w_core = [], [], [], []
        for chunk in chunks:
            source, held = chunk[0], chunk[1]

            def move(owner, peer):
                where = window(chunk, owner)
                return remote(held.at[where], held.at[where], peer)

            own = window(chunk, own_piece)
            w_y.append(remote(source.at[own], held.at[own], y_peer))
            w_z.append(move(own_piece, z1_peer))
            w_x.append([move(piece, x_peer) for piece in (own_piece, pair_piece)])
            w_core.append([move(piece, core_peer) for piece in (own_piece, pair_piece) + x_pieces])

        def hop1(i):
            w_y[i].wait_recv()
            go(w_z[i])
            go(w_x[i][0])
            go(w_core[i][0])

        def hop2(i):
            w_z[i].wait_recv()
            go(w_x[i][1])
            go(w_core[i][1])

        def hop3(i):
            for k in range(2):
                w_x[i][k].wait_recv()
                go(w_core[i][2 + k])

        def weights_done(i):
            for copy in w_core[i]:
                copy.wait_recv()

        for i in range(3):
            go(w_y[i])

        kv = r.kv
        value_bias = row(r.vb_in)
        scale = HEAD_DIM ** (-0.5)
        lane = lax.broadcasted_iota(jnp.int32, (T, 128), 1)

        def split_pair(target, p, pair):
            target[2 * p] = jnp.where(lane < 64, pair, 0.0).astype(BF16)
            target[2 * p + 1] = jnp.where(lane < 64, 0.0, pair).astype(BF16)

        def set_keys_values(slot):
            both = nn(r.xall[slot], r.wqkv[:, W:])
            for p in range(HP):
                kv[slot, p, 0] = both[:, p * 128 : (p + 1) * 128].astype(BF16)
                cols = slice(W + p * 128, W + (p + 1) * 128)
                kv[slot, p, 1] = (both[:, cols] + value_bias[:, p * 128 : (p + 1) * 128]).astype(BF16)

        def set_bias(slot):
            seg_keys = jnp.broadcast_to(r.segs[slot], (128, T)).T
            for j in range(T // 128):
                cols = slice(j * 128, (j + 1) * 128)
                r.bias[:, cols] = jnp.where(seg_keys == r.segs[0, :, cols], 0.0, masked)

        loads.x.wait()
        loads.wk.wait()
        loads.wv.wait()
        set_keys_values(0)
        loads.wq.wait()
        queries = (nn(r.xall[0], r.wqkv[:, :W]) + row(r.qb_in)).astype(BF16).astype(F32) * scale
        for p in range(HP):
            split_pair(r.qm, p, queries[:, p * 128 : (p + 1) * 128])

        m_s, l_s, acc = r.m_s, r.l_s, r.acc
        m_s[...] = jnp.full_like(m_s, masked)
        l_s[...] = jnp.zeros_like(l_s)
        acc[...] = jnp.zeros_like(acc)

        def attend(slot, p):
            pair_keys = kv[slot, p, 0]
            pair_values = kv[slot, p, 1].T
            for hh in range(2):
                h = 2 * p + hh
                s = nt(pair_keys, r.qm[h]) + r.bias[...]
                old = m_s[h]
                new = jnp.maximum(old, jnp.max(s, axis=0, keepdims=True))
                e = jnp.exp(s - new)
                alpha = jnp.exp(old - new)
                l_s[h] = l_s[h] * alpha + jnp.sum(e, axis=0, keepdims=True)
                m_s[h] = new
                acc[h] = acc[h] * alpha + nn(pair_values[hh * 64 : hh * 64 + 64], e.astype(BF16))

        def run(body, services=None):
            def step(p, carry):
                body(p)
                for at, fn in (services or {}).items():
                    pl.when(p == at)(fn)
                return carry

            lax.fori_loop(0, HP, step, 0)

        def together(*fns):
            def all_of():
                for fn, arg in fns:
                    fn(*arg)

            return all_of

        set_bias(0)

        def flip_inputs(slot):
            at = slot * T if isinstance(slot, int) else pl.multiple_of(slot * T, T)
            r.xt[:, pl.ds(at, T)] = r.xall[slot].T

        def next_block(o):
            block_here(o)
            set_keys_values(slots[o])
            set_bias(slots[o])

        hop1(0)
        run(lambda p: attend(0, p), {1: together((arrive, (1, 0))), 2: together((hop1, (1,)))})
        arrive(1, 1)
        go(w_y[3])
        hop1(2)
        flip_inputs(0)
        hop2(0)
        arrive(2, 0)
        hop2(1)
        hop3(0)
        arrive(2, 1)
        go(w_y[4])
        next_block(1)
        run(lambda p: attend(1, p), {0: together((hop3, (1,))), 2: together((hop2, (2,)), (hop1, (3,)))})
        arrive(3, 0)
        hop3(2)
        flip_inputs(1)
        arrive(3, 1)
        next_block(2)
        run(lambda p: attend(slots[2], p), {0: together((hop2, (3,))), 2: together((hop1, (4,)))})
        hop3(3)
        flip_inputs(slots[2])
        hop2(4)
        next_block(3)
        att_at = take(0, HP)

        def att_copy(p):
            cols = pl.ds(p * 128, 128)
            return remote(r.att.at[peer_rows, cols], r.att_o.at[:, cols], y_peer, att_at + p)

        for p in range(HP):
            attend(slots[3], p)
            for h in (2 * p, 2 * p + 1):
                acc[h] = acc[h] / l_s[h]
                m_s[h] = m_s[h] + jnp.log(l_s[h])
            pair = acc[2 * p : 2 * p + 2].reshape(128, T).T
            r.att[:, p * 128 : (p + 1) * 128] = pair.astype(BF16)
            att_copy(p).start()
        loads.wo.wait()
        weights_done(0)
        loads.cot.wait()

        mix = nn(r.att[my_rows, :], r.wo[0:W, :])
        flip_inputs(slots[3])
        for p in range(HP):
            att_copy(p).wait_recv()
        mix = mix + nn(r.att_o[...], r.wo[W : 2 * W, :])
        normed, recip = normalise(r.xall[0, my_rows, :].astype(F32) + mix + vec[0])
        r.n1[...] = normed
        r.r1[...] = jnp.broadcast_to(recip, (TM, 128))
        first = normed * vec[1] + vec[2]
        r.sec[...] = first + vec[3]
        r.fl[my_rows, :] = first.astype(BF16)
        fl_copy = remote(r.fl.at[my_rows], r.fl.at[my_rows], y_peer)
        loads.we.wait()
        loads.ws.wait()
        hop3(4)
        go(fl_copy)


        def tile_cols(j):
            return pl.ds(pl.multiple_of(j * TILE, TILE), TILE)

        def forward_tile(side, j):
            cols = tile_cols(j)
            pre = nn(r.fl[my_rows, :], r.we[side, :, cols]) + r.eb[side, :, cols]
            hidden, slope = gelu_parts(pre)
            hidden = hidden.astype(BF16)
            r.gp[side, :, cols] = slope
            if side == 0:
                r.hid[my_rows, cols] = hidden
            r.sec[...] += nn(hidden, r.ws[side, cols, :])

        def tiles(fn):
            def step(j, carry):
                fn(j)
                return carry

            lax.fori_loop(0, NTILE, step, 0)

        tiles(lambda j: forward_tile(0, j))
        eb_copy.wait_recv()
        for i in range(1, len(chunks)):
            weights_done(i)
        tiles(lambda j: forward_tile(1, j))
        normed2, recip2 = normalise(r.sec[...])
        upstream = r.cot[...].astype(F32)
        grad_second = denormalise(upstream * vec[4], normed2, recip2)
        r.gf[...] = grad_second
        r.gs[my_rows, :] = grad_second.astype(BF16)
        gs_copy = remote(r.gs.at[my_rows], r.gs.at[my_rows], y_peer)
        go(gs_copy)
        small = r.small
        small[0:1, :] = column_sum(upstream * normed2)
        small[1:2, :] = column_sum(upstream)
        small[2:3, :] = column_sum(grad_second)
        r.oy[...] = (normed2 * vec[4] + vec[5]).astype(BF16)
        oy_local = local(r.oy, r.out.at[my_rows])
        oy_local.start()


        def backward_tile(side, j):
            cols = tile_cols(j)
            low = (nt(r.gs[my_rows, :], r.ws[side, cols, :]) * r.gp[side, :, cols]).astype(BF16)
            if side == 0:
                r.gpre[my_rows, cols] = low
            r.gf[...] += nt(low, r.we[side, :, cols])

        tiles(lambda j: backward_tile(0, j))
        tiles(lambda j: backward_tile(1, j))
        grad_first = r.gf[...]
        normed = r.n1[...]
        grad_mix = denormalise(grad_first * vec[1], normed, r.r1[:, 0:1])
        r.gmix[...] = grad_mix
        r.gm[my_rows, :] = grad_mix.astype(BF16)
        gm_copy = remote(r.gm.at[my_rows], r.gm.at[my_rows], y_peer)
        go(gm_copy)
        small[3:4, :] = column_sum(grad_first * normed)
        small[4:5, :] = column_sum(grad_first)
        small[5:6, :] = column_sum(grad_mix)

        def rows_at(ref, first_row, rows):
            return ref.at[pl.ds(pl.multiple_of(first_row, rows), rows)]

        class Unit:
            def __init__(self, grad, whole, out, order, bufs):
                self.grad, self.order, self.bufs = grad, order, bufs
                self.first, self.rows, self.line = [0], [grad.shape[0]], None
                for stage in order:
                    self.rows.append(self.rows[-1] // (4 if stage == LINE else 2))
                    at = c if stage == LINE else bit_of[stage]
                    self.first.append(self.first[-1] + at * self.rows[-1])
                self.down, self.up = [], []
                for k, stage in enumerate(order):
                    rows, last = self.rows[k + 1], k == len(order) - 1
                    target = rows_at(whole, self.first[k + 1], rows)
                    source = target
                    if last:
                        source = rows_at(grad, self.first[k + 1], rows)
                        self.kept = local(source, target)
                    if stage == LINE:
                        self.line = k
                        self.far = self.first[k] + 2 * (1 - high_bit) * rows
                        self.edge = self.first[k] + 3 * high_bit * rows
                        near = self.first[k] + 2 * high_bit * rows
                        ends = grad.at[pl.ds(pl.multiple_of(self.first[k] + (1 - high_bit) * rows, rows), 3 * rows)]
                        self.down.append(
                            (
                                remote(ends, bufs[k][0], z1_peer),
                                remote(rows_at(grad, self.far, 2 * rows), bufs[k][1], z3_peer),
                                remote(rows_at(grad, self.edge, rows), bufs[k][2], z1_peer),
                            )
                        )
                        near, far = rows_at(whole, near, 2 * rows), rows_at(whole, self.far, 2 * rows)
                        self.up.append(
                            (remote(source, target, z1_peer), remote(near, near, z3_peer), remote(far, far, z1_peer))
                        )
                        continue
                    theirs = rows_at(grad, self.first[k] + (1 - bit_of[stage]) * rows, rows)
                    self.down.append(remote(theirs, bufs[k], peer_of[stage]))
                    self.up.append(remote(source, target, peer_of[stage]))
                self.stored = local(whole, out)

            def add_rows(self, first_row, rows, terms, step):

                def tile(i, carry):
                    window = self.grad.at[pl.ds(pl.multiple_of(first_row + i * step, step), step)]
                    total = window[...].astype(F32)
                    for buf, at in terms:
                        total = total + buf[pl.ds(pl.multiple_of(at + i * step, step), step), :].astype(F32)
                    window[...] = total.astype(BF16)
                    return carry

                lax.fori_loop(0, rows // step, tile, 0)

            def send(self, k):
                go(self.down[k])

            def add(self, k):
                self.down[k].wait_recv()
                self.add_rows(self.first[k + 1], self.rows[k + 1], [(self.bufs[k], 0)], min(96, self.rows[k + 1]))

            def forward(self, k):
                self.add(k)
                self.send(k + 1)

            def spread(self, k):
                go(self.up[k])
                if k == len(self.order) - 1:
                    self.kept.start()

            def back(self, k):
                if k == len(self.order) - 1:
                    self.kept.wait()
                self.up[k].wait_recv()
                if self.line is not None and k - 1 == self.line:
                    go(self.up[k - 1][0])
                else:
                    self.spread(k - 1)

            def za(self):
                go(self.down[self.line][0], is_end)

            def zb(self):
                k = self.line
                rows = self.rows[k + 1]

                @pl.when(is_mid)
                def _():
                    self.down[k][0].wait_recv()
                    self.add_rows(self.far, 2 * rows, [(self.bufs[k][0], (1 - high_bit) * rows)], rows)

                go(self.down[k][1], is_mid)

            def zc(self):
                k = self.line
                rows, (first_buf, second_buf, _) = self.rows[k + 1], self.bufs[k]

                @pl.when(is_mid)
                def _():
                    self.down[k][1].wait_recv()
                    self.add_rows(self.edge, rows, [(second_buf, high_bit * rows)], rows)

                go(self.down[k][2], is_mid)

                @pl.when(is_mid)
                def _():
                    terms = [(first_buf, 2 * high_bit * rows), (second_buf, (1 - high_bit) * rows)]
                    self.add_rows(self.first[k + 1], rows, terms, rows)
                    if k == len(self.order) - 1:
                        self.kept.start()
                        self.up[k][0].start()

            def zd(self):
                k = self.line

                @pl.when(is_end)
                def _():
                    self.down[k][2].wait_recv()
                    self.add_rows(self.first[k + 1], self.rows[k + 1], [(self.bufs[k][2], 0)], self.rows[k + 1])
                    if k == len(self.order) - 1:
                        self.kept.start()
                        self.up[k][0].start()

                if k == len(self.order) - 1:
                    unsent.append((self.up[k][0], None))

            def ze(self):
                k = self.line

                @pl.when(is_mid)
                def _():
                    if k == len(self.order) - 1:
                        self.kept.wait()
                    self.up[k][0].wait_recv()

                go(self.up[k][1], is_mid)

            def zf(self):
                pl.when(is_mid)(lambda: self.up[self.line][1].wait_recv())
                go(self.up[self.line][2], is_mid)

            def zg(self):
                k = self.line

                @pl.when(is_end)
                def _():
                    if k == len(self.order) - 1:
                        self.kept.wait()
                    self.up[k][0].wait_recv()
                    self.up[k][2].wait_recv()

                self.spread(k - 1)

            def turn(self):
                k = len(self.order) - 1
                self.add(k)
                self.spread(k)

            def store(self):
                self.up[0].wait_recv()
                self.stored.start()

        def all_sum(buf, slots, stages):
            copies = [remote(buf.at[k % 2], slots.at[k], peer_of[stage]) for k, stage in enumerate(stages)]

            def start(k):
                copies[k].start()

            def finish(k):
                copies[k].wait()
                total = buf[k % 2] + slots[k]
                if stages[k] == YS:
                    which = lax.broadcasted_iota(jnp.int32, total.shape, 0)
                    total = jnp.where(which < 6, total, buf[k % 2])
                buf[(k + 1) % 2] = total
                if k + 1 < len(stages):
                    start(k + 1)

            return start, finish

        fl_copy.wait_recv()
        gs_copy.wait_recv()

        def other_tile(j):
            cols = tile_cols(j)
            pre = nn(r.fl[peer_rows, :], r.we[0, :, cols]) + r.eb[0, :, cols]
            hidden, slope = gelu_parts(pre)
            r.hid[peer_rows, cols] = hidden.astype(BF16)
            r.gpre[peer_rows, cols] = (nt(r.gs[peer_rows, :], r.ws[0, cols, :]) * slope).astype(BF16)

        tiles(other_tile)
        wait_sends(gm_copy)
        by_line, by_pairs = (CORE, XS, LINE), (CORE, XS, Z1, Z2)
        half_d = D // 2

        def line_unit(grad, whole, out, first_buf, k):
            steps = (r.l0.at[k], r.l1.at[k], r.l2.at[k])
            return Unit(grad, whole, out, by_line, (first_buf, r.x0.at[k], steps))

        def pair_unit(grad, whole, out, k):
            return Unit(grad, whole, out, by_pairs, (r.p0.at[k], r.p1.at[k], r.p2.at[k], r.p3.at[k]))

        s1, s2 = [
            line_unit(r.ws.at[1, pl.ds(at, D)], r.ws.at[0, pl.ds(at, D)], r.us_out.at[pl.ds(at, D)], first_buf, k)
            for k, (at, first_buf) in enumerate(((0, r.s0.at[pl.ds(0, half_d)]), (D, r.s0.at[pl.ds(half_d, half_d)])))
        ]
        e1, e2 = [
            line_unit(
                r.we.at[1, :, pl.ds(at, D)], r.we.at[0, :, pl.ds(at, D)], r.ue_out.at[:, pl.ds(at, D)], r.e0.at[k - 2], k
            )
            for k, at in ((2, 0), (3, D))
        ]
        ua = pair_unit(r.ua, r.s0, r.ua_out, 0)
        ub = pair_unit(r.ub, r.wo, r.ub_out, 1)

        def half_of(which):
            return which * core + (1 - which) * (1 - core)

        def shrink_tiles(which):
            def tile(i, carry):
                at = pl.multiple_of(i * D + half_of(which) * half_d, 128)
                r.ws[1, pl.ds(at, half_d), :] = tn(r.hid[:, pl.ds(at, half_d)], r.gs[...]).astype(BF16)
                return carry

            lax.fori_loop(0, F // D, tile, 0)

        def half_rows(which):
            return pl.ds(pl.multiple_of(half_of(which) * (D // 2), D // 2), D // 2)

        def expand_tiles(which):
            rows = half_rows(which)

            def tile(j):
                cols = tile_cols(j)
                r.we[1, rows, cols] = nn(r.flt[rows, :], r.gpre[:, cols]).astype(BF16)

            tiles(tile)

        def sum_blocks():
            totals = column_sum(r.gpre[...].astype(F32))
            small[6:7, :] = totals[:, :D]
            small[7:8, :] = totals[:, D:]
            r.es[0] = small[...]

        early_start, early_finish = all_sum(r.es, r.es_r, (YS, CORE, XS, Z1, Z2))
        late_start, late_finish = all_sum(r.ls, r.ls_r, (CORE, XS, Z1, Z2))

        def grad_heads():
            gm_copy.wait_recv()
            grad_att = nt(r.gm[...], r.wo[0:W, :]).astype(BF16).astype(F32)
            flipped = grad_att.T.reshape(2 * HP, 64, T)
            r.delta[...] = jnp.sum(acc[...] * flipped, axis=1, keepdims=True)
            for p in range(HP):
                split_pair(r.dm, p, grad_att[:, p * 128 : (p + 1) * 128])
            acc[...] = jnp.zeros_like(acc)

        oy_send = remote(r.oy, r.out.at[my_rows], y_peer)
        dkv = r.dkv

        def pull(slot, p):
            pair_keys, pair_values = kv[slot, p, 0], kv[slot, p, 1]
            flipped_keys = pair_keys.T
            grad_k = jnp.zeros((T, 128), F32)
            grad_v = jnp.zeros((T, 128), F32)
            for hh in range(2):
                h = 2 * p + hh
                q, g = r.qm[h], r.dm[h]
                probs = jnp.exp(nt(pair_keys, q) + (r.bias[...] - m_s[h]))
                grad_p = nt(pair_values, g)
                grad_v = grad_v + nn(probs.astype(BF16), g)
                ds = (probs * (grad_p - r.delta[h])).astype(BF16)
                grad_k = grad_k + nn(ds, q)
                acc[h] += nn(flipped_keys[hh * 64 : hh * 64 + 64], ds)
            rows = slice(slot * T, (slot + 1) * T)
            dkv[rows, pl.ds(pl.multiple_of(p * 128, 128), 128)] = grad_k.astype(BF16)
            dkv[rows, pl.ds(pl.multiple_of(W + p * 128, 128), 128)] = grad_v.astype(BF16)

        dx_y = [remote(r.xall.at[k, pl.ds(0, TM)], r.dxy.at[k], y_peer) for k in range(SLOTS)]

        def dx_move(slot, target, peer):
            return remote(r.xall.at[slot, pl.ds(TM, TM)], r.dxz.at[target], peer)

        dx_end = {3: dx_move(3, 0, z1_peer), 2: dx_move(2, 1, z1_peer), 1: dx_move(1, 2, z1_peer)}
        dx_mid = {3: dx_move(3, 3, z3_peer), 2: dx_move(2, 4, z3_peer), 1: dx_move(1, 5, z1_peer)}

        def dx_rows(slot, rows):
            here = pl.ds(pl.multiple_of(slot * T + rows.start, TM), TM)
            return nt(dkv[here, :], r.wqkv[:, W:])

        def dx_part(slot):
            r.xall[slot, 0:TM] = dx_rows(slot, peer_rows).astype(BF16)
            go(dx_y[slot])
            r.xall[slot, TM:] = dx_rows(slot, my_rows).astype(BF16)

        def dx_sum(slot):
            dx_y[slot].wait_recv()
            total = r.xall[slot, TM:].astype(F32) + r.dxy[slot].astype(F32)
            r.xall[slot, TM:] = total.astype(BF16)
            go(dx_end[slot], is_end)

        def dx_pass(slot):
            came = {3: dx_end[2], 2: dx_end[3], 1: dx_mid[2]}[slot]
            at = {3: 1, 2: 0, 1: 4}[slot]

            @pl.when(is_mid)
            def _():
                came.wait_recv()
                total = r.xall[slot, TM:].astype(F32) + r.dxz[at].astype(F32)
                r.xall[slot, TM:] = total.astype(BF16)

            go(dx_mid[slot], is_mid)

        def dx_last():
            dx_y[0].wait_recv()
            r.gmix[...] += r.dxy[0].astype(F32)

            @pl.when(is_mid)
            def _():
                dx_end[1].wait_recv()
                dx_mid[3].wait_recv()
                r.gmix[...] += r.dxz[2].astype(F32) + r.dxz[3].astype(F32)

            @pl.when(is_end)
            def _():
                dx_mid[1].wait_recv()
                r.gmix[...] += r.dxz[5].astype(F32)

            r.igm[...] = r.gmix[...].astype(BF16)


        def key_value_tiles(which):
            rows = half_rows(which)
            r.ub[rows, :] = nn(r.xt[rows, :], dkv[...]).astype(BF16)

        def query_output_tiles(which):
            rows = half_rows(which)
            r.ua[rows, 0:W] = nn(r.xt[rows, 0:T], r.dq[...]).astype(BF16)
            cols = pl.ds(pl.multiple_of(half_of(which) * W, 128), W)
            r.ua[rows, W:] = tn(r.att[...], r.gm[:, cols]).astype(BF16)

        def query_grads():
            r.dq[...] = (acc[...].reshape(W, T).T * scale).astype(BF16)
            r.ls[0, 0:1, :] = column_sum(r.dq[...].astype(F32))
            r.ls[0, 1:2, :] = column_sum(dkv[:, W:].astype(F32))
            r.ls[0, 2:8, :] = jnp.zeros((6, W), F32)

        def dx_own():
            r.xall[0, 0:TM] = (dx_rows(0, peer_rows) + nt(r.dq[peer_rows, :], r.wqkv[:, :W])).astype(BF16)
            go(dx_y[0])
            r.gmix[...] += dx_rows(0, my_rows) + nt(r.dq[my_rows, :], r.wqkv[:, :W])

        ig_local = local(r.igm, r.ig_out.at[my_rows])
        ig_send = remote(r.igm, r.ig_out.at[my_rows], y_peer)

        def dx_out():
            dx_last()
            ig_local.start()
            go(ig_send)

        shrink_tiles(0)
        s1.send(0)
        s2.send(0)
        r.flt[...] = r.fl[...].T
        shrink_tiles(1)
        expand_tiles(0)
        e1.send(0)
        e2.send(0)
        go(oy_send)
        s1.forward(0)
        expand_tiles(1)
        sum_blocks()
        early_start(0)
        grad_heads()
        set_bias(3)

        def beside_30():
            e2.forward(0)

        run(lambda p: pull(3, p), {0: beside_30})
        s1.add(1)
        s1.za()
        dx_part(3)
        early_finish(0)
        e1.forward(0)
        set_bias(2)

        def beside_21():
            s1.zb()

        run(lambda p: pull(2, p), {1: beside_21})
        e2.add(1)
        e2.za()
        dx_part(2)
        early_finish(1)
        s2.forward(0)
        set_bias(1)

        def beside_10():
            s1.zc()


        def beside_11():
            e2.zb()
            e1.add(1)
            e1.za()

        run(lambda p: pull(1, p), {0: beside_10, 1: beside_11})
        s1.zd()
        dx_part(1)
        set_bias(0)

        def beside_00():
            e2.zc()
            e1.zb()
            s2.add(1)
            s2.za()

        run(lambda p: pull(0, p), {0: beside_00})
        e2.zd()
        query_grads()
        late_start(0)
        key_value_tiles(0)
        ub.send(0)
        late_finish(0)
        s1.ze()
        dx_sum(3)
        e1.zc()
        query_output_tiles(0)
        ua.send(0)
        key_value_tiles(1)
        ub.forward(0)
        s2.zb()
        s1.zf()
        query_output_tiles(1)
        early_finish(2)
        ua.forward(0)
        e1.zd()
        e2.ze()
        s2.zc()
        ub.forward(1)
        s2.zd()
        e1.ze()
        s1.zg()
        early_finish(3)
        late_finish(1)
        ub.forward(2)
        s2.ze()
        e1.zf()
        ua.forward(1)
        ub.turn()
        e1.zg()
        early_finish(4)
        ua.forward(2)
        ub.back(3)
        ua.turn()
        dx_sum(2)
        s2.zf()
        dx_pass(2)
        e1.back(1)
        e2.zf()
        dx_own()
        ub.back(2)
        late_finish(2)
        ua.back(3)
        dx_sum(1)
        s1.back(1)
        s2.zg()
        late_finish(3)
        dx_pass(3)
        ub.back(1)
        dx_pass(1)
        e2.zg()
        s2.back(1)
        s2.store()
        ua.back(2)
        dx_out()
        s1.store()
        e2.back(1)
        ua.back(1)
        e1.store()
        ua.store()
        e2.store()
        ub.store()
        r.small_out[...] = r.es[1]
        r.late_out[...] = r.ls[0]
        oy_local.wait()
        oy_send.wait_recv()
        ig_local.wait()
        ig_send.wait_recv()
        for unit in (s1, s2, e1, e2, ua, ub):
            unit.stored.wait()
        for p in range(HP):
            att_copy(p).wait_send()
        wait_sends()

    return kernel


def layer_call(sh, args):
    T, TM, D, W, F = sh.tokens, sh.mine, sh.width, sh.hw, sh.units
    HP = sh.pairs
    any_spec = pl.BlockSpec(memory_space=pl.ANY)
    vmem_spec = pl.BlockSpec(memory_space=pltpu.VMEM)
    ins = dict(
        seg_in=vmem_spec, qb_in=vmem_spec, vb_in=vmem_spec, ob_in=vmem_spec, ag_in=vmem_spec,
        as_in=vmem_spec, eb_in=vmem_spec, sb_in=vmem_spec, fg_in=vmem_spec, fs_in=vmem_spec,
        x_in=any_spec, wq_in=any_spec, wk_in=any_spec, wv_in=any_spec,
        wo_in=any_spec, we_in=any_spec, ws_in=any_spec, cot_in=any_spec,
    )
    outs = dict(
        out=((T, D), BF16, any_spec),
        ig_out=((T, D), BF16, any_spec),
        ue_out=((D, F), BF16, any_spec),
        us_out=((F, D), BF16, any_spec),
        ua_out=((D, 2 * W), BF16, any_spec),
        ub_out=((D, 2 * W), BF16, any_spec),
        small_out=((8, D), F32, vmem_spec),
        late_out=((8, W), F32, vmem_spec),
    )
    vm = lambda shape, kind: pltpu.VMEM(shape, kind)
    scratch = dict(
        send=pltpu.SemaphoreType.DMA((160,)),
        recv=pltpu.SemaphoreType.DMA((160,)),
        local=pltpu.SemaphoreType.DMA((24,)),
        xall=vm((4, T, D), BF16),
        xt=vm((D, 4 * T), BF16),
        wqkv=vm((D, 3 * W), BF16),
        wo=vm((2 * W, D), BF16),
        we=vm((2, D, F), BF16),
        ws=vm((2, F, D), BF16),
        eb=vm((2, 1, F), F32),
        cot=vm((TM, D), BF16),
        segs=vm((4, 1, T), F32),
        bias=vm((T, T), F32),
        kv=vm((4, HP, 2, T, 128), BF16),
        qm=vm((2 * HP, T, 128), BF16),
        dm=vm((2 * HP, T, 128), BF16),
        m_s=vm((2 * HP, 1, T), F32),
        l_s=vm((2 * HP, 1, T), F32),
        delta=vm((2 * HP, 1, T), F32),
        acc=vm((2 * HP, 64, T), F32),
        att=vm((T, W), BF16),
        att_o=vm((TM, W), BF16),
        n1=vm((TM, D), F32),
        r1=vm((TM, 128), F32),
        sec=vm((TM, D), F32),
        gf=vm((TM, D), F32),
        gmix=vm((TM, D), F32),
        fl=vm((T, D), BF16),
        flt=vm((D, T), BF16),
        gs=vm((T, D), BF16),
        gm=vm((T, D), BF16),
        gp=vm((2, TM, F), F32),
        hid=vm((T, F), BF16),
        gpre=vm((T, F), BF16),
        oy=vm((TM, D), BF16),
        small=vm((8, D), F32),
        es=vm((2, 8, D), F32),
        es_r=vm((5, 8, D), F32),
        ls=vm((2, 8, W), F32),
        ls_r=vm((4, 8, W), F32),
        dkv=vm((4 * T, 2 * W), BF16),
        dq=vm((T, W), BF16),
        dxy=vm((4, TM, D), BF16),
        dxz=vm((6, TM, D), BF16),
        igm=vm((TM, D), BF16),
        ua=vm((D, 2 * W), BF16),
        ub=vm((D, 2 * W), BF16),
        s0=vm((D, D), BF16),
        e0=vm((2, D // 2, D), BF16),
        x0=vm((4, D // 4, D), BF16),
        l0=vm((4, 3 * (D // 16), D), BF16),
        l1=vm((4, 2 * (D // 16), D), BF16),
        l2=vm((4, D // 16, D), BF16),
        p0=vm((2, D // 2, D), BF16),
        p1=vm((2, D // 4, D), BF16),
        p2=vm((2, D // 8, D), BF16),
        p3=vm((2, D // 16, D), BF16),
    )
    names = list(ins) + list(outs) + list(scratch)
    return pl.pallas_call(
        make_kernel(sh, names),
        out_shape=[jax.ShapeDtypeStruct(o[0], o[1]) for o in outs.values()],
        in_specs=list(ins.values()),
        out_specs=[o[2] for o in outs.values()],
        scratch_shapes=list(scratch.values()),
        compiler_params=pltpu.CompilerParams(
            collective_id=0, has_side_effects=True, vmem_limit_bytes=63 * 1024 * 1024
        ),
        name="layer",
    )(*args)


def finish_kernel(sh, names, *refs):
    r = types.SimpleNamespace(**dict(zip(names, refs)))
    W = sh.hw
    half = sh.units // 2
    pieces = []
    for at in range(2):
        pieces.append((r.us.at[pl.ds(at * half, half)], r.us_v.at[at], r.usf.at[at], r.us_out.at[pl.ds(at * half, half)]))
    for at in range(2):
        rows = pl.ds(at * W, W)
        pieces.append((r.ue.at[rows], r.ue_v.at[at], r.uef.at[at], r.ue_out.at[rows]))
    cols = [pl.ds(0, W), pl.ds(W, W)]
    pieces.append((r.ub.at[:, cols[0]], r.ab_v.at[0], r.abf.at[0], r.wk_out))
    pieces.append((r.ub.at[:, cols[1]], r.ab_v.at[1], r.abf.at[1], r.wv_out))
    pieces.append((r.ua.at[:, cols[0]], r.ab_v.at[2], r.abf.at[2], r.wq_out))
    for at in range(2):
        rows = pl.ds(at * W, W)
        pieces.append((r.ua.at[rows, cols[1]], r.o_v.at[at], r.of.at[at], r.wo_out.at[:, cols[at]]))
    pieces.append((r.ig, r.ig_v, r.igf, r.ig_out))
    taken = pltpu.make_async_copy(r.out, r.out_v, r.sems.at[0])
    taken.start()
    reads = [pltpu.make_async_copy(p[0], p[1], r.sems.at[1 + k]) for k, p in enumerate(pieces)]
    for copy in reads:
        copy.start()
    taken.wait()
    passed = pltpu.make_async_copy(r.out_v, r.out_out, r.sems.at[2 * len(pieces) + 1])
    passed.start()
    small = r.small[...]
    for name, at in (("fg", 0), ("fs", 1), ("sb", 2), ("ag", 3), ("as_", 4), ("ob", 5)):
        getattr(r, name)[...] = small[at]
    r.eb[0 : sh.width] = small[6]
    r.eb[sh.width :] = small[7]
    r.qb[...] = r.late[0]
    r.vb[...] = r.late[1]
    writes = []
    for k, (_, low, wide, target) in enumerate(pieces):
        reads[k].wait()
        rows = low.shape[0]
        step = 96 if rows % 96 == 0 else 64

        def tile(i, carry):
            at = pl.ds(pl.multiple_of(i * step, step), step)
            wide[at, :] = low[at, :].astype(F32)
            return carry

        lax.fori_loop(0, rows // step, tile, 0)
        copy = pltpu.make_async_copy(wide, target, r.sems.at[1 + len(pieces) + k])
        copy.start()
        writes.append(copy)
    passed.wait()
    for copy in writes:
        copy.wait()


def finish_call(sh, parts):
    T, D, W, F = sh.tokens, sh.width, sh.hw, sh.units
    any_spec = pl.BlockSpec(memory_space=pl.ANY)
    hbm_spec = pl.BlockSpec(memory_space=pltpu.HBM)
    vmem_spec = pl.BlockSpec(memory_space=pltpu.VMEM)
    ins = dict(
        out=hbm_spec, ig=hbm_spec, ue=hbm_spec, us=hbm_spec, ua=hbm_spec, ub=hbm_spec,
        small=vmem_spec, late=vmem_spec,
    )
    outs = dict(
        out_out=((T, D), BF16, any_spec),
        ig_out=((T, D), F32, any_spec),
        wq_out=((D, W), F32, any_spec),
        wk_out=((D, W), F32, any_spec),
        wv_out=((D, W), F32, any_spec),
        qb=((W,), F32, vmem_spec),
        vb=((W,), F32, vmem_spec),
        wo_out=((W, D), F32, any_spec),
        ob=((D,), F32, vmem_spec),
        ag=((D,), F32, vmem_spec),
        as_=((D,), F32, vmem_spec),
        ue_out=((D, F), F32, any_spec),
        eb=((F,), F32, vmem_spec),
        us_out=((F, D), F32, any_spec),
        sb=((D,), F32, vmem_spec),
        fg=((D,), F32, vmem_spec),
        fs=((D,), F32, vmem_spec),
    )
    scratch = dict(sems=pltpu.SemaphoreType.DMA((24,)), out_v=pltpu.VMEM((T, D), BF16))
    for low, wide, shape in (
        ("us_v", "usf", (2, F // 2, D)),
        ("ue_v", "uef", (2, W, F)),
        ("ab_v", "abf", (3, D, W)),
        ("o_v", "of", (2, W, W)),
        ("ig_v", "igf", (T, D)),
    ):
        scratch[low], scratch[wide] = pltpu.VMEM(shape, BF16), pltpu.VMEM(shape, F32)
    names = list(ins) + list(outs) + list(scratch)
    return pl.pallas_call(
        functools.partial(finish_kernel, sh, names),
        out_shape=[jax.ShapeDtypeStruct(o[0], o[1]) for o in outs.values()],
        in_specs=list(ins.values()),
        out_specs=[o[2] for o in outs.values()],
        scratch_shapes=list(scratch.values()),
        compiler_params=pltpu.CompilerParams(vmem_limit_bytes=63 * 1024 * 1024),
        name="finish",
    )(*parts)


def fused_body(
    mesh_sizes, inputs, segments, query_proj, key_proj, value_proj, query_bias, value_bias, output_proj,
    output_bias, attn_gain, attn_shift, expand_proj, expand_bias, shrink_proj, shrink_bias,
    final_gain, final_shift, cotangent,
):
    sh = Shapes(mesh_sizes, inputs.shape[0], inputs.shape[1], query_proj.shape[1], expand_proj.shape[1])
    parts = layer_call(
        sh,
        (
            segments, query_bias, value_bias, output_bias, attn_gain, attn_shift, expand_bias, shrink_bias,
            final_gain, final_shift, inputs, query_proj, key_proj, value_proj, output_proj, expand_proj,
            shrink_proj, cotangent,
        ),
    )
    return finish_call(sh, parts)


contract_rows = (((0,), (0,)), ((), ()))
contract_cols = (((1,), (1,)), ((), ()))


def matmul(left, right):
    return jnp.dot(left, right, preferred_element_type=jnp.float32)


def inner_rows(left, right):
    return lax.dot_general(left, right, contract_rows, preferred_element_type=jnp.float32)


def inner_cols(left, right):
    return lax.dot_general(left, right, contract_cols, preferred_element_type=jnp.float32)


def norm_forward(values, gain, shift):
    centred = values - jnp.mean(values, axis=-1, keepdims=True)
    spread = jnp.mean(centred * centred, axis=-1, keepdims=True)
    recip = lax.rsqrt(spread + norm_eps)
    normed = centred * recip
    return (normed * gain + shift, normed, recip)


def norm_backward(upstream, normed, recip, gain):
    scaled = upstream * gain
    centred = (
        scaled
        - jnp.mean(scaled, axis=-1, keepdims=True)
        - normed * jnp.mean(scaled * normed, axis=-1, keepdims=True)
    )
    return (centred * recip, jnp.sum(upstream * normed, axis=0), jnp.sum(upstream, axis=0))


def cross_scores(left, right):
    return inner_cols(left, right)


def spread_apply(weights_in, right):
    return matmul(weights_in, right)


def spread_transpose(weights_in, left):
    return inner_rows(weights_in, left)


def body(
    inputs,
    segments,
    query_proj,
    key_proj,
    value_proj,
    query_bias,
    value_bias,
    output_proj,
    output_bias,
    attn_gain,
    attn_shift,
    expand_proj,
    expand_bias,
    shrink_proj,
    shrink_bias,
    final_gain,
    final_shift,
    cotangent,
):
    head_count = query_proj.shape[1] // HEAD_DIM
    scale = HEAD_DIM ** (-0.5)
    seg_local = segments[0]
    queries = (matmul(inputs, query_proj) + query_bias.astype(jnp.float32)).astype(jnp.bfloat16)
    keys = matmul(inputs, key_proj).astype(jnp.bfloat16)
    values = (matmul(inputs, value_proj) + value_bias.astype(jnp.float32)).astype(jnp.bfloat16)
    all_keys, all_values, key_ids = (
        lax.all_gather(keys, "ctx", axis=0, tiled=True),
        lax.all_gather(values, "ctx", axis=0, tiled=True),
        lax.all_gather(seg_local.astype(jnp.bfloat16), "ctx", axis=0, tiled=True),
    )
    query_segs = seg_local.astype(jnp.float32)
    key_segs = key_ids.astype(jnp.float32)
    same_seg = query_segs[:, None] == key_segs[None, :]

    def split_heads(matrix):
        return jnp.swapaxes(matrix.reshape(matrix.shape[0], head_count, HEAD_DIM), 0, 1)

    def join_heads(stack):
        return jnp.swapaxes(stack, 0, 1).reshape(stack.shape[1], head_count * HEAD_DIM)

    query_heads = split_heads(queries)
    key_heads = split_heads(all_keys)
    value_heads = split_heads(all_values)

    def head_forward(state, triple):
        query_head, key_head, value_head = triple
        scores = cross_scores(query_head, key_head) * scale
        scores = jnp.where(same_seg, scores, masked)
        row_max = jnp.max(scores, axis=1, keepdims=True)
        exp_scores = jnp.where(same_seg, jnp.exp(scores - row_max), 0.0)
        row_sum = jnp.sum(exp_scores, axis=1, keepdims=True)
        attn_probs = (exp_scores / row_sum).astype(jnp.bfloat16)
        mixed = spread_apply(attn_probs, value_head)
        return (state, (mixed, row_max + jnp.log(row_sum)))

    mixed_heads, log_sums = lax.scan(head_forward, None, (query_heads, key_heads, value_heads))[1]
    attended = join_heads(mixed_heads).astype(jnp.bfloat16)
    attn_total = lax.psum(matmul(attended, output_proj).astype(jnp.bfloat16), "tensor").astype(
        jnp.float32
    )
    attn_gain_f = attn_gain.astype(jnp.float32)
    first, first_normed, first_recip = norm_forward(
        inputs.astype(jnp.float32) + attn_total + output_bias.astype(jnp.float32),
        attn_gain_f,
        attn_shift.astype(jnp.float32),
    )
    first_low = first.astype(jnp.bfloat16)
    pre_act = matmul(first_low, expand_proj) + expand_bias.astype(jnp.float32)
    activated, gelu_back = jax.vjp(lambda pre_in: jax.nn.gelu(pre_in, approximate=False), pre_act)
    hidden = activated.astype(jnp.bfloat16)
    feed_total = lax.psum(matmul(hidden, shrink_proj).astype(jnp.bfloat16), "tensor").astype(
        jnp.float32
    )
    second = first + feed_total + shrink_bias.astype(jnp.float32)
    final_gain_f = final_gain.astype(jnp.float32)
    output, second_normed, second_recip = norm_forward(
        second, final_gain_f, final_shift.astype(jnp.float32)
    )
    upstream = cotangent.astype(jnp.float32)
    grad_second, fgain_grad, fshift_grad = norm_backward(
        upstream, second_normed, second_recip, final_gain_f
    )
    sbias_grad = jnp.sum(grad_second, axis=0)
    grad_second_low = grad_second.astype(jnp.bfloat16)
    shrink_grad = inner_rows(hidden, grad_second_low)
    grad_act = inner_cols(grad_second_low, shrink_proj)
    grad_pre = gelu_back(grad_act)[0].astype(jnp.bfloat16)
    ebias_grad = jnp.sum(grad_pre.astype(jnp.float32), axis=0)
    expand_grad = inner_rows(first_low, grad_pre)
    grad_first = grad_second + lax.psum(
        inner_cols(grad_pre, expand_proj).astype(jnp.bfloat16), "tensor"
    ).astype(jnp.float32)
    grad_mix, again_grad, ashift_grad = norm_backward(
        grad_first, first_normed, first_recip, attn_gain_f
    )
    obias_grad = jnp.sum(grad_mix, axis=0)
    grad_mix_low = grad_mix.astype(jnp.bfloat16)
    oproj_grad = inner_rows(attended, grad_mix_low)
    grad_attended = inner_cols(grad_mix_low, output_proj).astype(jnp.bfloat16)
    grad_heads = split_heads(grad_attended)

    def head_backward(state, group):
        query_head, key_head, value_head, grad_head, log_sum = group
        scores = cross_scores(query_head, key_head) * scale
        attn_probs = jnp.where(same_seg, jnp.exp(scores - log_sum), 0.0)
        grad_probs = cross_scores(grad_head, value_head)
        row_dot = jnp.sum(attn_probs * grad_probs, axis=1, keepdims=True)
        grad_scores = (attn_probs * (grad_probs - row_dot)).astype(jnp.bfloat16)
        grad_query = spread_apply(grad_scores, key_head) * scale
        grad_key = spread_transpose(grad_scores, query_head) * scale
        grad_value = spread_transpose(attn_probs.astype(jnp.bfloat16), grad_head)
        return (state, (grad_query, grad_key, grad_value))

    query_back, key_back, value_back = lax.scan(
        head_backward, None, (query_heads, key_heads, value_heads, grad_heads, log_sums)
    )[1]
    grad_queries = join_heads(query_back).astype(jnp.bfloat16)
    key_sum, value_sum = (
        lax.psum_scatter(
            join_heads(key_back).astype(jnp.bfloat16), "ctx", scatter_dimension=0, tiled=True
        ).astype(jnp.float32),
        lax.psum_scatter(
            join_heads(value_back).astype(jnp.bfloat16), "ctx", scatter_dimension=0, tiled=True
        ).astype(jnp.float32),
    )
    grad_keys = key_sum.astype(jnp.bfloat16)
    grad_values = value_sum.astype(jnp.bfloat16)
    qbias_grad = jnp.sum(grad_queries.astype(jnp.float32), axis=0)
    vbias_grad = jnp.sum(grad_values.astype(jnp.float32), axis=0)
    query_grad = inner_rows(inputs, grad_queries)
    key_grad = inner_rows(inputs, grad_keys)
    value_grad = inner_rows(inputs, grad_values)
    back_terms = (
        inner_cols(grad_queries, query_proj)
        + inner_cols(grad_keys, key_proj)
        + inner_cols(grad_values, value_proj)
    )
    input_grad = grad_mix + lax.psum(back_terms.astype(jnp.bfloat16), "tensor").astype(jnp.float32)
    (
        query_grad,
        key_grad,
        value_grad,
        qbias_grad,
        vbias_grad,
        oproj_grad,
        obias_grad,
        again_grad,
        ashift_grad,
        expand_grad,
        ebias_grad,
        shrink_grad,
        sbias_grad,
        fgain_grad,
        fshift_grad,
    ) = lax.psum(
        (
            query_grad,
            key_grad,
            value_grad,
            qbias_grad,
            vbias_grad,
            oproj_grad,
            obias_grad,
            again_grad,
            ashift_grad,
            expand_grad,
            ebias_grad,
            shrink_grad,
            sbias_grad,
            fgain_grad,
            fshift_grad,
        ),
        ("dp", "ctx"),
    )
    return (
        output.astype(jnp.bfloat16),
        input_grad,
        query_grad,
        key_grad,
        value_grad,
        qbias_grad,
        vbias_grad,
        oproj_grad,
        obias_grad,
        again_grad,
        ashift_grad,
        expand_grad,
        ebias_grad,
        shrink_grad,
        sbias_grad,
        fgain_grad,
        fshift_grad,
    )


def solution(mesh):
    in_specs = (
        P(("dp", "ctx"), None),
        P("dp", "ctx"),
        P(None, "tensor"),
        P(None, "tensor"),
        P(None, "tensor"),
        P("tensor"),
        P("tensor"),
        P("tensor", None),
        P(),
        P(),
        P(),
        P(None, "tensor"),
        P("tensor"),
        P("tensor", None),
        P(),
        P(),
        P(),
        P(("dp", "ctx"), None),
    )
    out_specs = (
        P(("dp", "ctx"), None),
        P(("dp", "ctx"), None),
        P(None, "tensor"),
        P(None, "tensor"),
        P(None, "tensor"),
        P("tensor"),
        P("tensor"),
        P("tensor", None),
        P(),
        P(),
        P(),
        P(None, "tensor"),
        P("tensor"),
        P("tensor", None),
        P(),
        P(),
        P(),
    )
    sizes = dict(mesh.shape)
    fits = sizes == {"dp": 4, "ctx": 4, "tensor": 2}
    chosen = functools.partial(fused_body, sizes) if fits else body
    return jax.shard_map(chosen, mesh=mesh, in_specs=in_specs, out_specs=out_specs, check_vma=False)
```

```python
import functools
import types

import jax
import jax.numpy as jnp
from jax import lax
from jax.experimental import pallas as pl
from jax.experimental.pallas import tpu as pltpu
from jax.sharding import PartitionSpec as P

HEAD_DIM = 64
norm_eps = 1e-12
masked = -1e30
MESH = pl.DeviceIdType.MESH
CORE, XS, YS, Z1, Z2, LINE = range(6)
BF16, F32 = jnp.bfloat16, jnp.float32
INV_SQRT2 = 0.7071067811865476
INV_SQRT_2PI = 0.3989422804014327


def nn(left, right):
    return jnp.dot(left, right, preferred_element_type=F32)


def nt(left, right):
    return lax.dot_general(left, right, (((1,), (1,)), ((), ())), preferred_element_type=F32)


def tn(left, right):
    return lax.dot_general(left, right, (((0,), (0,)), ((), ())), preferred_element_type=F32)


def normalise(values):
    centred = values - jnp.mean(values, axis=-1, keepdims=True)
    spread = jnp.mean(centred * centred, axis=-1, keepdims=True)
    recip = lax.rsqrt(spread + norm_eps)
    return centred * recip, recip


def denormalise(scaled, normed, recip):
    return recip * (
        scaled
        - jnp.mean(scaled, axis=-1, keepdims=True)
        - normed * jnp.mean(scaled * normed, axis=-1, keepdims=True)
    )


def gelu_parts(pre):
    phi_sum = 0.5 + 0.5 * lax.erf(pre * INV_SQRT2)
    slope = phi_sum + pre * (INV_SQRT_2PI * jnp.exp(-0.5 * pre * pre))
    return pre * phi_sum, slope


def column_sum(values):
    return jnp.sum(values, axis=0, keepdims=True)


class Shapes:
    def __init__(self, mesh, tokens, width, heads_width, units):
        self.nd, self.nc = mesh["dp"], mesh["ctx"]
        self.nx = self.nd // 2
        self.tokens, self.mine = tokens, tokens // 2
        self.width, self.hw, self.units = width, heads_width, units
        self.pairs = heads_width // 128


def make_kernel(sh, names):
    T, TM, D, W, F = sh.tokens, sh.mine, sh.width, sh.hw, sh.units
    HP = sh.pairs
    TILE = 512
    NTILE = F // TILE
    SLOTS = 4
    PARTS = 2
    PR = TM // PARTS

    def kernel(*refs):
        r = types.SimpleNamespace(**dict(zip(names, refs)))
        send_ref, recv_ref, local_ref = r.send, r.recv, r.local
        d, c, t = lax.axis_index("dp"), lax.axis_index("ctx"), lax.axis_index("tensor")
        core, xpos = lax.rem(d, 2), d // 2
        low_bit, high_bit = lax.rem(c, 2), c // 2
        next_c = c + 1 - 2 * low_bit
        z1_peer, z2_peer = (d, next_c, t), (d, c + 2 - 4 * high_bit, t)
        z3_peer = (d, next_c + 2 - 4 * high_bit, t)
        y_peer = (d, c, 1 - t)
        core_peer = (d + 1 - 2 * core, c, t)
        x_peer = (d + 2 - 4 * xpos, c, t)
        peer_of = {CORE: core_peer, XS: x_peer, YS: y_peer, Z1: z1_peer, Z2: z2_peer}
        bit_of = {CORE: core, XS: xpos, YS: t, Z1: low_bit, Z2: high_bit}
        my_rows = pl.ds(pl.multiple_of(t * TM, TM), TM)
        peer_rows = pl.ds(pl.multiple_of((1 - t) * TM, TM), TM)
        counts = [0, 0]

        def take(kind, k=1):
            at = counts[kind]
            counts[kind] += k
            assert counts[kind] <= (send_ref, local_ref)[kind].shape[0], counts
            return at

        def remote(src, dst, device, at=None, recv_at=None):
            at = take(0) if at is None else at
            recv_at = at if recv_at is None else recv_at
            return pltpu.make_async_remote_copy(
                src_ref=src, dst_ref=dst, send_sem=send_ref.at[at], recv_sem=recv_ref.at[recv_at],
                device_id=device, device_id_type=MESH,
            )

        def local(src, dst):
            return pltpu.make_async_copy(src, dst, local_ref.at[take(1)])

        unsent = []

        def go(copy, where=None):
            if where is None:
                copy.start()
            else:
                pl.when(where)(lambda: copy.start())
            unsent.append((copy, where))

        def wait_sends(*but):
            kept = [entry for entry in unsent if any(entry[0] is other for other in but)]
            for copy, where in unsent:
                if any(copy is other for other in but):
                    continue
                if where is None:
                    copy.wait_send()
                else:
                    pl.when(where)(lambda copy=copy: copy.wait_send())
            unsent[:] = kept

        loads = types.SimpleNamespace(
            x=local(r.x_in, r.xall.at[0]),
            wk=local(r.wk_in, r.wqkv.at[:, pl.ds(W, W)]),
            wv=local(r.wv_in, r.wqkv.at[:, pl.ds(2 * W, W)]),
            wq=local(r.wq_in, r.wqkv.at[:, pl.ds(0, W)]),
            wo=local(r.wo_in, r.wo.at[pl.ds(0, W)]),
            we=local(r.we_in, r.we.at[0]),
            ws=local(r.ws_in, r.ws.at[0]),
            cot=local(r.cot_in.at[my_rows], r.cot),
        )
        for copy in vars(loads).values():
            copy.start()

        def row(ref):
            return ref[...].astype(F32).reshape(1, ref.shape[0])

        vec = [row(ref) for ref in (r.ob_in, r.ag_in, r.as_in, r.sb_in, r.fg_in, r.fs_in)]
        r.eb[0] = row(r.eb_in)
        r.segs[0] = r.seg_in[...].astype(F32)
        barrier = pltpu.get_barrier_semaphore()
        greeted = [y_peer, core_peer, x_peer, z1_peer, z2_peer, z3_peer]
        for device in greeted:
            pl.semaphore_signal(barrier, inc=1, device_id=device, device_id_type=MESH)
        pl.semaphore_wait(barrier, len(greeted))

        seg_copies = [None] + [
            remote(r.segs.at[0], r.segs.at[k], peer) for k, peer in ((1, z1_peer), (2, z2_peer), (3, z3_peer))
        ]
        eb_copy = remote(r.eb.at[0], r.eb.at[1], y_peer)
        x_rows = [pl.ds(pl.multiple_of(t * TM + k * PR, PR), PR) for k in range(PARTS)]
        mid = lax.rem(low_bit + high_bit, 2)
        is_mid, is_end = mid == 1, mid == 0
        slots = (0, 1, 2 + mid, 3 - mid)
        x_at = take(0, 3 * PARTS)

        def x_recv(slot, k):
            return x_at + (slot - 1) * PARTS + k

        def x_move(src_slot, dst_slot, peer, k):
            src = r.x_in.at[x_rows[k]] if src_slot == 0 else r.xall.at[src_slot, x_rows[k]]
            return remote(src, r.xall.at[dst_slot, x_rows[k]], peer, None, x_recv(dst_slot, k))

        x_near = [x_move(0, 1, z1_peer, k) for k in range(PARTS)]
        x_far = [x_move(0, 3, z3_peer, k) for k in range(PARTS)]
        x_next = (
            None,
            [x_move(1, 2, z3_peer, k) for k in range(PARTS)],
            [x_move(3, 2, z1_peer, k) for k in range(PARTS)],
            [x_move(2, 3, z1_peer, k) for k in range(PARTS)],
        )
        x_y = [None] + [
            [remote(r.xall.at[slots[o], x_rows[k]], r.xall.at[slots[o], x_rows[k]], y_peer) for k in range(PARTS)]
            for o in (1, 2, 3)
        ]
        for k in range(PARTS):
            go(x_near[k])
            go(x_far[k], is_mid)
        for copy in seg_copies[1:]:
            go(copy)
        go(eb_copy)

        def arrive(o, k):
            here = r.xall.at[slots[o], x_rows[k]]
            remote(here, here, z1_peer, x_at, x_recv(slots[o], k)).wait_recv()
            go(x_next[o][k], is_mid)
            go(x_y[o][k])

        def block_here(o):
            if o == 1:
                for copy in seg_copies[1:]:
                    copy.wait_recv()
            for k in range(PARTS):
                x_y[o][k].wait_recv()

        chunks = [
            (r.wo_in, r.wo.at[pl.ds(W, W)], W, 0, 1),
            (r.we_in, r.we.at[1], D, 0, 2),
            (r.we_in, r.we.at[1], D, 1, 2),
            (r.ws_in, r.ws.at[1], F, 0, 2),
            (r.ws_in, r.ws.at[1], F, 1, 2),
        ]
        pieces = sh.nd * 2

        def window(chunk, owner):
            rows, part, parts = chunk[2:]
            size = rows // pieces // parts
            return pl.ds(pl.multiple_of(owner * (rows // pieces) + part * size, size), size)

        own_piece, pair_piece = d * 2 + low_bit, d * 2 + 1 - low_bit
        x_d = d + 2 - 4 * xpos
        x_pieces = (x_d * 2 + low_bit, x_d * 2 + 1 - low_bit)
        w_y, w_z, w_x, w_core = [], [], [], []
        for chunk in chunks:
            source, held = chunk[0], chunk[1]

            def move(owner, peer):
                where = window(chunk, owner)
                return remote(held.at[where], held.at[where], peer)

            own = window(chunk, own_piece)
            w_y.append(remote(source.at[own], held.at[own], y_peer))
            w_z.append(move(own_piece, z1_peer))
            w_x.append([move(piece, x_peer) for piece in (own_piece, pair_piece)])
            w_core.append([move(piece, core_peer) for piece in (own_piece, pair_piece) + x_pieces])

        def hop1(i):
            w_y[i].wait_recv()
            go(w_z[i])
            go(w_x[i][0])
            go(w_core[i][0])

        def hop2(i):
            w_z[i].wait_recv()
            go(w_x[i][1])
            go(w_core[i][1])

        def hop3(i):
            for k in range(2):
                w_x[i][k].wait_recv()
                go(w_core[i][2 + k])

        def weights_done(i):
            for copy in w_core[i]:
                copy.wait_recv()


        kv, m_s, l_s, acc = r.kv, r.m_s, r.l_s, r.acc
        value_bias = row(r.vb_in)
        scale = HEAD_DIM ** (-0.5)
        lane = lax.broadcasted_iota(jnp.int32, (T, 128), 1)

        def split_pair(target, p, pair):
            target[2 * p] = jnp.where(lane < 64, pair, 0.0).astype(BF16)
            target[2 * p + 1] = jnp.where(lane < 64, 0.0, pair).astype(BF16)

        def set_keys_values(slot):
            both = nn(r.xall[slot], r.wqkv[:, W:])
            for p in range(HP):
                kv[slot, p, 0] = both[:, p * 128 : (p + 1) * 128].astype(BF16)
                cols = slice(W + p * 128, W + (p + 1) * 128)
                kv[slot, p, 1] = (both[:, cols] + value_bias[:, p * 128 : (p + 1) * 128]).astype(BF16)

        def set_bias(slot):
            seg_keys = jnp.broadcast_to(r.segs[slot], (128, T)).T
            for j in range(T // 128):
                cols = slice(j * 128, (j + 1) * 128)
                r.bias[:, cols] = jnp.where(seg_keys == r.segs[0, :, cols], 0.0, masked)

        def project():
            loads.x.wait()
            loads.wk.wait()
            loads.wv.wait()
            set_keys_values(0)
            loads.wq.wait()
            queries = (nn(r.xall[0], r.wqkv[:, :W]) + row(r.qb_in)).astype(BF16).astype(F32) * scale
            for p in range(HP):
                split_pair(r.qm, p, queries[:, p * 128 : (p + 1) * 128])
            m_s[...] = jnp.full_like(m_s, masked)
            l_s[...] = jnp.zeros_like(l_s)
            acc[...] = jnp.zeros_like(acc)
            set_bias(0)


        def attend(slot, p):
            pair_keys = kv[slot, p, 0]
            pair_values = kv[slot, p, 1].T
            for hh in range(2):
                h = 2 * p + hh
                s = nt(pair_keys, r.qm[h]) + r.bias[...]
                old = m_s[h]
                new = jnp.maximum(old, jnp.max(s, axis=0, keepdims=True))
                e = jnp.exp(s - new)
                alpha = jnp.exp(old - new)
                l_s[h] = l_s[h] * alpha + jnp.sum(e, axis=0, keepdims=True)
                m_s[h] = new
                acc[h] = acc[h] * alpha + nn(pair_values[hh * 64 : hh * 64 + 64], e.astype(BF16))

        def run(body, services=None):
            def step(p, carry):
                body(p)
                for at, fn in (services or {}).items():
                    pl.when(p == at)(fn)
                return carry

            lax.fori_loop(0, HP, step, 0)

        def together(*fns):
            def all_of():
                for fn, arg in fns:
                    fn(*arg)

            return all_of

        def flip_inputs(slot):
            at = slot * T if isinstance(slot, int) else pl.multiple_of(slot * T, T)
            r.xt[:, pl.ds(at, T)] = r.xall[slot].T

        def next_block(o):
            block_here(o)
            set_keys_values(slots[o])
            set_bias(slots[o])

        att_at = take(0, HP)

        def att_copy(p):
            cols = pl.ds(p * 128, 128)
            return remote(r.att.at[peer_rows, cols], r.att_o.at[:, cols], y_peer, att_at + p)

        def attend_last(p):
            attend(slots[3], p)
            for h in (2 * p, 2 * p + 1):
                acc[h] = acc[h] / l_s[h]
                m_s[h] = m_s[h] + jnp.log(l_s[h])
            pair = acc[2 * p : 2 * p + 2].reshape(128, T).T
            r.att[:, p * 128 : (p + 1) * 128] = pair.astype(BF16)
            att_copy(p).start()

        fl_copy = remote(r.fl.at[my_rows], r.fl.at[my_rows], y_peer)

        def out_project():
            loads.wo.wait()
            r.sec[...] = nn(r.att[my_rows, :], r.wo[0:W, :])

        def first_norm():
            for p in range(HP):
                att_copy(p).wait_recv()
            mix = r.sec[...] + nn(r.att_o[...], r.wo[W : 2 * W, :])
            normed, recip = normalise(r.xall[0, my_rows, :].astype(F32) + mix + vec[0])
            r.n1[...] = normed
            r.r1[...] = jnp.broadcast_to(recip, (TM, 128))
            first = normed * vec[1] + vec[2]
            r.sec[...] = first + vec[3]
            r.fl[my_rows, :] = first.astype(BF16)
            go(fl_copy)

        def tile_cols(j):
            return pl.ds(pl.multiple_of(j * TILE, TILE), TILE)

        def forward_tile(side, j):
            cols = tile_cols(j)
            pre = nn(r.fl[my_rows, :], r.we[side, :, cols]) + r.eb[side, :, cols]
            hidden, slope = gelu_parts(pre)
            hidden = hidden.astype(BF16)
            r.gp[side, :, cols] = slope
            if side == 0:
                r.hid[my_rows, cols] = hidden
            r.sec[...] += nn(hidden, r.ws[side, cols, :])

        def tiles(fn):
            def step(j, carry):
                fn(j)
                return carry

            lax.fori_loop(0, NTILE, step, 0)

        def own_units():
            loads.we.wait()
            loads.ws.wait()
            tiles(lambda j: forward_tile(0, j))

        def other_units():
            eb_copy.wait_recv()
            tiles(lambda j: forward_tile(1, j))

        go(w_y[0])
        go(w_y[1])
        project()
        arrive(1, 0)

        def with_00():
            go(w_y[2])
            go(w_y[3])
            hop1(0)
            arrive(1, 1)
            arrive(2, 0)
            hop2(0)
            hop1(1)


        def with_01():
            arrive(2, 1)

        run(lambda p: attend(slots[0], p), {0: with_00, 1: with_01})
        arrive(3, 0)
        hop2(1)
        next_block(1)

        def with_11():
            arrive(3, 1)
            hop1(2)
            go(w_y[4])
            hop3(0)

        run(lambda p: attend(slots[1], p), {1: with_11})
        hop1(3)
        next_block(2)

        def with_20():
            hop3(1)


        def with_21():
            hop2(2)

        run(lambda p: attend(slots[2], p), {0: with_20, 1: with_21})
        hop2(3)
        weights_done(0)
        next_block(3)
        attend_last(0)
        hop1(4)
        attend_last(1)
        attend_last(2)
        flip_inputs(slots[1])
        hop2(4)
        out_project()
        first_norm()
        hop3(2)
        flip_inputs(slots[2])
        flip_inputs(slots[3])
        weights_done(1)
        hop3(3)
        weights_done(2)
        flip_inputs(slots[0])
        hop3(4)
        own_units()
        weights_done(3)
        weights_done(4)
        other_units()
        loads.cot.wait()
        normed2, recip2 = normalise(r.sec[...])
        upstream = r.cot[...].astype(F32)
        grad_second = denormalise(upstream * vec[4], normed2, recip2)
        r.gf[...] = grad_second
        r.gs[my_rows, :] = grad_second.astype(BF16)
        gs_copy = remote(r.gs.at[my_rows], r.gs.at[my_rows], y_peer)
        go(gs_copy)
        small = r.small
        small[0:1, :] = column_sum(upstream * normed2)
        small[1:2, :] = column_sum(upstream)
        small[2:3, :] = column_sum(grad_second)
        r.oy[...] = (normed2 * vec[4] + vec[5]).astype(BF16)
        oy_local = local(r.oy, r.out.at[my_rows])
        oy_local.start()


        def backward_tile(side, j):
            cols = tile_cols(j)
            low = (nt(r.gs[my_rows, :], r.ws[side, cols, :]) * r.gp[side, :, cols]).astype(BF16)
            if side == 0:
                r.gpre[my_rows, cols] = low
            r.gf[...] += nt(low, r.we[side, :, cols])

        tiles(lambda j: backward_tile(0, j))
        tiles(lambda j: backward_tile(1, j))
        grad_first = r.gf[...]
        normed = r.n1[...]
        grad_mix = denormalise(grad_first * vec[1], normed, r.r1[:, 0:1])
        r.gmix[...] = grad_mix
        r.gm[my_rows, :] = grad_mix.astype(BF16)
        gm_copy = remote(r.gm.at[my_rows], r.gm.at[my_rows], y_peer)
        go(gm_copy)
        small[3:4, :] = column_sum(grad_first * normed)
        small[4:5, :] = column_sum(grad_first)
        small[5:6, :] = column_sum(grad_mix)

        def rows_at(ref, first_row, rows):
            return ref.at[pl.ds(pl.multiple_of(first_row, rows), rows)]

        class Unit:
            def __init__(self, grad, whole, out, order, bufs):
                self.grad, self.order, self.bufs = grad, order, bufs
                self.first, self.rows, self.line = [0], [grad.shape[0]], None
                for stage in order:
                    self.rows.append(self.rows[-1] // (4 if stage == LINE else 2))
                    at = c if stage == LINE else bit_of[stage]
                    self.first.append(self.first[-1] + at * self.rows[-1])
                self.down, self.up = [], []
                for k, stage in enumerate(order):
                    rows, last = self.rows[k + 1], k == len(order) - 1
                    target = rows_at(whole, self.first[k + 1], rows)
                    source = target
                    if last:
                        source = rows_at(grad, self.first[k + 1], rows)
                        self.kept = local(source, target)
                    if stage == LINE:
                        self.line = k
                        self.far = self.first[k] + 2 * (1 - high_bit) * rows
                        self.edge = self.first[k] + 3 * high_bit * rows
                        near = self.first[k] + 2 * high_bit * rows
                        ends = grad.at[pl.ds(pl.multiple_of(self.first[k] + (1 - high_bit) * rows, rows), 3 * rows)]
                        self.down.append(
                            (
                                remote(ends, bufs[k][0], z1_peer),
                                remote(rows_at(grad, self.far, 2 * rows), bufs[k][1], z3_peer),
                                remote(rows_at(grad, self.edge, rows), bufs[k][2], z1_peer),
                            )
                        )
                        near, far = rows_at(whole, near, 2 * rows), rows_at(whole, self.far, 2 * rows)
                        self.up.append(
                            (remote(source, target, z1_peer), remote(near, near, z3_peer), remote(far, far, z1_peer))
                        )
                        continue
                    theirs = rows_at(grad, self.first[k] + (1 - bit_of[stage]) * rows, rows)
                    self.down.append(remote(theirs, bufs[k], peer_of[stage]))
                    self.up.append(remote(source, target, peer_of[stage]))
                self.stored = local(whole, out)

            def add_rows(self, first_row, rows, terms, step):

                def tile(i, carry):
                    window = self.grad.at[pl.ds(pl.multiple_of(first_row + i * step, step), step)]
                    total = window[...].astype(F32)
                    for buf, at in terms:
                        total = total + buf[pl.ds(pl.multiple_of(at + i * step, step), step), :].astype(F32)
                    window[...] = total.astype(BF16)
                    return carry

                lax.fori_loop(0, rows // step, tile, 0)

            def send(self, k):
                go(self.down[k])

            def add(self, k):
                self.down[k].wait_recv()
                self.add_rows(self.first[k + 1], self.rows[k + 1], [(self.bufs[k], 0)], min(96, self.rows[k + 1]))

            def forward(self, k):
                self.add(k)
                self.send(k + 1)

            def spread(self, k):
                go(self.up[k])
                if k == len(self.order) - 1:
                    self.kept.start()

            def back(self, k):
                if k == len(self.order) - 1:
                    self.kept.wait()
                self.up[k].wait_recv()
                if self.line is not None and k - 1 == self.line:
                    go(self.up[k - 1][0])
                else:
                    self.spread(k - 1)

            def za(self):
                go(self.down[self.line][0], is_end)

            def zb(self):
                k = self.line
                rows = self.rows[k + 1]

                @pl.when(is_mid)
                def _():
                    self.down[k][0].wait_recv()
                    self.add_rows(self.far, 2 * rows, [(self.bufs[k][0], (1 - high_bit) * rows)], rows)

                go(self.down[k][1], is_mid)

            def zc(self):
                k = self.line
                rows, (first_buf, second_buf, _) = self.rows[k + 1], self.bufs[k]

                @pl.when(is_mid)
                def _():
                    self.down[k][1].wait_recv()
                    self.add_rows(self.edge, rows, [(second_buf, high_bit * rows)], rows)

                go(self.down[k][2], is_mid)

                @pl.when(is_mid)
                def _():
                    terms = [(first_buf, 2 * high_bit * rows), (second_buf, (1 - high_bit) * rows)]
                    self.add_rows(self.first[k + 1], rows, terms, rows)
                    if k == len(self.order) - 1:
                        self.kept.start()
                        self.up[k][0].start()

            def zd(self):
                k = self.line

                @pl.when(is_end)
                def _():
                    self.down[k][2].wait_recv()
                    self.add_rows(self.first[k + 1], self.rows[k + 1], [(self.bufs[k][2], 0)], self.rows[k + 1])
                    if k == len(self.order) - 1:
                        self.kept.start()
                        self.up[k][0].start()

                if k == len(self.order) - 1:
                    unsent.append((self.up[k][0], None))

            def ze(self):
                k = self.line

                @pl.when(is_mid)
                def _():
                    if k == len(self.order) - 1:
                        self.kept.wait()
                    self.up[k][0].wait_recv()

                go(self.up[k][1], is_mid)

            def zf(self):
                pl.when(is_mid)(lambda: self.up[self.line][1].wait_recv())
                go(self.up[self.line][2], is_mid)

            def zg(self):
                k = self.line

                @pl.when(is_end)
                def _():
                    if k == len(self.order) - 1:
                        self.kept.wait()
                    self.up[k][0].wait_recv()
                    self.up[k][2].wait_recv()

                self.spread(k - 1)

            def turn(self):
                k = len(self.order) - 1
                self.add(k)
                self.spread(k)

            def store(self):
                self.up[0].wait_recv()
                self.stored.start()

        def all_sum(buf, slots, stages):
            copies = [remote(buf.at[k % 2], slots.at[k], peer_of[stage]) for k, stage in enumerate(stages)]

            def start(k):
                copies[k].start()

            def finish(k):
                copies[k].wait()
                total = buf[k % 2] + slots[k]
                if stages[k] == YS:
                    which = lax.broadcasted_iota(jnp.int32, total.shape, 0)
                    total = jnp.where(which < 6, total, buf[k % 2])
                buf[(k + 1) % 2] = total
                if k + 1 < len(stages):
                    start(k + 1)

            return start, finish


        def other_hidden(j):
            cols = tile_cols(j)
            pre = nn(r.fl[peer_rows, :], r.we[0, :, cols]) + r.eb[0, :, cols]
            hidden, slope = gelu_parts(pre)
            r.hid[peer_rows, cols] = hidden.astype(BF16)
            r.gp[0, :, cols] = slope

        def other_slopes():
            def tile(j):
                cols = tile_cols(j)
                low = nt(r.gs[peer_rows, :], r.ws[0, cols, :]) * r.gp[0, :, cols]
                r.gpre[peer_rows, cols] = low.astype(BF16)

            tiles(tile)

        fl_copy.wait_recv()
        tiles(other_hidden)
        r.flt[...] = r.fl[...].T
        wait_sends(gm_copy)
        gs_copy.wait_recv()
        by_line, by_pairs = (CORE, XS, LINE), (CORE, XS, Z1, Z2)
        half_d = D // 2

        def line_unit(grad, whole, out, first_buf, k):
            steps = (r.l0.at[k], r.l1.at[k], r.l2.at[k])
            return Unit(grad, whole, out, by_line, (first_buf, r.x0.at[k], steps))

        def pair_unit(grad, whole, out, k):
            return Unit(grad, whole, out, by_pairs, (r.p0.at[k], r.p1.at[k], r.p2.at[k], r.p3.at[k]))

        s1 = Unit(
            r.ws.at[1, pl.ds(0, D)], r.ws.at[0, pl.ds(0, D)], r.us_out.at[pl.ds(0, D)], (CORE, LINE, XS),
            (r.s0.at[pl.ds(0, half_d)], (r.z0, r.z1, r.z2), r.z3),
        )
        s2 = line_unit(
            r.ws.at[1, pl.ds(D, D)], r.ws.at[0, pl.ds(D, D)], r.us_out.at[pl.ds(D, D)], r.s0.at[pl.ds(half_d, half_d)], 1
        )
        e1, e2 = [
            line_unit(
                r.we.at[1, :, pl.ds(at, D)], r.we.at[0, :, pl.ds(at, D)], r.ue_out.at[:, pl.ds(at, D)], r.e0.at[k - 2], k
            )
            for k, at in ((2, 0), (3, D))
        ]
        ua = pair_unit(r.ua, r.s0, r.ua_out, 0)
        ub = pair_unit(r.ub, r.wo, r.ub_out, 1)

        def half_of(which):
            return which * core + (1 - which) * (1 - core)

        def shrink_tiles(which):
            def tile(i, carry):
                at = pl.multiple_of(i * D + half_of(which) * half_d, 128)
                r.ws[1, pl.ds(at, half_d), :] = tn(r.hid[:, pl.ds(at, half_d)], r.gs[...]).astype(BF16)
                return carry

            lax.fori_loop(0, F // D, tile, 0)

        def half_rows(which):
            return pl.ds(pl.multiple_of(half_of(which) * (D // 2), D // 2), D // 2)

        def expand_tiles(which):
            rows = half_rows(which)

            def tile(j):
                cols = tile_cols(j)
                r.we[1, rows, cols] = nn(r.flt[rows, :], r.gpre[:, cols]).astype(BF16)

            tiles(tile)

        def sum_blocks():
            totals = column_sum(r.gpre[...].astype(F32))
            small[6:7, :] = totals[:, :D]
            small[7:8, :] = totals[:, D:]
            r.es[0] = small[...]

        early_start, early_finish = all_sum(r.es, r.es_r, (YS, CORE, XS, Z1, Z2))
        late_start, late_finish = all_sum(r.ls, r.ls_r, (CORE, XS, Z1, Z2))

        def grad_heads():
            gm_copy.wait_recv()
            grad_att = nt(r.gm[...], r.wo[0:W, :]).astype(BF16).astype(F32)
            flipped = grad_att.T.reshape(2 * HP, 64, T)
            r.delta[...] = jnp.sum(acc[...] * flipped, axis=1, keepdims=True)
            for p in range(HP):
                split_pair(r.dm, p, grad_att[:, p * 128 : (p + 1) * 128])
            acc[...] = jnp.zeros_like(acc)

        oy_send = remote(r.oy, r.out.at[my_rows], y_peer)
        dkv = r.dkv

        def pull(slot, p):
            pair_keys, pair_values = kv[slot, p, 0], kv[slot, p, 1]
            flipped_keys = pair_keys.T
            grad_k = jnp.zeros((T, 128), F32)
            grad_v = jnp.zeros((T, 128), F32)
            for hh in range(2):
                h = 2 * p + hh
                q, g = r.qm[h], r.dm[h]
                probs = jnp.exp(nt(pair_keys, q) + (r.bias[...] - m_s[h]))
                grad_p = nt(pair_values, g)
                grad_v = grad_v + nn(probs.astype(BF16), g)
                ds = (probs * (grad_p - r.delta[h])).astype(BF16)
                grad_k = grad_k + nn(ds, q)
                acc[h] += nn(flipped_keys[hh * 64 : hh * 64 + 64], ds)
            rows = slice(slot * T, (slot + 1) * T)
            dkv[rows, pl.ds(pl.multiple_of(p * 128, 128), 128)] = grad_k.astype(BF16)
            dkv[rows, pl.ds(pl.multiple_of(W + p * 128, 128), 128)] = grad_v.astype(BF16)

        dx_y = [remote(r.xall.at[k, pl.ds(0, TM)], r.dxy.at[k], y_peer) for k in range(SLOTS)]

        def dx_move(slot, target, peer):
            return remote(r.xall.at[slot, pl.ds(TM, TM)], r.dxz.at[target], peer)

        dx_end = {3: dx_move(3, 0, z1_peer), 2: dx_move(2, 1, z1_peer), 1: dx_move(1, 2, z1_peer)}
        dx_mid = {3: dx_move(3, 3, z3_peer), 2: dx_move(2, 4, z3_peer), 1: dx_move(1, 5, z1_peer)}

        def dx_rows(slot, rows):
            here = pl.ds(pl.multiple_of(slot * T + rows.start, TM), TM)
            return nt(dkv[here, :], r.wqkv[:, W:])

        def dx_part(slot):
            r.xall[slot, 0:TM] = dx_rows(slot, peer_rows).astype(BF16)
            go(dx_y[slot])
            r.xall[slot, TM:] = dx_rows(slot, my_rows).astype(BF16)

        def dx_sum(slot):
            dx_y[slot].wait_recv()
            total = r.xall[slot, TM:].astype(F32) + r.dxy[slot].astype(F32)
            r.xall[slot, TM:] = total.astype(BF16)
            go(dx_end[slot], is_end)

        def dx_pass(slot):
            came = {3: dx_end[2], 2: dx_end[3], 1: dx_mid[2]}[slot]
            at = {3: 1, 2: 0, 1: 4}[slot]

            @pl.when(is_mid)
            def _():
                came.wait_recv()
                total = r.xall[slot, TM:].astype(F32) + r.dxz[at].astype(F32)
                r.xall[slot, TM:] = total.astype(BF16)

            go(dx_mid[slot], is_mid)

        def dx_last():
            dx_y[0].wait_recv()
            r.gmix[...] += r.dxy[0].astype(F32)

            @pl.when(is_mid)
            def _():
                dx_end[1].wait_recv()
                dx_mid[3].wait_recv()
                r.gmix[...] += r.dxz[2].astype(F32) + r.dxz[3].astype(F32)

            @pl.when(is_end)
            def _():
                dx_mid[1].wait_recv()
                r.gmix[...] += r.dxz[5].astype(F32)

            r.igm[...] = r.gmix[...].astype(BF16)


        def key_value_tiles(which):
            rows = half_rows(which)
            r.ub[rows, :] = nn(r.xt[rows, :], dkv[...]).astype(BF16)

        def query_output_tiles(which):
            rows = half_rows(which)
            r.ua[rows, 0:W] = nn(r.xt[rows, 0:T], r.dq[...]).astype(BF16)
            cols = pl.ds(pl.multiple_of(half_of(which) * W, 128), W)
            r.ua[rows, W:] = tn(r.att[...], r.gm[:, cols]).astype(BF16)

        def query_grads():
            r.dq[...] = (acc[...].reshape(W, T).T * scale).astype(BF16)
            r.ls[0, 0:1, :] = column_sum(r.dq[...].astype(F32))
            r.ls[0, 1:2, :] = column_sum(dkv[:, W:].astype(F32))
            r.ls[0, 2:8, :] = jnp.zeros((6, W), F32)

        def dx_own():
            r.xall[0, 0:TM] = (dx_rows(0, peer_rows) + nt(r.dq[peer_rows, :], r.wqkv[:, :W])).astype(BF16)
            go(dx_y[0])
            r.gmix[...] += dx_rows(0, my_rows) + nt(r.dq[my_rows, :], r.wqkv[:, :W])

        ig_local = local(r.igm, r.ig_out.at[my_rows])
        ig_send = remote(r.igm, r.ig_out.at[my_rows], y_peer)

        def dx_out():
            dx_last()
            ig_local.start()
            go(ig_send)

        shrink_tiles(0)
        s1.send(0)
        s2.send(0)
        other_slopes()
        shrink_tiles(1)
        expand_tiles(0)
        e1.send(0)
        e2.send(0)
        go(oy_send)
        s1.add(0)
        s1.za()
        expand_tiles(1)
        sum_blocks()
        early_start(0)
        s2.forward(0)
        grad_heads()
        e1.forward(0)
        set_bias(3)
        run(lambda p: pull(3, p))
        set_bias(2)

        def beside_20():
            s2.add(1)
            s2.za()
            s1.zb()
            e2.forward(0)

        run(lambda p: pull(2, p), {0: beside_20})
        set_bias(1)

        def beside_10():
            e1.add(1)
            e1.za()
            early_finish(0)
            s2.zb()


        def beside_11():
            s1.zc()

        run(lambda p: pull(1, p), {0: beside_10, 1: beside_11})
        set_bias(0)

        def beside_00():
            e1.zb()
            early_finish(1)
            s2.zc()
            e2.add(1)
            e2.za()
            dx_part(3)
            s1.zd()
            s1.send(2)

        run(lambda p: pull(0, p), {0: beside_00})
        s1.add(2)
        s1.spread(2)
        query_grads()
        late_start(0)
        e1.zc()
        s2.zd()
        e2.zb()
        key_value_tiles(0)
        ub.send(0)
        s1.back(2)
        query_output_tiles(0)
        ua.send(0)
        s2.ze()
        e1.zd()
        key_value_tiles(1)
        ub.forward(0)
        dx_sum(3)
        e2.zc()
        s1.ze()
        e2.zd()
        late_finish(0)
        dx_part(2)
        s2.zf()
        query_output_tiles(1)
        ub.forward(1)
        early_finish(2)
        e1.ze()
        s2.zg()
        ua.forward(0)
        s1.zf()
        dx_part(1)
        e2.ze()
        late_finish(1)
        ub.forward(2)
        early_finish(3)
        dx_sum(2)
        e1.zf()
        dx_pass(2)
        e1.zg()
        late_finish(2)
        ua.forward(1)
        e2.zf()
        ub.turn()
        s2.back(1)
        s1.zg()
        e2.zg()
        early_finish(4)
        ua.forward(2)
        ub.back(3)
        dx_own()
        s1.store()
        ua.turn()
        dx_pass(3)
        dx_sum(1)
        dx_pass(1)
        e2.back(1)
        late_finish(3)
        s2.store()
        ub.back(2)
        ua.back(3)
        ua.back(2)
        dx_out()
        ub.back(1)
        e1.back(1)
        e2.store()
        e1.store()
        ua.back(1)
        ub.store()
        ua.store()
        small_copies = (local(r.es.at[1], r.small_out), local(r.ls.at[0], r.late_out))
        for copy in small_copies:
            copy.start()
        oy_local.wait()
        oy_send.wait_recv()
        ig_local.wait()
        ig_send.wait_recv()
        for copy in small_copies:
            copy.wait()
        for unit in (s1, s2, e1, e2, ua, ub):
            unit.stored.wait()
        for p in range(HP):
            att_copy(p).wait_send()
        wait_sends()

    return kernel


def layer_call(sh, args):
    T, TM, D, W, F = sh.tokens, sh.mine, sh.width, sh.hw, sh.units
    HP = sh.pairs
    any_spec = pl.BlockSpec(memory_space=pl.ANY)
    vmem_spec = pl.BlockSpec(memory_space=pltpu.VMEM)
    ins = dict(
        seg_in=vmem_spec, qb_in=vmem_spec, vb_in=vmem_spec, ob_in=vmem_spec, ag_in=vmem_spec,
        as_in=vmem_spec, eb_in=vmem_spec, sb_in=vmem_spec, fg_in=vmem_spec, fs_in=vmem_spec,
        x_in=any_spec, wq_in=any_spec, wk_in=any_spec, wv_in=any_spec,
        wo_in=any_spec, we_in=any_spec, ws_in=any_spec, cot_in=any_spec,
    )
    outs = dict(
        out=((T, D), BF16, any_spec),
        ig_out=((T, D), BF16, any_spec),
        ue_out=((D, F), BF16, any_spec),
        us_out=((F, D), BF16, any_spec),
        ua_out=((D, 2 * W), BF16, any_spec),
        ub_out=((D, 2 * W), BF16, any_spec),
        small_out=((8, D), F32, any_spec),
        late_out=((8, W), F32, any_spec),
    )
    vm = lambda shape, kind: pltpu.VMEM(shape, kind)
    scratch = dict(
        send=pltpu.SemaphoreType.DMA((160,)),
        recv=pltpu.SemaphoreType.DMA((160,)),
        local=pltpu.SemaphoreType.DMA((24,)),
        xall=vm((4, T, D), BF16),
        xt=vm((D, 4 * T), BF16),
        wqkv=vm((D, 3 * W), BF16),
        wo=vm((2 * W, D), BF16),
        we=vm((2, D, F), BF16),
        ws=vm((2, F, D), BF16),
        eb=vm((2, 1, F), F32),
        cot=vm((TM, D), BF16),
        segs=vm((4, 1, T), F32),
        bias=vm((T, T), F32),
        kv=vm((4, HP, 2, T, 128), BF16),
        qm=vm((2 * HP, T, 128), BF16),
        dm=vm((2 * HP, T, 128), BF16),
        m_s=vm((2 * HP, 1, T), F32),
        l_s=vm((2 * HP, 1, T), F32),
        delta=vm((2 * HP, 1, T), F32),
        acc=vm((2 * HP, 64, T), F32),
        att=vm((T, W), BF16),
        att_o=vm((TM, W), BF16),
        n1=vm((TM, D), F32),
        r1=vm((TM, 128), F32),
        sec=vm((TM, D), F32),
        gf=vm((TM, D), F32),
        gmix=vm((TM, D), F32),
        fl=vm((T, D), BF16),
        flt=vm((D, T), BF16),
        gs=vm((T, D), BF16),
        gm=vm((T, D), BF16),
        gp=vm((2, TM, F), F32),
        hid=vm((T, F), BF16),
        gpre=vm((T, F), BF16),
        oy=vm((TM, D), BF16),
        small=vm((8, D), F32),
        es=vm((2, 8, D), F32),
        es_r=vm((5, 8, D), F32),
        ls=vm((2, 8, W), F32),
        ls_r=vm((4, 8, W), F32),
        dkv=vm((4 * T, 2 * W), BF16),
        dq=vm((T, W), BF16),
        dxy=vm((4, TM, D), BF16),
        dxz=vm((6, TM, D), BF16),
        igm=vm((TM, D), BF16),
        ua=vm((D, 2 * W), BF16),
        ub=vm((D, 2 * W), BF16),
        s0=vm((D, D), BF16),
        e0=vm((2, D // 2, D), BF16),
        z0=vm((3 * (D // 8), D), BF16),
        z1=vm((2 * (D // 8), D), BF16),
        z2=vm((D // 8, D), BF16),
        z3=vm((D // 16, D), BF16),
        x0=vm((4, D // 4, D), BF16),
        l0=vm((4, 3 * (D // 16), D), BF16),
        l1=vm((4, 2 * (D // 16), D), BF16),
        l2=vm((4, D // 16, D), BF16),
        p0=vm((2, D // 2, D), BF16),
        p1=vm((2, D // 4, D), BF16),
        p2=vm((2, D // 8, D), BF16),
        p3=vm((2, D // 16, D), BF16),
    )
    names = list(ins) + list(outs) + list(scratch)
    return pl.pallas_call(
        make_kernel(sh, names),
        out_shape=[jax.ShapeDtypeStruct(o[0], o[1]) for o in outs.values()],
        in_specs=list(ins.values()),
        out_specs=[o[2] for o in outs.values()],
        scratch_shapes=list(scratch.values()),
        compiler_params=pltpu.CompilerParams(
            collective_id=0, has_side_effects=True, vmem_limit_bytes=63 * 1024 * 1024
        ),
        name="layer",
    )(*args)


def finish_kernel(sh, names, *refs):
    r = types.SimpleNamespace(**dict(zip(names, refs)))
    W = sh.hw
    half = sh.units // 2
    pieces = []
    for at in range(2):
        pieces.append((r.us.at[pl.ds(at * half, half)], r.us_v.at[at], r.usf.at[at], r.us_out.at[pl.ds(at * half, half)]))
    for at in range(2):
        rows = pl.ds(at * W, W)
        pieces.append((r.ue.at[rows], r.ue_v.at[at], r.uef.at[at], r.ue_out.at[rows]))
    cols = [pl.ds(0, W), pl.ds(W, W)]
    pieces.append((r.ub.at[:, cols[0]], r.ab_v.at[0], r.abf.at[0], r.wk_out))
    pieces.append((r.ub.at[:, cols[1]], r.ab_v.at[1], r.abf.at[1], r.wv_out))
    pieces.append((r.ua.at[:, cols[0]], r.ab_v.at[2], r.abf.at[2], r.wq_out))
    for at in range(2):
        rows = pl.ds(at * W, W)
        pieces.append((r.ua.at[rows, cols[1]], r.o_v.at[at], r.of.at[at], r.wo_out.at[:, cols[at]]))
    pieces.append((r.ig, r.ig_v, r.igf, r.ig_out))
    taken = pltpu.make_async_copy(r.out, r.out_v, r.sems.at[0])
    taken.start()
    reads = [pltpu.make_async_copy(p[0], p[1], r.sems.at[1 + k]) for k, p in enumerate(pieces)]
    for copy in reads:
        copy.start()
    at_small = 2 * len(pieces) + 2
    small_reads = [
        pltpu.make_async_copy(r.small, r.small_v, r.sems.at[at_small]),
        pltpu.make_async_copy(r.late, r.late_v, r.sems.at[at_small + 1]),
    ]
    for copy in small_reads:
        copy.start()
    taken.wait()
    passed = pltpu.make_async_copy(r.out_v, r.out_out, r.sems.at[2 * len(pieces) + 1])
    passed.start()
    writes = []

    def vectors():
        for copy in small_reads:
            copy.wait()
        for target, at in ((r.fg_v, 0), (r.fs_v, 1), (r.sb_v, 2), (r.ag_v, 3), (r.as_v, 4), (r.ob_v, 5)):
            target[...] = r.small_v[at]
        r.eb_v[0 : sh.width] = r.small_v[6]
        r.eb_v[sh.width :] = r.small_v[7]
        r.qb_v[...] = r.late_v[0]
        r.vb_v[...] = r.late_v[1]
        leaving = (
            (r.fg_v, r.fg), (r.fs_v, r.fs), (r.sb_v, r.sb), (r.ag_v, r.ag), (r.as_v, r.as_), (r.ob_v, r.ob),
            (r.eb_v, r.eb), (r.qb_v, r.qb), (r.vb_v, r.vb),
        )
        for k, (held, target) in enumerate(leaving):
            copy = pltpu.make_async_copy(held, target, r.sems.at[at_small + 2 + k])
            copy.start()
            writes.append(copy)

    for k, (_, low, wide, target) in enumerate(pieces):
        if k == 4:
            vectors()
        reads[k].wait()
        rows = low.shape[0]
        step = 96 if rows % 96 == 0 else 64

        def tile(i, carry):
            at = pl.ds(pl.multiple_of(i * step, step), step)
            wide[at, :] = low[at, :].astype(F32)
            return carry

        lax.fori_loop(0, rows // step, tile, 0)
        copy = pltpu.make_async_copy(wide, target, r.sems.at[1 + len(pieces) + k])
        copy.start()
        writes.append(copy)
    passed.wait()
    for k, copy in enumerate(writes):
        copy.wait()


def finish_call(sh, parts):
    T, D, W, F = sh.tokens, sh.width, sh.hw, sh.units
    any_spec = pl.BlockSpec(memory_space=pl.ANY)
    hbm_spec = pl.BlockSpec(memory_space=pltpu.HBM)
    ins = dict(
        out=hbm_spec, ig=hbm_spec, ue=hbm_spec, us=hbm_spec, ua=hbm_spec, ub=hbm_spec,
        small=hbm_spec, late=hbm_spec,
    )
    outs = dict(
        out_out=((T, D), BF16, any_spec),
        ig_out=((T, D), F32, any_spec),
        wq_out=((D, W), F32, any_spec),
        wk_out=((D, W), F32, any_spec),
        wv_out=((D, W), F32, any_spec),
        qb=((W,), F32, any_spec),
        vb=((W,), F32, any_spec),
        wo_out=((W, D), F32, any_spec),
        ob=((D,), F32, any_spec),
        ag=((D,), F32, any_spec),
        as_=((D,), F32, any_spec),
        ue_out=((D, F), F32, any_spec),
        eb=((F,), F32, any_spec),
        us_out=((F, D), F32, any_spec),
        sb=((D,), F32, any_spec),
        fg=((D,), F32, any_spec),
        fs=((D,), F32, any_spec),
    )
    scratch = dict(
        sems=pltpu.SemaphoreType.DMA((40,)),
        out_v=pltpu.VMEM((T, D), BF16),
        small_v=pltpu.VMEM((8, D), F32),
        late_v=pltpu.VMEM((8, W), F32),
        eb_v=pltpu.VMEM((F,), F32),
    )
    for name in ("fg_v", "fs_v", "sb_v", "ag_v", "as_v", "ob_v"):
        scratch[name] = pltpu.VMEM((D,), F32)
    for name in ("qb_v", "vb_v"):
        scratch[name] = pltpu.VMEM((W,), F32)
    for low, wide, shape in (
        ("us_v", "usf", (2, F // 2, D)),
        ("ue_v", "uef", (2, W, F)),
        ("ab_v", "abf", (3, D, W)),
        ("o_v", "of", (2, W, W)),
        ("ig_v", "igf", (T, D)),
    ):
        scratch[low], scratch[wide] = pltpu.VMEM(shape, BF16), pltpu.VMEM(shape, F32)
    names = list(ins) + list(outs) + list(scratch)
    return pl.pallas_call(
        functools.partial(finish_kernel, sh, names),
        out_shape=[jax.ShapeDtypeStruct(o[0], o[1]) for o in outs.values()],
        in_specs=list(ins.values()),
        out_specs=[o[2] for o in outs.values()],
        scratch_shapes=list(scratch.values()),
        compiler_params=pltpu.CompilerParams(vmem_limit_bytes=63 * 1024 * 1024),
        name="finish",
    )(*parts)


def fused_body(
    mesh_sizes, inputs, segments, query_proj, key_proj, value_proj, query_bias, value_bias, output_proj,
    output_bias, attn_gain, attn_shift, expand_proj, expand_bias, shrink_proj, shrink_bias,
    final_gain, final_shift, cotangent,
):
    sh = Shapes(mesh_sizes, inputs.shape[0], inputs.shape[1], query_proj.shape[1], expand_proj.shape[1])
    parts = layer_call(
        sh,
        (
            segments, query_bias, value_bias, output_bias, attn_gain, attn_shift, expand_bias, shrink_bias,
            final_gain, final_shift, inputs, query_proj, key_proj, value_proj, output_proj, expand_proj,
            shrink_proj, cotangent,
        ),
    )
    return finish_call(sh, parts)


contract_rows = (((0,), (0,)), ((), ()))
contract_cols = (((1,), (1,)), ((), ()))


def matmul(left, right):
    return jnp.dot(left, right, preferred_element_type=jnp.float32)


def inner_rows(left, right):
    return lax.dot_general(left, right, contract_rows, preferred_element_type=jnp.float32)


def inner_cols(left, right):
    return lax.dot_general(left, right, contract_cols, preferred_element_type=jnp.float32)


def norm_forward(values, gain, shift):
    centred = values - jnp.mean(values, axis=-1, keepdims=True)
    spread = jnp.mean(centred * centred, axis=-1, keepdims=True)
    recip = lax.rsqrt(spread + norm_eps)
    normed = centred * recip
    return (normed * gain + shift, normed, recip)


def norm_backward(upstream, normed, recip, gain):
    scaled = upstream * gain
    centred = (
        scaled
        - jnp.mean(scaled, axis=-1, keepdims=True)
        - normed * jnp.mean(scaled * normed, axis=-1, keepdims=True)
    )
    return (centred * recip, jnp.sum(upstream * normed, axis=0), jnp.sum(upstream, axis=0))


def cross_scores(left, right):
    return inner_cols(left, right)


def spread_apply(weights_in, right):
    return matmul(weights_in, right)


def spread_transpose(weights_in, left):
    return inner_rows(weights_in, left)


def body(
    inputs,
    segments,
    query_proj,
    key_proj,
    value_proj,
    query_bias,
    value_bias,
    output_proj,
    output_bias,
    attn_gain,
    attn_shift,
    expand_proj,
    expand_bias,
    shrink_proj,
    shrink_bias,
    final_gain,
    final_shift,
    cotangent,
):
    head_count = query_proj.shape[1] // HEAD_DIM
    scale = HEAD_DIM ** (-0.5)
    seg_local = segments[0]
    queries = (matmul(inputs, query_proj) + query_bias.astype(jnp.float32)).astype(jnp.bfloat16)
    keys = matmul(inputs, key_proj).astype(jnp.bfloat16)
    values = (matmul(inputs, value_proj) + value_bias.astype(jnp.float32)).astype(jnp.bfloat16)
    all_keys, all_values, key_ids = (
        lax.all_gather(keys, "ctx", axis=0, tiled=True),
        lax.all_gather(values, "ctx", axis=0, tiled=True),
        lax.all_gather(seg_local.astype(jnp.bfloat16), "ctx", axis=0, tiled=True),
    )
    query_segs = seg_local.astype(jnp.float32)
    key_segs = key_ids.astype(jnp.float32)
    same_seg = query_segs[:, None] == key_segs[None, :]

    def split_heads(matrix):
        return jnp.swapaxes(matrix.reshape(matrix.shape[0], head_count, HEAD_DIM), 0, 1)

    def join_heads(stack):
        return jnp.swapaxes(stack, 0, 1).reshape(stack.shape[1], head_count * HEAD_DIM)

    query_heads = split_heads(queries)
    key_heads = split_heads(all_keys)
    value_heads = split_heads(all_values)

    def head_forward(state, triple):
        query_head, key_head, value_head = triple
        scores = cross_scores(query_head, key_head) * scale
        scores = jnp.where(same_seg, scores, masked)
        row_max = jnp.max(scores, axis=1, keepdims=True)
        exp_scores = jnp.where(same_seg, jnp.exp(scores - row_max), 0.0)
        row_sum = jnp.sum(exp_scores, axis=1, keepdims=True)
        attn_probs = (exp_scores / row_sum).astype(jnp.bfloat16)
        mixed = spread_apply(attn_probs, value_head)
        return (state, (mixed, row_max + jnp.log(row_sum)))

    mixed_heads, log_sums = lax.scan(head_forward, None, (query_heads, key_heads, value_heads))[1]
    attended = join_heads(mixed_heads).astype(jnp.bfloat16)
    attn_total = lax.psum(matmul(attended, output_proj).astype(jnp.bfloat16), "tensor").astype(
        jnp.float32
    )
    attn_gain_f = attn_gain.astype(jnp.float32)
    first, first_normed, first_recip = norm_forward(
        inputs.astype(jnp.float32) + attn_total + output_bias.astype(jnp.float32),
        attn_gain_f,
        attn_shift.astype(jnp.float32),
    )
    first_low = first.astype(jnp.bfloat16)
    pre_act = matmul(first_low, expand_proj) + expand_bias.astype(jnp.float32)
    activated, gelu_back = jax.vjp(lambda pre_in: jax.nn.gelu(pre_in, approximate=False), pre_act)
    hidden = activated.astype(jnp.bfloat16)
    feed_total = lax.psum(matmul(hidden, shrink_proj).astype(jnp.bfloat16), "tensor").astype(
        jnp.float32
    )
    second = first + feed_total + shrink_bias.astype(jnp.float32)
    final_gain_f = final_gain.astype(jnp.float32)
    output, second_normed, second_recip = norm_forward(
        second, final_gain_f, final_shift.astype(jnp.float32)
    )
    upstream = cotangent.astype(jnp.float32)
    grad_second, fgain_grad, fshift_grad = norm_backward(
        upstream, second_normed, second_recip, final_gain_f
    )
    sbias_grad = jnp.sum(grad_second, axis=0)
    grad_second_low = grad_second.astype(jnp.bfloat16)
    shrink_grad = inner_rows(hidden, grad_second_low)
    grad_act = inner_cols(grad_second_low, shrink_proj)
    grad_pre = gelu_back(grad_act)[0].astype(jnp.bfloat16)
    ebias_grad = jnp.sum(grad_pre.astype(jnp.float32), axis=0)
    expand_grad = inner_rows(first_low, grad_pre)
    grad_first = grad_second + lax.psum(
        inner_cols(grad_pre, expand_proj).astype(jnp.bfloat16), "tensor"
    ).astype(jnp.float32)
    grad_mix, again_grad, ashift_grad = norm_backward(
        grad_first, first_normed, first_recip, attn_gain_f
    )
    obias_grad = jnp.sum(grad_mix, axis=0)
    grad_mix_low = grad_mix.astype(jnp.bfloat16)
    oproj_grad = inner_rows(attended, grad_mix_low)
    grad_attended = inner_cols(grad_mix_low, output_proj).astype(jnp.bfloat16)
    grad_heads = split_heads(grad_attended)

    def head_backward(state, group):
        query_head, key_head, value_head, grad_head, log_sum = group
        scores = cross_scores(query_head, key_head) * scale
        attn_probs = jnp.where(same_seg, jnp.exp(scores - log_sum), 0.0)
        grad_probs = cross_scores(grad_head, value_head)
        row_dot = jnp.sum(attn_probs * grad_probs, axis=1, keepdims=True)
        grad_scores = (attn_probs * (grad_probs - row_dot)).astype(jnp.bfloat16)
        grad_query = spread_apply(grad_scores, key_head) * scale
        grad_key = spread_transpose(grad_scores, query_head) * scale
        grad_value = spread_transpose(attn_probs.astype(jnp.bfloat16), grad_head)
        return (state, (grad_query, grad_key, grad_value))

    query_back, key_back, value_back = lax.scan(
        head_backward, None, (query_heads, key_heads, value_heads, grad_heads, log_sums)
    )[1]
    grad_queries = join_heads(query_back).astype(jnp.bfloat16)
    key_sum, value_sum = (
        lax.psum_scatter(
            join_heads(key_back).astype(jnp.bfloat16), "ctx", scatter_dimension=0, tiled=True
        ).astype(jnp.float32),
        lax.psum_scatter(
            join_heads(value_back).astype(jnp.bfloat16), "ctx", scatter_dimension=0, tiled=True
        ).astype(jnp.float32),
    )
    grad_keys = key_sum.astype(jnp.bfloat16)
    grad_values = value_sum.astype(jnp.bfloat16)
    qbias_grad = jnp.sum(grad_queries.astype(jnp.float32), axis=0)
    vbias_grad = jnp.sum(grad_values.astype(jnp.float32), axis=0)
    query_grad = inner_rows(inputs, grad_queries)
    key_grad = inner_rows(inputs, grad_keys)
    value_grad = inner_rows(inputs, grad_values)
    back_terms = (
        inner_cols(grad_queries, query_proj)
        + inner_cols(grad_keys, key_proj)
        + inner_cols(grad_values, value_proj)
    )
    input_grad = grad_mix + lax.psum(back_terms.astype(jnp.bfloat16), "tensor").astype(jnp.float32)
    (
        query_grad,
        key_grad,
        value_grad,
        qbias_grad,
        vbias_grad,
        oproj_grad,
        obias_grad,
        again_grad,
        ashift_grad,
        expand_grad,
        ebias_grad,
        shrink_grad,
        sbias_grad,
        fgain_grad,
        fshift_grad,
    ) = lax.psum(
        (
            query_grad,
            key_grad,
            value_grad,
            qbias_grad,
            vbias_grad,
            oproj_grad,
            obias_grad,
            again_grad,
            ashift_grad,
            expand_grad,
            ebias_grad,
            shrink_grad,
            sbias_grad,
            fgain_grad,
            fshift_grad,
        ),
        ("dp", "ctx"),
    )
    return (
        output.astype(jnp.bfloat16),
        input_grad,
        query_grad,
        key_grad,
        value_grad,
        qbias_grad,
        vbias_grad,
        oproj_grad,
        obias_grad,
        again_grad,
        ashift_grad,
        expand_grad,
        ebias_grad,
        shrink_grad,
        sbias_grad,
        fgain_grad,
        fshift_grad,
    )


def solution(mesh):
    in_specs = (
        P(("dp", "ctx"), None),
        P("dp", "ctx"),
        P(None, "tensor"),
        P(None, "tensor"),
        P(None, "tensor"),
        P("tensor"),
        P("tensor"),
        P("tensor", None),
        P(),
        P(),
        P(),
        P(None, "tensor"),
        P("tensor"),
        P("tensor", None),
        P(),
        P(),
        P(),
        P(("dp", "ctx"), None),
    )
    out_specs = (
        P(("dp", "ctx"), None),
        P(("dp", "ctx"), None),
        P(None, "tensor"),
        P(None, "tensor"),
        P(None, "tensor"),
        P("tensor"),
        P("tensor"),
        P("tensor", None),
        P(),
        P(),
        P(),
        P(None, "tensor"),
        P("tensor"),
        P("tensor", None),
        P(),
        P(),
        P(),
    )
    sizes = dict(mesh.shape)
    fits = sizes == {"dp": 4, "ctx": 4, "tensor": 2}
    chosen = functools.partial(fused_body, sizes) if fits else body
    return jax.shard_map(chosen, mesh=mesh, in_specs=in_specs, out_specs=out_specs, check_vma=False)
```

```python
import functools
import types

import jax
import jax.numpy as jnp
from jax import lax
from jax.experimental import pallas as pl
from jax.experimental.pallas import tpu as pltpu
from jax.sharding import PartitionSpec as P

HEAD_DIM = 64
norm_eps = 1e-12
masked = -1e30
MESH = pl.DeviceIdType.MESH
CORE, XS, YS, Z1, Z2, LINE = range(6)
BF16, F32 = jnp.bfloat16, jnp.float32
INV_SQRT2 = 0.7071067811865476
INV_SQRT_2PI = 0.3989422804014327


def nn(left, right):
    return jnp.dot(left, right, preferred_element_type=F32)


def nt(left, right):
    return lax.dot_general(left, right, (((1,), (1,)), ((), ())), preferred_element_type=F32)


def tn(left, right):
    return lax.dot_general(left, right, (((0,), (0,)), ((), ())), preferred_element_type=F32)


def normalise(values):
    centred = values - jnp.mean(values, axis=-1, keepdims=True)
    spread = jnp.mean(centred * centred, axis=-1, keepdims=True)
    recip = lax.rsqrt(spread + norm_eps)
    return centred * recip, recip


def denormalise(scaled, normed, recip):
    return recip * (
        scaled
        - jnp.mean(scaled, axis=-1, keepdims=True)
        - normed * jnp.mean(scaled * normed, axis=-1, keepdims=True)
    )


def gelu_parts(pre):
    phi_sum = 0.5 + 0.5 * lax.erf(pre * INV_SQRT2)
    slope = phi_sum + pre * (INV_SQRT_2PI * jnp.exp(-0.5 * pre * pre))
    return pre * phi_sum, slope


def column_sum(values):
    return jnp.sum(values, axis=0, keepdims=True)


class Shapes:
    def __init__(self, mesh, tokens, width, heads_width, units):
        self.nd, self.nc = mesh["dp"], mesh["ctx"]
        self.nx = self.nd // 2
        self.tokens, self.mine = tokens, tokens // 2
        self.width, self.hw, self.units = width, heads_width, units
        self.pairs = heads_width // 128


def make_kernel(sh, names):
    T, TM, D, W, F = sh.tokens, sh.mine, sh.width, sh.hw, sh.units
    HP = sh.pairs
    TILE = 512
    NTILE = F // TILE
    SLOTS = 4
    PARTS = 2
    PR = TM // PARTS

    def kernel(*refs):
        r = types.SimpleNamespace(**dict(zip(names, refs)))
        send_ref, recv_ref, local_ref = r.send, r.recv, r.local
        d, c, t = lax.axis_index("dp"), lax.axis_index("ctx"), lax.axis_index("tensor")
        core, xpos = lax.rem(d, 2), d // 2
        low_bit, high_bit = lax.rem(c, 2), c // 2
        next_c = c + 1 - 2 * low_bit
        z1_peer, z2_peer = (d, next_c, t), (d, c + 2 - 4 * high_bit, t)
        z3_peer = (d, next_c + 2 - 4 * high_bit, t)
        y_peer = (d, c, 1 - t)
        core_peer = (d + 1 - 2 * core, c, t)
        x_peer = (d + 2 - 4 * xpos, c, t)
        peer_of = {CORE: core_peer, XS: x_peer, YS: y_peer, Z1: z1_peer, Z2: z2_peer}
        bit_of = {CORE: core, XS: xpos, YS: t, Z1: low_bit, Z2: high_bit}
        my_rows = pl.ds(pl.multiple_of(t * TM, TM), TM)
        peer_rows = pl.ds(pl.multiple_of((1 - t) * TM, TM), TM)
        counts = [0, 0]

        def take(kind, k=1):
            at = counts[kind]
            counts[kind] += k
            assert counts[kind] <= (send_ref, local_ref)[kind].shape[0], counts
            return at

        def remote(src, dst, device, at=None, recv_at=None):
            at = take(0) if at is None else at
            recv_at = at if recv_at is None else recv_at
            return pltpu.make_async_remote_copy(
                src_ref=src, dst_ref=dst, send_sem=send_ref.at[at], recv_sem=recv_ref.at[recv_at],
                device_id=device, device_id_type=MESH,
            )

        def local(src, dst):
            return pltpu.make_async_copy(src, dst, local_ref.at[take(1)])

        unsent = []

        def go(copy, where=None):
            if where is None:
                copy.start()
            else:
                pl.when(where)(lambda: copy.start())
            unsent.append((copy, where))

        def wait_sends(*but):
            kept = [entry for entry in unsent if any(entry[0] is other for other in but)]
            for copy, where in unsent:
                if any(copy is other for other in but):
                    continue
                if where is None:
                    copy.wait_send()
                else:
                    pl.when(where)(lambda copy=copy: copy.wait_send())
            unsent[:] = kept

        loads = types.SimpleNamespace(
            x=local(r.x_in, r.xall.at[0]),
            wk=local(r.wk_in, r.wqkv.at[:, pl.ds(W, W)]),
            wv=local(r.wv_in, r.wqkv.at[:, pl.ds(2 * W, W)]),
            wq=local(r.wq_in, r.wqkv.at[:, pl.ds(0, W)]),
            wo=local(r.wo_in, r.wo.at[pl.ds(0, W)]),
            we=local(r.we_in, r.we.at[0]),
            ws=local(r.ws_in, r.ws.at[0]),
            cot=local(r.cot_in.at[my_rows], r.cot),
        )
        for copy in vars(loads).values():
            copy.start()

        def row(ref):
            return ref[...].astype(F32).reshape(1, ref.shape[0])

        vec = [row(ref) for ref in (r.ob_in, r.ag_in, r.as_in, r.sb_in, r.fg_in, r.fs_in)]
        r.eb[0] = row(r.eb_in)
        r.segs[0] = r.seg_in[...].astype(F32)
        barrier = pltpu.get_barrier_semaphore()
        greeted = [y_peer, core_peer, x_peer, z1_peer, z2_peer, z3_peer]
        for device in greeted:
            pl.semaphore_signal(barrier, inc=1, device_id=device, device_id_type=MESH)
        pl.semaphore_wait(barrier, len(greeted))

        seg_copies = [None] + [
            remote(r.segs.at[0], r.segs.at[k], peer) for k, peer in ((1, z1_peer), (2, z2_peer), (3, z3_peer))
        ]
        eb_copy = remote(r.eb.at[0], r.eb.at[1], y_peer)
        x_rows = [pl.ds(pl.multiple_of(t * TM + k * PR, PR), PR) for k in range(PARTS)]
        mid = lax.rem(low_bit + high_bit, 2)
        is_mid, is_end = mid == 1, mid == 0
        slots = (0, 1, 2 + mid, 3 - mid)
        x_at = take(0, 3 * PARTS)

        def x_recv(slot, k):
            return x_at + (slot - 1) * PARTS + k

        def x_move(src_slot, dst_slot, peer, k):
            src = r.x_in.at[x_rows[k]] if src_slot == 0 else r.xall.at[src_slot, x_rows[k]]
            return remote(src, r.xall.at[dst_slot, x_rows[k]], peer, None, x_recv(dst_slot, k))

        x_near = [x_move(0, 1, z1_peer, k) for k in range(PARTS)]
        x_far = [x_move(0, 3, z3_peer, k) for k in range(PARTS)]
        x_next = (
            None,
            [x_move(1, 2, z3_peer, k) for k in range(PARTS)],
            [x_move(3, 2, z1_peer, k) for k in range(PARTS)],
            [x_move(2, 3, z1_peer, k) for k in range(PARTS)],
        )
        x_y = [None] + [
            [remote(r.xall.at[slots[o], x_rows[k]], r.xall.at[slots[o], x_rows[k]], y_peer) for k in range(PARTS)]
            for o in (1, 2, 3)
        ]
        for k in range(PARTS):
            go(x_near[k])
            go(x_far[k], is_mid)
        for copy in seg_copies[1:]:
            go(copy)
        go(eb_copy)

        def arrive(o, k):
            here = r.xall.at[slots[o], x_rows[k]]
            remote(here, here, z1_peer, x_at, x_recv(slots[o], k)).wait_recv()
            go(x_next[o][k], is_mid)
            go(x_y[o][k])

        def block_here(o):
            if o == 1:
                for copy in seg_copies[1:]:
                    copy.wait_recv()
            for k in range(PARTS):
                x_y[o][k].wait_recv()

        chunks = [
            (r.wo_in, r.wo.at[pl.ds(W, W)], W, 0, 1),
            (r.we_in, r.we.at[1], D, 0, 2),
            (r.we_in, r.we.at[1], D, 1, 2),
            (r.ws_in, r.ws.at[1], F, 0, 2),
            (r.ws_in, r.ws.at[1], F, 1, 2),
        ]
        pieces = sh.nd * 2

        def window(chunk, owner):
            rows, part, parts = chunk[2:]
            size = rows // pieces // parts
            return pl.ds(pl.multiple_of(owner * (rows // pieces) + part * size, size), size)

        own_piece, pair_piece = d * 2 + low_bit, d * 2 + 1 - low_bit
        x_d = d + 2 - 4 * xpos
        x_pieces = (x_d * 2 + low_bit, x_d * 2 + 1 - low_bit)
        w_y, w_z, w_x, w_core = [], [], [], []
        for chunk in chunks:
            source, held = chunk[0], chunk[1]

            def move(owner, peer):
                where = window(chunk, owner)
                return remote(held.at[where], held.at[where], peer)

            own = window(chunk, own_piece)
            w_y.append(remote(source.at[own], held.at[own], y_peer))
            w_z.append(move(own_piece, z1_peer))
            w_x.append([move(piece, x_peer) for piece in (own_piece, pair_piece)])
            w_core.append([move(piece, core_peer) for piece in (own_piece, pair_piece) + x_pieces])

        def hop1(i):
            w_y[i].wait_recv()
            go(w_z[i])
            go(w_x[i][0])
            go(w_core[i][0])

        def hop2(i):
            w_z[i].wait_recv()
            go(w_x[i][1])
            go(w_core[i][1])

        def hop3(i):
            for k in range(2):
                w_x[i][k].wait_recv()
                go(w_core[i][2 + k])

        def weights_done(i):
            for copy in w_core[i]:
                copy.wait_recv()


        kv, m_s, l_s, acc = r.kv, r.m_s, r.l_s, r.acc
        value_bias = row(r.vb_in)
        scale = HEAD_DIM ** (-0.5)
        lane = lax.broadcasted_iota(jnp.int32, (T, 128), 1)

        def split_pair(target, p, pair):
            target[2 * p] = jnp.where(lane < 64, pair, 0.0).astype(BF16)
            target[2 * p + 1] = jnp.where(lane < 64, 0.0, pair).astype(BF16)

        def set_keys_values(slot):
            both = nn(r.xall[slot], r.wqkv[:, W:])
            for p in range(HP):
                kv[slot, p, 0] = both[:, p * 128 : (p + 1) * 128].astype(BF16)
                cols = slice(W + p * 128, W + (p + 1) * 128)
                kv[slot, p, 1] = (both[:, cols] + value_bias[:, p * 128 : (p + 1) * 128]).astype(BF16)

        def set_bias(slot):
            seg_keys = jnp.broadcast_to(r.segs[slot], (128, T)).T
            for j in range(T // 128):
                cols = slice(j * 128, (j + 1) * 128)
                r.bias[:, cols] = jnp.where(seg_keys == r.segs[0, :, cols], 0.0, masked)

        def project():
            loads.x.wait()
            loads.wk.wait()
            loads.wv.wait()
            set_keys_values(0)
            loads.wq.wait()
            queries = (nn(r.xall[0], r.wqkv[:, :W]) + row(r.qb_in)).astype(BF16).astype(F32) * scale
            for p in range(HP):
                split_pair(r.qm, p, queries[:, p * 128 : (p + 1) * 128])
            m_s[...] = jnp.full_like(m_s, masked)
            l_s[...] = jnp.zeros_like(l_s)
            acc[...] = jnp.zeros_like(acc)
            set_bias(0)


        def attend(slot, p):
            pair_keys = kv[slot, p, 0]
            pair_values = kv[slot, p, 1].T
            for hh in range(2):
                h = 2 * p + hh
                s = nt(pair_keys, r.qm[h]) + r.bias[...]
                old = m_s[h]
                new = jnp.maximum(old, jnp.max(s, axis=0, keepdims=True))
                e = jnp.exp(s - new)
                alpha = jnp.exp(old - new)
                l_s[h] = l_s[h] * alpha + jnp.sum(e, axis=0, keepdims=True)
                m_s[h] = new
                acc[h] = acc[h] * alpha + nn(pair_values[hh * 64 : hh * 64 + 64], e.astype(BF16))

        def run(body, services=None):
            def step(p, carry):
                body(p)
                for at, fn in (services or {}).items():
                    pl.when(p == at)(fn)
                return carry

            lax.fori_loop(0, HP, step, 0)

        def together(*fns):
            def all_of():
                for fn, arg in fns:
                    fn(*arg)

            return all_of

        def flip_inputs(slot):
            at = slot * T if isinstance(slot, int) else pl.multiple_of(slot * T, T)
            r.xt[:, pl.ds(at, T)] = r.xall[slot].T

        def next_block(o):
            block_here(o)
            set_keys_values(slots[o])
            set_bias(slots[o])

        att_at = take(0, HP)

        def att_copy(p):
            cols = pl.ds(p * 128, 128)
            return remote(r.att.at[peer_rows, cols], r.att_o.at[:, cols], y_peer, att_at + p)

        def attend_last(p):
            attend(slots[3], p)
            for h in (2 * p, 2 * p + 1):
                acc[h] = acc[h] / l_s[h]
                m_s[h] = m_s[h] + jnp.log(l_s[h])
            pair = acc[2 * p : 2 * p + 2].reshape(128, T).T
            r.att[:, p * 128 : (p + 1) * 128] = pair.astype(BF16)
            att_copy(p).start()

        fl_copy = remote(r.fl.at[my_rows], r.fl.at[my_rows], y_peer)

        def out_project():
            loads.wo.wait()
            r.sec[...] = nn(r.att[my_rows, :], r.wo[0:W, :])

        def first_norm():
            for p in range(HP):
                att_copy(p).wait_recv()
            mix = r.sec[...] + nn(r.att_o[...], r.wo[W : 2 * W, :])
            normed, recip = normalise(r.xall[0, my_rows, :].astype(F32) + mix + vec[0])
            r.n1[...] = normed
            r.r1[...] = jnp.broadcast_to(recip, (TM, 128))
            first = normed * vec[1] + vec[2]
            r.sec[...] = first + vec[3]
            r.fl[my_rows, :] = first.astype(BF16)
            go(fl_copy)

        def tile_cols(j):
            return pl.ds(pl.multiple_of(j * TILE, TILE), TILE)

        def forward_tile(side, j):
            cols = tile_cols(j)
            pre = nn(r.fl[my_rows, :], r.we[side, :, cols]) + r.eb[side, :, cols]
            hidden, slope = gelu_parts(pre)
            hidden = hidden.astype(BF16)
            r.gp[side, :, cols] = slope
            if side == 0:
                r.hid[my_rows, cols] = hidden
            r.sec[...] += nn(hidden, r.ws[side, cols, :])

        def tiles(fn):
            def step(j, carry):
                fn(j)
                return carry

            lax.fori_loop(0, NTILE, step, 0)

        def own_units():
            loads.we.wait()
            loads.ws.wait()
            tiles(lambda j: forward_tile(0, j))

        def other_units():
            eb_copy.wait_recv()
            tiles(lambda j: forward_tile(1, j))

        go(w_y[0])
        go(w_y[1])
        project()
        arrive(1, 0)

        def with_00():
            go(w_y[2])
            go(w_y[3])
            hop1(0)
            arrive(1, 1)
            arrive(2, 0)
            hop2(0)
            hop1(1)


        def with_01():
            arrive(2, 1)

        run(lambda p: attend(slots[0], p), {0: with_00, 1: with_01})
        arrive(3, 0)
        hop2(1)
        next_block(1)

        def with_11():
            arrive(3, 1)
            hop1(2)
            go(w_y[4])
            hop3(0)

        run(lambda p: attend(slots[1], p), {1: with_11})
        hop1(3)
        next_block(2)

        def with_20():
            hop3(1)


        def with_21():
            hop2(2)

        run(lambda p: attend(slots[2], p), {0: with_20, 1: with_21})
        hop2(3)
        weights_done(0)
        next_block(3)
        attend_last(0)
        hop1(4)
        attend_last(1)
        attend_last(2)
        flip_inputs(slots[1])
        hop2(4)
        out_project()
        first_norm()
        hop3(2)
        flip_inputs(slots[2])
        flip_inputs(slots[3])
        weights_done(1)
        hop3(3)
        weights_done(2)
        flip_inputs(slots[0])
        hop3(4)
        own_units()
        weights_done(3)
        weights_done(4)
        other_units()
        loads.cot.wait()
        normed2, recip2 = normalise(r.sec[...])
        upstream = r.cot[...].astype(F32)
        grad_second = denormalise(upstream * vec[4], normed2, recip2)
        r.gf[...] = grad_second
        r.gs[my_rows, :] = grad_second.astype(BF16)
        gs_copy = remote(r.gs.at[my_rows], r.gs.at[my_rows], y_peer)
        go(gs_copy)
        small = r.small
        small[0:1, :] = column_sum(upstream * normed2)
        small[1:2, :] = column_sum(upstream)
        small[2:3, :] = column_sum(grad_second)
        r.oy[...] = (normed2 * vec[4] + vec[5]).astype(BF16)
        oy_local = local(r.oy, r.out.at[my_rows])
        oy_local.start()


        def backward_tile(side, j):
            cols = tile_cols(j)
            low = (nt(r.gs[my_rows, :], r.ws[side, cols, :]) * r.gp[side, :, cols]).astype(BF16)
            if side == 0:
                r.gpre[my_rows, cols] = low
            r.gf[...] += nt(low, r.we[side, :, cols])

        tiles(lambda j: backward_tile(0, j))
        tiles(lambda j: backward_tile(1, j))
        grad_first = r.gf[...]
        normed = r.n1[...]
        grad_mix = denormalise(grad_first * vec[1], normed, r.r1[:, 0:1])
        r.gmix[...] = grad_mix
        r.gm[my_rows, :] = grad_mix.astype(BF16)
        gm_copy = remote(r.gm.at[my_rows], r.gm.at[my_rows], y_peer)
        go(gm_copy)
        small[3:4, :] = column_sum(grad_first * normed)
        small[4:5, :] = column_sum(grad_first)
        small[5:6, :] = column_sum(grad_mix)

        def rows_at(ref, first_row, rows):
            return ref.at[pl.ds(pl.multiple_of(first_row, rows), rows)]

        class Unit:
            def __init__(self, grad, whole, out, order, bufs):
                self.grad, self.order, self.bufs = grad, order, bufs
                self.first, self.rows, self.line = [0], [grad.shape[0]], None
                for stage in order:
                    self.rows.append(self.rows[-1] // (4 if stage == LINE else 2))
                    at = c if stage == LINE else bit_of[stage]
                    self.first.append(self.first[-1] + at * self.rows[-1])
                self.down, self.up = [], []
                for k, stage in enumerate(order):
                    rows, last = self.rows[k + 1], k == len(order) - 1
                    target = rows_at(whole, self.first[k + 1], rows)
                    source = target
                    if last:
                        source = rows_at(grad, self.first[k + 1], rows)
                        self.kept = local(source, target)
                    if stage == LINE:
                        self.line = k
                        self.far = self.first[k] + 2 * (1 - high_bit) * rows
                        self.edge = self.first[k] + 3 * high_bit * rows
                        near = self.first[k] + 2 * high_bit * rows
                        ends = grad.at[pl.ds(pl.multiple_of(self.first[k] + (1 - high_bit) * rows, rows), 3 * rows)]
                        self.down.append(
                            (
                                remote(ends, bufs[k][0], z1_peer),
                                remote(rows_at(grad, self.far, 2 * rows), bufs[k][1], z3_peer),
                                remote(rows_at(grad, self.edge, rows), bufs[k][2], z1_peer),
                            )
                        )
                        near, far = rows_at(whole, near, 2 * rows), rows_at(whole, self.far, 2 * rows)
                        self.up.append(
                            (remote(source, target, z1_peer), remote(near, near, z3_peer), remote(far, far, z1_peer))
                        )
                        continue
                    theirs = rows_at(grad, self.first[k] + (1 - bit_of[stage]) * rows, rows)
                    self.down.append(remote(theirs, bufs[k], peer_of[stage]))
                    self.up.append(remote(source, target, peer_of[stage]))
                self.stored = local(whole, out)

            def add_rows(self, first_row, rows, terms, step):

                def tile(i, carry):
                    window = self.grad.at[pl.ds(pl.multiple_of(first_row + i * step, step), step)]
                    total = window[...].astype(F32)
                    for buf, at in terms:
                        total = total + buf[pl.ds(pl.multiple_of(at + i * step, step), step), :].astype(F32)
                    window[...] = total.astype(BF16)
                    return carry

                lax.fori_loop(0, rows // step, tile, 0)

            def send(self, k):
                go(self.down[k])

            def add(self, k):
                self.down[k].wait_recv()
                self.add_rows(self.first[k + 1], self.rows[k + 1], [(self.bufs[k], 0)], min(96, self.rows[k + 1]))

            def forward(self, k):
                self.add(k)
                self.send(k + 1)

            def spread(self, k):
                go(self.up[k])
                if k == len(self.order) - 1:
                    self.kept.start()

            def back(self, k):
                if k == len(self.order) - 1:
                    self.kept.wait()
                self.up[k].wait_recv()
                if self.line is not None and k - 1 == self.line:
                    go(self.up[k - 1][0])
                else:
                    self.spread(k - 1)

            def za(self):
                go(self.down[self.line][0], is_end)

            def zb(self):
                k = self.line
                rows = self.rows[k + 1]

                @pl.when(is_mid)
                def _():
                    self.down[k][0].wait_recv()
                    self.add_rows(self.far, 2 * rows, [(self.bufs[k][0], (1 - high_bit) * rows)], rows)

                go(self.down[k][1], is_mid)

            def zc(self):
                k = self.line
                rows, (first_buf, second_buf, _) = self.rows[k + 1], self.bufs[k]

                @pl.when(is_mid)
                def _():
                    self.down[k][1].wait_recv()
                    self.add_rows(self.edge, rows, [(second_buf, high_bit * rows)], rows)

                go(self.down[k][2], is_mid)

                @pl.when(is_mid)
                def _():
                    terms = [(first_buf, 2 * high_bit * rows), (second_buf, (1 - high_bit) * rows)]
                    self.add_rows(self.first[k + 1], rows, terms, rows)
                    if k == len(self.order) - 1:
                        self.kept.start()
                        self.up[k][0].start()

            def zd(self):
                k = self.line

                @pl.when(is_end)
                def _():
                    self.down[k][2].wait_recv()
                    self.add_rows(self.first[k + 1], self.rows[k + 1], [(self.bufs[k][2], 0)], self.rows[k + 1])
                    if k == len(self.order) - 1:
                        self.kept.start()
                        self.up[k][0].start()

                if k == len(self.order) - 1:
                    unsent.append((self.up[k][0], None))

            def ze(self):
                k = self.line

                @pl.when(is_mid)
                def _():
                    if k == len(self.order) - 1:
                        self.kept.wait()
                    self.up[k][0].wait_recv()

                go(self.up[k][1], is_mid)

            def zf(self):
                pl.when(is_mid)(lambda: self.up[self.line][1].wait_recv())
                go(self.up[self.line][2], is_mid)

            def zg(self):
                k = self.line

                @pl.when(is_end)
                def _():
                    if k == len(self.order) - 1:
                        self.kept.wait()
                    self.up[k][0].wait_recv()
                    self.up[k][2].wait_recv()

                self.spread(k - 1)

            def turn(self):
                k = len(self.order) - 1
                self.add(k)
                self.spread(k)

            def store(self):
                self.up[0].wait_recv()
                self.stored.start()

        def all_sum(buf, slots, stages):
            copies = [remote(buf.at[k % 2], slots.at[k], peer_of[stage]) for k, stage in enumerate(stages)]

            def start(k):
                copies[k].start()

            def finish(k):
                copies[k].wait()
                total = buf[k % 2] + slots[k]
                if stages[k] == YS:
                    which = lax.broadcasted_iota(jnp.int32, total.shape, 0)
                    total = jnp.where(which < 6, total, buf[k % 2])
                buf[(k + 1) % 2] = total
                if k + 1 < len(stages):
                    start(k + 1)

            return start, finish


        def other_hidden(j):
            cols = tile_cols(j)
            pre = nn(r.fl[peer_rows, :], r.we[0, :, cols]) + r.eb[0, :, cols]
            hidden, slope = gelu_parts(pre)
            r.hid[peer_rows, cols] = hidden.astype(BF16)
            r.gp[0, :, cols] = slope

        def other_slopes():
            def tile(j):
                cols = tile_cols(j)
                low = nt(r.gs[peer_rows, :], r.ws[0, cols, :]) * r.gp[0, :, cols]
                r.gpre[peer_rows, cols] = low.astype(BF16)

            tiles(tile)

        fl_copy.wait_recv()
        tiles(other_hidden)
        r.flt[...] = r.fl[...].T
        wait_sends(gm_copy)
        gs_copy.wait_recv()
        by_line, by_pairs = (CORE, XS, LINE), (CORE, XS, Z1, Z2)
        half_d = D // 2

        def line_unit(grad, whole, out, first_buf, k):
            steps = (r.l0.at[k], r.l1.at[k], r.l2.at[k])
            return Unit(grad, whole, out, by_line, (first_buf, r.x0.at[k], steps))

        def pair_unit(grad, whole, out, k):
            return Unit(grad, whole, out, by_pairs, (r.p0.at[k], r.p1.at[k], r.p2.at[k], r.p3.at[k]))

        s1 = Unit(
            r.ws.at[1, pl.ds(0, D)], r.ws.at[0, pl.ds(0, D)], r.us_out.at[pl.ds(0, D)], (CORE, LINE, XS),
            (r.s0.at[pl.ds(0, half_d)], (r.z0, r.z1, r.z2), r.z3),
        )
        s2 = line_unit(
            r.ws.at[1, pl.ds(D, D)], r.ws.at[0, pl.ds(D, D)], r.us_out.at[pl.ds(D, D)], r.s0.at[pl.ds(half_d, half_d)], 1
        )
        e1, e2 = [
            line_unit(
                r.we.at[1, :, pl.ds(at, D)], r.we.at[0, :, pl.ds(at, D)], r.ue_out.at[:, pl.ds(at, D)], r.e0.at[k - 2], k
            )
            for k, at in ((2, 0), (3, D))
        ]
        ua = pair_unit(r.ua, r.s0, r.ua_out, 0)
        ub = pair_unit(r.ub, r.wo, r.ub_out, 1)

        def half_of(which):
            return which * core + (1 - which) * (1 - core)

        def shrink_tiles(which):
            def tile(i, carry):
                at = pl.multiple_of(i * D + half_of(which) * half_d, 128)
                r.ws[1, pl.ds(at, half_d), :] = tn(r.hid[:, pl.ds(at, half_d)], r.gs[...]).astype(BF16)
                return carry

            lax.fori_loop(0, F // D, tile, 0)

        def half_rows(which):
            return pl.ds(pl.multiple_of(half_of(which) * (D // 2), D // 2), D // 2)

        def expand_tiles(which):
            rows = half_rows(which)

            def tile(j):
                cols = tile_cols(j)
                r.we[1, rows, cols] = nn(r.flt[rows, :], r.gpre[:, cols]).astype(BF16)

            tiles(tile)

        def sum_blocks():
            totals = column_sum(r.gpre[...].astype(F32))
            small[6:7, :] = totals[:, :D]
            small[7:8, :] = totals[:, D:]
            r.es[0] = small[...]

        early_start, early_finish = all_sum(r.es, r.es_r, (YS, CORE, XS, Z1, Z2))
        late_start, late_finish = all_sum(r.ls, r.ls_r, (CORE, XS, Z1, Z2))

        def grad_heads():
            gm_copy.wait_recv()
            grad_att = nt(r.gm[...], r.wo[0:W, :]).astype(BF16).astype(F32)
            flipped = grad_att.T.reshape(2 * HP, 64, T)
            r.delta[...] = jnp.sum(acc[...] * flipped, axis=1, keepdims=True)
            for p in range(HP):
                split_pair(r.dm, p, grad_att[:, p * 128 : (p + 1) * 128])
            acc[...] = jnp.zeros_like(acc)

        oy_send = remote(r.oy, r.out.at[my_rows], y_peer)
        dkv = r.dkv

        def pull(slot, p):
            pair_keys, pair_values = kv[slot, p, 0], kv[slot, p, 1]
            flipped_keys = pair_keys.T
            grad_k = jnp.zeros((T, 128), F32)
            grad_v = jnp.zeros((T, 128), F32)
            for hh in range(2):
                h = 2 * p + hh
                q, g = r.qm[h], r.dm[h]
                probs = jnp.exp(nt(pair_keys, q) + (r.bias[...] - m_s[h]))
                grad_p = nt(pair_values, g)
                grad_v = grad_v + nn(probs.astype(BF16), g)
                ds = (probs * (grad_p - r.delta[h])).astype(BF16)
                grad_k = grad_k + nn(ds, q)
                acc[h] += nn(flipped_keys[hh * 64 : hh * 64 + 64], ds)
            rows = slice(slot * T, (slot + 1) * T)
            dkv[rows, pl.ds(pl.multiple_of(p * 128, 128), 128)] = grad_k.astype(BF16)
            dkv[rows, pl.ds(pl.multiple_of(W + p * 128, 128), 128)] = grad_v.astype(BF16)

        HR = TM // 2

        def half(at, h):
            return pl.ds(at + h * HR, HR)

        dx_y = [
            [remote(r.xall.at[k, half(0, h)], r.dxy.at[k, half(0, h)], y_peer) for h in range(2)] for k in range(SLOTS)
        ]

        def dx_move(slot, target, peer):
            return [remote(r.xall.at[slot, half(TM, h)], r.dxz.at[target, half(0, h)], peer) for h in range(2)]

        dx_end = {3: dx_move(3, 0, z1_peer), 2: dx_move(2, 1, z1_peer), 1: dx_move(1, 2, z1_peer)}
        dx_mid = {3: dx_move(3, 3, z3_peer), 2: dx_move(2, 4, z3_peer), 1: dx_move(1, 5, z1_peer)}

        def dx_rows(slot, rows):
            here = pl.ds(pl.multiple_of(slot * T + rows.start, TM), TM)
            return nt(dkv[here, :], r.wqkv[:, W:])

        def dx_part(slot):
            r.xall[slot, 0:TM] = dx_rows(slot, peer_rows).astype(BF16)
            for h in range(2):
                go(dx_y[slot][h])
            r.xall[slot, TM:] = dx_rows(slot, my_rows).astype(BF16)

        def add_to(slot, h, buf, at):
            rows, kept = slice(h * HR, (h + 1) * HR), slice(TM + h * HR, TM + (h + 1) * HR)
            total = r.xall[slot, kept].astype(F32) + buf[at, rows].astype(F32)
            r.xall[slot, kept] = total.astype(BF16)

        def dx_sum(slot, h):
            dx_y[slot][h].wait_recv()
            add_to(slot, h, r.dxy, slot)
            go(dx_end[slot][h], is_end)

        def dx_pass(slot, h):
            came = {3: dx_end[2], 2: dx_end[3], 1: dx_mid[2]}[slot][h]
            at = {3: 1, 2: 0, 1: 4}[slot]

            @pl.when(is_mid)
            def _():
                came.wait_recv()
                add_to(slot, h, r.dxz, at)

            go(dx_mid[slot][h], is_mid)

        ig_rows = [pl.ds(pl.multiple_of(t * TM + h * HR, HR), HR) for h in range(2)]
        ig_local = [local(r.igm.at[half(0, h)], r.ig_out.at[ig_rows[h]]) for h in range(2)]
        ig_send = [remote(r.igm.at[half(0, h)], r.ig_out.at[ig_rows[h]], y_peer) for h in range(2)]

        def dx_out(h):
            rows = slice(h * HR, (h + 1) * HR)
            dx_y[0][h].wait_recv()
            r.gmix[rows] += r.dxy[0, rows].astype(F32)

            @pl.when(is_mid)
            def _():
                dx_end[1][h].wait_recv()
                dx_mid[3][h].wait_recv()
                r.gmix[rows] += r.dxz[2, rows].astype(F32) + r.dxz[3, rows].astype(F32)

            @pl.when(is_end)
            def _():
                dx_mid[1][h].wait_recv()
                r.gmix[rows] += r.dxz[5, rows].astype(F32)

            r.igm[rows] = r.gmix[rows].astype(BF16)
            ig_local[h].start()
            go(ig_send[h])


        def key_value_tiles(which):
            rows = half_rows(which)
            r.ub[rows, :] = nn(r.xt[rows, :], dkv[...]).astype(BF16)

        def query_output_tiles(which):
            rows = half_rows(which)
            r.ua[rows, 0:W] = nn(r.xt[rows, 0:T], r.dq[...]).astype(BF16)
            cols = pl.ds(pl.multiple_of(half_of(which) * W, 128), W)
            r.ua[rows, W:] = tn(r.att[...], r.gm[:, cols]).astype(BF16)

        def query_grads():
            r.dq[...] = (acc[...].reshape(W, T).T * scale).astype(BF16)
            r.ls[0, 0:1, :] = column_sum(r.dq[...].astype(F32))
            r.ls[0, 1:2, :] = column_sum(dkv[:, W:].astype(F32))
            r.ls[0, 2:8, :] = jnp.zeros((6, W), F32)

        def dx_own():
            r.xall[0, 0:TM] = (dx_rows(0, peer_rows) + nt(r.dq[peer_rows, :], r.wqkv[:, :W])).astype(BF16)
            for h in range(2):
                go(dx_y[0][h])
            r.gmix[...] += dx_rows(0, my_rows) + nt(r.dq[my_rows, :], r.wqkv[:, :W])

        shrink_tiles(0)
        s1.send(0)
        s2.send(0)
        other_slopes()
        shrink_tiles(1)
        expand_tiles(0)
        e1.send(0)
        e2.send(0)
        expand_tiles(1)
        sum_blocks()
        s2.forward(0)
        s1.add(0)
        s1.za()
        grad_heads()
        set_bias(3)

        def beside_31():
            e1.forward(0)

        run(lambda p: pull(3, p), {1: beside_31})
        dx_part(3)
        s2.add(1)
        s2.za()
        set_bias(2)

        def beside_20():
            s1.zb()

        run(lambda p: pull(2, p), {0: beside_20})
        e1.add(1)
        e1.za()
        e2.forward(0)
        dx_part(2)
        dx_sum(3, 0)
        s2.zb()
        set_bias(1)

        def beside_11():
            s1.zc()

        run(lambda p: pull(1, p), {1: beside_11})
        e1.zb()
        set_bias(0)

        def beside_00():
            e2.add(1)
            e2.za()
            early_start(0)
            s1.zd()
            s2.zc()
            go(oy_send)
            s1.send(2)


        def beside_01():
            s2.zd()
            dx_sum(2, 0)
            dx_pass(2, 0)
            e1.zc()

        run(lambda p: pull(0, p), {0: beside_00, 1: beside_01})
        s1.add(2)
        s1.spread(2)
        query_grads()
        key_value_tiles(0)
        ub.send(0)
        e1.zd()
        e2.zb()
        dx_sum(3, 1)
        s2.ze()
        s1.back(2)
        query_output_tiles(0)
        ua.send(0)
        key_value_tiles(1)
        ub.forward(0)
        early_finish(0)
        e2.zc()
        early_finish(1)
        late_start(0)
        e1.ze()
        s2.zf()
        dx_pass(3, 0)
        late_finish(0)
        query_output_tiles(1)
        ua.forward(0)
        e2.zd()
        ub.forward(1)
        e2.ze()
        e1.zf()
        s2.zg()
        early_finish(2)
        ub.forward(2)
        ua.forward(1)
        ub.turn()
        e1.zg()
        e2.zf()
        ua.forward(2)
        dx_sum(2, 1)
        dx_part(1)
        dx_pass(2, 1)
        dx_own()
        ub.back(3)
        late_finish(1)
        ua.turn()
        dx_sum(1, 0)
        dx_pass(1, 0)
        e2.zg()
        ub.back(2)
        s1.ze()
        dx_pass(3, 1)
        ua.back(3)
        dx_out(0)
        dx_sum(1, 1)
        dx_pass(1, 1)
        e1.back(1)
        s2.back(1)
        ua.back(2)
        s1.zf()
        dx_out(1)
        e2.back(1)
        early_finish(3)
        ub.back(1)
        ua.back(1)
        s1.zg()
        late_finish(2)
        e2.store()
        e1.store()
        late_finish(3)
        ub.store()
        ua.store()
        s2.store()
        early_finish(4)
        s1.store()
        small_copies = (local(r.es.at[1], r.small_out), local(r.ls.at[0], r.late_out))
        for copy in small_copies:
            copy.start()
        oy_local.wait()
        oy_send.wait_recv()
        for h in range(2):
            ig_local[h].wait()
            ig_send[h].wait_recv()
        for copy in small_copies:
            copy.wait()
        for unit in (s1, s2, e1, e2, ua, ub):
            unit.stored.wait()
        for p in range(HP):
            att_copy(p).wait_send()
        wait_sends()

    return kernel


def layer_call(sh, args):
    T, TM, D, W, F = sh.tokens, sh.mine, sh.width, sh.hw, sh.units
    HP = sh.pairs
    any_spec = pl.BlockSpec(memory_space=pl.ANY)
    vmem_spec = pl.BlockSpec(memory_space=pltpu.VMEM)
    ins = dict(
        seg_in=vmem_spec, qb_in=vmem_spec, vb_in=vmem_spec, ob_in=vmem_spec, ag_in=vmem_spec,
        as_in=vmem_spec, eb_in=vmem_spec, sb_in=vmem_spec, fg_in=vmem_spec, fs_in=vmem_spec,
        x_in=any_spec, wq_in=any_spec, wk_in=any_spec, wv_in=any_spec,
        wo_in=any_spec, we_in=any_spec, ws_in=any_spec, cot_in=any_spec,
    )
    outs = dict(
        out=((T, D), BF16, any_spec),
        ig_out=((T, D), BF16, any_spec),
        ue_out=((D, F), BF16, any_spec),
        us_out=((F, D), BF16, any_spec),
        ua_out=((D, 2 * W), BF16, any_spec),
        ub_out=((D, 2 * W), BF16, any_spec),
        small_out=((8, D), F32, any_spec),
        late_out=((8, W), F32, any_spec),
    )
    vm = lambda shape, kind: pltpu.VMEM(shape, kind)
    scratch = dict(
        send=pltpu.SemaphoreType.DMA((192,)),
        recv=pltpu.SemaphoreType.DMA((192,)),
        local=pltpu.SemaphoreType.DMA((32,)),
        xall=vm((4, T, D), BF16),
        xt=vm((D, 4 * T), BF16),
        wqkv=vm((D, 3 * W), BF16),
        wo=vm((2 * W, D), BF16),
        we=vm((2, D, F), BF16),
        ws=vm((2, F, D), BF16),
        eb=vm((2, 1, F), F32),
        cot=vm((TM, D), BF16),
        segs=vm((4, 1, T), F32),
        bias=vm((T, T), F32),
        kv=vm((4, HP, 2, T, 128), BF16),
        qm=vm((2 * HP, T, 128), BF16),
        dm=vm((2 * HP, T, 128), BF16),
        m_s=vm((2 * HP, 1, T), F32),
        l_s=vm((2 * HP, 1, T), F32),
        delta=vm((2 * HP, 1, T), F32),
        acc=vm((2 * HP, 64, T), F32),
        att=vm((T, W), BF16),
        att_o=vm((TM, W), BF16),
        n1=vm((TM, D), F32),
        r1=vm((TM, 128), F32),
        sec=vm((TM, D), F32),
        gf=vm((TM, D), F32),
        gmix=vm((TM, D), F32),
        fl=vm((T, D), BF16),
        flt=vm((D, T), BF16),
        gs=vm((T, D), BF16),
        gm=vm((T, D), BF16),
        gp=vm((2, TM, F), F32),
        hid=vm((T, F), BF16),
        gpre=vm((T, F), BF16),
        oy=vm((TM, D), BF16),
        small=vm((8, D), F32),
        es=vm((2, 8, D), F32),
        es_r=vm((5, 8, D), F32),
        ls=vm((2, 8, W), F32),
        ls_r=vm((4, 8, W), F32),
        dkv=vm((4 * T, 2 * W), BF16),
        dq=vm((T, W), BF16),
        dxy=vm((4, TM, D), BF16),
        dxz=vm((6, TM, D), BF16),
        igm=vm((TM, D), BF16),
        ua=vm((D, 2 * W), BF16),
        ub=vm((D, 2 * W), BF16),
        s0=vm((D, D), BF16),
        e0=vm((2, D // 2, D), BF16),
        z0=vm((3 * (D // 8), D), BF16),
        z1=vm((2 * (D // 8), D), BF16),
        z2=vm((D // 8, D), BF16),
        z3=vm((D // 16, D), BF16),
        x0=vm((4, D // 4, D), BF16),
        l0=vm((4, 3 * (D // 16), D), BF16),
        l1=vm((4, 2 * (D // 16), D), BF16),
        l2=vm((4, D // 16, D), BF16),
        p0=vm((2, D // 2, D), BF16),
        p1=vm((2, D // 4, D), BF16),
        p2=vm((2, D // 8, D), BF16),
        p3=vm((2, D // 16, D), BF16),
    )
    names = list(ins) + list(outs) + list(scratch)
    return pl.pallas_call(
        make_kernel(sh, names),
        out_shape=[jax.ShapeDtypeStruct(o[0], o[1]) for o in outs.values()],
        in_specs=list(ins.values()),
        out_specs=[o[2] for o in outs.values()],
        scratch_shapes=list(scratch.values()),
        compiler_params=pltpu.CompilerParams(
            collective_id=0, has_side_effects=True, vmem_limit_bytes=63 * 1024 * 1024
        ),
        name="layer",
    )(*args)


def finish_kernel(sh, names, *refs):
    r = types.SimpleNamespace(**dict(zip(names, refs)))
    W = sh.hw
    half = sh.units // 2
    pieces = []
    for at in range(2):
        pieces.append((r.us.at[pl.ds(at * half, half)], r.us_v.at[at], r.usf.at[at], r.us_out.at[pl.ds(at * half, half)]))
    for at in range(2):
        rows = pl.ds(at * W, W)
        pieces.append((r.ue.at[rows], r.ue_v.at[at], r.uef.at[at], r.ue_out.at[rows]))
    cols = [pl.ds(0, W), pl.ds(W, W)]
    pieces.append((r.ub.at[:, cols[0]], r.ab_v.at[0], r.abf.at[0], r.wk_out))
    pieces.append((r.ub.at[:, cols[1]], r.ab_v.at[1], r.abf.at[1], r.wv_out))
    pieces.append((r.ua.at[:, cols[0]], r.ab_v.at[2], r.abf.at[2], r.wq_out))
    for at in range(2):
        rows = pl.ds(at * W, W)
        pieces.append((r.ua.at[rows, cols[1]], r.o_v.at[at], r.of.at[at], r.wo_out.at[:, cols[at]]))
    pieces.append((r.ig, r.ig_v, r.igf, r.ig_out))
    taken = pltpu.make_async_copy(r.out, r.out_v, r.sems.at[0])
    taken.start()
    reads = [pltpu.make_async_copy(p[0], p[1], r.sems.at[1 + k]) for k, p in enumerate(pieces)]
    for copy in reads:
        copy.start()
    at_small = 2 * len(pieces) + 2
    small_reads = [
        pltpu.make_async_copy(r.small, r.small_v, r.sems.at[at_small]),
        pltpu.make_async_copy(r.late, r.late_v, r.sems.at[at_small + 1]),
    ]
    for copy in small_reads:
        copy.start()
    taken.wait()
    passed = pltpu.make_async_copy(r.out_v, r.out_out, r.sems.at[2 * len(pieces) + 1])
    passed.start()
    writes = []

    def vectors():
        for copy in small_reads:
            copy.wait()
        for target, at in ((r.fg_v, 0), (r.fs_v, 1), (r.sb_v, 2), (r.ag_v, 3), (r.as_v, 4), (r.ob_v, 5)):
            target[...] = r.small_v[at]
        r.eb_v[0 : sh.width] = r.small_v[6]
        r.eb_v[sh.width :] = r.small_v[7]
        r.qb_v[...] = r.late_v[0]
        r.vb_v[...] = r.late_v[1]
        leaving = (
            (r.fg_v, r.fg), (r.fs_v, r.fs), (r.sb_v, r.sb), (r.ag_v, r.ag), (r.as_v, r.as_), (r.ob_v, r.ob),
            (r.eb_v, r.eb), (r.qb_v, r.qb), (r.vb_v, r.vb),
        )
        for k, (held, target) in enumerate(leaving):
            copy = pltpu.make_async_copy(held, target, r.sems.at[at_small + 2 + k])
            copy.start()
            writes.append(copy)

    for k, (_, low, wide, target) in enumerate(pieces):
        if k == 4:
            vectors()
        reads[k].wait()
        rows = low.shape[0]
        step = 96 if rows % 96 == 0 else 64

        def tile(i, carry):
            at = pl.ds(pl.multiple_of(i * step, step), step)
            wide[at, :] = low[at, :].astype(F32)
            return carry

        lax.fori_loop(0, rows // step, tile, 0)
        copy = pltpu.make_async_copy(wide, target, r.sems.at[1 + len(pieces) + k])
        copy.start()
        writes.append(copy)
    passed.wait()
    for k, copy in enumerate(writes):
        copy.wait()


def finish_call(sh, parts):
    T, D, W, F = sh.tokens, sh.width, sh.hw, sh.units
    any_spec = pl.BlockSpec(memory_space=pl.ANY)
    hbm_spec = pl.BlockSpec(memory_space=pltpu.HBM)
    ins = dict(
        out=hbm_spec, ig=hbm_spec, ue=hbm_spec, us=hbm_spec, ua=hbm_spec, ub=hbm_spec,
        small=hbm_spec, late=hbm_spec,
    )
    outs = dict(
        out_out=((T, D), BF16, any_spec),
        ig_out=((T, D), F32, any_spec),
        wq_out=((D, W), F32, any_spec),
        wk_out=((D, W), F32, any_spec),
        wv_out=((D, W), F32, any_spec),
        qb=((W,), F32, any_spec),
        vb=((W,), F32, any_spec),
        wo_out=((W, D), F32, any_spec),
        ob=((D,), F32, any_spec),
        ag=((D,), F32, any_spec),
        as_=((D,), F32, any_spec),
        ue_out=((D, F), F32, any_spec),
        eb=((F,), F32, any_spec),
        us_out=((F, D), F32, any_spec),
        sb=((D,), F32, any_spec),
        fg=((D,), F32, any_spec),
        fs=((D,), F32, any_spec),
    )
    scratch = dict(
        sems=pltpu.SemaphoreType.DMA((40,)),
        out_v=pltpu.VMEM((T, D), BF16),
        small_v=pltpu.VMEM((8, D), F32),
        late_v=pltpu.VMEM((8, W), F32),
        eb_v=pltpu.VMEM((F,), F32),
    )
    for name in ("fg_v", "fs_v", "sb_v", "ag_v", "as_v", "ob_v"):
        scratch[name] = pltpu.VMEM((D,), F32)
    for name in ("qb_v", "vb_v"):
        scratch[name] = pltpu.VMEM((W,), F32)
    for low, wide, shape in (
        ("us_v", "usf", (2, F // 2, D)),
        ("ue_v", "uef", (2, W, F)),
        ("ab_v", "abf", (3, D, W)),
        ("o_v", "of", (2, W, W)),
        ("ig_v", "igf", (T, D)),
    ):
        scratch[low], scratch[wide] = pltpu.VMEM(shape, BF16), pltpu.VMEM(shape, F32)
    names = list(ins) + list(outs) + list(scratch)
    return pl.pallas_call(
        functools.partial(finish_kernel, sh, names),
        out_shape=[jax.ShapeDtypeStruct(o[0], o[1]) for o in outs.values()],
        in_specs=list(ins.values()),
        out_specs=[o[2] for o in outs.values()],
        scratch_shapes=list(scratch.values()),
        compiler_params=pltpu.CompilerParams(vmem_limit_bytes=63 * 1024 * 1024),
        name="finish",
    )(*parts)


def fused_body(
    mesh_sizes, inputs, segments, query_proj, key_proj, value_proj, query_bias, value_bias, output_proj,
    output_bias, attn_gain, attn_shift, expand_proj, expand_bias, shrink_proj, shrink_bias,
    final_gain, final_shift, cotangent,
):
    sh = Shapes(mesh_sizes, inputs.shape[0], inputs.shape[1], query_proj.shape[1], expand_proj.shape[1])
    parts = layer_call(
        sh,
        (
            segments, query_bias, value_bias, output_bias, attn_gain, attn_shift, expand_bias, shrink_bias,
            final_gain, final_shift, inputs, query_proj, key_proj, value_proj, output_proj, expand_proj,
            shrink_proj, cotangent,
        ),
    )
    return finish_call(sh, parts)


contract_rows = (((0,), (0,)), ((), ()))
contract_cols = (((1,), (1,)), ((), ()))


def matmul(left, right):
    return jnp.dot(left, right, preferred_element_type=jnp.float32)


def inner_rows(left, right):
    return lax.dot_general(left, right, contract_rows, preferred_element_type=jnp.float32)


def inner_cols(left, right):
    return lax.dot_general(left, right, contract_cols, preferred_element_type=jnp.float32)


def norm_forward(values, gain, shift):
    centred = values - jnp.mean(values, axis=-1, keepdims=True)
    spread = jnp.mean(centred * centred, axis=-1, keepdims=True)
    recip = lax.rsqrt(spread + norm_eps)
    normed = centred * recip
    return (normed * gain + shift, normed, recip)


def norm_backward(upstream, normed, recip, gain):
    scaled = upstream * gain
    centred = (
        scaled
        - jnp.mean(scaled, axis=-1, keepdims=True)
        - normed * jnp.mean(scaled * normed, axis=-1, keepdims=True)
    )
    return (centred * recip, jnp.sum(upstream * normed, axis=0), jnp.sum(upstream, axis=0))


def cross_scores(left, right):
    return inner_cols(left, right)


def spread_apply(weights_in, right):
    return matmul(weights_in, right)


def spread_transpose(weights_in, left):
    return inner_rows(weights_in, left)


def body(
    inputs,
    segments,
    query_proj,
    key_proj,
    value_proj,
    query_bias,
    value_bias,
    output_proj,
    output_bias,
    attn_gain,
    attn_shift,
    expand_proj,
    expand_bias,
    shrink_proj,
    shrink_bias,
    final_gain,
    final_shift,
    cotangent,
):
    head_count = query_proj.shape[1] // HEAD_DIM
    scale = HEAD_DIM ** (-0.5)
    seg_local = segments[0]
    queries = (matmul(inputs, query_proj) + query_bias.astype(jnp.float32)).astype(jnp.bfloat16)
    keys = matmul(inputs, key_proj).astype(jnp.bfloat16)
    values = (matmul(inputs, value_proj) + value_bias.astype(jnp.float32)).astype(jnp.bfloat16)
    all_keys, all_values, key_ids = (
        lax.all_gather(keys, "ctx", axis=0, tiled=True),
        lax.all_gather(values, "ctx", axis=0, tiled=True),
        lax.all_gather(seg_local.astype(jnp.bfloat16), "ctx", axis=0, tiled=True),
    )
    query_segs = seg_local.astype(jnp.float32)
    key_segs = key_ids.astype(jnp.float32)
    same_seg = query_segs[:, None] == key_segs[None, :]

    def split_heads(matrix):
        return jnp.swapaxes(matrix.reshape(matrix.shape[0], head_count, HEAD_DIM), 0, 1)

    def join_heads(stack):
        return jnp.swapaxes(stack, 0, 1).reshape(stack.shape[1], head_count * HEAD_DIM)

    query_heads = split_heads(queries)
    key_heads = split_heads(all_keys)
    value_heads = split_heads(all_values)

    def head_forward(state, triple):
        query_head, key_head, value_head = triple
        scores = cross_scores(query_head, key_head) * scale
        scores = jnp.where(same_seg, scores, masked)
        row_max = jnp.max(scores, axis=1, keepdims=True)
        exp_scores = jnp.where(same_seg, jnp.exp(scores - row_max), 0.0)
        row_sum = jnp.sum(exp_scores, axis=1, keepdims=True)
        attn_probs = (exp_scores / row_sum).astype(jnp.bfloat16)
        mixed = spread_apply(attn_probs, value_head)
        return (state, (mixed, row_max + jnp.log(row_sum)))

    mixed_heads, log_sums = lax.scan(head_forward, None, (query_heads, key_heads, value_heads))[1]
    attended = join_heads(mixed_heads).astype(jnp.bfloat16)
    attn_total = lax.psum(matmul(attended, output_proj).astype(jnp.bfloat16), "tensor").astype(
        jnp.float32
    )
    attn_gain_f = attn_gain.astype(jnp.float32)
    first, first_normed, first_recip = norm_forward(
        inputs.astype(jnp.float32) + attn_total + output_bias.astype(jnp.float32),
        attn_gain_f,
        attn_shift.astype(jnp.float32),
    )
    first_low = first.astype(jnp.bfloat16)
    pre_act = matmul(first_low, expand_proj) + expand_bias.astype(jnp.float32)
    activated, gelu_back = jax.vjp(lambda pre_in: jax.nn.gelu(pre_in, approximate=False), pre_act)
    hidden = activated.astype(jnp.bfloat16)
    feed_total = lax.psum(matmul(hidden, shrink_proj).astype(jnp.bfloat16), "tensor").astype(
        jnp.float32
    )
    second = first + feed_total + shrink_bias.astype(jnp.float32)
    final_gain_f = final_gain.astype(jnp.float32)
    output, second_normed, second_recip = norm_forward(
        second, final_gain_f, final_shift.astype(jnp.float32)
    )
    upstream = cotangent.astype(jnp.float32)
    grad_second, fgain_grad, fshift_grad = norm_backward(
        upstream, second_normed, second_recip, final_gain_f
    )
    sbias_grad = jnp.sum(grad_second, axis=0)
    grad_second_low = grad_second.astype(jnp.bfloat16)
    shrink_grad = inner_rows(hidden, grad_second_low)
    grad_act = inner_cols(grad_second_low, shrink_proj)
    grad_pre = gelu_back(grad_act)[0].astype(jnp.bfloat16)
    ebias_grad = jnp.sum(grad_pre.astype(jnp.float32), axis=0)
    expand_grad = inner_rows(first_low, grad_pre)
    grad_first = grad_second + lax.psum(
        inner_cols(grad_pre, expand_proj).astype(jnp.bfloat16), "tensor"
    ).astype(jnp.float32)
    grad_mix, again_grad, ashift_grad = norm_backward(
        grad_first, first_normed, first_recip, attn_gain_f
    )
    obias_grad = jnp.sum(grad_mix, axis=0)
    grad_mix_low = grad_mix.astype(jnp.bfloat16)
    oproj_grad = inner_rows(attended, grad_mix_low)
    grad_attended = inner_cols(grad_mix_low, output_proj).astype(jnp.bfloat16)
    grad_heads = split_heads(grad_attended)

    def head_backward(state, group):
        query_head, key_head, value_head, grad_head, log_sum = group
        scores = cross_scores(query_head, key_head) * scale
        attn_probs = jnp.where(same_seg, jnp.exp(scores - log_sum), 0.0)
        grad_probs = cross_scores(grad_head, value_head)
        row_dot = jnp.sum(attn_probs * grad_probs, axis=1, keepdims=True)
        grad_scores = (attn_probs * (grad_probs - row_dot)).astype(jnp.bfloat16)
        grad_query = spread_apply(grad_scores, key_head) * scale
        grad_key = spread_transpose(grad_scores, query_head) * scale
        grad_value = spread_transpose(attn_probs.astype(jnp.bfloat16), grad_head)
        return (state, (grad_query, grad_key, grad_value))

    query_back, key_back, value_back = lax.scan(
        head_backward, None, (query_heads, key_heads, value_heads, grad_heads, log_sums)
    )[1]
    grad_queries = join_heads(query_back).astype(jnp.bfloat16)
    key_sum, value_sum = (
        lax.psum_scatter(
            join_heads(key_back).astype(jnp.bfloat16), "ctx", scatter_dimension=0, tiled=True
        ).astype(jnp.float32),
        lax.psum_scatter(
            join_heads(value_back).astype(jnp.bfloat16), "ctx", scatter_dimension=0, tiled=True
        ).astype(jnp.float32),
    )
    grad_keys = key_sum.astype(jnp.bfloat16)
    grad_values = value_sum.astype(jnp.bfloat16)
    qbias_grad = jnp.sum(grad_queries.astype(jnp.float32), axis=0)
    vbias_grad = jnp.sum(grad_values.astype(jnp.float32), axis=0)
    query_grad = inner_rows(inputs, grad_queries)
    key_grad = inner_rows(inputs, grad_keys)
    value_grad = inner_rows(inputs, grad_values)
    back_terms = (
        inner_cols(grad_queries, query_proj)
        + inner_cols(grad_keys, key_proj)
        + inner_cols(grad_values, value_proj)
    )
    input_grad = grad_mix + lax.psum(back_terms.astype(jnp.bfloat16), "tensor").astype(jnp.float32)
    (
        query_grad,
        key_grad,
        value_grad,
        qbias_grad,
        vbias_grad,
        oproj_grad,
        obias_grad,
        again_grad,
        ashift_grad,
        expand_grad,
        ebias_grad,
        shrink_grad,
        sbias_grad,
        fgain_grad,
        fshift_grad,
    ) = lax.psum(
        (
            query_grad,
            key_grad,
            value_grad,
            qbias_grad,
            vbias_grad,
            oproj_grad,
            obias_grad,
            again_grad,
            ashift_grad,
            expand_grad,
            ebias_grad,
            shrink_grad,
            sbias_grad,
            fgain_grad,
            fshift_grad,
        ),
        ("dp", "ctx"),
    )
    return (
        output.astype(jnp.bfloat16),
        input_grad,
        query_grad,
        key_grad,
        value_grad,
        qbias_grad,
        vbias_grad,
        oproj_grad,
        obias_grad,
        again_grad,
        ashift_grad,
        expand_grad,
        ebias_grad,
        shrink_grad,
        sbias_grad,
        fgain_grad,
        fshift_grad,
    )


def solution(mesh):
    in_specs = (
        P(("dp", "ctx"), None),
        P("dp", "ctx"),
        P(None, "tensor"),
        P(None, "tensor"),
        P(None, "tensor"),
        P("tensor"),
        P("tensor"),
        P("tensor", None),
        P(),
        P(),
        P(),
        P(None, "tensor"),
        P("tensor"),
        P("tensor", None),
        P(),
        P(),
        P(),
        P(("dp", "ctx"), None),
    )
    out_specs = (
        P(("dp", "ctx"), None),
        P(("dp", "ctx"), None),
        P(None, "tensor"),
        P(None, "tensor"),
        P(None, "tensor"),
        P("tensor"),
        P("tensor"),
        P("tensor", None),
        P(),
        P(),
        P(),
        P(None, "tensor"),
        P("tensor"),
        P("tensor", None),
        P(),
        P(),
        P(),
    )
    sizes = dict(mesh.shape)
    fits = sizes == {"dp": 4, "ctx": 4, "tensor": 2}
    chosen = functools.partial(fused_body, sizes) if fits else body
    return jax.shard_map(chosen, mesh=mesh, in_specs=in_specs, out_specs=out_specs, check_vma=False)
```

```python
import functools
import types

import jax
import jax.numpy as jnp
from jax import lax
from jax.experimental import pallas as pl
from jax.experimental.pallas import tpu as pltpu
from jax.sharding import PartitionSpec as P

HEAD_DIM = 64
norm_eps = 1e-12
masked = -1e30
MESH = pl.DeviceIdType.MESH
CORE, XS, YS, Z1, Z2, LINE = range(6)
BF16, F32 = jnp.bfloat16, jnp.float32
INV_SQRT2 = 0.7071067811865476
INV_SQRT_2PI = 0.3989422804014327


def nn(left, right):
    return jnp.dot(left, right, preferred_element_type=F32)


def nt(left, right):
    return lax.dot_general(left, right, (((1,), (1,)), ((), ())), preferred_element_type=F32)


def tn(left, right):
    return lax.dot_general(left, right, (((0,), (0,)), ((), ())), preferred_element_type=F32)


def normalise(values):
    centred = values - jnp.mean(values, axis=-1, keepdims=True)
    spread = jnp.mean(centred * centred, axis=-1, keepdims=True)
    recip = lax.rsqrt(spread + norm_eps)
    return centred * recip, recip


def denormalise(scaled, normed, recip):
    return recip * (
        scaled
        - jnp.mean(scaled, axis=-1, keepdims=True)
        - normed * jnp.mean(scaled * normed, axis=-1, keepdims=True)
    )


def gelu_parts(pre):
    phi_sum = 0.5 + 0.5 * lax.erf(pre * INV_SQRT2)
    slope = phi_sum + pre * (INV_SQRT_2PI * jnp.exp(-0.5 * pre * pre))
    return pre * phi_sum, slope


def column_sum(values):
    return jnp.sum(values, axis=0, keepdims=True)


class Shapes:
    def __init__(self, mesh, tokens, width, heads_width, units):
        self.nd, self.nc = mesh["dp"], mesh["ctx"]
        self.nx = self.nd // 2
        self.tokens, self.mine = tokens, tokens // 2
        self.width, self.hw, self.units = width, heads_width, units
        self.pairs = heads_width // 128


def make_kernel(sh, names):
    T, TM, D, W, F = sh.tokens, sh.mine, sh.width, sh.hw, sh.units
    HP = sh.pairs
    TILE = 512
    NTILE = F // TILE
    SLOTS = 4
    PARTS = 4
    PR = TM // PARTS

    def kernel(*refs):
        r = types.SimpleNamespace(**dict(zip(names, refs)))
        send_ref, recv_ref, local_ref = r.send, r.recv, r.local
        d, c, t = lax.axis_index("dp"), lax.axis_index("ctx"), lax.axis_index("tensor")
        core, xpos = lax.rem(d, 2), d // 2
        low_bit, high_bit = lax.rem(c, 2), c // 2
        next_c = c + 1 - 2 * low_bit
        z1_peer, z2_peer = (d, next_c, t), (d, c + 2 - 4 * high_bit, t)
        z3_peer = (d, next_c + 2 - 4 * high_bit, t)
        y_peer = (d, c, 1 - t)
        core_peer = (d + 1 - 2 * core, c, t)
        x_peer = (d + 2 - 4 * xpos, c, t)
        peer_of = {CORE: core_peer, XS: x_peer, YS: y_peer, Z1: z1_peer, Z2: z2_peer}
        bit_of = {CORE: core, XS: xpos, YS: t, Z1: low_bit, Z2: high_bit}
        my_rows = pl.ds(pl.multiple_of(t * TM, TM), TM)
        peer_rows = pl.ds(pl.multiple_of((1 - t) * TM, TM), TM)
        counts = [0, 0]

        def take(kind, k=1):
            at = counts[kind]
            counts[kind] += k
            assert counts[kind] <= (send_ref, local_ref)[kind].shape[0], counts
            return at

        def remote(src, dst, device, at=None, recv_at=None):
            at = take(0) if at is None else at
            recv_at = at if recv_at is None else recv_at
            return pltpu.make_async_remote_copy(
                src_ref=src, dst_ref=dst, send_sem=send_ref.at[at], recv_sem=recv_ref.at[recv_at],
                device_id=device, device_id_type=MESH,
            )

        def local(src, dst):
            return pltpu.make_async_copy(src, dst, local_ref.at[take(1)])

        unsent = []

        def go(copy, where=None):
            if where is None:
                copy.start()
            else:
                pl.when(where)(lambda: copy.start())
            unsent.append((copy, where))

        def wait_sends(*but):
            kept = [entry for entry in unsent if any(entry[0] is other for other in but)]
            for copy, where in unsent:
                if any(copy is other for other in but):
                    continue
                if where is None:
                    copy.wait_send()
                else:
                    pl.when(where)(lambda copy=copy: copy.wait_send())
            unsent[:] = kept

        loads = types.SimpleNamespace(
            x=local(r.x_in, r.xall.at[0]),
            wk=local(r.wk_in, r.wqkv.at[:, pl.ds(W, W)]),
            wv=local(r.wv_in, r.wqkv.at[:, pl.ds(2 * W, W)]),
            wq=local(r.wq_in, r.wqkv.at[:, pl.ds(0, W)]),
            wo=local(r.wo_in, r.wo.at[pl.ds(0, W)]),
            we=local(r.we_in, r.we.at[0]),
            ws=local(r.ws_in, r.ws.at[0]),
            cot=local(r.cot_in.at[my_rows], r.cot),
        )
        for copy in vars(loads).values():
            copy.start()

        def row(ref):
            return ref[...].astype(F32).reshape(1, ref.shape[0])

        vec = [row(ref) for ref in (r.ob_in, r.ag_in, r.as_in, r.sb_in, r.fg_in, r.fs_in)]
        r.eb[0] = row(r.eb_in)
        r.segs[0] = r.seg_in[...].astype(F32)
        barrier = pltpu.get_barrier_semaphore()
        greeted = [y_peer, core_peer, x_peer, z1_peer, z2_peer, z3_peer]
        for device in greeted:
            pl.semaphore_signal(barrier, inc=1, device_id=device, device_id_type=MESH)
        pl.semaphore_wait(barrier, len(greeted))

        seg_copies = [None] + [
            remote(r.segs.at[0], r.segs.at[k], peer) for k, peer in ((1, z1_peer), (2, z2_peer), (3, z3_peer))
        ]
        eb_copy = remote(r.eb.at[0], r.eb.at[1], y_peer)
        x_rows = [pl.ds(pl.multiple_of(t * TM + k * PR, PR), PR) for k in range(PARTS)]
        mid = lax.rem(low_bit + high_bit, 2)
        is_mid, is_end = mid == 1, mid == 0
        slots = (0, 1, 2 + mid, 3 - mid)
        x_at = take(0, 3 * PARTS)

        def x_recv(slot, k):
            return x_at + (slot - 1) * PARTS + k

        def x_move(src_slot, dst_slot, peer, k):
            src = r.x_in.at[x_rows[k]] if src_slot == 0 else r.xall.at[src_slot, x_rows[k]]
            return remote(src, r.xall.at[dst_slot, x_rows[k]], peer, None, x_recv(dst_slot, k))

        x_near = [x_move(0, 1, z1_peer, k) for k in range(PARTS)]
        x_far = [x_move(0, 3, z3_peer, k) for k in range(PARTS)]
        x_next = (
            None,
            [x_move(1, 2, z3_peer, k) for k in range(PARTS)],
            [x_move(3, 2, z1_peer, k) for k in range(PARTS)],
            [x_move(2, 3, z1_peer, k) for k in range(PARTS)],
        )
        x_y = [None] + [
            [remote(r.xall.at[slots[o], x_rows[k]], r.xall.at[slots[o], x_rows[k]], y_peer) for k in range(PARTS)]
            for o in (1, 2, 3)
        ]
        for k in range(PARTS):
            go(x_near[k])
            go(x_far[k], is_mid)
        for copy in seg_copies[1:]:
            go(copy)
        go(eb_copy)

        def arrive(o, k):
            here = r.xall.at[slots[o], x_rows[k]]
            remote(here, here, z1_peer, x_at, x_recv(slots[o], k)).wait_recv()
            go(x_next[o][k], is_mid)
            go(x_y[o][k])

        def block_here(o):
            if o == 1:
                for copy in seg_copies[1:]:
                    copy.wait_recv()
            for k in range(PARTS):
                x_y[o][k].wait_recv()

        chunks = [
            (r.wo_in, r.wo.at[pl.ds(W, W)], W, 0, 1),
            (r.we_in, r.we.at[1], D, 0, 2),
            (r.we_in, r.we.at[1], D, 1, 2),
            (r.ws_in, r.ws.at[1], F, 0, 2),
            (r.ws_in, r.ws.at[1], F, 1, 2),
        ]
        pieces = sh.nd * 2

        def window(chunk, owner):
            rows, part, parts = chunk[2:]
            size = rows // pieces // parts
            return pl.ds(pl.multiple_of(owner * (rows // pieces) + part * size, size), size)

        own_piece, pair_piece = d * 2 + low_bit, d * 2 + 1 - low_bit
        x_d = d + 2 - 4 * xpos
        x_pieces = (x_d * 2 + low_bit, x_d * 2 + 1 - low_bit)
        w_y, w_z, w_x, w_core = [], [], [], []
        for chunk in chunks:
            source, held = chunk[0], chunk[1]

            def move(owner, peer):
                where = window(chunk, owner)
                return remote(held.at[where], held.at[where], peer)

            own = window(chunk, own_piece)
            w_y.append(remote(source.at[own], held.at[own], y_peer))
            w_z.append(move(own_piece, z1_peer))
            w_x.append([move(piece, x_peer) for piece in (own_piece, pair_piece)])
            w_core.append([move(piece, core_peer) for piece in (own_piece, pair_piece) + x_pieces])

        def hop1(i):
            w_y[i].wait_recv()
            go(w_z[i])
            go(w_x[i][0])
            go(w_core[i][0])

        def hop2(i):
            w_z[i].wait_recv()
            go(w_x[i][1])
            go(w_core[i][1])

        def hop3(i):
            for k in range(2):
                w_x[i][k].wait_recv()
                go(w_core[i][2 + k])

        def weights_done(i):
            for copy in w_core[i]:
                copy.wait_recv()


        kv, m_s, l_s, acc = r.kv, r.m_s, r.l_s, r.acc
        value_bias = row(r.vb_in)
        scale = HEAD_DIM ** (-0.5)
        lane = lax.broadcasted_iota(jnp.int32, (T, 128), 1)

        def split_pair(target, p, pair):
            target[2 * p] = jnp.where(lane < 64, pair, 0.0).astype(BF16)
            target[2 * p + 1] = jnp.where(lane < 64, 0.0, pair).astype(BF16)

        def set_keys_values(slot):
            both = nn(r.xall[slot], r.wqkv[:, W:])
            for p in range(HP):
                kv[slot, p, 0] = both[:, p * 128 : (p + 1) * 128].astype(BF16)
                cols = slice(W + p * 128, W + (p + 1) * 128)
                kv[slot, p, 1] = (both[:, cols] + value_bias[:, p * 128 : (p + 1) * 128]).astype(BF16)

        def set_bias(slot):
            seg_keys = jnp.broadcast_to(r.segs[slot], (128, T)).T
            for j in range(T // 128):
                cols = slice(j * 128, (j + 1) * 128)
                r.bias[:, cols] = jnp.where(seg_keys == r.segs[0, :, cols], 0.0, masked)

        def project():
            loads.x.wait()
            loads.wk.wait()
            loads.wv.wait()
            set_keys_values(0)
            loads.wq.wait()
            queries = (nn(r.xall[0], r.wqkv[:, :W]) + row(r.qb_in)).astype(BF16).astype(F32) * scale
            for p in range(HP):
                split_pair(r.qm, p, queries[:, p * 128 : (p + 1) * 128])
            m_s[...] = jnp.full_like(m_s, masked)
            l_s[...] = jnp.zeros_like(l_s)
            acc[...] = jnp.zeros_like(acc)
            set_bias(0)


        def attend(slot, p):
            pair_keys = kv[slot, p, 0]
            pair_values = kv[slot, p, 1].T
            for hh in range(2):
                h = 2 * p + hh
                s = nt(pair_keys, r.qm[h]) + r.bias[...]
                old = m_s[h]
                new = jnp.maximum(old, jnp.max(s, axis=0, keepdims=True))
                e = jnp.exp(s - new)
                alpha = jnp.exp(old - new)
                l_s[h] = l_s[h] * alpha + jnp.sum(e, axis=0, keepdims=True)
                m_s[h] = new
                acc[h] = acc[h] * alpha + nn(pair_values[hh * 64 : hh * 64 + 64], e.astype(BF16))

        def run(body, services=None):
            def step(p, carry):
                body(p)
                for at, fn in (services or {}).items():
                    pl.when(p == at)(fn)
                return carry

            lax.fori_loop(0, HP, step, 0)

        def together(*fns):
            def all_of():
                for fn, arg in fns:
                    fn(*arg)

            return all_of

        def flip_inputs(slot):
            at = slot * T if isinstance(slot, int) else pl.multiple_of(slot * T, T)
            r.xt[:, pl.ds(at, T)] = r.xall[slot].T

        def next_block(o):
            block_here(o)
            set_keys_values(slots[o])
            set_bias(slots[o])

        att_at = take(0, HP)

        def att_copy(p):
            cols = pl.ds(p * 128, 128)
            return remote(r.att.at[peer_rows, cols], r.att_o.at[:, cols], y_peer, att_at + p)

        def attend_last(p):
            attend(slots[3], p)
            for h in (2 * p, 2 * p + 1):
                acc[h] = acc[h] / l_s[h]
                m_s[h] = m_s[h] + jnp.log(l_s[h])
            pair = acc[2 * p : 2 * p + 2].reshape(128, T).T
            r.att[:, p * 128 : (p + 1) * 128] = pair.astype(BF16)
            att_copy(p).start()

        fl_copy = remote(r.fl.at[my_rows], r.fl.at[my_rows], y_peer)

        def out_project():
            loads.wo.wait()
            r.sec[...] = nn(r.att[my_rows, :], r.wo[0:W, :])

        def first_norm():
            for p in range(HP):
                att_copy(p).wait_recv()
            mix = r.sec[...] + nn(r.att_o[...], r.wo[W : 2 * W, :])
            normed, recip = normalise(r.xall[0, my_rows, :].astype(F32) + mix + vec[0])
            r.n1[...] = normed
            r.r1[...] = jnp.broadcast_to(recip, (TM, 128))
            first = normed * vec[1] + vec[2]
            r.sec[...] = first + vec[3]
            r.fl[my_rows, :] = first.astype(BF16)
            go(fl_copy)

        def tile_cols(j):
            return pl.ds(pl.multiple_of(j * TILE, TILE), TILE)

        def forward_tile(side, j):
            cols = tile_cols(j)
            pre = nn(r.fl[my_rows, :], r.we[side, :, cols]) + r.eb[side, :, cols]
            hidden, slope = gelu_parts(pre)
            hidden = hidden.astype(BF16)
            r.gp[side, :, cols] = slope
            if side == 0:
                r.hid[my_rows, cols] = hidden
            r.sec[...] += nn(hidden, r.ws[side, cols, :])

        def tiles(fn):
            def step(j, carry):
                fn(j)
                return carry

            lax.fori_loop(0, NTILE, step, 0)

        def own_units():
            loads.we.wait()
            loads.ws.wait()
            tiles(lambda j: forward_tile(0, j))

        def other_units():
            eb_copy.wait_recv()
            tiles(lambda j: forward_tile(1, j))

        go(w_y[0])
        go(w_y[1])
        arrive(1, 0)
        hop1(0)
        project()

        def with_00():
            go(w_y[2])


        def with_01():
            hop1(1)

        run(lambda p: attend(slots[0], p), {0: with_00, 1: with_01})
        arrive(1, 1)
        arrive(1, 2)
        arrive(1, 3)
        hop2(0)
        go(w_y[3])
        arrive(2, 0)
        arrive(2, 1)
        arrive(2, 2)
        arrive(2, 3)
        next_block(1)
        hop1(2)

        def with_10():
            arrive(3, 0)


        def with_11():
            hop2(1)
            arrive(3, 1)

        run(lambda p: attend(slots[1], p), {0: with_10, 1: with_11})
        flip_inputs(slots[1])
        arrive(3, 2)
        hop2(2)
        hop3(0)
        next_block(2)
        arrive(3, 3)
        go(w_y[4])
        hop1(3)
        run(lambda p: attend(slots[2], p))
        next_block(3)
        hop2(3)
        attend_last(0)
        hop1(4)
        attend_last(1)
        hop3(1)
        attend_last(2)
        hop3(2)
        hop2(4)
        hop3(3)
        weights_done(0)
        out_project()
        first_norm()
        weights_done(1)
        flip_inputs(slots[0])
        weights_done(2)
        hop3(4)
        weights_done(3)
        own_units()
        weights_done(4)
        other_units()
        flip_inputs(slots[2])
        flip_inputs(slots[3])
        loads.cot.wait()
        normed2, recip2 = normalise(r.sec[...])
        upstream = r.cot[...].astype(F32)
        grad_second = denormalise(upstream * vec[4], normed2, recip2)
        r.gf[...] = grad_second
        r.gs[my_rows, :] = grad_second.astype(BF16)
        gs_copy = remote(r.gs.at[my_rows], r.gs.at[my_rows], y_peer)
        go(gs_copy)
        small = r.small
        small[0:1, :] = column_sum(upstream * normed2)
        small[1:2, :] = column_sum(upstream)
        small[2:3, :] = column_sum(grad_second)
        r.oy[...] = (normed2 * vec[4] + vec[5]).astype(BF16)
        oy_local = local(r.oy, r.out.at[my_rows])
        oy_local.start()


        def backward_tile(side, j):
            cols = tile_cols(j)
            low = (nt(r.gs[my_rows, :], r.ws[side, cols, :]) * r.gp[side, :, cols]).astype(BF16)
            if side == 0:
                r.gpre[my_rows, cols] = low
            r.gf[...] += nt(low, r.we[side, :, cols])

        tiles(lambda j: backward_tile(0, j))
        tiles(lambda j: backward_tile(1, j))
        grad_first = r.gf[...]
        normed = r.n1[...]
        grad_mix = denormalise(grad_first * vec[1], normed, r.r1[:, 0:1])
        r.gmix[...] = grad_mix
        r.gm[my_rows, :] = grad_mix.astype(BF16)
        gm_copy = remote(r.gm.at[my_rows], r.gm.at[my_rows], y_peer)
        go(gm_copy)
        small[3:4, :] = column_sum(grad_first * normed)
        small[4:5, :] = column_sum(grad_first)
        small[5:6, :] = column_sum(grad_mix)

        def rows_at(ref, first_row, rows):
            return ref.at[pl.ds(pl.multiple_of(first_row, rows), rows)]

        class Unit:
            def __init__(self, grad, whole, out, order, bufs):
                self.grad, self.order, self.bufs = grad, order, bufs
                self.first, self.rows, self.line = [0], [grad.shape[0]], None
                for stage in order:
                    self.rows.append(self.rows[-1] // (4 if stage == LINE else 2))
                    at = c if stage == LINE else bit_of[stage]
                    self.first.append(self.first[-1] + at * self.rows[-1])
                self.down, self.up = [], []
                for k, stage in enumerate(order):
                    rows, last = self.rows[k + 1], k == len(order) - 1
                    target = rows_at(whole, self.first[k + 1], rows)
                    source = target
                    if last:
                        source = rows_at(grad, self.first[k + 1], rows)
                        self.kept = local(source, target)
                    if stage == LINE:
                        self.line = k
                        self.far = self.first[k] + 2 * (1 - high_bit) * rows
                        self.edge = self.first[k] + 3 * high_bit * rows
                        near = self.first[k] + 2 * high_bit * rows
                        ends = grad.at[pl.ds(pl.multiple_of(self.first[k] + (1 - high_bit) * rows, rows), 3 * rows)]
                        self.down.append(
                            (
                                remote(ends, bufs[k][0], z1_peer),
                                remote(rows_at(grad, self.far, 2 * rows), bufs[k][1], z3_peer),
                                remote(rows_at(grad, self.edge, rows), bufs[k][2], z1_peer),
                            )
                        )
                        near, far = rows_at(whole, near, 2 * rows), rows_at(whole, self.far, 2 * rows)
                        self.up.append(
                            (remote(source, target, z1_peer), remote(near, near, z3_peer), remote(far, far, z1_peer))
                        )
                        continue
                    theirs = rows_at(grad, self.first[k] + (1 - bit_of[stage]) * rows, rows)
                    self.down.append(remote(theirs, bufs[k], peer_of[stage]))
                    self.up.append(remote(source, target, peer_of[stage]))
                self.stored = local(whole, out)

            def add_rows(self, first_row, rows, terms, step):

                def tile(i, carry):
                    window = self.grad.at[pl.ds(pl.multiple_of(first_row + i * step, step), step)]
                    total = window[...].astype(F32)
                    for buf, at in terms:
                        total = total + buf[pl.ds(pl.multiple_of(at + i * step, step), step), :].astype(F32)
                    window[...] = total.astype(BF16)
                    return carry

                lax.fori_loop(0, rows // step, tile, 0)

            def send(self, k):
                go(self.down[k])

            def add(self, k):
                self.down[k].wait_recv()
                self.add_rows(self.first[k + 1], self.rows[k + 1], [(self.bufs[k], 0)], min(96, self.rows[k + 1]))

            def forward(self, k):
                self.add(k)
                self.send(k + 1)

            def spread(self, k):
                go(self.up[k])
                if k == len(self.order) - 1:
                    self.kept.start()

            def back(self, k):
                if k == len(self.order) - 1:
                    self.kept.wait()
                self.up[k].wait_recv()
                if self.line is not None and k - 1 == self.line:
                    go(self.up[k - 1][0])
                else:
                    self.spread(k - 1)

            def za(self):
                go(self.down[self.line][0], is_end)

            def zb(self):
                k = self.line
                rows = self.rows[k + 1]

                @pl.when(is_mid)
                def _():
                    self.down[k][0].wait_recv()
                    self.add_rows(self.far, 2 * rows, [(self.bufs[k][0], (1 - high_bit) * rows)], rows)

                go(self.down[k][1], is_mid)

            def zc(self):
                k = self.line
                rows, (first_buf, second_buf, _) = self.rows[k + 1], self.bufs[k]

                @pl.when(is_mid)
                def _():
                    self.down[k][1].wait_recv()
                    self.add_rows(self.edge, rows, [(second_buf, high_bit * rows)], rows)

                go(self.down[k][2], is_mid)

                @pl.when(is_mid)
                def _():
                    terms = [(first_buf, 2 * high_bit * rows), (second_buf, (1 - high_bit) * rows)]
                    self.add_rows(self.first[k + 1], rows, terms, rows)
                    if k == len(self.order) - 1:
                        self.kept.start()
                        self.up[k][0].start()

            def zd(self):
                k = self.line

                @pl.when(is_end)
                def _():
                    self.down[k][2].wait_recv()
                    self.add_rows(self.first[k + 1], self.rows[k + 1], [(self.bufs[k][2], 0)], self.rows[k + 1])
                    if k == len(self.order) - 1:
                        self.kept.start()
                        self.up[k][0].start()

                if k == len(self.order) - 1:
                    unsent.append((self.up[k][0], None))

            def ze(self):
                k = self.line

                @pl.when(is_mid)
                def _():
                    if k == len(self.order) - 1:
                        self.kept.wait()
                    self.up[k][0].wait_recv()

                go(self.up[k][1], is_mid)

            def zf(self):
                pl.when(is_mid)(lambda: self.up[self.line][1].wait_recv())
                go(self.up[self.line][2], is_mid)

            def zg(self):
                k = self.line

                @pl.when(is_end)
                def _():
                    if k == len(self.order) - 1:
                        self.kept.wait()
                    self.up[k][0].wait_recv()
                    self.up[k][2].wait_recv()

                self.spread(k - 1)

            def turn(self):
                k = len(self.order) - 1
                self.add(k)
                self.spread(k)

            def store(self):
                self.up[0].wait_recv()
                self.stored.start()

        def all_sum(buf, slots, stages):
            copies = [remote(buf.at[k % 2], slots.at[k], peer_of[stage]) for k, stage in enumerate(stages)]

            def start(k):
                copies[k].start()

            def finish(k):
                copies[k].wait()
                total = buf[k % 2] + slots[k]
                if stages[k] == YS:
                    which = lax.broadcasted_iota(jnp.int32, total.shape, 0)
                    total = jnp.where(which < 6, total, buf[k % 2])
                buf[(k + 1) % 2] = total
                if k + 1 < len(stages):
                    start(k + 1)

            return start, finish


        def other_hidden(j):
            cols = tile_cols(j)
            pre = nn(r.fl[peer_rows, :], r.we[0, :, cols]) + r.eb[0, :, cols]
            hidden, slope = gelu_parts(pre)
            r.hid[peer_rows, cols] = hidden.astype(BF16)
            r.gp[0, :, cols] = slope

        def other_slopes():
            def tile(j):
                cols = tile_cols(j)
                low = nt(r.gs[peer_rows, :], r.ws[0, cols, :]) * r.gp[0, :, cols]
                r.gpre[peer_rows, cols] = low.astype(BF16)

            tiles(tile)

        fl_copy.wait_recv()
        tiles(other_hidden)
        r.flt[...] = r.fl[...].T
        wait_sends(gm_copy)
        gs_copy.wait_recv()
        by_line, by_pairs = (CORE, XS, LINE), (CORE, XS, Z1, Z2)
        half_d = D // 2

        def line_unit(grad, whole, out, first_buf, k):
            steps = (r.l0.at[k], r.l1.at[k], r.l2.at[k])
            return Unit(grad, whole, out, by_line, (first_buf, r.x0.at[k], steps))

        def pair_unit(grad, whole, out, k):
            return Unit(grad, whole, out, by_pairs, (r.p0.at[k], r.p1.at[k], r.p2.at[k], r.p3.at[k]))

        s1 = Unit(
            r.ws.at[1, pl.ds(0, D)], r.ws.at[0, pl.ds(0, D)], r.us_out.at[pl.ds(0, D)], (CORE, LINE, XS),
            (r.s0.at[pl.ds(0, half_d)], (r.z0, r.z1, r.z2), r.z3),
        )
        s2 = line_unit(
            r.ws.at[1, pl.ds(D, D)], r.ws.at[0, pl.ds(D, D)], r.us_out.at[pl.ds(D, D)], r.s0.at[pl.ds(half_d, half_d)], 1
        )
        e1, e2 = [
            line_unit(
                r.we.at[1, :, pl.ds(at, D)], r.we.at[0, :, pl.ds(at, D)], r.ue_out.at[:, pl.ds(at, D)], r.e0.at[k - 2], k
            )
            for k, at in ((2, 0), (3, D))
        ]
        ua = pair_unit(r.ua, r.s0, r.ua_out, 0)
        ub = pair_unit(r.ub, r.wo, r.ub_out, 1)

        def half_of(which):
            return which * core + (1 - which) * (1 - core)

        def shrink_tiles(which):
            def tile(i, carry):
                at = pl.multiple_of(i * D + half_of(which) * half_d, 128)
                r.ws[1, pl.ds(at, half_d), :] = tn(r.hid[:, pl.ds(at, half_d)], r.gs[...]).astype(BF16)
                return carry

            lax.fori_loop(0, F // D, tile, 0)

        def half_rows(which):
            return pl.ds(pl.multiple_of(half_of(which) * (D // 2), D // 2), D // 2)

        def expand_tiles(which):
            rows = half_rows(which)

            def tile(j):
                cols = tile_cols(j)
                r.we[1, rows, cols] = nn(r.flt[rows, :], r.gpre[:, cols]).astype(BF16)

            tiles(tile)

        def sum_blocks():
            totals = column_sum(r.gpre[...].astype(F32))
            small[6:7, :] = totals[:, :D]
            small[7:8, :] = totals[:, D:]
            r.es[0] = small[...]

        early_start, early_finish = all_sum(r.es, r.es_r, (YS, CORE, XS, Z1, Z2))
        late_start, late_finish = all_sum(r.ls, r.ls_r, (CORE, XS, Z1, Z2))

        def grad_heads():
            gm_copy.wait_recv()
            grad_att = nt(r.gm[...], r.wo[0:W, :]).astype(BF16).astype(F32)
            flipped = grad_att.T.reshape(2 * HP, 64, T)
            r.delta[...] = jnp.sum(acc[...] * flipped, axis=1, keepdims=True)
            for p in range(HP):
                split_pair(r.dm, p, grad_att[:, p * 128 : (p + 1) * 128])
            acc[...] = jnp.zeros_like(acc)

        oy_send = remote(r.oy, r.out.at[my_rows], y_peer)
        dkv = r.dkv

        def pull(slot, p):
            pair_keys, pair_values = kv[slot, p, 0], kv[slot, p, 1]
            flipped_keys = pair_keys.T
            grad_k = jnp.zeros((T, 128), F32)
            grad_v = jnp.zeros((T, 128), F32)
            for hh in range(2):
                h = 2 * p + hh
                q, g = r.qm[h], r.dm[h]
                probs = jnp.exp(nt(pair_keys, q) + (r.bias[...] - m_s[h]))
                grad_p = nt(pair_values, g)
                grad_v = grad_v + nn(probs.astype(BF16), g)
                ds = (probs * (grad_p - r.delta[h])).astype(BF16)
                grad_k = grad_k + nn(ds, q)
                acc[h] += nn(flipped_keys[hh * 64 : hh * 64 + 64], ds)
            rows = slice(slot * T, (slot + 1) * T)
            dkv[rows, pl.ds(pl.multiple_of(p * 128, 128), 128)] = grad_k.astype(BF16)
            dkv[rows, pl.ds(pl.multiple_of(W + p * 128, 128), 128)] = grad_v.astype(BF16)

        HR = TM // 2

        def half(at, h):
            return pl.ds(at + h * HR, HR)

        dx_y = [
            [remote(r.xall.at[k, half(0, h)], r.dxy.at[k, half(0, h)], y_peer) for h in range(2)] for k in range(SLOTS)
        ]

        def dx_move(slot, target, peer):
            return [remote(r.xall.at[slot, half(TM, h)], r.dxz.at[target, half(0, h)], peer) for h in range(2)]

        dx_end = {3: dx_move(3, 0, z1_peer), 2: dx_move(2, 1, z1_peer), 1: dx_move(1, 2, z1_peer)}
        dx_mid = {3: dx_move(3, 3, z3_peer), 2: dx_move(2, 4, z3_peer), 1: dx_move(1, 5, z1_peer)}

        def dx_rows(slot, rows):
            here = pl.ds(pl.multiple_of(slot * T + rows.start, TM), TM)
            return nt(dkv[here, :], r.wqkv[:, W:])

        def dx_part(slot):
            r.xall[slot, 0:TM] = dx_rows(slot, peer_rows).astype(BF16)
            for h in range(2):
                go(dx_y[slot][h])
            r.xall[slot, TM:] = dx_rows(slot, my_rows).astype(BF16)

        def add_to(slot, h, buf, at):
            rows, kept = slice(h * HR, (h + 1) * HR), slice(TM + h * HR, TM + (h + 1) * HR)
            total = r.xall[slot, kept].astype(F32) + buf[at, rows].astype(F32)
            r.xall[slot, kept] = total.astype(BF16)

        def dx_sum(slot, h):
            dx_y[slot][h].wait_recv()
            add_to(slot, h, r.dxy, slot)
            go(dx_end[slot][h], is_end)

        def dx_pass(slot, h):
            came = {3: dx_end[2], 2: dx_end[3], 1: dx_mid[2]}[slot][h]
            at = {3: 1, 2: 0, 1: 4}[slot]

            @pl.when(is_mid)
            def _():
                came.wait_recv()
                add_to(slot, h, r.dxz, at)

            go(dx_mid[slot][h], is_mid)

        ig_rows = [pl.ds(pl.multiple_of(t * TM + h * HR, HR), HR) for h in range(2)]
        ig_local = [local(r.igm.at[half(0, h)], r.ig_out.at[ig_rows[h]]) for h in range(2)]
        ig_send = [remote(r.igm.at[half(0, h)], r.ig_out.at[ig_rows[h]], y_peer) for h in range(2)]

        def dx_out(h):
            rows = slice(h * HR, (h + 1) * HR)
            dx_y[0][h].wait_recv()
            r.gmix[rows] += r.dxy[0, rows].astype(F32)

            @pl.when(is_mid)
            def _():
                dx_end[1][h].wait_recv()
                dx_mid[3][h].wait_recv()
                r.gmix[rows] += r.dxz[2, rows].astype(F32) + r.dxz[3, rows].astype(F32)

            @pl.when(is_end)
            def _():
                dx_mid[1][h].wait_recv()
                r.gmix[rows] += r.dxz[5, rows].astype(F32)

            r.igm[rows] = r.gmix[rows].astype(BF16)
            ig_local[h].start()
            go(ig_send[h])


        def key_value_tiles(which):
            rows = half_rows(which)
            r.ub[rows, :] = nn(r.xt[rows, :], dkv[...]).astype(BF16)

        def query_output_tiles(which):
            rows = half_rows(which)
            r.ua[rows, 0:W] = nn(r.xt[rows, 0:T], r.dq[...]).astype(BF16)
            cols = pl.ds(pl.multiple_of(half_of(which) * W, 128), W)
            r.ua[rows, W:] = tn(r.att[...], r.gm[:, cols]).astype(BF16)

        def query_grads():
            r.dq[...] = (acc[...].reshape(W, T).T * scale).astype(BF16)
            r.ls[0, 0:1, :] = column_sum(r.dq[...].astype(F32))
            r.ls[0, 1:2, :] = column_sum(dkv[:, W:].astype(F32))
            r.ls[0, 2:8, :] = jnp.zeros((6, W), F32)

        def dx_own():
            r.xall[0, 0:TM] = (dx_rows(0, peer_rows) + nt(r.dq[peer_rows, :], r.wqkv[:, :W])).astype(BF16)
            for h in range(2):
                go(dx_y[0][h])
            r.gmix[...] += dx_rows(0, my_rows) + nt(r.dq[my_rows, :], r.wqkv[:, :W])

        shrink_tiles(0)
        s1.send(0)
        s2.send(0)
        other_slopes()
        shrink_tiles(1)
        expand_tiles(0)
        e1.send(0)
        e2.send(0)
        s1.add(0)
        s1.za()
        s2.forward(0)
        go(oy_send)
        expand_tiles(1)
        sum_blocks()
        grad_heads()
        e1.forward(0)
        set_bias(3)

        def beside_31():
            e2.forward(0)

        run(lambda p: pull(3, p), {1: beside_31})
        s2.add(1)
        s2.za()
        s1.zb()
        dx_part(3)
        set_bias(2)

        def beside_21():
            e1.add(1)
            e1.za()

        run(lambda p: pull(2, p), {1: beside_21})
        s2.zb()
        dx_part(2)
        dx_sum(3, 0)
        early_start(0)
        s1.zc()
        set_bias(1)

        def beside_11():
            s2.zc()
            e1.zb()
            e2.add(1)
            e2.za()

        run(lambda p: pull(1, p), {1: beside_11})
        set_bias(0)

        def beside_00():
            s2.zd()
            dx_sum(2, 0)
            dx_pass(2, 0)
            s1.zd()
            s1.send(2)

        run(lambda p: pull(0, p), {0: beside_00})
        s1.add(2)
        s1.spread(2)
        query_grads()
        e2.zb()
        e1.zc()
        key_value_tiles(0)
        ub.send(0)
        query_output_tiles(0)
        ua.send(0)
        early_finish(0)
        s1.back(2)
        s2.ze()
        key_value_tiles(1)
        ub.forward(0)
        e1.zd()
        query_output_tiles(1)
        dx_pass(3, 0)
        e2.zc()
        s2.zf()
        dx_sum(3, 1)
        dx_own()
        e1.ze()
        late_start(0)
        late_finish(0)
        e2.zd()
        ua.forward(0)
        ub.forward(1)
        e1.zf()
        late_finish(1)
        e2.ze()
        ub.forward(2)
        ua.forward(1)
        early_finish(1)
        e1.zg()
        ub.turn()
        s2.zg()
        early_finish(2)
        e2.zf()
        dx_part(1)
        ua.forward(2)
        dx_sum(2, 1)
        ub.back(3)
        dx_pass(2, 1)
        ua.turn()
        s1.ze()
        e2.zg()
        dx_sum(1, 0)
        dx_pass(1, 0)
        ub.back(2)
        ua.back(3)
        e1.back(1)
        dx_sum(1, 1)
        dx_pass(1, 1)
        s1.zf()
        ua.back(2)
        dx_pass(3, 1)
        e1.store()
        early_finish(3)
        dx_out(0)
        e2.back(1)
        s2.back(1)
        dx_out(1)
        late_finish(2)
        ub.back(1)
        ua.back(1)
        s2.store()
        s1.zg()
        early_finish(4)
        ua.store()
        e2.store()
        late_finish(3)
        ub.store()
        s1.store()
        small_copies = (local(r.es.at[1], r.small_out), local(r.ls.at[0], r.late_out))
        for copy in small_copies:
            copy.start()
        oy_local.wait()
        oy_send.wait_recv()
        for h in range(2):
            ig_local[h].wait()
            ig_send[h].wait_recv()
        for copy in small_copies:
            copy.wait()
        for unit in (s1, s2, e1, e2, ua, ub):
            unit.stored.wait()
        for p in range(HP):
            att_copy(p).wait_send()
        wait_sends()

    return kernel


def layer_call(sh, args):
    T, TM, D, W, F = sh.tokens, sh.mine, sh.width, sh.hw, sh.units
    HP = sh.pairs
    any_spec = pl.BlockSpec(memory_space=pl.ANY)
    vmem_spec = pl.BlockSpec(memory_space=pltpu.VMEM)
    ins = dict(
        seg_in=vmem_spec, qb_in=vmem_spec, vb_in=vmem_spec, ob_in=vmem_spec, ag_in=vmem_spec,
        as_in=vmem_spec, eb_in=vmem_spec, sb_in=vmem_spec, fg_in=vmem_spec, fs_in=vmem_spec,
        x_in=any_spec, wq_in=any_spec, wk_in=any_spec, wv_in=any_spec,
        wo_in=any_spec, we_in=any_spec, ws_in=any_spec, cot_in=any_spec,
    )
    outs = dict(
        out=((T, D), BF16, any_spec),
        ig_out=((T, D), BF16, any_spec),
        ue_out=((D, F), BF16, any_spec),
        us_out=((F, D), BF16, any_spec),
        ua_out=((D, 2 * W), BF16, any_spec),
        ub_out=((D, 2 * W), BF16, any_spec),
        small_out=((8, D), F32, any_spec),
        late_out=((8, W), F32, any_spec),
    )
    vm = lambda shape, kind: pltpu.VMEM(shape, kind)
    scratch = dict(
        send=pltpu.SemaphoreType.DMA((224,)),
        recv=pltpu.SemaphoreType.DMA((224,)),
        local=pltpu.SemaphoreType.DMA((32,)),
        xall=vm((4, T, D), BF16),
        xt=vm((D, 4 * T), BF16),
        wqkv=vm((D, 3 * W), BF16),
        wo=vm((2 * W, D), BF16),
        we=vm((2, D, F), BF16),
        ws=vm((2, F, D), BF16),
        eb=vm((2, 1, F), F32),
        cot=vm((TM, D), BF16),
        segs=vm((4, 1, T), F32),
        bias=vm((T, T), F32),
        kv=vm((4, HP, 2, T, 128), BF16),
        qm=vm((2 * HP, T, 128), BF16),
        dm=vm((2 * HP, T, 128), BF16),
        m_s=vm((2 * HP, 1, T), F32),
        l_s=vm((2 * HP, 1, T), F32),
        delta=vm((2 * HP, 1, T), F32),
        acc=vm((2 * HP, 64, T), F32),
        att=vm((T, W), BF16),
        att_o=vm((TM, W), BF16),
        n1=vm((TM, D), F32),
        r1=vm((TM, 128), F32),
        sec=vm((TM, D), F32),
        gf=vm((TM, D), F32),
        gmix=vm((TM, D), F32),
        fl=vm((T, D), BF16),
        flt=vm((D, T), BF16),
        gs=vm((T, D), BF16),
        gm=vm((T, D), BF16),
        gp=vm((2, TM, F), F32),
        hid=vm((T, F), BF16),
        gpre=vm((T, F), BF16),
        oy=vm((TM, D), BF16),
        small=vm((8, D), F32),
        es=vm((2, 8, D), F32),
        es_r=vm((5, 8, D), F32),
        ls=vm((2, 8, W), F32),
        ls_r=vm((4, 8, W), F32),
        dkv=vm((4 * T, 2 * W), BF16),
        dq=vm((T, W), BF16),
        dxy=vm((4, TM, D), BF16),
        dxz=vm((6, TM, D), BF16),
        igm=vm((TM, D), BF16),
        ua=vm((D, 2 * W), BF16),
        ub=vm((D, 2 * W), BF16),
        s0=vm((D, D), BF16),
        e0=vm((2, D // 2, D), BF16),
        z0=vm((3 * (D // 8), D), BF16),
        z1=vm((2 * (D // 8), D), BF16),
        z2=vm((D // 8, D), BF16),
        z3=vm((D // 16, D), BF16),
        x0=vm((4, D // 4, D), BF16),
        l0=vm((4, 3 * (D // 16), D), BF16),
        l1=vm((4, 2 * (D // 16), D), BF16),
        l2=vm((4, D // 16, D), BF16),
        p0=vm((2, D // 2, D), BF16),
        p1=vm((2, D // 4, D), BF16),
        p2=vm((2, D // 8, D), BF16),
        p3=vm((2, D // 16, D), BF16),
    )
    names = list(ins) + list(outs) + list(scratch)
    return pl.pallas_call(
        make_kernel(sh, names),
        out_shape=[jax.ShapeDtypeStruct(o[0], o[1]) for o in outs.values()],
        in_specs=list(ins.values()),
        out_specs=[o[2] for o in outs.values()],
        scratch_shapes=list(scratch.values()),
        compiler_params=pltpu.CompilerParams(
            collective_id=0, has_side_effects=True, vmem_limit_bytes=63 * 1024 * 1024
        ),
        name="layer",
    )(*args)


def finish_kernel(sh, names, *refs):
    r = types.SimpleNamespace(**dict(zip(names, refs)))
    W = sh.hw
    half = sh.units // 2
    pieces = []
    for at in range(2):
        pieces.append((r.us.at[pl.ds(at * half, half)], r.us_v.at[at], r.usf.at[at], r.us_out.at[pl.ds(at * half, half)]))
    for at in range(2):
        rows = pl.ds(at * W, W)
        pieces.append((r.ue.at[rows], r.ue_v.at[at], r.uef.at[at], r.ue_out.at[rows]))
    cols = [pl.ds(0, W), pl.ds(W, W)]
    pieces.append((r.ub.at[:, cols[0]], r.ab_v.at[0], r.abf.at[0], r.wk_out))
    pieces.append((r.ub.at[:, cols[1]], r.ab_v.at[1], r.abf.at[1], r.wv_out))
    pieces.append((r.ua.at[:, cols[0]], r.ab_v.at[2], r.abf.at[2], r.wq_out))
    for at in range(2):
        rows = pl.ds(at * W, W)
        pieces.append((r.ua.at[rows, cols[1]], r.o_v.at[at], r.of.at[at], r.wo_out.at[:, cols[at]]))
    pieces.append((r.ig, r.ig_v, r.igf, r.ig_out))
    taken = pltpu.make_async_copy(r.out, r.out_v, r.sems.at[0])
    taken.start()
    reads = [pltpu.make_async_copy(p[0], p[1], r.sems.at[1 + k]) for k, p in enumerate(pieces)]
    for copy in reads:
        copy.start()
    at_small = 2 * len(pieces) + 2
    small_reads = [
        pltpu.make_async_copy(r.small, r.small_v, r.sems.at[at_small]),
        pltpu.make_async_copy(r.late, r.late_v, r.sems.at[at_small + 1]),
    ]
    for copy in small_reads:
        copy.start()
    taken.wait()
    passed = pltpu.make_async_copy(r.out_v, r.out_out, r.sems.at[2 * len(pieces) + 1])
    passed.start()
    writes = []

    def vectors():
        for copy in small_reads:
            copy.wait()
        for target, at in ((r.fg_v, 0), (r.fs_v, 1), (r.sb_v, 2), (r.ag_v, 3), (r.as_v, 4), (r.ob_v, 5)):
            target[...] = r.small_v[at]
        r.eb_v[0 : sh.width] = r.small_v[6]
        r.eb_v[sh.width :] = r.small_v[7]
        r.qb_v[...] = r.late_v[0]
        r.vb_v[...] = r.late_v[1]
        leaving = (
            (r.fg_v, r.fg), (r.fs_v, r.fs), (r.sb_v, r.sb), (r.ag_v, r.ag), (r.as_v, r.as_), (r.ob_v, r.ob),
            (r.eb_v, r.eb), (r.qb_v, r.qb), (r.vb_v, r.vb),
        )
        for k, (held, target) in enumerate(leaving):
            copy = pltpu.make_async_copy(held, target, r.sems.at[at_small + 2 + k])
            copy.start()
            writes.append(copy)

    for k, (_, low, wide, target) in enumerate(pieces):
        if k == 4:
            vectors()
        reads[k].wait()
        rows = low.shape[0]
        step = 96 if rows % 96 == 0 else 64

        def tile(i, carry):
            at = pl.ds(pl.multiple_of(i * step, step), step)
            wide[at, :] = low[at, :].astype(F32)
            return carry

        lax.fori_loop(0, rows // step, tile, 0)
        copy = pltpu.make_async_copy(wide, target, r.sems.at[1 + len(pieces) + k])
        copy.start()
        writes.append(copy)
    passed.wait()
    for k, copy in enumerate(writes):
        copy.wait()


def finish_call(sh, parts):
    T, D, W, F = sh.tokens, sh.width, sh.hw, sh.units
    any_spec = pl.BlockSpec(memory_space=pl.ANY)
    hbm_spec = pl.BlockSpec(memory_space=pltpu.HBM)
    ins = dict(
        out=hbm_spec, ig=hbm_spec, ue=hbm_spec, us=hbm_spec, ua=hbm_spec, ub=hbm_spec,
        small=hbm_spec, late=hbm_spec,
    )
    outs = dict(
        out_out=((T, D), BF16, any_spec),
        ig_out=((T, D), F32, any_spec),
        wq_out=((D, W), F32, any_spec),
        wk_out=((D, W), F32, any_spec),
        wv_out=((D, W), F32, any_spec),
        qb=((W,), F32, any_spec),
        vb=((W,), F32, any_spec),
        wo_out=((W, D), F32, any_spec),
        ob=((D,), F32, any_spec),
        ag=((D,), F32, any_spec),
        as_=((D,), F32, any_spec),
        ue_out=((D, F), F32, any_spec),
        eb=((F,), F32, any_spec),
        us_out=((F, D), F32, any_spec),
        sb=((D,), F32, any_spec),
        fg=((D,), F32, any_spec),
        fs=((D,), F32, any_spec),
    )
    scratch = dict(
        sems=pltpu.SemaphoreType.DMA((40,)),
        out_v=pltpu.VMEM((T, D), BF16),
        small_v=pltpu.VMEM((8, D), F32),
        late_v=pltpu.VMEM((8, W), F32),
        eb_v=pltpu.VMEM((F,), F32),
    )
    for name in ("fg_v", "fs_v", "sb_v", "ag_v", "as_v", "ob_v"):
        scratch[name] = pltpu.VMEM((D,), F32)
    for name in ("qb_v", "vb_v"):
        scratch[name] = pltpu.VMEM((W,), F32)
    for low, wide, shape in (
        ("us_v", "usf", (2, F // 2, D)),
        ("ue_v", "uef", (2, W, F)),
        ("ab_v", "abf", (3, D, W)),
        ("o_v", "of", (2, W, W)),
        ("ig_v", "igf", (T, D)),
    ):
        scratch[low], scratch[wide] = pltpu.VMEM(shape, BF16), pltpu.VMEM(shape, F32)
    names = list(ins) + list(outs) + list(scratch)
    return pl.pallas_call(
        functools.partial(finish_kernel, sh, names),
        out_shape=[jax.ShapeDtypeStruct(o[0], o[1]) for o in outs.values()],
        in_specs=list(ins.values()),
        out_specs=[o[2] for o in outs.values()],
        scratch_shapes=list(scratch.values()),
        compiler_params=pltpu.CompilerParams(vmem_limit_bytes=63 * 1024 * 1024),
        name="finish",
    )(*parts)


def fused_body(
    mesh_sizes, inputs, segments, query_proj, key_proj, value_proj, query_bias, value_bias, output_proj,
    output_bias, attn_gain, attn_shift, expand_proj, expand_bias, shrink_proj, shrink_bias,
    final_gain, final_shift, cotangent,
):
    sh = Shapes(mesh_sizes, inputs.shape[0], inputs.shape[1], query_proj.shape[1], expand_proj.shape[1])
    parts = layer_call(
        sh,
        (
            segments, query_bias, value_bias, output_bias, attn_gain, attn_shift, expand_bias, shrink_bias,
            final_gain, final_shift, inputs, query_proj, key_proj, value_proj, output_proj, expand_proj,
            shrink_proj, cotangent,
        ),
    )
    return finish_call(sh, parts)


contract_rows = (((0,), (0,)), ((), ()))
contract_cols = (((1,), (1,)), ((), ()))


def matmul(left, right):
    return jnp.dot(left, right, preferred_element_type=jnp.float32)


def inner_rows(left, right):
    return lax.dot_general(left, right, contract_rows, preferred_element_type=jnp.float32)


def inner_cols(left, right):
    return lax.dot_general(left, right, contract_cols, preferred_element_type=jnp.float32)


def norm_forward(values, gain, shift):
    centred = values - jnp.mean(values, axis=-1, keepdims=True)
    spread = jnp.mean(centred * centred, axis=-1, keepdims=True)
    recip = lax.rsqrt(spread + norm_eps)
    normed = centred * recip
    return (normed * gain + shift, normed, recip)


def norm_backward(upstream, normed, recip, gain):
    scaled = upstream * gain
    centred = (
        scaled
        - jnp.mean(scaled, axis=-1, keepdims=True)
        - normed * jnp.mean(scaled * normed, axis=-1, keepdims=True)
    )
    return (centred * recip, jnp.sum(upstream * normed, axis=0), jnp.sum(upstream, axis=0))


def cross_scores(left, right):
    return inner_cols(left, right)


def spread_apply(weights_in, right):
    return matmul(weights_in, right)


def spread_transpose(weights_in, left):
    return inner_rows(weights_in, left)


def body(
    inputs,
    segments,
    query_proj,
    key_proj,
    value_proj,
    query_bias,
    value_bias,
    output_proj,
    output_bias,
    attn_gain,
    attn_shift,
    expand_proj,
    expand_bias,
    shrink_proj,
    shrink_bias,
    final_gain,
    final_shift,
    cotangent,
):
    head_count = query_proj.shape[1] // HEAD_DIM
    scale = HEAD_DIM ** (-0.5)
    seg_local = segments[0]
    queries = (matmul(inputs, query_proj) + query_bias.astype(jnp.float32)).astype(jnp.bfloat16)
    keys = matmul(inputs, key_proj).astype(jnp.bfloat16)
    values = (matmul(inputs, value_proj) + value_bias.astype(jnp.float32)).astype(jnp.bfloat16)
    all_keys, all_values, key_ids = (
        lax.all_gather(keys, "ctx", axis=0, tiled=True),
        lax.all_gather(values, "ctx", axis=0, tiled=True),
        lax.all_gather(seg_local.astype(jnp.bfloat16), "ctx", axis=0, tiled=True),
    )
    query_segs = seg_local.astype(jnp.float32)
    key_segs = key_ids.astype(jnp.float32)
    same_seg = query_segs[:, None] == key_segs[None, :]

    def split_heads(matrix):
        return jnp.swapaxes(matrix.reshape(matrix.shape[0], head_count, HEAD_DIM), 0, 1)

    def join_heads(stack):
        return jnp.swapaxes(stack, 0, 1).reshape(stack.shape[1], head_count * HEAD_DIM)

    query_heads = split_heads(queries)
    key_heads = split_heads(all_keys)
    value_heads = split_heads(all_values)

    def head_forward(state, triple):
        query_head, key_head, value_head = triple
        scores = cross_scores(query_head, key_head) * scale
        scores = jnp.where(same_seg, scores, masked)
        row_max = jnp.max(scores, axis=1, keepdims=True)
        exp_scores = jnp.where(same_seg, jnp.exp(scores - row_max), 0.0)
        row_sum = jnp.sum(exp_scores, axis=1, keepdims=True)
        attn_probs = (exp_scores / row_sum).astype(jnp.bfloat16)
        mixed = spread_apply(attn_probs, value_head)
        return (state, (mixed, row_max + jnp.log(row_sum)))

    mixed_heads, log_sums = lax.scan(head_forward, None, (query_heads, key_heads, value_heads))[1]
    attended = join_heads(mixed_heads).astype(jnp.bfloat16)
    attn_total = lax.psum(matmul(attended, output_proj).astype(jnp.bfloat16), "tensor").astype(
        jnp.float32
    )
    attn_gain_f = attn_gain.astype(jnp.float32)
    first, first_normed, first_recip = norm_forward(
        inputs.astype(jnp.float32) + attn_total + output_bias.astype(jnp.float32),
        attn_gain_f,
        attn_shift.astype(jnp.float32),
    )
    first_low = first.astype(jnp.bfloat16)
    pre_act = matmul(first_low, expand_proj) + expand_bias.astype(jnp.float32)
    activated, gelu_back = jax.vjp(lambda pre_in: jax.nn.gelu(pre_in, approximate=False), pre_act)
    hidden = activated.astype(jnp.bfloat16)
    feed_total = lax.psum(matmul(hidden, shrink_proj).astype(jnp.bfloat16), "tensor").astype(
        jnp.float32
    )
    second = first + feed_total + shrink_bias.astype(jnp.float32)
    final_gain_f = final_gain.astype(jnp.float32)
    output, second_normed, second_recip = norm_forward(
        second, final_gain_f, final_shift.astype(jnp.float32)
    )
    upstream = cotangent.astype(jnp.float32)
    grad_second, fgain_grad, fshift_grad = norm_backward(
        upstream, second_normed, second_recip, final_gain_f
    )
    sbias_grad = jnp.sum(grad_second, axis=0)
    grad_second_low = grad_second.astype(jnp.bfloat16)
    shrink_grad = inner_rows(hidden, grad_second_low)
    grad_act = inner_cols(grad_second_low, shrink_proj)
    grad_pre = gelu_back(grad_act)[0].astype(jnp.bfloat16)
    ebias_grad = jnp.sum(grad_pre.astype(jnp.float32), axis=0)
    expand_grad = inner_rows(first_low, grad_pre)
    grad_first = grad_second + lax.psum(
        inner_cols(grad_pre, expand_proj).astype(jnp.bfloat16), "tensor"
    ).astype(jnp.float32)
    grad_mix, again_grad, ashift_grad = norm_backward(
        grad_first, first_normed, first_recip, attn_gain_f
    )
    obias_grad = jnp.sum(grad_mix, axis=0)
    grad_mix_low = grad_mix.astype(jnp.bfloat16)
    oproj_grad = inner_rows(attended, grad_mix_low)
    grad_attended = inner_cols(grad_mix_low, output_proj).astype(jnp.bfloat16)
    grad_heads = split_heads(grad_attended)

    def head_backward(state, group):
        query_head, key_head, value_head, grad_head, log_sum = group
        scores = cross_scores(query_head, key_head) * scale
        attn_probs = jnp.where(same_seg, jnp.exp(scores - log_sum), 0.0)
        grad_probs = cross_scores(grad_head, value_head)
        row_dot = jnp.sum(attn_probs * grad_probs, axis=1, keepdims=True)
        grad_scores = (attn_probs * (grad_probs - row_dot)).astype(jnp.bfloat16)
        grad_query = spread_apply(grad_scores, key_head) * scale
        grad_key = spread_transpose(grad_scores, query_head) * scale
        grad_value = spread_transpose(attn_probs.astype(jnp.bfloat16), grad_head)
        return (state, (grad_query, grad_key, grad_value))

    query_back, key_back, value_back = lax.scan(
        head_backward, None, (query_heads, key_heads, value_heads, grad_heads, log_sums)
    )[1]
    grad_queries = join_heads(query_back).astype(jnp.bfloat16)
    key_sum, value_sum = (
        lax.psum_scatter(
            join_heads(key_back).astype(jnp.bfloat16), "ctx", scatter_dimension=0, tiled=True
        ).astype(jnp.float32),
        lax.psum_scatter(
            join_heads(value_back).astype(jnp.bfloat16), "ctx", scatter_dimension=0, tiled=True
        ).astype(jnp.float32),
    )
    grad_keys = key_sum.astype(jnp.bfloat16)
    grad_values = value_sum.astype(jnp.bfloat16)
    qbias_grad = jnp.sum(grad_queries.astype(jnp.float32), axis=0)
    vbias_grad = jnp.sum(grad_values.astype(jnp.float32), axis=0)
    query_grad = inner_rows(inputs, grad_queries)
    key_grad = inner_rows(inputs, grad_keys)
    value_grad = inner_rows(inputs, grad_values)
    back_terms = (
        inner_cols(grad_queries, query_proj)
        + inner_cols(grad_keys, key_proj)
        + inner_cols(grad_values, value_proj)
    )
    input_grad = grad_mix + lax.psum(back_terms.astype(jnp.bfloat16), "tensor").astype(jnp.float32)
    (
        query_grad,
        key_grad,
        value_grad,
        qbias_grad,
        vbias_grad,
        oproj_grad,
        obias_grad,
        again_grad,
        ashift_grad,
        expand_grad,
        ebias_grad,
        shrink_grad,
        sbias_grad,
        fgain_grad,
        fshift_grad,
    ) = lax.psum(
        (
            query_grad,
            key_grad,
            value_grad,
            qbias_grad,
            vbias_grad,
            oproj_grad,
            obias_grad,
            again_grad,
            ashift_grad,
            expand_grad,
            ebias_grad,
            shrink_grad,
            sbias_grad,
            fgain_grad,
            fshift_grad,
        ),
        ("dp", "ctx"),
    )
    return (
        output.astype(jnp.bfloat16),
        input_grad,
        query_grad,
        key_grad,
        value_grad,
        qbias_grad,
        vbias_grad,
        oproj_grad,
        obias_grad,
        again_grad,
        ashift_grad,
        expand_grad,
        ebias_grad,
        shrink_grad,
        sbias_grad,
        fgain_grad,
        fshift_grad,
    )


def solution(mesh):
    in_specs = (
        P(("dp", "ctx"), None),
        P("dp", "ctx"),
        P(None, "tensor"),
        P(None, "tensor"),
        P(None, "tensor"),
        P("tensor"),
        P("tensor"),
        P("tensor", None),
        P(),
        P(),
        P(),
        P(None, "tensor"),
        P("tensor"),
        P("tensor", None),
        P(),
        P(),
        P(),
        P(("dp", "ctx"), None),
    )
    out_specs = (
        P(("dp", "ctx"), None),
        P(("dp", "ctx"), None),
        P(None, "tensor"),
        P(None, "tensor"),
        P(None, "tensor"),
        P("tensor"),
        P("tensor"),
        P("tensor", None),
        P(),
        P(),
        P(),
        P(None, "tensor"),
        P("tensor"),
        P("tensor", None),
        P(),
        P(),
        P(),
    )
    sizes = dict(mesh.shape)
    fits = sizes == {"dp": 4, "ctx": 4, "tensor": 2}
    chosen = functools.partial(fused_body, sizes) if fits else body
    return jax.shard_map(chosen, mesh=mesh, in_specs=in_specs, out_specs=out_specs, check_vma=False)
```

```python
import functools
import types

import jax
import jax.numpy as jnp
from jax import lax
from jax.experimental import pallas as pl
from jax.experimental.pallas import tpu as pltpu
from jax.sharding import PartitionSpec as P

HEAD_DIM = 64
norm_eps = 1e-12
masked = -1e30
MESH = pl.DeviceIdType.MESH
CORE, XS, YS, Z1, Z2, LINE = range(6)
BF16, F32 = jnp.bfloat16, jnp.float32
INV_SQRT2 = 0.7071067811865476
INV_SQRT_2PI = 0.3989422804014327


def nn(left, right):
    return jnp.dot(left, right, preferred_element_type=F32)


def nt(left, right):
    return lax.dot_general(left, right, (((1,), (1,)), ((), ())), preferred_element_type=F32)


def tn(left, right):
    return lax.dot_general(left, right, (((0,), (0,)), ((), ())), preferred_element_type=F32)


def normalise(values):
    centred = values - jnp.mean(values, axis=-1, keepdims=True)
    spread = jnp.mean(centred * centred, axis=-1, keepdims=True)
    recip = lax.rsqrt(spread + norm_eps)
    return centred * recip, recip


def denormalise(scaled, normed, recip):
    return recip * (
        scaled
        - jnp.mean(scaled, axis=-1, keepdims=True)
        - normed * jnp.mean(scaled * normed, axis=-1, keepdims=True)
    )


def gelu_parts(pre):
    phi_sum = 0.5 + 0.5 * lax.erf(pre * INV_SQRT2)
    slope = phi_sum + pre * (INV_SQRT_2PI * jnp.exp(-0.5 * pre * pre))
    return pre * phi_sum, slope


def column_sum(values):
    return jnp.sum(values, axis=0, keepdims=True)


class Shapes:
    def __init__(self, mesh, tokens, width, heads_width, units):
        self.nd, self.nc = mesh["dp"], mesh["ctx"]
        self.nx = self.nd // 2
        self.tokens, self.mine = tokens, tokens // 2
        self.width, self.hw, self.units = width, heads_width, units
        self.pairs = heads_width // 128


def make_kernel(sh, names):
    T, TM, D, W, F = sh.tokens, sh.mine, sh.width, sh.hw, sh.units
    HP = sh.pairs
    TILE = 512
    NTILE = F // TILE
    SLOTS = 4
    PARTS = 4
    PR = TM // PARTS

    def kernel(*refs):
        r = types.SimpleNamespace(**dict(zip(names, refs)))
        send_ref, recv_ref, local_ref = r.send, r.recv, r.local
        d, c, t = lax.axis_index("dp"), lax.axis_index("ctx"), lax.axis_index("tensor")
        core, xpos = lax.rem(d, 2), d // 2
        low_bit, high_bit = lax.rem(c, 2), c // 2
        next_c = c + 1 - 2 * low_bit
        z1_peer, z2_peer = (d, next_c, t), (d, c + 2 - 4 * high_bit, t)
        z3_peer = (d, next_c + 2 - 4 * high_bit, t)
        y_peer = (d, c, 1 - t)
        core_peer = (d + 1 - 2 * core, c, t)
        x_peer = (d + 2 - 4 * xpos, c, t)
        peer_of = {CORE: core_peer, XS: x_peer, YS: y_peer, Z1: z1_peer, Z2: z2_peer}
        bit_of = {CORE: core, XS: xpos, YS: t, Z1: low_bit, Z2: high_bit}
        my_rows = pl.ds(pl.multiple_of(t * TM, TM), TM)
        peer_rows = pl.ds(pl.multiple_of((1 - t) * TM, TM), TM)
        counts = [0, 0]

        def take(kind, k=1):
            at = counts[kind]
            counts[kind] += k
            assert counts[kind] <= (send_ref, local_ref)[kind].shape[0], counts
            return at

        def remote(src, dst, device, at=None, recv_at=None):
            at = take(0) if at is None else at
            recv_at = at if recv_at is None else recv_at
            return pltpu.make_async_remote_copy(
                src_ref=src, dst_ref=dst, send_sem=send_ref.at[at], recv_sem=recv_ref.at[recv_at],
                device_id=device, device_id_type=MESH,
            )

        def local(src, dst):
            return pltpu.make_async_copy(src, dst, local_ref.at[take(1)])

        unsent = []

        def go(copy, where=None):
            if where is None:
                copy.start()
            else:
                pl.when(where)(lambda: copy.start())
            unsent.append((copy, where))

        def wait_sends(*but):
            kept = [entry for entry in unsent if any(entry[0] is other for other in but)]
            for copy, where in unsent:
                if any(copy is other for other in but):
                    continue
                if where is None:
                    copy.wait_send()
                else:
                    pl.when(where)(lambda copy=copy: copy.wait_send())
            unsent[:] = kept

        def wait_first(count):
            for copy, where in unsent[:count]:
                if where is None:
                    copy.wait_send()
                else:
                    pl.when(where)(lambda copy=copy: copy.wait_send())
            del unsent[:count]

        loads = types.SimpleNamespace(
            x=local(r.x_in, r.xall.at[0]),
            wk=local(r.wk_in, r.wqkv.at[:, pl.ds(W, W)]),
            wv=local(r.wv_in, r.wqkv.at[:, pl.ds(2 * W, W)]),
            wq=local(r.wq_in, r.wqkv.at[:, pl.ds(0, W)]),
            wo=local(r.wo_in, r.wo.at[pl.ds(0, W)]),
            we=local(r.we_in, r.we.at[0]),
            ws=local(r.ws_in, r.ws.at[0]),
            cot=local(r.cot_in.at[my_rows], r.cot),
        )
        for copy in vars(loads).values():
            copy.start()

        def row(ref):
            return ref[...].astype(F32).reshape(1, ref.shape[0])

        vec = [row(ref) for ref in (r.ob_in, r.ag_in, r.as_in, r.sb_in, r.fg_in, r.fs_in)]
        r.eb[0] = row(r.eb_in)
        r.segs[0] = r.seg_in[...].astype(F32)
        barrier = pltpu.get_barrier_semaphore()
        greeted = [y_peer, core_peer, x_peer, z1_peer, z2_peer, z3_peer]
        for device in greeted:
            pl.semaphore_signal(barrier, inc=1, device_id=device, device_id_type=MESH)
        pl.semaphore_wait(barrier, len(greeted))

        seg_copies = [None] + [
            remote(r.segs.at[0], r.segs.at[k], peer) for k, peer in ((1, z1_peer), (2, z2_peer), (3, z3_peer))
        ]
        eb_copy = remote(r.eb.at[0], r.eb.at[1], y_peer)
        x_rows = [pl.ds(pl.multiple_of(t * TM + k * PR, PR), PR) for k in range(PARTS)]
        mid = lax.rem(low_bit + high_bit, 2)
        is_mid, is_end = mid == 1, mid == 0
        slots = (0, 1, 2 + mid, 3 - mid)
        x_at = take(0, 3 * PARTS)

        def x_recv(slot, k):
            return x_at + (slot - 1) * PARTS + k

        def x_move(src_slot, dst_slot, peer, k):
            src = r.x_in.at[x_rows[k]] if src_slot == 0 else r.xall.at[src_slot, x_rows[k]]
            return remote(src, r.xall.at[dst_slot, x_rows[k]], peer, None, x_recv(dst_slot, k))

        x_near = [x_move(0, 1, z1_peer, k) for k in range(PARTS)]
        x_far = [x_move(0, 3, z3_peer, k) for k in range(PARTS)]
        x_next = (
            None,
            [x_move(1, 2, z3_peer, k) for k in range(PARTS)],
            [x_move(3, 2, z1_peer, k) for k in range(PARTS)],
            [x_move(2, 3, z1_peer, k) for k in range(PARTS)],
        )
        x_y = [None] + [
            [remote(r.xall.at[slots[o], x_rows[k]], r.xall.at[slots[o], x_rows[k]], y_peer) for k in range(PARTS)]
            for o in (1, 2, 3)
        ]
        for k in range(PARTS):
            go(x_near[k])
            go(x_far[k], is_mid)
        for copy in seg_copies[1:]:
            go(copy)
        go(eb_copy)

        def arrive(o, k):
            here = r.xall.at[slots[o], x_rows[k]]
            remote(here, here, z1_peer, x_at, x_recv(slots[o], k)).wait_recv()
            go(x_next[o][k], is_mid)
            go(x_y[o][k])

        def block_here(o):
            if o == 1:
                for copy in seg_copies[1:]:
                    copy.wait_recv()
            for k in range(PARTS):
                x_y[o][k].wait_recv()

        chunks = [
            (r.wo_in, r.wo.at[pl.ds(W, W)], W, 0, 1),
            (r.we_in, r.we.at[1], D, 0, 2),
            (r.we_in, r.we.at[1], D, 1, 2),
            (r.ws_in, r.ws.at[1], F, 0, 2),
            (r.ws_in, r.ws.at[1], F, 1, 2),
        ]
        pieces = sh.nd * 2

        def window(chunk, owner):
            rows, part, parts = chunk[2:]
            size = rows // pieces // parts
            return pl.ds(pl.multiple_of(owner * (rows // pieces) + part * size, size), size)

        own_piece, pair_piece = d * 2 + low_bit, d * 2 + 1 - low_bit
        x_d = d + 2 - 4 * xpos
        x_pieces = (x_d * 2 + low_bit, x_d * 2 + 1 - low_bit)
        w_y, w_z, w_x, w_core = [], [], [], []
        for chunk in chunks:
            source, held = chunk[0], chunk[1]

            def move(owner, peer):
                where = window(chunk, owner)
                return remote(held.at[where], held.at[where], peer)

            own = window(chunk, own_piece)
            w_y.append(remote(source.at[own], held.at[own], y_peer))
            w_z.append(move(own_piece, z1_peer))
            w_x.append([move(piece, x_peer) for piece in (own_piece, pair_piece)])
            w_core.append([move(piece, core_peer) for piece in (own_piece, pair_piece) + x_pieces])

        def hop1(i):
            w_y[i].wait_recv()
            go(w_z[i])
            go(w_x[i][0])
            go(w_core[i][0])

        def hop2(i):
            w_z[i].wait_recv()
            go(w_x[i][1])
            go(w_core[i][1])

        def hop3(i):
            for k in range(2):
                w_x[i][k].wait_recv()
                go(w_core[i][2 + k])

        def weights_done(i):
            for copy in w_core[i]:
                copy.wait_recv()


        kv, m_s, l_s, acc = r.kv, r.m_s, r.l_s, r.acc
        value_bias = row(r.vb_in)
        scale = HEAD_DIM ** (-0.5)
        lane = lax.broadcasted_iota(jnp.int32, (T, 128), 1)

        def split_pair(target, p, pair):
            target[2 * p] = jnp.where(lane < 64, pair, 0.0).astype(BF16)
            target[2 * p + 1] = jnp.where(lane < 64, 0.0, pair).astype(BF16)

        def set_keys_values(slot):
            both = nn(r.xall[slot], r.wqkv[:, W:])
            for p in range(HP):
                kv[slot, p, 0] = both[:, p * 128 : (p + 1) * 128].astype(BF16)
                cols = slice(W + p * 128, W + (p + 1) * 128)
                kv[slot, p, 1] = (both[:, cols] + value_bias[:, p * 128 : (p + 1) * 128]).astype(BF16)

        def set_bias(slot):
            seg_keys = jnp.broadcast_to(r.segs[slot], (128, T)).T
            for j in range(T // 128):
                cols = slice(j * 128, (j + 1) * 128)
                r.bias[:, cols] = jnp.where(seg_keys == r.segs[0, :, cols], 0.0, masked)

        def project():
            loads.x.wait()
            loads.wk.wait()
            loads.wv.wait()
            set_keys_values(0)
            loads.wq.wait()
            queries = (nn(r.xall[0], r.wqkv[:, :W]) + row(r.qb_in)).astype(BF16).astype(F32) * scale
            for p in range(HP):
                split_pair(r.qm, p, queries[:, p * 128 : (p + 1) * 128])
            m_s[...] = jnp.full_like(m_s, masked)
            l_s[...] = jnp.zeros_like(l_s)
            acc[...] = jnp.zeros_like(acc)
            set_bias(0)


        def attend(slot, p):
            pair_keys = kv[slot, p, 0]
            pair_values = kv[slot, p, 1].T
            for hh in range(2):
                h = 2 * p + hh
                s = nt(pair_keys, r.qm[h]) + r.bias[...]
                old = m_s[h]
                new = jnp.maximum(old, jnp.max(s, axis=0, keepdims=True))
                e = jnp.exp(s - new)
                alpha = jnp.exp(old - new)
                l_s[h] = l_s[h] * alpha + jnp.sum(e, axis=0, keepdims=True)
                m_s[h] = new
                acc[h] = acc[h] * alpha + nn(pair_values[hh * 64 : hh * 64 + 64], e.astype(BF16))

        def run(body, services=None):
            def step(p, carry):
                body(p)
                for at, fn in (services or {}).items():
                    pl.when(p == at)(fn)
                return carry

            lax.fori_loop(0, HP, step, 0)

        def together(*fns):
            def all_of():
                for fn, arg in fns:
                    fn(*arg)

            return all_of

        def flip_inputs(slot):
            at = slot * T if isinstance(slot, int) else pl.multiple_of(slot * T, T)
            r.xt[:, pl.ds(at, T)] = r.xall[slot].T

        def next_block(o):
            block_here(o)
            set_keys_values(slots[o])
            set_bias(slots[o])

        att_at = take(0, HP)

        def att_copy(p):
            cols = pl.ds(p * 128, 128)
            return remote(r.att.at[peer_rows, cols], r.att_o.at[:, cols], y_peer, att_at + p)

        def attend_last(p):
            attend(slots[3], p)
            for h in (2 * p, 2 * p + 1):
                acc[h] = acc[h] / l_s[h]
                m_s[h] = m_s[h] + jnp.log(l_s[h])
            pair = acc[2 * p : 2 * p + 2].reshape(128, T).T
            r.att[:, p * 128 : (p + 1) * 128] = pair.astype(BF16)
            att_copy(p).start()

        fl_copy = remote(r.fl.at[my_rows], r.fl.at[my_rows], y_peer)

        def out_project():
            loads.wo.wait()
            r.sec[...] = nn(r.att[my_rows, :], r.wo[0:W, :])

        def first_norm():
            for p in range(HP):
                att_copy(p).wait_recv()
            mix = r.sec[...] + nn(r.att_o[...], r.wo[W : 2 * W, :])
            normed, recip = normalise(r.xall[0, my_rows, :].astype(F32) + mix + vec[0])
            r.n1[...] = normed
            r.r1[...] = jnp.broadcast_to(recip, (TM, 128))
            first = normed * vec[1] + vec[2]
            r.sec[...] = first + vec[3]
            r.fl[my_rows, :] = first.astype(BF16)
            go(fl_copy)

        def tile_cols(j):
            return pl.ds(pl.multiple_of(j * TILE, TILE), TILE)

        def forward_tile(side, j):
            cols = tile_cols(j)
            pre = nn(r.fl[my_rows, :], r.we[side, :, cols]) + r.eb[side, :, cols]
            hidden, slope = gelu_parts(pre)
            hidden = hidden.astype(BF16)
            r.gp[side, :, cols] = slope
            if side == 0:
                r.hid[my_rows, cols] = hidden
            r.sec[...] += nn(hidden, r.ws[side, cols, :])

        def tiles(fn):
            def step(j, carry):
                fn(j)
                return carry

            lax.fori_loop(0, NTILE, step, 0)

        def own_units():
            loads.we.wait()
            loads.ws.wait()
            tiles(lambda j: forward_tile(0, j))

        def other_units():
            eb_copy.wait_recv()
            tiles(lambda j: forward_tile(1, j))

        go(w_y[0])
        go(w_y[1])
        arrive(1, 0)
        hop1(0)
        project()

        def with_00():
            go(w_y[2])


        def with_01():
            hop1(1)

        run(lambda p: attend(slots[0], p), {0: with_00, 1: with_01})
        arrive(1, 1)
        arrive(1, 2)
        arrive(1, 3)
        hop2(0)
        go(w_y[3])
        arrive(2, 0)
        arrive(2, 1)
        arrive(2, 2)
        arrive(2, 3)
        next_block(1)
        hop1(2)

        def with_10():
            arrive(3, 0)


        def with_11():
            hop2(1)
            arrive(3, 1)

        run(lambda p: attend(slots[1], p), {0: with_10, 1: with_11})
        flip_inputs(slots[1])
        arrive(3, 2)
        hop2(2)
        hop3(0)
        next_block(2)
        arrive(3, 3)
        go(w_y[4])
        hop1(3)
        run(lambda p: attend(slots[2], p))
        next_block(3)
        hop2(3)
        attend_last(0)
        hop1(4)
        attend_last(1)
        hop3(1)
        attend_last(2)
        hop3(2)
        hop2(4)
        hop3(3)
        weights_done(0)
        out_project()
        first_norm()
        weights_done(1)
        flip_inputs(slots[0])
        weights_done(2)
        hop3(4)
        weights_done(3)
        own_units()
        weights_done(4)
        other_units()
        flip_inputs(slots[2])
        flip_inputs(slots[3])
        loads.cot.wait()
        normed2, recip2 = normalise(r.sec[...])
        upstream = r.cot[...].astype(F32)
        grad_second = denormalise(upstream * vec[4], normed2, recip2)
        r.gf[...] = grad_second
        r.gs[my_rows, :] = grad_second.astype(BF16)
        gs_copy = remote(r.gs.at[my_rows], r.gs.at[my_rows], y_peer)
        go(gs_copy)
        small = r.small
        small[0:1, :] = column_sum(upstream * normed2)
        small[1:2, :] = column_sum(upstream)
        small[2:3, :] = column_sum(grad_second)
        r.oy[...] = (normed2 * vec[4] + vec[5]).astype(BF16)
        oy_local = local(r.oy, r.out.at[my_rows])
        oy_local.start()


        def backward_tile(side, j):
            cols = tile_cols(j)
            low = (nt(r.gs[my_rows, :], r.ws[side, cols, :]) * r.gp[side, :, cols]).astype(BF16)
            if side == 0:
                r.gpre[my_rows, cols] = low
            r.gf[...] += nt(low, r.we[side, :, cols])

        tiles(lambda j: backward_tile(0, j))
        tiles(lambda j: backward_tile(1, j))
        grad_first = r.gf[...]
        normed = r.n1[...]
        grad_mix = denormalise(grad_first * vec[1], normed, r.r1[:, 0:1])
        r.gmix[...] = grad_mix
        r.gm[my_rows, :] = grad_mix.astype(BF16)
        gm_copy = remote(r.gm.at[my_rows], r.gm.at[my_rows], y_peer)
        go(gm_copy)
        small[3:4, :] = column_sum(grad_first * normed)
        small[4:5, :] = column_sum(grad_first)
        small[5:6, :] = column_sum(grad_mix)

        def rows_at(ref, first_row, rows):
            return ref.at[pl.ds(pl.multiple_of(first_row, rows), rows)]

        class Unit:
            def __init__(self, grad, whole, out, order, bufs):
                self.grad, self.order, self.bufs = grad, order, bufs
                self.first, self.rows, self.line = [0], [grad.shape[0]], None
                for stage in order:
                    self.rows.append(self.rows[-1] // (4 if stage == LINE else 2))
                    at = c if stage == LINE else bit_of[stage]
                    self.first.append(self.first[-1] + at * self.rows[-1])
                self.down, self.up = [], []
                for k, stage in enumerate(order):
                    rows, last = self.rows[k + 1], k == len(order) - 1
                    target = rows_at(whole, self.first[k + 1], rows)
                    source = target
                    if last:
                        source = rows_at(grad, self.first[k + 1], rows)
                        self.kept = local(source, target)
                    if stage == LINE:
                        self.line = k
                        self.far = self.first[k] + 2 * (1 - high_bit) * rows
                        self.edge = self.first[k] + 3 * high_bit * rows
                        near = self.first[k] + 2 * high_bit * rows
                        ends = grad.at[pl.ds(pl.multiple_of(self.first[k] + (1 - high_bit) * rows, rows), 3 * rows)]
                        self.down.append(
                            (
                                remote(ends, bufs[k][0], z1_peer),
                                remote(rows_at(grad, self.far, 2 * rows), bufs[k][1], z3_peer),
                                remote(rows_at(grad, self.edge, rows), bufs[k][2], z1_peer),
                            )
                        )
                        near, far = rows_at(whole, near, 2 * rows), rows_at(whole, self.far, 2 * rows)
                        self.up.append(
                            (remote(source, target, z1_peer), remote(near, near, z3_peer), remote(far, far, z1_peer))
                        )
                        continue
                    theirs = rows_at(grad, self.first[k] + (1 - bit_of[stage]) * rows, rows)
                    self.down.append(remote(theirs, bufs[k], peer_of[stage]))
                    self.up.append(remote(source, target, peer_of[stage]))
                self.stored = local(whole, out)

            def add_rows(self, first_row, rows, terms, step):

                def tile(i, carry):
                    window = self.grad.at[pl.ds(pl.multiple_of(first_row + i * step, step), step)]
                    total = window[...].astype(F32)
                    for buf, at in terms:
                        total = total + buf[pl.ds(pl.multiple_of(at + i * step, step), step), :].astype(F32)
                    window[...] = total.astype(BF16)
                    return carry

                lax.fori_loop(0, rows // step, tile, 0)

            def send(self, k):
                go(self.down[k])

            def add(self, k):
                self.down[k].wait_recv()
                self.add_rows(self.first[k + 1], self.rows[k + 1], [(self.bufs[k], 0)], min(96, self.rows[k + 1]))

            def forward(self, k):
                self.add(k)
                self.send(k + 1)

            def spread(self, k):
                go(self.up[k])
                if k == len(self.order) - 1:
                    self.kept.start()

            def back(self, k):
                if k == len(self.order) - 1:
                    self.kept.wait()
                self.up[k].wait_recv()
                if self.line is not None and k - 1 == self.line:
                    go(self.up[k - 1][0])
                else:
                    self.spread(k - 1)

            def za(self):
                go(self.down[self.line][0], is_end)

            def zb(self):
                k = self.line
                rows = self.rows[k + 1]

                @pl.when(is_mid)
                def _():
                    self.down[k][0].wait_recv()
                    self.add_rows(self.far, 2 * rows, [(self.bufs[k][0], (1 - high_bit) * rows)], rows)

                go(self.down[k][1], is_mid)

            def zc(self):
                k = self.line
                rows, (first_buf, second_buf, _) = self.rows[k + 1], self.bufs[k]

                @pl.when(is_mid)
                def _():
                    self.down[k][1].wait_recv()
                    self.add_rows(self.edge, rows, [(second_buf, high_bit * rows)], rows)

                go(self.down[k][2], is_mid)

                @pl.when(is_mid)
                def _():
                    terms = [(first_buf, 2 * high_bit * rows), (second_buf, (1 - high_bit) * rows)]
                    self.add_rows(self.first[k + 1], rows, terms, rows)
                    if k == len(self.order) - 1:
                        self.kept.start()
                        self.up[k][0].start()

            def zd(self):
                k = self.line

                @pl.when(is_end)
                def _():
                    self.down[k][2].wait_recv()
                    self.add_rows(self.first[k + 1], self.rows[k + 1], [(self.bufs[k][2], 0)], self.rows[k + 1])
                    if k == len(self.order) - 1:
                        self.kept.start()
                        self.up[k][0].start()

                if k == len(self.order) - 1:
                    unsent.append((self.up[k][0], None))

            def ze(self):
                k = self.line

                @pl.when(is_mid)
                def _():
                    if k == len(self.order) - 1:
                        self.kept.wait()
                    self.up[k][0].wait_recv()

                go(self.up[k][1], is_mid)

            def zf(self):
                pl.when(is_mid)(lambda: self.up[self.line][1].wait_recv())
                go(self.up[self.line][2], is_mid)

            def zg(self):
                k = self.line

                @pl.when(is_end)
                def _():
                    if k == len(self.order) - 1:
                        self.kept.wait()
                    self.up[k][0].wait_recv()
                    self.up[k][2].wait_recv()

                self.spread(k - 1)

            def turn(self):
                k = len(self.order) - 1
                self.add(k)
                self.spread(k)

            def store(self):
                self.up[0].wait_recv()
                self.stored.start()

        def all_sum(buf, slots, stages):
            copies = [remote(buf.at[k % 2], slots.at[k], peer_of[stage]) for k, stage in enumerate(stages)]

            def start(k):
                copies[k].start()

            def finish(k):
                copies[k].wait()
                total = buf[k % 2] + slots[k]
                if stages[k] == YS:
                    which = lax.broadcasted_iota(jnp.int32, total.shape, 0)
                    total = jnp.where(which < 6, total, buf[k % 2])
                buf[(k + 1) % 2] = total
                if k + 1 < len(stages):
                    start(k + 1)

            return start, finish


        def other_hidden(j):
            cols = tile_cols(j)
            pre = nn(r.fl[peer_rows, :], r.we[0, :, cols]) + r.eb[0, :, cols]
            hidden, slope = gelu_parts(pre)
            r.hid[peer_rows, cols] = hidden.astype(BF16)
            r.gp[0, :, cols] = slope

        def other_slopes():
            def tile(j):
                cols = tile_cols(j)
                low = nt(r.gs[peer_rows, :], r.ws[0, cols, :]) * r.gp[0, :, cols]
                r.gpre[peer_rows, cols] = low.astype(BF16)

            tiles(tile)

        fl_copy.wait_recv()
        tiles(other_hidden)
        r.flt[...] = r.fl[...].T
        wait_sends(gm_copy)
        gs_copy.wait_recv()
        by_line, by_pairs = (CORE, XS, LINE), (CORE, XS, Z1, Z2)
        half_d = D // 2

        def line_unit(grad, whole, out, first_buf, k):
            steps = (r.l0.at[k], r.l1.at[k], r.l2.at[k])
            return Unit(grad, whole, out, by_line, (first_buf, r.x0.at[k], steps))

        def pair_unit(grad, whole, out, k):
            return Unit(grad, whole, out, by_pairs, (r.p0.at[k], r.p1.at[k], r.p2.at[k], r.p3.at[k]))

        s1 = Unit(
            r.ws.at[1, pl.ds(0, D)], r.ws.at[0, pl.ds(0, D)], r.us_out.at[pl.ds(0, D)], (CORE, LINE, XS),
            (r.s0.at[pl.ds(0, half_d)], (r.z0, r.z1, r.z2), r.z3),
        )
        s2 = line_unit(
            r.ws.at[1, pl.ds(D, D)], r.ws.at[0, pl.ds(D, D)], r.us_out.at[pl.ds(D, D)], r.s0.at[pl.ds(half_d, half_d)], 1
        )
        e1, e2 = [
            line_unit(
                r.we.at[1, :, pl.ds(at, D)], r.we.at[0, :, pl.ds(at, D)], r.ue_out.at[:, pl.ds(at, D)], r.e0.at[k - 2], k
            )
            for k, at in ((2, 0), (3, D))
        ]
        ua = pair_unit(r.ua, r.s0, r.ua_out, 0)
        ub = pair_unit(r.ub, r.wo, r.ub_out, 1)

        def half_of(which):
            return which * core + (1 - which) * (1 - core)

        def shrink_tiles(which):
            def tile(i, carry):
                at = pl.multiple_of(i * D + half_of(which) * half_d, 128)
                r.ws[1, pl.ds(at, half_d), :] = tn(r.hid[:, pl.ds(at, half_d)], r.gs[...]).astype(BF16)
                return carry

            lax.fori_loop(0, F // D, tile, 0)

        def half_rows(which):
            return pl.ds(pl.multiple_of(half_of(which) * (D // 2), D // 2), D // 2)

        def expand_tiles(which):
            rows = half_rows(which)

            def tile(j):
                cols = tile_cols(j)
                r.we[1, rows, cols] = nn(r.flt[rows, :], r.gpre[:, cols]).astype(BF16)

            tiles(tile)

        def sum_blocks():
            totals = column_sum(r.gpre[...].astype(F32))
            small[6:7, :] = totals[:, :D]
            small[7:8, :] = totals[:, D:]
            r.es[0] = small[...]

        early_start, early_finish = all_sum(r.es, r.es_r, (YS, CORE, XS, Z1, Z2))
        late_start, late_finish = all_sum(r.ls, r.ls_r, (CORE, XS, Z1, Z2))

        def grad_heads():
            gm_copy.wait_recv()
            grad_att = nt(r.gm[...], r.wo[0:W, :]).astype(BF16).astype(F32)
            flipped = grad_att.T.reshape(2 * HP, 64, T)
            r.delta[...] = jnp.sum(acc[...] * flipped, axis=1, keepdims=True)
            for p in range(HP):
                split_pair(r.dm, p, grad_att[:, p * 128 : (p + 1) * 128])
            acc[...] = jnp.zeros_like(acc)

        oy_send = remote(r.oy, r.out.at[my_rows], y_peer)
        dkv = r.dkv

        def pull(slot, p):
            pair_keys, pair_values = kv[slot, p, 0], kv[slot, p, 1]
            flipped_keys = pair_keys.T
            grad_k = jnp.zeros((T, 128), F32)
            grad_v = jnp.zeros((T, 128), F32)
            for hh in range(2):
                h = 2 * p + hh
                q, g = r.qm[h], r.dm[h]
                probs = jnp.exp(nt(pair_keys, q) + (r.bias[...] - m_s[h]))
                grad_p = nt(pair_values, g)
                grad_v = grad_v + nn(probs.astype(BF16), g)
                ds = (probs * (grad_p - r.delta[h])).astype(BF16)
                grad_k = grad_k + nn(ds, q)
                acc[h] += nn(flipped_keys[hh * 64 : hh * 64 + 64], ds)
            rows = slice(slot * T, (slot + 1) * T)
            dkv[rows, pl.ds(pl.multiple_of(p * 128, 128), 128)] = grad_k.astype(BF16)
            dkv[rows, pl.ds(pl.multiple_of(W + p * 128, 128), 128)] = grad_v.astype(BF16)

        HR = TM // 2

        def half(at, h):
            return pl.ds(at + h * HR, HR)

        dx_y = [
            [remote(r.xall.at[k, half(0, h)], r.dxy.at[k, half(0, h)], y_peer) for h in range(2)] for k in range(SLOTS)
        ]

        def dx_move(slot, target, peer):
            return [remote(r.xall.at[slot, half(TM, h)], r.dxz.at[target, half(0, h)], peer) for h in range(2)]

        dx_end = {3: dx_move(3, 0, z1_peer), 2: dx_move(2, 1, z1_peer), 1: dx_move(1, 2, z1_peer)}
        dx_mid = {3: dx_move(3, 3, z3_peer), 2: dx_move(2, 4, z3_peer), 1: dx_move(1, 5, z1_peer)}

        def dx_rows(slot, rows):
            here = pl.ds(pl.multiple_of(slot * T + rows.start, TM), TM)
            return nt(dkv[here, :], r.wqkv[:, W:])

        def dx_part(slot):
            r.xall[slot, 0:TM] = dx_rows(slot, peer_rows).astype(BF16)
            for h in range(2):
                go(dx_y[slot][h])
            r.xall[slot, TM:] = dx_rows(slot, my_rows).astype(BF16)

        def add_to(slot, h, buf, at):
            rows, kept = slice(h * HR, (h + 1) * HR), slice(TM + h * HR, TM + (h + 1) * HR)
            total = r.xall[slot, kept].astype(F32) + buf[at, rows].astype(F32)
            r.xall[slot, kept] = total.astype(BF16)

        def dx_sum(slot, h):
            dx_y[slot][h].wait_recv()
            add_to(slot, h, r.dxy, slot)
            go(dx_end[slot][h], is_end)

        def dx_pass(slot, h):
            came = {3: dx_end[2], 2: dx_end[3], 1: dx_mid[2]}[slot][h]
            at = {3: 1, 2: 0, 1: 4}[slot]

            @pl.when(is_mid)
            def _():
                came.wait_recv()
                add_to(slot, h, r.dxz, at)

            go(dx_mid[slot][h], is_mid)

        ig_rows = [pl.ds(pl.multiple_of(t * TM + h * HR, HR), HR) for h in range(2)]
        ig_local = [local(r.igm.at[half(0, h)], r.ig_out.at[ig_rows[h]]) for h in range(2)]
        ig_send = [remote(r.igm.at[half(0, h)], r.ig_out.at[ig_rows[h]], y_peer) for h in range(2)]

        def dx_out(h):
            rows = slice(h * HR, (h + 1) * HR)
            dx_y[0][h].wait_recv()
            r.gmix[rows] += r.dxy[0, rows].astype(F32)

            @pl.when(is_mid)
            def _():
                dx_end[1][h].wait_recv()
                dx_mid[3][h].wait_recv()
                r.gmix[rows] += r.dxz[2, rows].astype(F32) + r.dxz[3, rows].astype(F32)

            @pl.when(is_end)
            def _():
                dx_mid[1][h].wait_recv()
                r.gmix[rows] += r.dxz[5, rows].astype(F32)

            r.igm[rows] = r.gmix[rows].astype(BF16)
            ig_local[h].start()
            go(ig_send[h])


        def key_value_tiles(which):
            rows = half_rows(which)
            r.ub[rows, :] = nn(r.xt[rows, :], dkv[...]).astype(BF16)

        def query_output_tiles(which):
            rows = half_rows(which)
            r.ua[rows, 0:W] = nn(r.xt[rows, 0:T], r.dq[...]).astype(BF16)
            cols = pl.ds(pl.multiple_of(half_of(which) * W, 128), W)
            r.ua[rows, W:] = tn(r.att[...], r.gm[:, cols]).astype(BF16)

        def query_grads():
            r.dq[...] = (acc[...].reshape(W, T).T * scale).astype(BF16)
            r.ls[0, 0:1, :] = column_sum(r.dq[...].astype(F32))
            r.ls[0, 1:2, :] = column_sum(dkv[:, W:].astype(F32))
            r.ls[0, 2:8, :] = jnp.zeros((6, W), F32)

        def dx_own():
            r.xall[0, 0:TM] = (dx_rows(0, peer_rows) + nt(r.dq[peer_rows, :], r.wqkv[:, :W])).astype(BF16)
            for h in range(2):
                go(dx_y[0][h])
            r.gmix[...] += dx_rows(0, my_rows) + nt(r.dq[my_rows, :], r.wqkv[:, :W])

        shrink_tiles(0)
        s1.send(0)
        s2.send(0)
        other_slopes()
        shrink_tiles(1)
        expand_tiles(0)
        e1.send(0)
        e2.send(0)
        s1.add(0)
        s1.za()
        s2.forward(0)
        go(oy_send)
        expand_tiles(1)
        sum_blocks()
        grad_heads()
        e1.forward(0)
        set_bias(3)

        def beside_31():
            e2.forward(0)

        run(lambda p: pull(3, p), {1: beside_31})
        s2.add(1)
        s2.za()
        s1.zb()
        dx_part(3)
        set_bias(2)

        def beside_21():
            e1.add(1)
            e1.za()

        run(lambda p: pull(2, p), {1: beside_21})
        s2.zb()
        dx_part(2)
        dx_sum(3, 0)
        early_start(0)
        s1.zc()
        set_bias(1)

        def beside_11():
            s2.zc()
            e1.zb()
            e2.add(1)
            e2.za()

        run(lambda p: pull(1, p), {1: beside_11})
        set_bias(0)

        def beside_00():
            s2.zd()
            dx_sum(2, 0)
            dx_pass(2, 0)
            s1.zd()
            s1.send(2)

        run(lambda p: pull(0, p), {0: beside_00})
        s1.add(2)
        s1.spread(2)
        query_grads()
        e2.zb()
        e1.zc()
        key_value_tiles(0)
        ub.send(0)
        query_output_tiles(0)
        ua.send(0)
        early_finish(0)
        s1.back(2)
        s2.ze()
        key_value_tiles(1)
        ub.forward(0)
        e1.zd()
        query_output_tiles(1)
        dx_pass(3, 0)
        e2.zc()
        s2.zf()
        dx_sum(3, 1)
        dx_own()
        e1.ze()
        late_start(0)
        late_finish(0)
        e2.zd()
        ua.forward(0)
        ub.forward(1)
        e1.zf()
        late_finish(1)
        e2.ze()
        ub.forward(2)
        ua.forward(1)
        early_finish(1)
        e1.zg()
        ub.turn()
        s2.zg()
        early_finish(2)
        e2.zf()
        dx_part(1)
        ua.forward(2)
        dx_sum(2, 1)
        ub.back(3)
        dx_pass(2, 1)
        ua.turn()
        s1.ze()
        e2.zg()
        dx_sum(1, 0)
        dx_pass(1, 0)
        ub.back(2)
        ua.back(3)
        e1.back(1)
        dx_sum(1, 1)
        dx_pass(1, 1)
        s1.zf()
        ua.back(2)
        dx_pass(3, 1)
        e1.store()
        early_finish(3)
        dx_out(0)
        e2.back(1)
        old_sends = len(unsent)
        s2.back(1)
        dx_out(1)
        late_finish(2)
        ub.back(1)
        ua.back(1)
        s2.store()
        s1.zg()
        early_finish(4)
        wait_first(old_sends)
        ua.store()
        e2.store()
        late_finish(3)
        ub.store()
        s1.store()
        small_copies = (local(r.es.at[1], r.small_out), local(r.ls.at[0], r.late_out))
        for copy in small_copies:
            copy.start()
        oy_local.wait()
        oy_send.wait_recv()
        for h in range(2):
            ig_local[h].wait()
            ig_send[h].wait_recv()
        for copy in small_copies:
            copy.wait()
        for unit in (s1, s2, e1, e2, ua, ub):
            unit.stored.wait()
        for p in range(HP):
            att_copy(p).wait_send()
        wait_sends()

    return kernel


def layer_call(sh, args):
    T, TM, D, W, F = sh.tokens, sh.mine, sh.width, sh.hw, sh.units
    HP = sh.pairs
    any_spec = pl.BlockSpec(memory_space=pl.ANY)
    vmem_spec = pl.BlockSpec(memory_space=pltpu.VMEM)
    ins = dict(
        seg_in=vmem_spec, qb_in=vmem_spec, vb_in=vmem_spec, ob_in=vmem_spec, ag_in=vmem_spec,
        as_in=vmem_spec, eb_in=vmem_spec, sb_in=vmem_spec, fg_in=vmem_spec, fs_in=vmem_spec,
        x_in=any_spec, wq_in=any_spec, wk_in=any_spec, wv_in=any_spec,
        wo_in=any_spec, we_in=any_spec, ws_in=any_spec, cot_in=any_spec,
    )
    outs = dict(
        out=((T, D), BF16, any_spec),
        ig_out=((T, D), BF16, any_spec),
        ue_out=((D, F), BF16, any_spec),
        us_out=((F, D), BF16, any_spec),
        ua_out=((D, 2 * W), BF16, any_spec),
        ub_out=((D, 2 * W), BF16, any_spec),
        small_out=((8, D), F32, any_spec),
        late_out=((8, W), F32, any_spec),
    )
    vm = lambda shape, kind: pltpu.VMEM(shape, kind)
    scratch = dict(
        send=pltpu.SemaphoreType.DMA((224,)),
        recv=pltpu.SemaphoreType.DMA((224,)),
        local=pltpu.SemaphoreType.DMA((32,)),
        xall=vm((4, T, D), BF16),
        xt=vm((D, 4 * T), BF16),
        wqkv=vm((D, 3 * W), BF16),
        wo=vm((2 * W, D), BF16),
        we=vm((2, D, F), BF16),
        ws=vm((2, F, D), BF16),
        eb=vm((2, 1, F), F32),
        cot=vm((TM, D), BF16),
        segs=vm((4, 1, T), F32),
        bias=vm((T, T), F32),
        kv=vm((4, HP, 2, T, 128), BF16),
        qm=vm((2 * HP, T, 128), BF16),
        dm=vm((2 * HP, T, 128), BF16),
        m_s=vm((2 * HP, 1, T), F32),
        l_s=vm((2 * HP, 1, T), F32),
        delta=vm((2 * HP, 1, T), F32),
        acc=vm((2 * HP, 64, T), F32),
        att=vm((T, W), BF16),
        att_o=vm((TM, W), BF16),
        n1=vm((TM, D), F32),
        r1=vm((TM, 128), F32),
        sec=vm((TM, D), F32),
        gf=vm((TM, D), F32),
        gmix=vm((TM, D), F32),
        fl=vm((T, D), BF16),
        flt=vm((D, T), BF16),
        gs=vm((T, D), BF16),
        gm=vm((T, D), BF16),
        gp=vm((2, TM, F), F32),
        hid=vm((T, F), BF16),
        gpre=vm((T, F), BF16),
        oy=vm((TM, D), BF16),
        small=vm((8, D), F32),
        es=vm((2, 8, D), F32),
        es_r=vm((5, 8, D), F32),
        ls=vm((2, 8, W), F32),
        ls_r=vm((4, 8, W), F32),
        dkv=vm((4 * T, 2 * W), BF16),
        dq=vm((T, W), BF16),
        dxy=vm((4, TM, D), BF16),
        dxz=vm((6, TM, D), BF16),
        igm=vm((TM, D), BF16),
        ua=vm((D, 2 * W), BF16),
        ub=vm((D, 2 * W), BF16),
        s0=vm((D, D), BF16),
        e0=vm((2, D // 2, D), BF16),
        z0=vm((3 * (D // 8), D), BF16),
        z1=vm((2 * (D // 8), D), BF16),
        z2=vm((D // 8, D), BF16),
        z3=vm((D // 16, D), BF16),
        x0=vm((4, D // 4, D), BF16),
        l0=vm((4, 3 * (D // 16), D), BF16),
        l1=vm((4, 2 * (D // 16), D), BF16),
        l2=vm((4, D // 16, D), BF16),
        p0=vm((2, D // 2, D), BF16),
        p1=vm((2, D // 4, D), BF16),
        p2=vm((2, D // 8, D), BF16),
        p3=vm((2, D // 16, D), BF16),
    )
    names = list(ins) + list(outs) + list(scratch)
    return pl.pallas_call(
        make_kernel(sh, names),
        out_shape=[jax.ShapeDtypeStruct(o[0], o[1]) for o in outs.values()],
        in_specs=list(ins.values()),
        out_specs=[o[2] for o in outs.values()],
        scratch_shapes=list(scratch.values()),
        compiler_params=pltpu.CompilerParams(
            collective_id=0, has_side_effects=True, vmem_limit_bytes=63 * 1024 * 1024
        ),
        name="layer",
    )(*args)


def finish_kernel(sh, names, *refs):
    r = types.SimpleNamespace(**dict(zip(names, refs)))
    W = sh.hw
    half = sh.units // 2
    pieces = []
    for at in range(2):
        pieces.append((r.us.at[pl.ds(at * half, half)], r.us_v.at[at], r.usf.at[at], r.us_out.at[pl.ds(at * half, half)]))
    for at in range(2):
        rows = pl.ds(at * W, W)
        pieces.append((r.ue.at[rows], r.ue_v.at[at], r.uef.at[at], r.ue_out.at[rows]))
    cols = [pl.ds(0, W), pl.ds(W, W)]
    pieces.append((r.ub.at[:, cols[0]], r.ab_v.at[0], r.abf.at[0], r.wk_out))
    pieces.append((r.ub.at[:, cols[1]], r.ab_v.at[1], r.abf.at[1], r.wv_out))
    pieces.append((r.ua.at[:, cols[0]], r.ab_v.at[2], r.abf.at[2], r.wq_out))
    for at in range(2):
        rows = pl.ds(at * W, W)
        pieces.append((r.ua.at[rows, cols[1]], r.o_v.at[at], r.of.at[at], r.wo_out.at[:, cols[at]]))
    pieces.append((r.ig, r.ig_v, r.igf, r.ig_out))
    taken = pltpu.make_async_copy(r.out, r.out_v, r.sems.at[0])
    taken.start()
    reads = [pltpu.make_async_copy(p[0], p[1], r.sems.at[1 + k]) for k, p in enumerate(pieces)]
    for copy in reads:
        copy.start()
    at_small = 2 * len(pieces) + 2
    small_reads = [
        pltpu.make_async_copy(r.small, r.small_v, r.sems.at[at_small]),
        pltpu.make_async_copy(r.late, r.late_v, r.sems.at[at_small + 1]),
    ]
    for copy in small_reads:
        copy.start()
    taken.wait()
    passed = pltpu.make_async_copy(r.out_v, r.out_out, r.sems.at[2 * len(pieces) + 1])
    passed.start()
    writes = []

    def vectors():
        for copy in small_reads:
            copy.wait()
        for target, at in ((r.fg_v, 0), (r.fs_v, 1), (r.sb_v, 2), (r.ag_v, 3), (r.as_v, 4), (r.ob_v, 5)):
            target[...] = r.small_v[at]
        r.eb_v[0 : sh.width] = r.small_v[6]
        r.eb_v[sh.width :] = r.small_v[7]
        r.qb_v[...] = r.late_v[0]
        r.vb_v[...] = r.late_v[1]
        leaving = (
            (r.fg_v, r.fg), (r.fs_v, r.fs), (r.sb_v, r.sb), (r.ag_v, r.ag), (r.as_v, r.as_), (r.ob_v, r.ob),
            (r.eb_v, r.eb), (r.qb_v, r.qb), (r.vb_v, r.vb),
        )
        for k, (held, target) in enumerate(leaving):
            copy = pltpu.make_async_copy(held, target, r.sems.at[at_small + 2 + k])
            copy.start()
            writes.append(copy)

    for k, (_, low, wide, target) in enumerate(pieces):
        if k == 4:
            vectors()
        reads[k].wait()
        rows = low.shape[0]
        step = 96 if rows % 96 == 0 else 64

        def tile(i, carry):
            at = pl.ds(pl.multiple_of(i * step, step), step)
            wide[at, :] = low[at, :].astype(F32)
            return carry

        lax.fori_loop(0, rows // step, tile, 0)
        copy = pltpu.make_async_copy(wide, target, r.sems.at[1 + len(pieces) + k])
        copy.start()
        writes.append(copy)
    passed.wait()
    for k, copy in enumerate(writes):
        copy.wait()


def finish_call(sh, parts):
    T, D, W, F = sh.tokens, sh.width, sh.hw, sh.units
    any_spec = pl.BlockSpec(memory_space=pl.ANY)
    hbm_spec = pl.BlockSpec(memory_space=pltpu.HBM)
    ins = dict(
        out=hbm_spec, ig=hbm_spec, ue=hbm_spec, us=hbm_spec, ua=hbm_spec, ub=hbm_spec,
        small=hbm_spec, late=hbm_spec,
    )
    outs = dict(
        out_out=((T, D), BF16, any_spec),
        ig_out=((T, D), F32, any_spec),
        wq_out=((D, W), F32, any_spec),
        wk_out=((D, W), F32, any_spec),
        wv_out=((D, W), F32, any_spec),
        qb=((W,), F32, any_spec),
        vb=((W,), F32, any_spec),
        wo_out=((W, D), F32, any_spec),
        ob=((D,), F32, any_spec),
        ag=((D,), F32, any_spec),
        as_=((D,), F32, any_spec),
        ue_out=((D, F), F32, any_spec),
        eb=((F,), F32, any_spec),
        us_out=((F, D), F32, any_spec),
        sb=((D,), F32, any_spec),
        fg=((D,), F32, any_spec),
        fs=((D,), F32, any_spec),
    )
    scratch = dict(
        sems=pltpu.SemaphoreType.DMA((40,)),
        out_v=pltpu.VMEM((T, D), BF16),
        small_v=pltpu.VMEM((8, D), F32),
        late_v=pltpu.VMEM((8, W), F32),
        eb_v=pltpu.VMEM((F,), F32),
    )
    for name in ("fg_v", "fs_v", "sb_v", "ag_v", "as_v", "ob_v"):
        scratch[name] = pltpu.VMEM((D,), F32)
    for name in ("qb_v", "vb_v"):
        scratch[name] = pltpu.VMEM((W,), F32)
    for low, wide, shape in (
        ("us_v", "usf", (2, F // 2, D)),
        ("ue_v", "uef", (2, W, F)),
        ("ab_v", "abf", (3, D, W)),
        ("o_v", "of", (2, W, W)),
        ("ig_v", "igf", (T, D)),
    ):
        scratch[low], scratch[wide] = pltpu.VMEM(shape, BF16), pltpu.VMEM(shape, F32)
    names = list(ins) + list(outs) + list(scratch)
    return pl.pallas_call(
        functools.partial(finish_kernel, sh, names),
        out_shape=[jax.ShapeDtypeStruct(o[0], o[1]) for o in outs.values()],
        in_specs=list(ins.values()),
        out_specs=[o[2] for o in outs.values()],
        scratch_shapes=list(scratch.values()),
        compiler_params=pltpu.CompilerParams(vmem_limit_bytes=63 * 1024 * 1024),
        name="finish",
    )(*parts)


def fused_body(
    mesh_sizes, inputs, segments, query_proj, key_proj, value_proj, query_bias, value_bias, output_proj,
    output_bias, attn_gain, attn_shift, expand_proj, expand_bias, shrink_proj, shrink_bias,
    final_gain, final_shift, cotangent,
):
    sh = Shapes(mesh_sizes, inputs.shape[0], inputs.shape[1], query_proj.shape[1], expand_proj.shape[1])
    parts = layer_call(
        sh,
        (
            segments, query_bias, value_bias, output_bias, attn_gain, attn_shift, expand_bias, shrink_bias,
            final_gain, final_shift, inputs, query_proj, key_proj, value_proj, output_proj, expand_proj,
            shrink_proj, cotangent,
        ),
    )
    return finish_call(sh, parts)


contract_rows = (((0,), (0,)), ((), ()))
contract_cols = (((1,), (1,)), ((), ()))


def matmul(left, right):
    return jnp.dot(left, right, preferred_element_type=jnp.float32)


def inner_rows(left, right):
    return lax.dot_general(left, right, contract_rows, preferred_element_type=jnp.float32)


def inner_cols(left, right):
    return lax.dot_general(left, right, contract_cols, preferred_element_type=jnp.float32)


def norm_forward(values, gain, shift):
    centred = values - jnp.mean(values, axis=-1, keepdims=True)
    spread = jnp.mean(centred * centred, axis=-1, keepdims=True)
    recip = lax.rsqrt(spread + norm_eps)
    normed = centred * recip
    return (normed * gain + shift, normed, recip)


def norm_backward(upstream, normed, recip, gain):
    scaled = upstream * gain
    centred = (
        scaled
        - jnp.mean(scaled, axis=-1, keepdims=True)
        - normed * jnp.mean(scaled * normed, axis=-1, keepdims=True)
    )
    return (centred * recip, jnp.sum(upstream * normed, axis=0), jnp.sum(upstream, axis=0))


def cross_scores(left, right):
    return inner_cols(left, right)


def spread_apply(weights_in, right):
    return matmul(weights_in, right)


def spread_transpose(weights_in, left):
    return inner_rows(weights_in, left)


def body(
    inputs,
    segments,
    query_proj,
    key_proj,
    value_proj,
    query_bias,
    value_bias,
    output_proj,
    output_bias,
    attn_gain,
    attn_shift,
    expand_proj,
    expand_bias,
    shrink_proj,
    shrink_bias,
    final_gain,
    final_shift,
    cotangent,
):
    head_count = query_proj.shape[1] // HEAD_DIM
    scale = HEAD_DIM ** (-0.5)
    seg_local = segments[0]
    queries = (matmul(inputs, query_proj) + query_bias.astype(jnp.float32)).astype(jnp.bfloat16)
    keys = matmul(inputs, key_proj).astype(jnp.bfloat16)
    values = (matmul(inputs, value_proj) + value_bias.astype(jnp.float32)).astype(jnp.bfloat16)
    all_keys, all_values, key_ids = (
        lax.all_gather(keys, "ctx", axis=0, tiled=True),
        lax.all_gather(values, "ctx", axis=0, tiled=True),
        lax.all_gather(seg_local.astype(jnp.bfloat16), "ctx", axis=0, tiled=True),
    )
    query_segs = seg_local.astype(jnp.float32)
    key_segs = key_ids.astype(jnp.float32)
    same_seg = query_segs[:, None] == key_segs[None, :]

    def split_heads(matrix):
        return jnp.swapaxes(matrix.reshape(matrix.shape[0], head_count, HEAD_DIM), 0, 1)

    def join_heads(stack):
        return jnp.swapaxes(stack, 0, 1).reshape(stack.shape[1], head_count * HEAD_DIM)

    query_heads = split_heads(queries)
    key_heads = split_heads(all_keys)
    value_heads = split_heads(all_values)

    def head_forward(state, triple):
        query_head, key_head, value_head = triple
        scores = cross_scores(query_head, key_head) * scale
        scores = jnp.where(same_seg, scores, masked)
        row_max = jnp.max(scores, axis=1, keepdims=True)
        exp_scores = jnp.where(same_seg, jnp.exp(scores - row_max), 0.0)
        row_sum = jnp.sum(exp_scores, axis=1, keepdims=True)
        attn_probs = (exp_scores / row_sum).astype(jnp.bfloat16)
        mixed = spread_apply(attn_probs, value_head)
        return (state, (mixed, row_max + jnp.log(row_sum)))

    mixed_heads, log_sums = lax.scan(head_forward, None, (query_heads, key_heads, value_heads))[1]
    attended = join_heads(mixed_heads).astype(jnp.bfloat16)
    attn_total = lax.psum(matmul(attended, output_proj).astype(jnp.bfloat16), "tensor").astype(
        jnp.float32
    )
    attn_gain_f = attn_gain.astype(jnp.float32)
    first, first_normed, first_recip = norm_forward(
        inputs.astype(jnp.float32) + attn_total + output_bias.astype(jnp.float32),
        attn_gain_f,
        attn_shift.astype(jnp.float32),
    )
    first_low = first.astype(jnp.bfloat16)
    pre_act = matmul(first_low, expand_proj) + expand_bias.astype(jnp.float32)
    activated, gelu_back = jax.vjp(lambda pre_in: jax.nn.gelu(pre_in, approximate=False), pre_act)
    hidden = activated.astype(jnp.bfloat16)
    feed_total = lax.psum(matmul(hidden, shrink_proj).astype(jnp.bfloat16), "tensor").astype(
        jnp.float32
    )
    second = first + feed_total + shrink_bias.astype(jnp.float32)
    final_gain_f = final_gain.astype(jnp.float32)
    output, second_normed, second_recip = norm_forward(
        second, final_gain_f, final_shift.astype(jnp.float32)
    )
    upstream = cotangent.astype(jnp.float32)
    grad_second, fgain_grad, fshift_grad = norm_backward(
        upstream, second_normed, second_recip, final_gain_f
    )
    sbias_grad = jnp.sum(grad_second, axis=0)
    grad_second_low = grad_second.astype(jnp.bfloat16)
    shrink_grad = inner_rows(hidden, grad_second_low)
    grad_act = inner_cols(grad_second_low, shrink_proj)
    grad_pre = gelu_back(grad_act)[0].astype(jnp.bfloat16)
    ebias_grad = jnp.sum(grad_pre.astype(jnp.float32), axis=0)
    expand_grad = inner_rows(first_low, grad_pre)
    grad_first = grad_second + lax.psum(
        inner_cols(grad_pre, expand_proj).astype(jnp.bfloat16), "tensor"
    ).astype(jnp.float32)
    grad_mix, again_grad, ashift_grad = norm_backward(
        grad_first, first_normed, first_recip, attn_gain_f
    )
    obias_grad = jnp.sum(grad_mix, axis=0)
    grad_mix_low = grad_mix.astype(jnp.bfloat16)
    oproj_grad = inner_rows(attended, grad_mix_low)
    grad_attended = inner_cols(grad_mix_low, output_proj).astype(jnp.bfloat16)
    grad_heads = split_heads(grad_attended)

    def head_backward(state, group):
        query_head, key_head, value_head, grad_head, log_sum = group
        scores = cross_scores(query_head, key_head) * scale
        attn_probs = jnp.where(same_seg, jnp.exp(scores - log_sum), 0.0)
        grad_probs = cross_scores(grad_head, value_head)
        row_dot = jnp.sum(attn_probs * grad_probs, axis=1, keepdims=True)
        grad_scores = (attn_probs * (grad_probs - row_dot)).astype(jnp.bfloat16)
        grad_query = spread_apply(grad_scores, key_head) * scale
        grad_key = spread_transpose(grad_scores, query_head) * scale
        grad_value = spread_transpose(attn_probs.astype(jnp.bfloat16), grad_head)
        return (state, (grad_query, grad_key, grad_value))

    query_back, key_back, value_back = lax.scan(
        head_backward, None, (query_heads, key_heads, value_heads, grad_heads, log_sums)
    )[1]
    grad_queries = join_heads(query_back).astype(jnp.bfloat16)
    key_sum, value_sum = (
        lax.psum_scatter(
            join_heads(key_back).astype(jnp.bfloat16), "ctx", scatter_dimension=0, tiled=True
        ).astype(jnp.float32),
        lax.psum_scatter(
            join_heads(value_back).astype(jnp.bfloat16), "ctx", scatter_dimension=0, tiled=True
        ).astype(jnp.float32),
    )
    grad_keys = key_sum.astype(jnp.bfloat16)
    grad_values = value_sum.astype(jnp.bfloat16)
    qbias_grad = jnp.sum(grad_queries.astype(jnp.float32), axis=0)
    vbias_grad = jnp.sum(grad_values.astype(jnp.float32), axis=0)
    query_grad = inner_rows(inputs, grad_queries)
    key_grad = inner_rows(inputs, grad_keys)
    value_grad = inner_rows(inputs, grad_values)
    back_terms = (
        inner_cols(grad_queries, query_proj)
        + inner_cols(grad_keys, key_proj)
        + inner_cols(grad_values, value_proj)
    )
    input_grad = grad_mix + lax.psum(back_terms.astype(jnp.bfloat16), "tensor").astype(jnp.float32)
    (
        query_grad,
        key_grad,
        value_grad,
        qbias_grad,
        vbias_grad,
        oproj_grad,
        obias_grad,
        again_grad,
        ashift_grad,
        expand_grad,
        ebias_grad,
        shrink_grad,
        sbias_grad,
        fgain_grad,
        fshift_grad,
    ) = lax.psum(
        (
            query_grad,
            key_grad,
            value_grad,
            qbias_grad,
            vbias_grad,
            oproj_grad,
            obias_grad,
            again_grad,
            ashift_grad,
            expand_grad,
            ebias_grad,
            shrink_grad,
            sbias_grad,
            fgain_grad,
            fshift_grad,
        ),
        ("dp", "ctx"),
    )
    return (
        output.astype(jnp.bfloat16),
        input_grad,
        query_grad,
        key_grad,
        value_grad,
        qbias_grad,
        vbias_grad,
        oproj_grad,
        obias_grad,
        again_grad,
        ashift_grad,
        expand_grad,
        ebias_grad,
        shrink_grad,
        sbias_grad,
        fgain_grad,
        fshift_grad,
    )


def solution(mesh):
    in_specs = (
        P(("dp", "ctx"), None),
        P("dp", "ctx"),
        P(None, "tensor"),
        P(None, "tensor"),
        P(None, "tensor"),
        P("tensor"),
        P("tensor"),
        P("tensor", None),
        P(),
        P(),
        P(),
        P(None, "tensor"),
        P("tensor"),
        P("tensor", None),
        P(),
        P(),
        P(),
        P(("dp", "ctx"), None),
    )
    out_specs = (
        P(("dp", "ctx"), None),
        P(("dp", "ctx"), None),
        P(None, "tensor"),
        P(None, "tensor"),
        P(None, "tensor"),
        P("tensor"),
        P("tensor"),
        P("tensor", None),
        P(),
        P(),
        P(),
        P(None, "tensor"),
        P("tensor"),
        P("tensor", None),
        P(),
        P(),
        P(),
    )
    sizes = dict(mesh.shape)
    fits = sizes == {"dp": 4, "ctx": 4, "tensor": 2}
    chosen = functools.partial(fused_body, sizes) if fits else body
    return jax.shard_map(chosen, mesh=mesh, in_specs=in_specs, out_specs=out_specs, check_vma=False)
```
